32 devices in a mesh: dp: 4 (over y, x), ctx: 2 (over core), tensor: 4 (over z).
Axes of the slice: x: 2, y: 2, z: 4, core: 2. Of those that a mesh axis runs over, the one named last changes fastest.
Arguments:
- hidden: bfloat16 [4, 1024, 1408], P('dp', 'ctx'), may hold values from -6 to 6
- long_skip_input: bfloat16 [4, 1024, 1408], P('dp', 'ctx'), may hold values from -6 to 6
- condition: bfloat16 [4, 1408], P('dp'), may hold values from -6 to 6
- projected_text_tokens: bfloat16 [4, 333, 1024], P('dp'), may hold values from -6 to 6
- sequence_adapter_index: int32 [4], P('dp'), may hold values from 0 to 7
- skip_projection_weight: bfloat16 [2816, 1408], P('tensor', 'dp'), may hold values from -0.109375 to 0.109375
- shift_modulation_weight: bfloat16 [1408, 1408], P('dp'), may hold values from -0.15625 to 0.15625
- self_query_weight: bfloat16 [1408, 1408], P('dp', 'tensor'), may hold values from -0.15625 to 0.15625
- self_key_weight: bfloat16 [1408, 1408], P('dp', 'tensor'), may hold values from -0.15625 to 0.15625
- self_value_weight: bfloat16 [1408, 1408], P('dp', 'tensor'), may hold values from -0.15625 to 0.15625
- attention_output_weight: bfloat16 [1408, 1408], P('tensor', 'dp'), may hold values from -0.625 to 0.625
- cross_query_weight: bfloat16 [1408, 1408], P('dp', 'tensor'), may hold values from -0.15625 to 0.15625
- cross_key_weight: bfloat16 [1024, 1408], P('dp', 'tensor'), may hold values from -0.1875 to 0.1875
- cross_value_weight: bfloat16 [1024, 1408], P('dp', 'tensor'), may hold values from -0.1875 to 0.1875
- cross_output_weight: bfloat16 [1408, 1408], P('tensor', 'dp'), may hold values from -0.4375 to 0.4375
- feedforward_up_weight: bfloat16 [1408, 6144], P('dp', 'tensor'), may hold values from -0.15625 to 0.15625
- feedforward_down_weight: bfloat16 [6144, 1408], P('tensor', 'dp'), may hold values from -0.078125 to 0.078125
- skip_norm_gain: float32 [2816], replicated, may hold values from 0.1 to 1.9
- norm_gain_rows: float32 [3, 1408], replicated, may hold values from 0.1 to 1.9
- adapter_down_factor: bfloat16 [8, 16, 22272], replicated, may hold values from -0.15625 to 0.15625
- adapter_up_factor: bfloat16 [8, 16, 21632], replicated, may hold values from -0.75 to 0.75
- cotangent: bfloat16 [4, 1024, 1408], P('dp', 'ctx'), may hold values from -6 to 6
Outputs:
- block_out: bfloat16 [4, 1024, 1408], P('dp', 'ctx')
- hidden_grad: float32 [4, 1024, 1408], P('dp', 'ctx')
- skip_grad: float32 [4, 1024, 1408], P('dp', 'ctx')
- condition_gradient: float32 [5632], P(('dp', 'ctx', 'tensor'))
- adapter_down_gradient: float32 [2850816], P(('dp', 'ctx', 'tensor'))
- adapter_up_gradient: float32 [2768896], P(('dp', 'ctx', 'tensor'))
The draws below stay inside these ranges and needn't reach their ends.
Inputs may be any that keep to these rules, and one draw needn't show every extreme that they name: `sequence_adapter_index`: the adapter of each sequence, one of 8.
All inputs are finite; a program needn't handle non-finite values.
Results may differ from the reference program's by a relative error of at most 0.024.
Values may be sent and summed in bfloat16 or wider, within the bound.
A program may use at most 192 MiB of HBM per device.

```python
import math
import jax
import jax.numpy as jnp
import numpy as np
from jax import lax

MODEL_WIDTH = 1408
HEADS = 16
HD = 88
FF = 6144
TW = 1024
TEXT = 333
ADAPTER_RANK = 16
ADAPTER_COUNT = 8
LEN = 1024
SEQS = 4
INPUT_WIDTH_SUM = 22272
OUTPUT_WIDTH_SUM = 21632


def set_ends(values, own_key, least, high):
    shape = values.shape
    place = [jax.random.randint(jax.random.fold_in(own_key, axis), (), 0, shape[axis]) for axis in range(len(shape))]
    values = values.at[tuple(place)].set(least)
    longest = shape.index(max(shape))
    place[longest] = (place[longest] + 1) % shape[longest]
    return values.at[tuple(place)].set(high)


def block_levels(own_key, extent, cuts, least, top_value):
    level, own = 1.0, jax.random.fold_in(own_key, 6)
    for position, shards_of in cuts:
        heights = jnp.exp(jax.random.uniform(jax.random.fold_in(own, position), (shards_of,), jnp.float32, least / len(cuts), top_value / len(cuts)))
        level = level * jnp.repeat(heights, extent[position] // shards_of).reshape([-1 if axis == position else 1 for axis in range(len(extent))])
    return level


def rank_table(amount, skew):
    portions = [(1 << 20) // math.isqrt(standing ** skew) + 1 for standing in range(1, amount + 1)]
    scale = 1 + sum(portions) // (1 << 30)
    return np.cumsum(np.array([max(1, weight // scale) for weight in portions]))


def ranked_ids(rng, shape, number_of, lean):
    table = rank_table(number_of, lean)
    ticket = jax.random.randint(jax.random.fold_in(rng, 1), shape, 0, int(table[number_of - 1]))
    standing = jnp.searchsorted(jnp.asarray(table, jnp.int32), ticket, side="right")
    return jax.random.permutation(jax.random.fold_in(rng, 2), number_of)[standing].astype(jnp.int32)


def centred(stream_key, dims, spread, most, cuts=(), dtype=jnp.bfloat16):
    loudness = block_levels(stream_key, dims, cuts, -0.22, 0.18) if cuts else 1.0
    array = jax.random.normal(stream_key, dims, jnp.float32) * spread * loudness
    return jnp.minimum(jnp.maximum(array, -most), most).astype(dtype)


def setup_inputs(seed: int = 0) -> dict:
    arg_keys = jax.random.split(jax.random.key(seed), 23)
    return {
        "hidden": centred(arg_keys[0], (SEQS, LEN, MODEL_WIDTH), 1.0, 6.0, ((0, 4), (1, 2))),
        "long_skip_input": centred(arg_keys[1], (SEQS, LEN, MODEL_WIDTH), 1.0, 6.0, ((0, 4), (1, 2))),
        "condition": centred(arg_keys[2], (SEQS, MODEL_WIDTH), 1.0, 6.0, ((0, 4),)),
        "projected_text_tokens": centred(arg_keys[3], (SEQS, TEXT, TW), 1.0, 6.0, ((0, 4),)),
        "sequence_adapter_index": set_ends(ranked_ids(arg_keys[4], (SEQS,), ADAPTER_COUNT, 2), jax.random.fold_in(arg_keys[4], 3), 0, ADAPTER_COUNT - 1).astype(jnp.int32),
        "skip_projection_weight": centred(arg_keys[5], (2 * MODEL_WIDTH, MODEL_WIDTH), (2 * MODEL_WIDTH) ** -0.5, 0.109375, ((0, 4), (1, 4))),
        "shift_modulation_weight": centred(arg_keys[6], (MODEL_WIDTH, MODEL_WIDTH), MODEL_WIDTH ** -0.5, 0.15625, ((0, 4),)),
        "self_query_weight": centred(arg_keys[7], (MODEL_WIDTH, MODEL_WIDTH), MODEL_WIDTH ** -0.5, 0.15625, ((0, 4), (1, 4))),
        "self_key_weight": centred(arg_keys[8], (MODEL_WIDTH, MODEL_WIDTH), MODEL_WIDTH ** -0.5, 0.15625, ((0, 4), (1, 4))),
        "self_value_weight": centred(arg_keys[9], (MODEL_WIDTH, MODEL_WIDTH), MODEL_WIDTH ** -0.5, 0.15625, ((0, 4), (1, 4))),
        "attention_output_weight": centred(arg_keys[10], (MODEL_WIDTH, MODEL_WIDTH), (MODEL_WIDTH // 16) ** -0.5, 0.625, ((0, 4), (1, 4))),
        "cross_query_weight": centred(arg_keys[11], (MODEL_WIDTH, MODEL_WIDTH), MODEL_WIDTH ** -0.5, 0.15625, ((0, 4), (1, 4))),
        "cross_key_weight": centred(arg_keys[12], (TW, MODEL_WIDTH), TW ** -0.5, 0.1875, ((0, 4), (1, 4))),
        "cross_value_weight": centred(arg_keys[13], (TW, MODEL_WIDTH), TW ** -0.5, 0.1875, ((0, 4), (1, 4))),
        "cross_output_weight": centred(arg_keys[14], (MODEL_WIDTH, MODEL_WIDTH), (MODEL_WIDTH // 8) ** -0.5, 0.4375, ((0, 4), (1, 4))),
        "feedforward_up_weight": centred(arg_keys[15], (MODEL_WIDTH, FF), MODEL_WIDTH ** -0.5, 0.15625, ((0, 4), (1, 4))),
        "feedforward_down_weight": centred(arg_keys[16], (FF, MODEL_WIDTH), FF ** -0.5, 0.078125, ((0, 4), (1, 4))),
        "skip_norm_gain": jnp.clip(1.0 + 0.18 * jax.random.normal(arg_keys[17], (2 * MODEL_WIDTH,), jnp.float32), 0.1, 1.9),
        "norm_gain_rows": jnp.clip(1.0 + 0.18 * jax.random.normal(arg_keys[18], (3, MODEL_WIDTH), jnp.float32), 0.1, 1.9),
        "adapter_down_factor": centred(arg_keys[19], (ADAPTER_COUNT, ADAPTER_RANK, INPUT_WIDTH_SUM), MODEL_WIDTH ** -0.5, 0.15625),
        "adapter_up_factor": centred(arg_keys[20], (ADAPTER_COUNT, ADAPTER_RANK, OUTPUT_WIDTH_SUM), (4 * ADAPTER_RANK) ** -0.5, 0.75),
        "cotangent": centred(arg_keys[21], (SEQS, LEN, MODEL_WIDTH), 1.0, 6.0, ((0, 4), (1, 2))),
    }


@jax.custom_vjp
def low(v):
    return lax.optimization_barrier(v.astype(jnp.bfloat16)).astype(jnp.float32)

@jax.custom_vjp
def low_back(v):
    return v

def low_keep(v):
    return (low(v), None)

def low_pass(kept, grad):
    return (grad,)

def back_keep(v):
    return (v, None)

def back_low(kept, grad):
    return (low(grad),)
low.defvjp(low_keep, low_pass)
low_back.defvjp(back_keep, back_low)
PRECISE = lax.Precision.HIGHEST
NORM_EPS = 1e-06

def row_norm(values, gain_row):
    centered = values - lax.optimization_barrier(jnp.mean(values, axis=-1, keepdims=True))
    return centered * lax.rsqrt(lax.optimization_barrier(jnp.mean(centered * centered, axis=-1, keepdims=True)) + NORM_EPS) * gain_row

def head_norm(values):
    shaped = values.reshape(values.shape[0], HEADS, HD)
    centered = shaped - lax.optimization_barrier(jnp.mean(shaped, axis=-1, keepdims=True))
    return centered * lax.rsqrt(lax.optimization_barrier(jnp.mean(centered * centered, axis=-1, keepdims=True)) + NORM_EPS)

def linear(input_list, weight_matrix, adapter_pair):
    rank_activation = jnp.dot(input_list, adapter_pair[0].T, precision=PRECISE)
    return jnp.dot(input_list, weight_matrix, precision=PRECISE) + jnp.dot(rank_activation, adapter_pair[1], precision=PRECISE)

def attend(query, key_low, value_low):
    scores = low_back(jnp.einsum('qhd,khd->hqk', query, key_low, precision=PRECISE) * HD ** (-0.5))
    attn_probs = jax.nn.softmax(scores, axis=-1)
    result = jnp.einsum('hqk,khd->qhd', low(attn_probs), value_low, precision=PRECISE)
    return result.reshape(query.shape[0], MODEL_WIDTH)

def split_tables(down_table, up_table):
    in_sizes = [2 * MODEL_WIDTH, MODEL_WIDTH, MODEL_WIDTH, MODEL_WIDTH, MODEL_WIDTH, MODEL_WIDTH, MODEL_WIDTH, TW, TW, MODEL_WIDTH, MODEL_WIDTH, FF]
    out_sizes = [MODEL_WIDTH] * 10 + [FF, MODEL_WIDTH]
    pieces = []
    down_start = 0
    up_start = 0
    for number in range(12):
        pieces.append((down_table[:, down_start:down_start + in_sizes[number]], up_table[:, up_start:up_start + out_sizes[number]]))
        down_start = down_start + in_sizes[number]
        up_start = up_start + out_sizes[number]
    return pieces

def block(tokens, skip_rows, cond_row, text_rows, down_table, up_table, weights, skip_norm_gain, norm_gain_rows):
    skip_projection_weight, shift_modulation_weight, self_query_weight, self_key_weight, self_value_weight, attention_output_weight, cross_query_weight, cross_key_weight, cross_value_weight, cross_output_weight, feedforward_up_weight, feedforward_down_weight = weights
    pieces = split_tables(down_table, up_table)
    joined = low(row_norm(jnp.concatenate([tokens, skip_rows], axis=-1), skip_norm_gain))
    skip_out = low_back(linear(joined, skip_projection_weight, pieces[0]))
    act_low = low(jax.nn.silu(cond_row))[None, :]
    shift_row = linear(act_low, shift_modulation_weight, pieces[1])
    attn_in = low(row_norm(skip_out, norm_gain_rows[0]) + shift_row)
    query_low = low(head_norm(low_back(linear(attn_in, self_query_weight, pieces[2]))))
    key_low = low(head_norm(low_back(linear(attn_in, self_key_weight, pieces[3]))))
    value_low = low_back(low(linear(attn_in, self_value_weight, pieces[4]))).reshape(-1, HEADS, HD)
    attn_low = low_back(low(attend(query_low, key_low, value_low)))
    first_res = skip_out + low_back(linear(attn_low, attention_output_weight, pieces[5]))
    cross_in = low(row_norm(first_res, norm_gain_rows[1]))
    cross_query_low = low(head_norm(low_back(linear(cross_in, cross_query_weight, pieces[6]))))
    cross_key_low = low(head_norm(linear(text_rows, cross_key_weight, pieces[7])))
    cross_value_low = low(linear(text_rows, cross_value_weight, pieces[8])).reshape(-1, HEADS, HD)
    cross_low = low_back(low(attend(cross_query_low, cross_key_low, cross_value_low)))
    second_res = first_res + low_back(linear(cross_low, cross_output_weight, pieces[9]))
    mlp_in = low(row_norm(second_res, norm_gain_rows[2]))
    activated = low(jax.nn.gelu(low_back(linear(mlp_in, feedforward_up_weight, pieces[10])), approximate=True))
    return second_res + low_back(linear(activated, feedforward_down_weight, pieces[11]))

def reference(hidden, long_skip_input, condition, projected_text_tokens, sequence_adapter_index, skip_projection_weight, shift_modulation_weight, self_query_weight, self_key_weight, self_value_weight, attention_output_weight, cross_query_weight, cross_key_weight, cross_value_weight, cross_output_weight, feedforward_up_weight, feedforward_down_weight, skip_norm_gain, norm_gain_rows, adapter_down_factor, adapter_up_factor, cotangent):
    weights = tuple((weight_matrix.astype(jnp.float32) for weight_matrix in (skip_projection_weight, shift_modulation_weight, self_query_weight, self_key_weight, self_value_weight, attention_output_weight, cross_query_weight, cross_key_weight, cross_value_weight, cross_output_weight, feedforward_up_weight, feedforward_down_weight)))
    down_factor_wide = adapter_down_factor.astype(jnp.float32)
    up_factor_wide = adapter_up_factor.astype(jnp.float32)

    def per_sequence(carry, sequence_item):
        down_sum, up_sum = carry
        token_rows, skip_rows, cond_row, text_rows, which_adapter, cot_rows = sequence_item

        def forward(token_arg, skip_arg, cond_arg, down_all, up_all):
            down_table = lax.dynamic_index_in_dim(down_all, which_adapter, 0, keepdims=False)
            up_table = lax.dynamic_index_in_dim(up_all, which_adapter, 0, keepdims=False)
            return block(token_arg, skip_arg, cond_arg, text_rows, down_table, up_table, weights, skip_norm_gain, norm_gain_rows)
        result, pull_back = jax.vjp(forward, token_rows, skip_rows, cond_row, down_factor_wide, up_factor_wide)
        grad_tokens, grad_skip, grad_cond, grad_down, grad_up = pull_back(cot_rows)
        return ((down_sum + grad_down, up_sum + grad_up), (result.astype(jnp.bfloat16), grad_tokens, grad_skip, grad_cond))
    offset_running = (jnp.zeros(adapter_down_factor.shape, jnp.float32), jnp.zeros(adapter_up_factor.shape, jnp.float32))
    sequence_items = (hidden.astype(jnp.float32), long_skip_input.astype(jnp.float32), condition.astype(jnp.float32), projected_text_tokens.astype(jnp.float32), sequence_adapter_index.astype(jnp.int32), cotangent.astype(jnp.float32))
    (down_total, up_total), (block_out, hidden_grad, skip_grad, cond_rows) = lax.scan(per_sequence, offset_running, sequence_items)
    return (block_out, hidden_grad, skip_grad, cond_rows.reshape(-1), down_total.reshape(-1), up_total.reshape(-1))
```

```python
from functools import partial

import jax
import jax.numpy as jnp
from jax import lax
from jax.experimental import pallas as pl
from jax.experimental.pallas import tpu as pltpu
from jax.sharding import PartitionSpec as P

MODEL_WIDTH = 1408
HD = 88
FF = 6144
TW = 1024


PRECISE = lax.Precision.HIGHEST
NORM_EPS = 1e-06


def row_norm(values):
    centered = values - jnp.mean(values, axis=-1, keepdims=True)
    inverse = lax.rsqrt(jnp.mean(centered * centered, axis=-1, keepdims=True) + NORM_EPS)
    return (centered * inverse, inverse)


def head_norm(values, head_width):
    shaped = values.reshape(values.shape[:-1] + (values.shape[-1] // head_width, head_width))
    centered = shaped - jnp.mean(shaped, axis=-1, keepdims=True)
    inverse = lax.rsqrt(jnp.mean(centered * centered, axis=-1, keepdims=True) + NORM_EPS)
    return (centered * inverse, inverse)


def norm_back(normal, inverse, grad_normal):
    return inverse * (
        grad_normal
        - jnp.mean(grad_normal, axis=-1, keepdims=True)
        - normal * jnp.mean(grad_normal * normal, axis=-1, keepdims=True)
    )


def split_parts(values):
    if values.dtype == jnp.bfloat16:
        return [values]
    upper_half = values.astype(jnp.bfloat16)
    lower_half = (values - upper_half.astype(jnp.float32)).astype(jnp.bfloat16)
    return [upper_half, lower_half]


def paired_product(form, left, right):
    total = None
    for left_number, left_part in enumerate(split_parts(left)):
        for right_number, right_part in enumerate(split_parts(right)):
            if left_number + right_number < 2:
                term = jnp.einsum(form, left_part, right_part, preferred_element_type=jnp.float32)
                total = term if total is None else total + term
    return total


def lowrank_out(input_list, weight_matrix, down_piece, up_factor_piece):
    frozen_term = jnp.einsum(
        "gtb,bx->gtx", input_list, weight_matrix, preferred_element_type=jnp.float32
    )
    rank_activation = jnp.einsum(
        "snd,srd->snr", input_list, down_piece, preferred_element_type=jnp.float32
    )
    adapter_term = paired_product("dti,dip->dtp", rank_activation, up_factor_piece)
    return (frozen_term + adapter_term, rank_activation)


def lowrank_back(
    input_list,
    weight_matrix,
    down_piece,
    up_factor_piece,
    rank_activation,
    output_gradient,
    want_input,
):
    upper_gradient = paired_product("pmf,pmz->pfz", rank_activation, output_gradient)
    rank_gradient = paired_product("hzu,hlu->hzl", output_gradient, up_factor_piece)
    grad_lower = paired_product("snr,snd->srd", rank_gradient, input_list)
    if want_input:
        input_gradients = paired_product("lga,wa->lgw", output_gradient, weight_matrix)
        input_gradients = input_gradients + paired_product(
            "snr,srd->snd", rank_gradient, down_piece
        )
        return (input_gradients, grad_lower, upper_gradient)
    return (None, grad_lower, upper_gradient)


def attend_forward(query, key_rows, values_in, scale_factor):
    scores = (
        jnp.einsum("snhe,smhe->shnm", query, key_rows, preferred_element_type=jnp.float32)
        * scale_factor
    )
    row_top = jnp.max(scores, axis=-1, keepdims=True)
    exp_scores = jnp.exp(scores - row_top)
    row_total = jnp.sum(exp_scores, axis=-1, keepdims=True)
    attn_probs = (exp_scores / row_total).astype(jnp.bfloat16)
    result = jnp.einsum(
        "shnm,smhe->snhe", attn_probs, values_in, preferred_element_type=jnp.float32
    )
    return (result, row_top + jnp.log(row_total))


def attend_back(query, key_rows, values_in, log_total, grad_result, scale_factor):
    scores = (
        jnp.einsum("snhe,smhe->shnm", query, key_rows, preferred_element_type=jnp.float32)
        * scale_factor
    )
    attn_probs = jnp.exp(scores - log_total)
    grad_probs = jnp.einsum(
        "snhe,smhe->shnm", grad_result, values_in, preferred_element_type=jnp.float32
    )
    row_inner = jnp.sum(attn_probs * grad_probs, axis=-1, keepdims=True)
    grad_scores = (attn_probs * (grad_probs - row_inner)).astype(jnp.bfloat16)
    grad_query = (
        jnp.einsum("shnm,smhe->snhe", grad_scores, key_rows, preferred_element_type=jnp.float32)
        * scale_factor
    )
    grad_keys = (
        jnp.einsum("shnm,snhe->smhe", grad_scores, query, preferred_element_type=jnp.float32)
        * scale_factor
    )
    grad_values = jnp.einsum(
        "shnm,snhe->smhe",
        attn_probs.astype(jnp.bfloat16),
        grad_result,
        preferred_element_type=jnp.float32,
    )
    return (grad_query, grad_keys, grad_values)


def body(
    hidden,
    long_skip_input,
    condition,
    projected_text_tokens,
    sequence_adapter_index,
    skip_projection_weight,
    shift_modulation_weight,
    self_query_weight,
    self_key_weight,
    self_value_weight,
    attention_output_weight,
    cross_query_weight,
    cross_key_weight,
    cross_value_weight,
    cross_output_weight,
    feedforward_up_weight,
    feedforward_down_weight,
    skip_norm_gain,
    norm_gain_rows,
    adapter_down_factor,
    adapter_up_factor,
    cotangent,
):
    (
        skip_projection_weight,
        shift_modulation_weight,
        self_query_weight,
        self_key_weight,
        self_value_weight,
        attention_output_weight,
        cross_query_weight,
        cross_key_weight,
        cross_value_weight,
        cross_output_weight,
        feedforward_up_weight,
        feedforward_down_weight,
    ) = (
        lax.all_gather(skip_projection_weight, "dp", axis=1, tiled=True),
        lax.all_gather(shift_modulation_weight, "dp", axis=0, tiled=True),
        lax.all_gather(self_query_weight, "dp", axis=0, tiled=True),
        lax.all_gather(self_key_weight, "dp", axis=0, tiled=True),
        lax.all_gather(self_value_weight, "dp", axis=0, tiled=True),
        lax.all_gather(attention_output_weight, "dp", axis=1, tiled=True),
        lax.all_gather(cross_query_weight, "dp", axis=0, tiled=True),
        lax.all_gather(cross_key_weight, "dp", axis=0, tiled=True),
        lax.all_gather(cross_value_weight, "dp", axis=0, tiled=True),
        lax.all_gather(cross_output_weight, "dp", axis=1, tiled=True),
        lax.all_gather(feedforward_up_weight, "dp", axis=0, tiled=True),
        lax.all_gather(feedforward_down_weight, "dp", axis=1, tiled=True),
    )
    tensor_rank = lax.axis_index("tensor")
    tensor_count = lax.axis_size("tensor")
    seqs_local = hidden.shape[0]
    tokens_local = hidden.shape[1]
    local_width = self_query_weight.shape[1]
    heads_local = local_width // HD
    ff_local = feedforward_up_weight.shape[1]
    skip_width = skip_projection_weight.shape[0]
    scale_factor = HD ** (-0.5)
    in_sizes = [
        2 * MODEL_WIDTH,
        MODEL_WIDTH,
        MODEL_WIDTH,
        MODEL_WIDTH,
        MODEL_WIDTH,
        MODEL_WIDTH,
        MODEL_WIDTH,
        TW,
        TW,
        MODEL_WIDTH,
        MODEL_WIDTH,
        FF,
    ]
    out_sizes = [MODEL_WIDTH] * 10 + [FF, MODEL_WIDTH]
    input_offsets = [sum(in_sizes[:number]) for number in range(12)]
    output_offsets = [sum(out_sizes[:number]) for number in range(12)]
    select_adapter = (
        sequence_adapter_index[:, None]
        == jnp.arange(adapter_down_factor.shape[0], dtype=jnp.int32)[None, :]
    )
    choose_wide = select_adapter.astype(jnp.float32)
    down_seq = jnp.einsum(
        "fn,nge->fge",
        select_adapter.astype(jnp.bfloat16),
        adapter_down_factor,
        preferred_element_type=jnp.float32,
    ).astype(jnp.bfloat16)
    up_seq = jnp.einsum(
        "fn,nge->fge",
        select_adapter.astype(jnp.bfloat16),
        adapter_up_factor,
        preferred_element_type=jnp.float32,
    ).astype(jnp.bfloat16)

    def down_full(number):
        return down_seq[:, :, input_offsets[number] : input_offsets[number] + in_sizes[number]]

    def up_full(number):
        return up_seq[:, :, output_offsets[number] : output_offsets[number] + out_sizes[number]]

    def down_local(number, span_width):
        return lax.dynamic_slice_in_dim(
            down_seq, input_offsets[number] + tensor_rank * span_width, span_width, 2
        )

    def up_local(number, span_width):
        return lax.dynamic_slice_in_dim(
            up_seq, output_offsets[number] + tensor_rank * span_width, span_width, 2
        )

    def to_slots(grad_piece):
        return jnp.einsum("si,srd->ird", choose_wide, grad_piece, precision=PRECISE)

    joined = jnp.concatenate([hidden, long_skip_input], axis=-1).astype(jnp.float32)
    joined_normal, joined_inverse = row_norm(joined)
    joined_low = (joined_normal * skip_norm_gain).astype(jnp.bfloat16)
    joined_part = lax.dynamic_slice_in_dim(joined_low, tensor_rank * skip_width, skip_width, 2)
    skip_partial, skip_rank = lowrank_out(
        joined_part, skip_projection_weight, down_local(0, skip_width), up_full(0)
    )
    skip_out = lax.psum(skip_partial.astype(jnp.bfloat16), "tensor").astype(jnp.float32)
    act_wide, silu_pull = jax.vjp(jax.nn.silu, condition.astype(jnp.float32))
    act_low = act_wide.astype(jnp.bfloat16)[:, None, :]
    shift_row, mod_rank = lowrank_out(act_low, shift_modulation_weight, down_full(1), up_full(1))
    first_normal, first_inverse = row_norm(skip_out)
    attn_in = (first_normal * norm_gain_rows[0] + shift_row).astype(jnp.bfloat16)
    query_proj, query_rank = lowrank_out(
        attn_in, self_query_weight, down_full(2), up_local(2, local_width)
    )
    key_proj, key_rank = lowrank_out(
        attn_in, self_key_weight, down_full(3), up_local(3, local_width)
    )
    value_proj, value_rank = lowrank_out(
        attn_in, self_value_weight, down_full(4), up_local(4, local_width)
    )
    query_normal, query_inverse = head_norm(query_proj, HD)
    key_normal, key_inverse = head_norm(key_proj, HD)
    query_low = query_normal.astype(jnp.bfloat16)
    key_low = key_normal.astype(jnp.bfloat16).reshape(seqs_local, tokens_local, local_width)
    value_low = value_proj.astype(jnp.bfloat16)
    keys_all, values_all = (
        lax.all_gather(key_low, "ctx", axis=1, tiled=True),
        lax.all_gather(value_low, "ctx", axis=1, tiled=True),
    )
    keys_four = keys_all.reshape(seqs_local, -1, heads_local, HD)
    values_four = values_all.reshape(seqs_local, -1, heads_local, HD)
    attn_result, attn_log = attend_forward(query_low, keys_four, values_four, scale_factor)
    attn_low = attn_result.reshape(seqs_local, tokens_local, local_width).astype(jnp.bfloat16)
    attn_partial, out_rank = lowrank_out(
        attn_low, attention_output_weight, down_local(5, local_width), up_full(5)
    )
    first_res = skip_out + lax.psum(attn_partial.astype(jnp.bfloat16), "tensor").astype(jnp.float32)
    second_normal, second_inverse = row_norm(first_res)
    cross_in = (second_normal * norm_gain_rows[1]).astype(jnp.bfloat16)
    cquery_proj, cquery_rank = lowrank_out(
        cross_in, cross_query_weight, down_full(6), up_local(6, local_width)
    )
    ckey_proj, ckey_rank = lowrank_out(
        projected_text_tokens, cross_key_weight, down_full(7), up_local(7, local_width)
    )
    cvalue_proj, cvalue_rank = lowrank_out(
        projected_text_tokens, cross_value_weight, down_full(8), up_local(8, local_width)
    )
    cquery_normal, cquery_inverse = head_norm(cquery_proj, HD)
    ckey_normal, ckey_inverse = head_norm(ckey_proj, HD)
    cquery_low = cquery_normal.astype(jnp.bfloat16)
    ckey_low = ckey_normal.astype(jnp.bfloat16)
    cvalue_low = cvalue_proj.astype(jnp.bfloat16).reshape(seqs_local, -1, heads_local, HD)
    cross_result, cross_log = attend_forward(cquery_low, ckey_low, cvalue_low, scale_factor)
    cross_low = cross_result.reshape(seqs_local, tokens_local, local_width).astype(jnp.bfloat16)
    cross_partial, cout_rank = lowrank_out(
        cross_low, cross_output_weight, down_local(9, local_width), up_full(9)
    )
    second_res = first_res + lax.psum(cross_partial.astype(jnp.bfloat16), "tensor").astype(
        jnp.float32
    )
    third_normal, third_inverse = row_norm(second_res)
    mlp_in = (third_normal * norm_gain_rows[2]).astype(jnp.bfloat16)
    up_proj, up_rank = lowrank_out(
        mlp_in, feedforward_up_weight, down_full(10), up_local(10, ff_local)
    )
    activated, gelu_pull = jax.vjp(partial(jax.nn.gelu, approximate=True), up_proj)
    activated_low = activated.astype(jnp.bfloat16)
    down_partial, down_rank = lowrank_out(
        activated_low, feedforward_down_weight, down_local(11, ff_local), up_full(11)
    )
    block_out = second_res + lax.psum(down_partial.astype(jnp.bfloat16), "tensor").astype(
        jnp.float32
    )
    grad_act, grad_down_lower, grad_down_upper = lowrank_back(
        activated_low,
        feedforward_down_weight,
        down_local(11, ff_local),
        up_full(11),
        down_rank,
        cotangent,
        True,
    )
    grad_pre = gelu_pull(grad_act)[0].astype(jnp.bfloat16)
    grad_mlp_in, grad_up_lower, grad_up_upper = lowrank_back(
        mlp_in,
        feedforward_up_weight,
        down_full(10),
        up_local(10, ff_local),
        up_rank,
        grad_pre,
        True,
    )
    grad_mlp_in = lax.psum(grad_mlp_in.astype(jnp.bfloat16), "tensor").astype(jnp.float32)
    grad_second = cotangent.astype(jnp.float32) + norm_back(
        third_normal, third_inverse, grad_mlp_in * norm_gain_rows[2]
    )
    grad_cross_low, grad_cout_lower, grad_cout_upper = lowrank_back(
        cross_low,
        cross_output_weight,
        down_local(9, local_width),
        up_full(9),
        cout_rank,
        grad_second.astype(jnp.bfloat16),
        True,
    )
    grad_cross_result = grad_cross_low.astype(jnp.bfloat16).reshape(
        seqs_local, tokens_local, heads_local, HD
    )
    grad_cquery, grad_ckey, grad_cvalue = attend_back(
        cquery_low, ckey_low, cvalue_low, cross_log, grad_cross_result, scale_factor
    )
    grad_cquery_proj = (
        norm_back(cquery_normal, cquery_inverse, grad_cquery)
        .reshape(seqs_local, tokens_local, local_width)
        .astype(jnp.bfloat16)
    )
    grad_ckey_proj = norm_back(ckey_normal, ckey_inverse, grad_ckey).reshape(
        seqs_local, -1, local_width
    )
    none_first, grad_ckey_lower, grad_ckey_upper = lowrank_back(
        projected_text_tokens,
        cross_key_weight,
        down_full(7),
        up_local(7, local_width),
        ckey_rank,
        grad_ckey_proj,
        False,
    )
    none_second, grad_cvalue_lower, grad_cvalue_upper = lowrank_back(
        projected_text_tokens,
        cross_value_weight,
        down_full(8),
        up_local(8, local_width),
        cvalue_rank,
        grad_cvalue.reshape(seqs_local, -1, local_width),
        False,
    )
    grad_cross_in, grad_cquery_lower, grad_cquery_upper = lowrank_back(
        cross_in,
        cross_query_weight,
        down_full(6),
        up_local(6, local_width),
        cquery_rank,
        grad_cquery_proj,
        True,
    )
    grad_cross_in = lax.psum(grad_cross_in.astype(jnp.bfloat16), "tensor").astype(jnp.float32)
    grad_first = grad_second + norm_back(
        second_normal, second_inverse, grad_cross_in * norm_gain_rows[1]
    )
    grad_attn_low, grad_aout_lower, grad_aout_upper = lowrank_back(
        attn_low,
        attention_output_weight,
        down_local(5, local_width),
        up_full(5),
        out_rank,
        grad_first.astype(jnp.bfloat16),
        True,
    )
    grad_attn_result = grad_attn_low.astype(jnp.bfloat16).reshape(
        seqs_local, tokens_local, heads_local, HD
    )
    grad_query, grad_keys_all, grad_values_all = attend_back(
        query_low, keys_four, values_four, attn_log, grad_attn_result, scale_factor
    )
    grad_keys, grad_values = (
        lax.psum_scatter(
            grad_keys_all.reshape(seqs_local, -1, local_width).astype(jnp.bfloat16),
            "ctx",
            scatter_dimension=1,
            tiled=True,
        ).astype(jnp.float32),
        lax.psum_scatter(
            grad_values_all.reshape(seqs_local, -1, local_width).astype(jnp.bfloat16),
            "ctx",
            scatter_dimension=1,
            tiled=True,
        ).astype(jnp.float32),
    )
    grad_query_proj = (
        norm_back(query_normal, query_inverse, grad_query)
        .reshape(seqs_local, tokens_local, local_width)
        .astype(jnp.bfloat16)
    )
    grad_key_proj = (
        norm_back(
            key_normal, key_inverse, grad_keys.reshape(seqs_local, tokens_local, heads_local, HD)
        )
        .reshape(seqs_local, tokens_local, local_width)
        .astype(jnp.bfloat16)
    )
    grad_value_proj = grad_values.astype(jnp.bfloat16)
    grad_in_query, grad_query_lower, grad_query_upper = lowrank_back(
        attn_in,
        self_query_weight,
        down_full(2),
        up_local(2, local_width),
        query_rank,
        grad_query_proj,
        True,
    )
    grad_in_key, grad_key_lower, grad_key_upper = lowrank_back(
        attn_in,
        self_key_weight,
        down_full(3),
        up_local(3, local_width),
        key_rank,
        grad_key_proj,
        True,
    )
    grad_in_value, grad_value_lower, grad_value_upper = lowrank_back(
        attn_in,
        self_value_weight,
        down_full(4),
        up_local(4, local_width),
        value_rank,
        grad_value_proj,
        True,
    )
    grad_attn_in = lax.psum(
        (grad_in_query + grad_in_key + grad_in_value).astype(jnp.bfloat16), "tensor"
    ).astype(jnp.float32)
    grad_shift = jnp.sum(grad_attn_in, axis=1, keepdims=True) / tensor_count
    grad_act_low, grad_mod_lower, grad_mod_upper = lowrank_back(
        act_low, shift_modulation_weight, down_full(1), up_full(1), mod_rank, grad_shift, True
    )
    grad_condition = silu_pull(grad_act_low[:, 0, :])[0]
    grad_skip_out = grad_first + norm_back(
        first_normal, first_inverse, grad_attn_in * norm_gain_rows[0]
    )
    grad_joined_part, grad_skip_lower, grad_skip_upper = lowrank_back(
        joined_part,
        skip_projection_weight,
        down_local(0, skip_width),
        up_full(0),
        skip_rank,
        grad_skip_out.astype(jnp.bfloat16),
        True,
    )
    grad_joined = lax.all_gather(
        grad_joined_part.astype(jnp.bfloat16), "tensor", axis=2, tiled=True
    ).astype(grad_joined_part.dtype)
    grad_joined_full = norm_back(joined_normal, joined_inverse, grad_joined * skip_norm_gain)
    hidden_grad = grad_joined_full[:, :, :MODEL_WIDTH]
    skip_grad = grad_joined_full[:, :, MODEL_WIDTH:]
    lower_factor_parts = [
        (0, grad_skip_lower, True),
        (1, grad_mod_lower, False),
        (2, grad_query_lower, False),
        (3, grad_key_lower, False),
        (4, grad_value_lower, False),
        (5, grad_aout_lower, True),
        (6, grad_cquery_lower, False),
        (7, grad_ckey_lower, False),
        (8, grad_cvalue_lower, False),
        (9, grad_cout_lower, True),
        (10, grad_up_lower, False),
        (11, grad_down_lower, True),
    ]
    upper_factor_parts = [
        (0, grad_skip_upper, False),
        (1, grad_mod_upper, False),
        (2, grad_query_upper, True),
        (3, grad_key_upper, True),
        (4, grad_value_upper, True),
        (5, grad_aout_upper, False),
        (6, grad_cquery_upper, True),
        (7, grad_ckey_upper, True),
        (8, grad_cvalue_upper, True),
        (9, grad_cout_upper, False),
        (10, grad_up_upper, True),
        (11, grad_down_upper, False),
    ]
    slot_total = adapter_down_factor.shape[0]
    rank_total = adapter_down_factor.shape[1]
    cond_buffer = jnp.zeros((lax.axis_size("dp") * seqs_local, MODEL_WIDTH), jnp.float32)
    cond_buffer = lax.dynamic_update_slice_in_dim(
        cond_buffer, grad_condition, lax.axis_index("dp") * seqs_local, 0
    )
    cond_flat = cond_buffer.reshape(-1)

    def dense_table(parts_list, starts, total_width, row_count, slot_pieces):
        table = jnp.zeros((row_count, total_width), jnp.float32)
        for position, (number, grad_piece, is_local) in enumerate(parts_list):
            span_width = grad_piece.shape[2]
            column_start = starts[number] + tensor_rank * span_width if is_local else starts[number]
            table = lax.dynamic_update_slice_in_dim(table, slot_pieces[position], column_start, 1)
        return table

    down_factor_slots = [
        to_slots(grad_piece).reshape(slot_total * rank_total, -1)
        for number, grad_piece, is_local in lower_factor_parts
    ]
    up_factor_slots = [
        to_slots(grad_piece).reshape(slot_total * rank_total, -1)
        for number, grad_piece, is_local in upper_factor_parts
    ]
    down_compact = jnp.concatenate(down_factor_slots, axis=1)
    up_compact = jnp.concatenate(up_factor_slots, axis=1)
    cond_rows, down_rows, up_rows = (
        lax.psum_scatter(
            cond_flat.astype(jnp.bfloat16), ("dp", "ctx"), scatter_dimension=0, tiled=True
        ).astype(jnp.float32),
        lax.psum_scatter(
            down_compact.astype(jnp.bfloat16), ("dp", "ctx"), scatter_dimension=0, tiled=True
        ).astype(jnp.float32),
        lax.psum_scatter(
            up_compact.astype(jnp.bfloat16), ("dp", "ctx"), scatter_dimension=0, tiled=True
        ).astype(jnp.float32),
    )
    row_count = down_rows.shape[0]
    down_widths = [grad_piece.shape[2] for number, grad_piece, is_local in lower_factor_parts]
    up_widths = [grad_piece.shape[2] for number, grad_piece, is_local in upper_factor_parts]
    down_pieces = [
        down_rows[:, sum(down_widths[:position]) : sum(down_widths[: position + 1])]
        for position in range(12)
    ]
    up_pieces = [
        up_rows[:, sum(up_widths[:position]) : sum(up_widths[: position + 1])]
        for position in range(12)
    ]
    down_block = dense_table(
        lower_factor_parts, input_offsets, adapter_down_factor.shape[2], row_count, down_pieces
    ).reshape(-1)
    up_block = dense_table(
        upper_factor_parts, output_offsets, adapter_up_factor.shape[2], row_count, up_pieces
    ).reshape(-1)
    condition_gradient, adapter_down_gradient, adapter_up_gradient = (
        lax.psum_scatter(
            cond_rows.astype(jnp.bfloat16), "tensor", scatter_dimension=0, tiled=True
        ).astype(jnp.float32),
        lax.psum_scatter(
            down_block.astype(jnp.bfloat16), "tensor", scatter_dimension=0, tiled=True
        ).astype(jnp.float32),
        lax.psum_scatter(
            up_block.astype(jnp.bfloat16), "tensor", scatter_dimension=0, tiled=True
        ).astype(jnp.float32),
    )
    return (
        block_out.astype(jnp.bfloat16),
        hidden_grad,
        skip_grad,
        condition_gradient,
        adapter_down_gradient,
        adapter_up_gradient,
    )


BF = jnp.bfloat16
F32 = jnp.float32
MESH_ID = pl.DeviceIdType.MESH
RANK = 16
VMEM_BYTES = 60 << 20


def dot_nn(left, right):
    return jnp.dot(left, right, preferred_element_type=F32)


def dot_nt(left, right):
    return lax.dot_general(left, right, (((1,), (1,)), ((), ())), preferred_element_type=F32)


def dot_tn(left, right):
    return lax.dot_general(left, right, (((0,), (0,)), ((), ())), preferred_element_type=F32)


def stats(values):
    centered = values - jnp.mean(values, axis=-1, keepdims=True)
    inverse = lax.rsqrt(jnp.mean(centered * centered, axis=-1, keepdims=True) + NORM_EPS)
    return centered * inverse, inverse


def greet(partners):
    barrier = pltpu.get_barrier_semaphore()
    for condition, device in partners:
        @pl.when(condition)
        def _(device=device):
            pl.semaphore_signal(barrier, inc=1, device_id=device, device_id_type=MESH_ID)
    expected = sum(jnp.where(condition, 1, 0) for condition, _ in partners)
    pl.semaphore_wait(barrier, expected)


def line_partners(me, count):
    return [(me > 0, {"tensor": lax.max(me - 1, 0)}), (me < count - 1, {"tensor": lax.min(me + 1, count - 1)})]


def push(source, target, send_sem, recv_sem, device):
    return pltpu.make_async_remote_copy(
        src_ref=source,
        dst_ref=target,
        send_sem=send_sem,
        recv_sem=recv_sem,
        device_id=device,
        device_id_type=MESH_ID,
    )


class Line:
    def __init__(self, me, count, send_right, recv_left, send_left, recv_right):
        self.me, self.count = me, count
        self.sems = (send_right, recv_left, send_left, recv_right)
        self.left = {"tensor": lax.max(me - 1, 0)}
        self.right = {"tensor": lax.min(me + 1, count - 1)}
        self.has_left, self.has_right = me > 0, me < count - 1

    def to_right(self, source, target, slot):
        return push(source, target, self.sems[0].at[slot], self.sems[1].at[slot], self.right)

    def to_left(self, source, target, slot):
        return push(source, target, self.sems[2].at[slot], self.sems[3].at[slot], self.left)


def line_reduce_all(line, steps, compute, partial_ref, from_left, from_right, stage_right, stage_left, finish):
    me, count = line.me, line.count
    far = count - 1 - me

    def step(number, carry):
        @pl.when(number < steps)
        def _():
            compute(number)

        slot_r = number - me

        @pl.when((slot_r >= 0) & (slot_r < steps))
        def _():
            slot = lax.clamp(0, slot_r, steps - 1)

            @pl.when(line.has_left)
            def _():
                line.to_right(stage_right.at[slot], from_left.at[slot], slot).wait_recv()

            @pl.when(line.has_right)
            def _():
                @pl.when(line.has_left)
                def _():
                    total = partial_ref[slot].astype(F32) + from_left[slot].astype(F32)
                    stage_right[slot] = total.astype(BF)

                @pl.when(jnp.logical_not(line.has_left))
                def _():
                    stage_right[slot] = partial_ref[slot]

                line.to_right(stage_right.at[slot], from_left.at[slot], slot).start()

        slot_l = number - far

        @pl.when((slot_l >= 0) & (slot_l < steps))
        def _():
            slot = lax.clamp(0, slot_l, steps - 1)

            @pl.when(line.has_right)
            def _():
                line.to_left(stage_left.at[slot], from_right.at[slot], slot).wait_recv()

            @pl.when(line.has_left)
            def _():
                @pl.when(line.has_right)
                def _():
                    total = partial_ref[slot].astype(F32) + from_right[slot].astype(F32)
                    stage_left[slot] = total.astype(BF)

                @pl.when(jnp.logical_not(line.has_right))
                def _():
                    stage_left[slot] = partial_ref[slot]

                line.to_left(stage_left.at[slot], from_right.at[slot], slot).start()

        slot_f = number - lax.max(me, far)

        @pl.when((slot_f >= 0) & (slot_f < steps))
        def _():
            slot = lax.clamp(0, slot_f, steps - 1)

            @pl.when(jnp.logical_not(line.has_left))
            def _():
                finish(slot, partial_ref[slot].astype(F32) + from_right[slot].astype(F32))

            @pl.when(line.has_left)
            def _():
                @pl.when(line.has_right)
                def _():
                    finish(
                        slot,
                        partial_ref[slot].astype(F32)
                        + from_left[slot].astype(F32)
                        + from_right[slot].astype(F32),
                    )

                @pl.when(jnp.logical_not(line.has_right))
                def _():
                    finish(slot, partial_ref[slot].astype(F32) + from_left[slot].astype(F32))

        return carry

    lax.fori_loop(0, steps + count - 1, step, 0)

    def drain(slot, carry):
        @pl.when(line.has_right)
        def _():
            line.to_right(stage_right.at[slot], from_left.at[slot], slot).wait_send()

        @pl.when(line.has_left)
        def _():
            line.to_left(stage_left.at[slot], from_right.at[slot], slot).wait_send()

        return carry

    lax.fori_loop(0, steps, drain, 0)


def scatter_order(me, count, place):
    near = lax.min(me, count - 1 - me)
    base = count - 1 - 2 * near
    index = place - base
    block = jnp.where(
        place < base,
        count - 1 - place,
        jnp.where(index % 2 == 0, 2 * near - index // 2, index // 2),
    )
    return jnp.where(2 * me > count - 1, count - 1 - block, block)


def line_scatter_step(line, number, partial_ref, from_left, from_right, stage_right, stage_left):
    me, count = line.me, line.count
    block_r = count - 1 - number + me

    @pl.when((number >= me) & line.has_right & (block_r > me))
    def _():
        block = lax.clamp(0, block_r, count - 1)

        @pl.when(line.has_left)
        def _():
            line.to_right(stage_right.at[block], from_left.at[block], block).wait_recv()
            total = partial_ref[block].astype(F32) + from_left[block].astype(F32)
            stage_right[block] = total.astype(BF)

        @pl.when(jnp.logical_not(line.has_left))
        def _():
            stage_right[block] = partial_ref[block]

        line.to_right(stage_right.at[block], from_left.at[block], block).start()

    block_l = number - (count - 1 - me)

    @pl.when((block_l >= 0) & line.has_left & (block_l < me))
    def _():
        block = lax.clamp(0, block_l, count - 1)

        @pl.when(line.has_right)
        def _():
            line.to_left(stage_left.at[block], from_right.at[block], block).wait_recv()
            total = partial_ref[block].astype(F32) + from_right[block].astype(F32)
            stage_left[block] = total.astype(BF)

        @pl.when(jnp.logical_not(line.has_right))
        def _():
            stage_left[block] = partial_ref[block]

        line.to_left(stage_left.at[block], from_right.at[block], block).start()


def line_scatter_finish(line, partial_ref, from_left, from_right, stage_right, stage_left, total_ref):
    me, count = line.me, line.count
    total_ref[...] = partial_ref[me].astype(F32)

    @pl.when(line.has_left)
    def _():
        line.to_right(stage_right.at[me], from_left.at[me], me).wait_recv()
        total_ref[...] += from_left[me].astype(F32)

    @pl.when(line.has_right)
    def _():
        line.to_left(stage_left.at[me], from_right.at[me], me).wait_recv()
        total_ref[...] += from_right[me].astype(F32)

    def drain(block, carry):
        @pl.when(block > me)
        def _():
            line.to_right(stage_right.at[block], from_left.at[block], block).wait_send()

        @pl.when(block < me)
        def _():
            line.to_left(stage_left.at[block], from_right.at[block], block).wait_send()

        return carry

    lax.fori_loop(0, count, drain, 0)


def line_gather_step(line, number, slots):
    me, count = line.me, line.count
    block_l = lax.clamp(0, me - number, count - 1)
    block_r = lax.clamp(0, me + number, count - 1)

    @pl.when(number <= me)
    def _():
        @pl.when(number > 0)
        def _():
            line.to_right(slots.at[block_l], slots.at[block_l], block_l).wait_recv()

        @pl.when(line.has_right)
        def _():
            line.to_right(slots.at[block_l], slots.at[block_l], block_l).start()

    @pl.when(me + number <= count - 1)
    def _():
        @pl.when(number > 0)
        def _():
            line.to_left(slots.at[block_r], slots.at[block_r], block_r).wait_recv()

        @pl.when(line.has_left)
        def _():
            line.to_left(slots.at[block_r], slots.at[block_r], block_r).start()


def line_gather_drain(line, slots):
    me, count = line.me, line.count

    def drain(block, carry):
        @pl.when((block <= me) & line.has_right)
        def _():
            line.to_right(slots.at[block], slots.at[block], block).wait_send()

        @pl.when((block >= me) & line.has_left)
        def _():
            line.to_left(slots.at[block], slots.at[block], block).wait_send()

        return carry

    lax.fori_loop(0, count, drain, 0)


def line_gather(line, slots, compute):
    me, count = line.me, line.count

    def step(number, carry):
        line_gather_step(line, number, slots)

        def side(which, inner):
            block = me + (2 * which - 1) * number

            @pl.when((block >= 0) & (block < count) & ((number > 0) | (which == 0)))
            def _():
                compute(lax.clamp(0, block, count - 1))

            return inner

        return lax.fori_loop(0, 2, side, carry)

    lax.fori_loop(0, count, step, 0)
    line_gather_drain(line, slots)


def xor_place(place, number):
    if number == 0:
        return place
    if number == 1:
        return place + 1 - 2 * (place % 2)
    if number == 2:
        return place + 2 - 4 * (place // 2)
    return 3 - place


def assemble(target, own, pieces, offset, sem, lead=None):
    dp = lax.axis_index("dp")
    core = lax.axis_index("ctx")
    rows = own.shape[-2]
    half = rows // 2
    copies = []

    def view(ref, start, size, place):
        if lead is None:
            return ref.at[pl.ds(start, size), :]
        return ref.at[lead[place], pl.ds(start, size), :]

    copies.append(
        pltpu.make_async_copy(
            view(own, 0, rows, 0), view(target, pl.multiple_of(dp * rows, 16), rows, 1), sem
        )
    )
    first = jnp.where(core == 0, xor_place(dp, 1), xor_place(dp, 2))
    second = jnp.where(core == 0, xor_place(dp, 2), xor_place(dp, 1))
    third = xor_place(dp, 3)
    blocks = (first, second, third, second, first, third)
    halves = (core, core, core, 1 - core, 1 - core, 1 - core)
    for piece, block, which in zip(pieces, blocks, halves):
        start = pl.multiple_of(block * rows + which * half, 16)
        copies.append(
            pltpu.make_async_copy(view(piece, offset, half, 0), view(target, start, half, 1), sem)
        )
    return copies


def call(kernel, inputs, outs, scratch, collective=None, cost=None):
    space = {True: pltpu.VMEM, False: pl.ANY}
    return pl.pallas_call(
        kernel,
        out_shape=[jax.ShapeDtypeStruct(shape, dtype) for shape, dtype, _ in outs],
        in_specs=[pl.BlockSpec(memory_space=space[where]) for _, where in inputs],
        out_specs=[pl.BlockSpec(memory_space=space[where]) for _, _, where in outs],
        scratch_shapes=scratch,
        cost_estimate=cost,
        compiler_params=pltpu.CompilerParams(
            collective_id=collective,
            has_side_effects=collective is not None,
            vmem_limit_bytes=VMEM_BYTES,
        ),
    )(*[array for array, _ in inputs])


def cost_of(flops, moved):
    return pl.CostEstimate(flops=int(flops), bytes_accessed=int(moved), transcendentals=0)


def vmem(*shape, dtype=BF):
    return pltpu.VMEM(shape, dtype)


def dma(*shape):
    return pltpu.SemaphoreType.DMA(shape)


def whole_wait(target, sem):
    pltpu.make_async_copy(target, target, sem).wait()


def rows_of(index, size):
    return pl.ds(pl.multiple_of(index * size, size), size)


def skip_forward(count, own, pieces, hidden, long_skip, part, part_gain, down, up, gain_row, shift_row):
    tokens, width = hidden.shape
    span = part.shape[1]
    block = min(128, tokens)
    chunk = min(64, tokens)
    steps = tokens // chunk
    each = block // chunk

    def kernel(own_ref, *refs):
        piece_refs = refs[:6]
        (hid, lsk, par, pgain, a_ref, b_ref, gain, shift, skip_out, attn_in, w, partial_ref, from_left, from_right,
         stage_right, stage_left, wsem, *sems) = refs[6:]
        me = lax.axis_index("tensor")
        line = Line(me, count, *sems)
        for copy in assemble(w, own_ref, piece_refs, 0, wsem):
            copy.start()
        greet(line_partners(me, count))
        whole_wait(w, wsem)

        def compute(number):
            @pl.when(number % each == 0)
            def _():
                rows = rows_of(number // each, block)
                left = hid[rows, :].astype(F32)
                right = lsk[rows, :].astype(F32)
                mean = (jnp.sum(left, axis=-1, keepdims=True) + jnp.sum(right, axis=-1, keepdims=True)) / (2 * width)
                spread = jnp.sum((left - mean) ** 2, axis=-1, keepdims=True)
                spread += jnp.sum((right - mean) ** 2, axis=-1, keepdims=True)
                inverse = lax.rsqrt(spread / (2 * width) + NORM_EPS)
                x = ((par[rows, :].astype(F32) - mean) * inverse * pgain[...]).astype(BF)
                u = dot_nt(x, a_ref[...]).astype(BF)
                y = (dot_nt(x, w[...]) + dot_nn(u, b_ref[...])).astype(BF)
                for piece in range(each):
                    partial_ref[number + piece] = y[piece * chunk : (piece + 1) * chunk]

        def finish(slot, total):
            rows = rows_of(slot, chunk)
            skip_out[rows, :] = total
            normal, _ = stats(total)
            attn_in[rows, :] = (normal * gain[...] + shift[...]).astype(BF)

        line_reduce_all(line, steps, compute, partial_ref, from_left, from_right, stage_right, stage_left, finish)

    buffers = [vmem(steps, chunk, width) for _ in range(5)]
    return call(
        kernel,
        [(own, False)] + [(piece, False) for piece in pieces]
        + [(array, True) for array in (hidden, long_skip, part, part_gain, down, up, gain_row, shift_row)],
        [((tokens, width), F32, True), ((tokens, width), BF, True)],
        [vmem(width, span)] + buffers + [dma()] + [dma(steps) for _ in range(4)],
        collective=1,
        cost=cost_of(2 * tokens * width * span, 40e6),
    )


def text_forward(heads, text, own_key, own_value, pieces, key_row, value_row, down, up_key, up_value):
    tokens, width = text.shape
    local = own_key.shape[1]

    def kernel(own_k, own_v, *refs):
        piece_refs = refs[:6]
        t_ref, a_ref, bk, bv, out, w, wsem = refs[6:]
        core = lax.axis_index("ctx")

        @pl.when(core == 0)
        def _():
            for copy in assemble(w, own_k, piece_refs, key_row, wsem):
                copy.start()

        @pl.when(core == 1)
        def _():
            for copy in assemble(w, own_v, piece_refs, value_row, wsem):
                copy.start()

        whole_wait(w, wsem)
        x = t_ref[...]
        u = dot_nt(x, a_ref[...]).astype(BF)
        y = dot_nn(x, w[...])

        @pl.when(core == 0)
        def _():
            z = y + dot_nn(u[:, :RANK], bk[...])
            for head in range(heads):
                normal, inverse = stats(z[:, head * HD : (head + 1) * HD])
                upper = inverse.astype(BF)
                lower = (inverse - upper.astype(F32)).astype(BF)
                out[head] = jnp.concatenate([normal.astype(BF), upper, lower], axis=1)

        @pl.when(core == 1)
        def _():
            z = (y + dot_nn(u[:, RANK:], bv[...])).astype(BF)
            filler = jnp.zeros((tokens, 2), BF)
            for head in range(heads):
                out[head] = jnp.concatenate([z[:, head * HD : (head + 1) * HD], filler], axis=1)

    return call(
        kernel,
        [(own_key, False), (own_value, False)] + [(piece, False) for piece in pieces]
        + [(array, True) for array in (text, down, up_key, up_value)],
        [((heads, tokens, HD + 2), BF, True)],
        [vmem(width, local), dma()],
        cost=cost_of(2 * tokens * width * local, 3e6),
    )[0]


def attention_forward(count, heads, attn_in, own_list, pieces, offsets, down, ups, out_down, out_up):
    tokens, width = attn_in.shape
    local = own_list[0].shape[1]
    share = tokens // count
    block = min(128, tokens)
    scale = HD ** (-0.5)

    def kernel(x_ref, *refs):
        owns = refs[:4]
        piece_refs = refs[4:10]
        (a_ref, bq, bk, bv, ao, bo, q_out, keys, values, low_out, log_out, inv_q, inv_k, summed, wq, wk, wv, wo,
         partial_ref, from_left, from_right, stage_right, stage_left, wsem, xsend, xrecv, *sems) = refs[10:]
        me = lax.axis_index("tensor")
        core = lax.axis_index("ctx")
        line = Line(me, count, *sems)
        for number, (w, own) in enumerate(zip((wq, wk, wv, wo), owns)):
            for copy in assemble(w, own, piece_refs, offsets[number], wsem.at[number]):
                copy.start()
        peer = {"ctx": 1 - core}
        greet(line_partners(me, count) + [(core >= 0, peer)])
        for number, w in enumerate((wq, wk, wv)):
            whole_wait(w, wsem.at[number])

        def project(number, carry):
            rows = rows_of(number, block)
            x = x_ref[rows, :]
            u = dot_nt(x, a_ref[...]).astype(BF)
            yq = dot_nn(x, wq[...]) + dot_nn(u[:, :RANK], bq[...])
            yk = dot_nn(x, wk[...]) + dot_nn(u[:, RANK : 2 * RANK], bk[...])
            yv = (dot_nn(x, wv[...]) + dot_nn(u[:, 2 * RANK :], bv[...])).astype(BF)
            for head in range(heads):
                span = slice(head * HD, (head + 1) * HD)
                normal, inverse = stats(yq[:, span])
                q_out[head, rows, :] = normal.astype(BF)
                inv_q[head, rows, :] = inverse
                normal, inverse = stats(yk[:, span])
                keys[core, head, rows, :] = normal.astype(BF)
                inv_k[head, rows, :] = inverse
                values[core, head, rows, :] = yv[:, span]
            return carry

        lax.fori_loop(0, tokens // block, project, 0)
        swaps = [
            push(ref.at[core], ref.at[core], xsend.at[number], xrecv.at[number], peer)
            for number, ref in enumerate((keys, values))
        ]
        for swap in swaps:
            swap.start()
        whole_wait(wo, wsem.at[3])
        for number, ref in enumerate((keys, values)):
            push(ref.at[1 - core], ref.at[1 - core], xsend.at[number], xrecv.at[number], peer).wait_recv()

        def attend(place, carry):
            dest = scatter_order(me, count, place)
            rows = rows_of(dest, share)
            outs = []
            for head in range(heads):
                q = q_out[head, rows, :]
                s0 = dot_nt(q, keys[0, head]) * scale
                s1 = dot_nt(q, keys[1, head]) * scale
                top = jnp.maximum(jnp.max(s0, axis=-1, keepdims=True), jnp.max(s1, axis=-1, keepdims=True))
                e0 = jnp.exp(s0 - top)
                e1 = jnp.exp(s1 - top)
                total = jnp.sum(e0, axis=-1, keepdims=True) + jnp.sum(e1, axis=-1, keepdims=True)
                share_of = 1.0 / total
                p0 = (e0 * share_of).astype(BF)
                p1 = (e1 * share_of).astype(BF)
                outs.append(dot_nn(p0, values[0, head]) + dot_nn(p1, values[1, head]))
                log_out[head, rows, :] = top + jnp.log(total)
            low = jnp.concatenate(outs, axis=1).astype(BF)
            low_out[rows, :] = low
            u = dot_nt(low, ao[...]).astype(BF)
            partial_ref[dest] = (dot_nt(low, wo[...]) + dot_nn(u, bo[...])).astype(BF)

            @pl.when(place < count - 1)
            def _():
                line_scatter_step(line, place, partial_ref, from_left, from_right, stage_right, stage_left)

            return carry

        lax.fori_loop(0, count, attend, 0)
        line_scatter_finish(line, partial_ref, from_left, from_right, stage_right, stage_left, summed)
        for swap in swaps:
            swap.wait_send()

    buffers = [vmem(count, share, width) for _ in range(5)]
    return call(
        kernel,
        [(attn_in, True)] + [(own, False) for own in own_list] + [(piece, False) for piece in pieces]
        + [(array, True) for array in (down, *ups, out_down, out_up)],
        [
            ((heads, tokens, HD), BF, True),
            ((2, heads, tokens, HD), BF, True),
            ((2, heads, tokens, HD), BF, True),
            ((tokens, local), BF, True),
            ((heads, tokens, 1), F32, True),
            ((heads, tokens, 1), F32, True),
            ((heads, tokens, 1), F32, True),
            ((share, width), F32, True),
        ],
        [vmem(width, local) for _ in range(4)] + buffers + [dma(4), dma(2), dma(2)] + [dma(count) for _ in range(4)],
        collective=2,
        cost=cost_of(8 * tokens * width * local, 60e6),
    )


def cross_forward(count, heads, summed, skip_out, query_stack, out_stack, keys, values, gains, down, up, out_down,
                  out_up, offsets):
    share, width = summed.shape
    local = query_stack[0].shape[-1]
    scale = HD ** (-0.5)
    text = keys.shape[2]

    def kernel(sum_ref, skip_ref, *refs):
        own_q, own_o = refs[:2]
        piece_refs = refs[2:8]
        (kc, vc, gain, a_ref, b_ref, ao, bo, first_out, second_out, in_out, mlp_out, q_out, inv_out, log_out, low_out,
         uo_out, wq, wo, wsem) = refs[8:]
        me = lax.axis_index("tensor")
        for number, (w, own) in enumerate(((wq, own_q), (wo, own_o))):
            for far in range(count):
                lead = (far, xor_place(me, far))
                for copy in assemble(w, own, piece_refs, offsets[number], wsem.at[number], lead):
                    copy.start()
        first = skip_ref[rows_of(me, share), :] + sum_ref[...]
        first_out[...] = first
        normal, _ = stats(first)
        x = (normal * gain[1:2, :]).astype(BF)
        in_out[...] = x
        u = dot_nt(x, a_ref[...]).astype(BF)
        second_out[...] = first
        whole_wait(wq, wsem.at[0])
        whole_wait(wo, wsem.at[1])

        def chunk(place, u_low):
            y = dot_nn(x, wq[place]) + dot_nn(u, b_ref[place])
            outs = []
            for head in range(heads):
                normal, inverse = stats(y[:, head * HD : (head + 1) * HD])
                q = normal.astype(BF)
                q_out[place, head] = q
                inv_out[place, head] = inverse
                s = dot_nt(q, kc[place, head, :, :HD]) * scale
                top = jnp.max(s, axis=-1, keepdims=True)
                e = jnp.exp(s - top)
                total = jnp.sum(e, axis=-1, keepdims=True)
                p = (e * (1.0 / total)).astype(BF)
                outs.append(dot_nn(p, vc[place, head, :, :HD]))
                log_out[place, head] = top + jnp.log(total)
            low = jnp.concatenate(outs, axis=1).astype(BF)
            low_out[place] = low
            second_out[...] += dot_nt(low, wo[place])
            return u_low + dot_nt(low, ao[place])

        u_low = lax.fori_loop(0, count, chunk, jnp.zeros((share, RANK), F32)).astype(BF)
        uo_out[...] = u_low
        second = second_out[...] + dot_nn(u_low, bo[...])
        second_out[...] = second
        normal, _ = stats(second)
        mlp_out[...] = (normal * gain[2:3, :]).astype(BF)

    return call(
        kernel,
        [(summed, True), (skip_out, True), (query_stack[0], False), (out_stack[0], False)]
        + [(piece, False) for piece in query_stack[1]]
        + [(array, True) for array in (keys, values, gains, down, up, out_down, out_up)],
        [
            ((share, width), F32, True),
            ((share, width), F32, True),
            ((share, width), BF, True),
            ((share, width), BF, True),
            ((count, heads, share, HD), BF, True),
            ((count, heads, share, 1), F32, True),
            ((count, heads, share, 1), F32, True),
            ((count, share, local), BF, True),
            ((share, RANK), BF, True),
        ],
        [vmem(count, width, local), vmem(count, width, local), dma(2)],
        cost=cost_of(4 * share * width * width, 20e6),
    )


def feed_forward(count, block_in, cotangent, second, own_up, own_down, pieces, offsets, up_a, up_b, down_a, down_b):
    share, width = block_in.shape
    tokens = cotangent.shape[0]
    hidden_units = own_up.shape[1]

    def kernel(x_ref, cot, sec, own_u, own_d, *refs):
        piece_refs = refs[:6]
        (ua, ub, da, db, summed, down_out, g_ua, g_ub, g_da, g_db, slots, wu, wd, partial_ref, from_left, from_right,
         stage_right, stage_left, wsem, *sems) = refs[6:]
        me = lax.axis_index("tensor")
        gather_line = Line(me, count, *sems[:4])
        scatter_line = Line(me, count, *sems[4:])
        for number, (w, own) in enumerate(((wu, own_u), (wd, own_d))):
            for copy in assemble(w, own, piece_refs, offsets[number], wsem.at[number]):
                copy.start()
        slots[me] = x_ref[...]
        for ref in (g_ua, g_ub, g_da, g_db):
            ref[...] = jnp.zeros_like(ref)
        greet(line_partners(me, count))
        line_gather_step(gather_line, 0, slots)
        whole_wait(wu, wsem.at[0])
        whole_wait(wd, wsem.at[1])

        def compute(block):
            rows = rows_of(block, share)
            x = slots[block]
            ct = cot[rows, :]
            u = dot_nt(x, ua[...]).astype(BF)
            up = dot_nn(x, wu[...]) + dot_nn(u, ub[...])
            square = up * up
            curve = jnp.tanh(0.7978845608028654 * (up + 0.044715 * square * up))
            half = 0.5 * (1.0 + curve)
            active = (up * half).astype(BF)
            slope = half + 0.5 * up * (1.0 - curve * curve) * (0.7978845608028654 * (1.0 + 0.134145 * square))
            ud = dot_nt(active, da[...]).astype(BF)
            down = dot_nt(active, wd[...]) + dot_nn(ud, db[...])
            down_out[rows, :] = down.astype(BF)

            @pl.when(block == me)
            def _():
                down_out[rows, :] = (down + sec[...]).astype(BF)

            gd = dot_nt(ct, db[...]).astype(BF)
            g_active = dot_nn(ct, wd[...]) + dot_nn(gd, da[...])
            g_up = (g_active * slope).astype(BF)
            gu = dot_nt(g_up, ub[...]).astype(BF)
            partial_ref[block] = (dot_nt(g_up, wu[...]) + dot_nn(gu, ua[...])).astype(BF)
            g_ub[...] += dot_tn(u, g_up)
            g_ua[...] += dot_tn(gu, x)
            g_db[...] += dot_tn(ud, ct)
            g_da[...] += dot_tn(gd, active)

        compute(me)

        def step(number, carry):
            line_gather_step(gather_line, number, slots)

            def side(which, inner):
                block = me + (2 * which - 1) * number

                @pl.when((block >= 0) & (block < count))
                def _():
                    compute(lax.clamp(0, block, count - 1))

                return inner

            return lax.fori_loop(0, 2, side, carry)

        lax.fori_loop(1, count, step, 0)

        def scatter(number, carry):
            line_scatter_step(scatter_line, number, partial_ref, from_left, from_right, stage_right, stage_left)
            return carry

        lax.fori_loop(0, count - 1, scatter, 0)
        line_gather_drain(gather_line, slots)
        line_scatter_finish(scatter_line, partial_ref, from_left, from_right, stage_right, stage_left, summed)

    buffers = [vmem(count, share, width) for _ in range(5)]
    return call(
        kernel,
        [(block_in, True), (cotangent, True), (second, True), (own_up, False), (own_down, False)]
        + [(piece, False) for piece in pieces]
        + [(array, True) for array in (up_a, up_b, down_a, down_b)],
        [
            ((share, width), F32, True),
            ((tokens, width), BF, True),
            ((RANK, width), F32, True),
            ((RANK, hidden_units), F32, True),
            ((RANK, hidden_units), F32, True),
            ((RANK, width), F32, True),
        ],
        [vmem(count, share, width), vmem(width, hidden_units), vmem(width, hidden_units)]
        + buffers + [dma(2)] + [dma(count) for _ in range(8)],
        collective=3,
        cost=cost_of(8 * tokens * width * hidden_units, 60e6),
    )


def norm_backward(normal, inverse, grad):
    return inverse * (
        grad
        - jnp.mean(grad, axis=-1, keepdims=True)
        - normal * jnp.mean(grad * normal, axis=-1, keepdims=True)
    )


def cross_backward(count, heads, g_in, cotangent, first, second, block_in, query, inverses, logs, low, u_low, text,
                   query_stack, out_stack, keys, values, gains, down, up, out_down, out_up, text_down, up_key,
                   up_value, offsets):
    share, width = g_in.shape
    local = query_stack[0].shape[-1]
    words, text_width = text.shape
    scale = HD ** (-0.5)

    def kernel(g_ref, cot, first_ref, second_ref, x_ref, q_ref, inv_ref, log_ref, low_ref, uo_ref, t_ref, *refs):
        own_q, own_o = refs[:2]
        piece_refs = refs[2:8]
        (kc, vc, gain, a_ref, b_ref, ao, bo, at, bk, bv, g_first, ga_q, gb_q, ga_k, gb_k, ga_v, gb_v, ga_o, gb_o,
         acc, wq, wo, wsem) = refs[8:]
        me = lax.axis_index("tensor")
        for number, (w, own) in enumerate(((wq, own_q), (wo, own_o))):
            for far in range(count):
                lead = (far, xor_place(me, far))
                for copy in assemble(w, own, piece_refs, offsets[number], wsem.at[number], lead):
                    copy.start()
        normal, inverse = stats(second_ref[...])
        g_second = cot[rows_of(me, share), :].astype(F32) + norm_backward(normal, inverse, g_ref[...] * gain[2:3, :])
        g_low = g_second.astype(BF)
        go = dot_nt(g_low, bo[...]).astype(BF)
        gb_o[...] = dot_tn(uo_ref[...], g_low)
        x = x_ref[...]
        uq = dot_nt(x, a_ref[...]).astype(BF)
        words_in = t_ref[...]
        ut = dot_nt(words_in, at[...]).astype(BF)
        uk, uv = ut[:, :RANK], ut[:, RANK:]
        acc[...] = jnp.zeros_like(acc)
        whole_wait(wq, wsem.at[0])
        whole_wait(wo, wsem.at[1])

        def chunk(place, carry):
            gq_sum, gk_sum, gv_sum = carry
            g_attn = (dot_nn(g_low, wo[place]) + dot_nn(go, ao[place])).astype(BF)
            ga_o[place] = dot_tn(go, low_ref[place])
            gq_parts, gk_parts, gv_parts = [], [], []
            for head in range(heads):
                gh = g_attn[:, head * HD : (head + 1) * HD]
                q = q_ref[place, head]
                kfull = kc[place, head]
                k = kfull[:, :HD]
                v = vc[place, head, :, :HD]
                p = jnp.exp(dot_nt(q, k) * scale - log_ref[place, head])
                dp = dot_nt(gh, v)
                inner = jnp.sum(p * dp, axis=-1, keepdims=True)
                ds = (p * (dp - inner)).astype(BF)
                dq = dot_nn(ds, k) * scale
                dk = dot_tn(ds, q) * scale
                dv = dot_tn(p.astype(BF), gh)
                gq_parts.append(norm_backward(q.astype(F32), inv_ref[place, head], dq))
                inv_k = kfull[:, HD : HD + 1].astype(F32) + kfull[:, HD + 1 : HD + 2].astype(F32)
                gk_parts.append(norm_backward(k.astype(F32), inv_k, dk))
                gv_parts.append(dv)
            gq = jnp.concatenate(gq_parts, axis=1).astype(BF)
            gk = jnp.concatenate(gk_parts, axis=1).astype(BF)
            gv = jnp.concatenate(gv_parts, axis=1).astype(BF)
            acc[...] += dot_nt(gq, wq[place])
            gb_q[place] = dot_tn(uq, gq)
            gb_k[place] = dot_tn(uk, gk)
            gb_v[place] = dot_tn(uv, gv)
            return (
                gq_sum + dot_nt(gq, b_ref[place]),
                gk_sum + dot_nt(gk, bk[place]),
                gv_sum + dot_nt(gv, bv[place]),
            )

        start = (jnp.zeros((share, RANK), F32), jnp.zeros((words, RANK), F32), jnp.zeros((words, RANK), F32))
        gq_sum, gk_sum, gv_sum = lax.fori_loop(0, count, chunk, start)
        gq_sum = gq_sum.astype(BF)
        ga_q[...] = dot_tn(gq_sum, x)
        ga_k[...] = dot_tn(gk_sum.astype(BF), words_in)
        ga_v[...] = dot_tn(gv_sum.astype(BF), words_in)
        g_x = acc[...] + dot_nn(gq_sum, a_ref[...])
        normal, inverse = stats(first_ref[...])
        g_first[...] = (g_second + norm_backward(normal, inverse, g_x * gain[1:2, :])).astype(BF)

    return call(
        kernel,
        [(array, True) for array in (g_in, cotangent, first, second, block_in, query, inverses, logs, low, u_low, text)]
        + [(query_stack[0], False), (out_stack[0], False)]
        + [(piece, False) for piece in query_stack[1]]
        + [(array, True) for array in (keys, values, gains, down, up, out_down, out_up, text_down, up_key, up_value)],
        [
            ((share, width), BF, True),
            ((RANK, width), F32, True),
            ((count, RANK, local), F32, True),
            ((RANK, text_width), F32, True),
            ((count, RANK, local), F32, True),
            ((RANK, text_width), F32, True),
            ((count, RANK, local), F32, True),
            ((count, RANK, local), F32, True),
            ((RANK, width), F32, True),
        ],
        [vmem(share, width, dtype=F32), vmem(count, width, local), vmem(count, width, local), dma(2)],
        cost=cost_of(8 * share * width * width, 20e6),
    )


def attention_backward(count, heads, g_first, attn_in, query, keys, values, low, logs, inv_q, inv_k, own_list, pieces,
                       offsets, down, ups, out_down, out_up):
    share, width = g_first.shape
    tokens = attn_in.shape[0]
    local = own_list[0].shape[1]
    block = min(128, tokens)
    chunk = min(64, tokens)
    steps = tokens // chunk
    each = block // chunk
    scale = HD ** (-0.5)

    def kernel(g_ref, x_ref, q_ref, k_ref, v_ref, low_ref, log_ref, iq_ref, ik_ref, *refs):
        owns = refs[:4]
        piece_refs = refs[4:10]
        (a_ref, bq, bk, bv, ao, bo, total_out, gall, ga_in, gb_q, gb_k, gb_v, ga_o, gb_o, wq, wk, wv, wo, gq_low, gk_acc,
         gv_acc, swap_out, swap_in, partial_ref, from_left, from_right, stage_right, stage_left, wsem, xsend, xrecv,
         *sems) = refs[10:]
        me = lax.axis_index("tensor")
        core = lax.axis_index("ctx")
        peer = {"ctx": 1 - core}
        gather_line = Line(me, count, *sems[:4])
        reduce_line = Line(me, count, *sems[4:])
        for number, (w, own) in enumerate(zip((wq, wk, wv, wo), owns)):
            for copy in assemble(w, own, piece_refs, offsets[number], wsem.at[number]):
                copy.start()
        gall[me] = g_ref[...]
        for ref in (ga_in, gb_q, gb_k, gb_v, ga_o, gb_o, gk_acc, gv_acc):
            ref[...] = jnp.zeros_like(ref)
        greet(line_partners(me, count) + [(core >= 0, peer)])
        line_gather_step(gather_line, 0, gall)
        for number, w in enumerate((wq, wk, wv, wo)):
            whole_wait(w, wsem.at[number])

        def attend(place):
            rows = rows_of(place, share)
            g = gall[place]
            go = dot_nt(g, bo[...]).astype(BF)
            g_attn = (dot_nn(g, wo[...]) + dot_nn(go, ao[...])).astype(BF)
            low = low_ref[rows, :]
            uo = dot_nt(low, ao[...]).astype(BF)
            gb_o[...] += dot_tn(uo, g)
            ga_o[...] += dot_tn(go, low)
            parts = []
            for head in range(heads):
                gh = g_attn[:, head * HD : (head + 1) * HD]
                q = q_ref[head, rows, :]
                probs, grads = [], []
                inner = 0.0
                for half in range(2):
                    p = jnp.exp(dot_nt(q, k_ref[half, head]) * scale - log_ref[head, rows, :])
                    dp = dot_nt(gh, v_ref[half, head])
                    inner = inner + jnp.sum(p * dp, axis=-1, keepdims=True)
                    probs.append(p)
                    grads.append(dp)
                dq = 0.0
                for half in range(2):
                    ds = (probs[half] * (grads[half] - inner)).astype(BF)
                    dq = dq + dot_nn(ds, k_ref[half, head])
                    gk_acc[half, head] += dot_tn(ds, q)
                    gv_acc[half, head] += dot_tn(probs[half].astype(BF), gh)
                parts.append(norm_backward(q.astype(F32), iq_ref[head, rows, :], dq * scale))
            gq_low[rows, :] = jnp.concatenate(parts, axis=1).astype(BF)

        attend(me)

        def gather(number, carry):
            line_gather_step(gather_line, number, gall)

            def side(which, inner):
                place = me + (2 * which - 1) * number

                @pl.when((place >= 0) & (place < count))
                def _():
                    attend(lax.clamp(0, place, count - 1))

                return inner

            return lax.fori_loop(0, 2, side, carry)

        lax.fori_loop(1, count, gather, 0)
        swap_out[0] = (gk_acc[1 - core] * scale).astype(BF)
        swap_out[1] = gv_acc[1 - core].astype(BF)
        swap = push(swap_out, swap_in, xsend, xrecv, peer)
        swap.start()
        line_gather_drain(gather_line, gall)
        swap.wait()

        def compute(number):
            @pl.when(number % each == 0)
            def _():
                rows = rows_of(number // each, block)
                x = x_ref[rows, :]
                u = dot_nt(x, a_ref[...]).astype(BF)
                parts_k, parts_v = [], []
                for head in range(heads):
                    dk = gk_acc[core, head, rows, :] * scale + swap_in[0, head, rows, :].astype(F32)
                    normal = k_ref[core, head, rows, :].astype(F32)
                    parts_k.append(norm_backward(normal, ik_ref[head, rows, :], dk))
                    parts_v.append(gv_acc[core, head, rows, :] + swap_in[1, head, rows, :].astype(F32))
                gq = gq_low[rows, :]
                gk = jnp.concatenate(parts_k, axis=1).astype(BF)
                gv = jnp.concatenate(parts_v, axis=1).astype(BF)
                gu = jnp.concatenate([dot_nt(gq, bq[...]), dot_nt(gk, bk[...]), dot_nt(gv, bv[...])], axis=1).astype(BF)
                y = dot_nt(gq, wq[...]) + dot_nt(gk, wk[...]) + dot_nt(gv, wv[...]) + dot_nn(gu, a_ref[...])
                y = y.astype(BF)
                for piece in range(each):
                    partial_ref[number + piece] = y[piece * chunk : (piece + 1) * chunk]
                ga_in[...] += dot_tn(gu, x)
                gb_q[...] += dot_tn(u[:, :RANK], gq)
                gb_k[...] += dot_tn(u[:, RANK : 2 * RANK], gk)
                gb_v[...] += dot_tn(u[:, 2 * RANK :], gv)

        def finish(slot, total):
            total_out[rows_of(slot, chunk), :] = total

        line_reduce_all(
            reduce_line, steps, compute, partial_ref, from_left, from_right, stage_right, stage_left, finish
        )

    buffers = [vmem(steps, chunk, width) for _ in range(5)]
    return call(
        kernel,
        [(array, True) for array in (g_first, attn_in, query, keys, values, low, logs, inv_q, inv_k)]
        + [(own, False) for own in own_list] + [(piece, False) for piece in pieces]
        + [(array, True) for array in (down, *ups, out_down, out_up)],
        [
            ((tokens, width), F32, True),
            ((count, share, width), BF, True),
            ((3 * RANK, width), F32, True),
            ((RANK, local), F32, True),
            ((RANK, local), F32, True),
            ((RANK, local), F32, True),
            ((RANK, local), F32, True),
            ((RANK, width), F32, True),
        ],
        [vmem(width, local) for _ in range(4)]
        + [vmem(tokens, local), vmem(2, heads, tokens, HD, dtype=F32), vmem(2, heads, tokens, HD, dtype=F32)]
        + [vmem(2, heads, tokens, HD), vmem(2, heads, tokens, HD)]
        + buffers + [dma(4), dma(), dma()] + [dma(count) for _ in range(4)] + [dma(steps) for _ in range(4)],
        collective=4,
        cost=cost_of(16 * tokens * width * local, 60e6),
    )


def skip_backward(count, g_attn, g_first, skip_out, hidden, long_skip, own, pieces, gain_halves, down, up, gain_row):
    tokens, width = hidden.shape
    span = own.shape[-1]
    share = tokens // count
    block = share

    def kernel(g_ref, gf_ref, skip_ref, hid, lsk, own_ref, *refs):
        piece_refs = refs[:6]
        (gains, a_ref, b_ref, gain, out_h, out_l, g_shift, ga, gb, w, buf_h, buf_l, low, grads, wsem, osem) = refs[6:]
        me = lax.axis_index("tensor")
        for far in range(count):
            lead = (far, xor_place(me, far))
            for copy in assemble(w, own_ref, piece_refs, 0, wsem, lead):
                copy.start()
        g_shift[...] = jnp.zeros_like(g_shift)
        whole_wait(w, wsem)

        def step(number, carry):
            rows = rows_of(number, block)
            ga_in = g_ref[rows, :]
            g_shift[...] += jnp.sum(ga_in, axis=0, keepdims=True)
            normal, inverse = stats(skip_ref[rows, :])
            g_low = (
                gf_ref[number].astype(F32) + norm_backward(normal, inverse, ga_in * gain[...])
            ).astype(BF)
            left = hid[rows, :].astype(F32)
            right = lsk[rows, :].astype(F32)
            mean = (jnp.sum(left, axis=-1, keepdims=True) + jnp.sum(right, axis=-1, keepdims=True)) / (2 * width)
            left = left - mean
            right = right - mean
            spread = jnp.sum(left * left, axis=-1, keepdims=True) + jnp.sum(right * right, axis=-1, keepdims=True)
            inverse = lax.rsqrt(spread / (2 * width) + NORM_EPS)
            left = left * inverse
            right = right * inverse
            gu = dot_nt(g_low, b_ref[...]).astype(BF)

            @pl.when(number == me)
            def _():
                low_l = (left * gains[0:1, :]).astype(BF)
                low_r = (right * gains[1:2, :]).astype(BF)
                u = (dot_nt(low_l, a_ref[0]) + dot_nt(low_r, a_ref[1])).astype(BF)
                ga[0] = dot_tn(gu, low_l)
                ga[1] = dot_tn(gu, low_r)
                gb[...] = dot_tn(u, g_low)

            for place in range(count):
                low[:, place * span : (place + 1) * span] = dot_nn(g_low, w[place])
            gl = (low[:, :width] + dot_nn(gu, a_ref[0])) * gains[0:1, :]
            gr = (low[:, width:] + dot_nn(gu, a_ref[1])) * gains[1:2, :]
            mean = (jnp.sum(gl, axis=-1, keepdims=True) + jnp.sum(gr, axis=-1, keepdims=True)) / (2 * width)
            inner = (
                jnp.sum(gl * left, axis=-1, keepdims=True) + jnp.sum(gr * right, axis=-1, keepdims=True)
            ) / (2 * width)
            buf_h[number] = inverse * (gl - mean - left * inner)
            buf_l[number] = inverse * (gr - mean - right * inner)
            pltpu.make_async_copy(buf_h.at[number], out_h.at[rows, :], osem.at[0, number]).start()
            pltpu.make_async_copy(buf_l.at[number], out_l.at[rows, :], osem.at[1, number]).start()
            return carry

        lax.fori_loop(0, tokens // block, step, 0)

        def drain(number, carry):
            rows = rows_of(number, block)
            pltpu.make_async_copy(buf_h.at[number], out_h.at[rows, :], osem.at[0, number]).wait()
            pltpu.make_async_copy(buf_l.at[number], out_l.at[rows, :], osem.at[1, number]).wait()
            return carry

        lax.fori_loop(0, tokens // block, drain, 0)

    blocks = tokens // block
    return call(
        kernel,
        [(array, True) for array in (g_attn, g_first, skip_out, hidden, long_skip)]
        + [(own, False)] + [(piece, False) for piece in pieces]
        + [(array, True) for array in (gain_halves, down, up, gain_row)],
        [
            ((tokens, width), F32, False),
            ((tokens, width), F32, False),
            ((1, width), F32, True),
            ((2, RANK, width), F32, True),
            ((RANK, width), F32, True),
        ],
        [
            vmem(count, width, span),
            vmem(blocks, block, width, dtype=F32),
            vmem(blocks, block, width, dtype=F32),
            vmem(block, 2 * width, dtype=F32),
            vmem(8, 128, dtype=F32),
            dma(),
            dma(2, blocks),
        ],
        cost=cost_of(4 * tokens * width * width, 30e6),
    )


def adapter_reduce(count, table, chosen):
    ranks, tiles, lanes = table.shape
    half = tiles // 2
    own_rows = ranks // count

    def kernel(t_ref, sel, out, swap_out, swap_in, partial_ref, from_left, from_right, stage_right, stage_left, summed,
               slots, other_out, other_in, ssem, rsem, dsend, drecv, *sems):
        me = lax.axis_index("tensor")
        core = lax.axis_index("ctx")
        dp = lax.axis_index("dp")
        peer = {"ctx": 1 - core}
        line = Line(me, count, *sems)
        peers = [{"dp": xor_place(dp, number)} for number in (1, 2, 3)]
        greet(line_partners(me, count) + [(core >= 0, peer)] + [(core >= 0, device) for device in peers])
        swap_out[...] = t_ref[:, pl.ds(pl.multiple_of((1 - core) * half, 16), half), :].astype(BF)
        swap = push(swap_out, swap_in, ssem.at[0], rsem.at[0], peer)
        swap.start()
        swap.wait()
        for number in range(count):
            part = slice(number * own_rows, (number + 1) * own_rows)
            mine = t_ref[part, pl.ds(pl.multiple_of(core * half, 16), half), :]
            partial_ref[number] = (mine + swap_in[part].astype(F32)).astype(BF)

        def scatter(number, carry):
            line_scatter_step(line, number, partial_ref, from_left, from_right, stage_right, stage_left)
            return carry

        lax.fori_loop(0, count - 1, scatter, 0)
        line_scatter_finish(line, partial_ref, from_left, from_right, stage_right, stage_left, summed)
        slots[dp] = summed[...].astype(BF)
        sends = [
            push(slots.at[dp], slots.at[dp], dsend.at[number], drecv.at[number], device)
            for number, device in enumerate(peers)
        ]
        for send in sends:
            send.start()
        for number in (1, 2, 3):
            source = slots.at[xor_place(dp, number)]
            push(source, source, dsend.at[number - 1], drecv.at[number - 1], peers[number - 1]).wait_recv()

        def total(which):
            result = jnp.zeros((own_rows, half, lanes), F32)
            for sequence in range(4):
                result = result + slots[sequence].astype(F32) * sel[which, sequence]
            return result

        other_out[...] = total(1 - core).astype(BF)
        swap = push(other_out, other_in, ssem.at[1], rsem.at[1], peer)
        swap.start()
        out[core] = total(core)
        for send in sends:
            send.wait_send()
        swap.wait()
        out[1 - core] = other_in[...].astype(F32)

    block = (own_rows, half, lanes)
    return call(
        kernel,
        [(table, True), (chosen, True)],
        [((2, *block), F32, True)],
        [vmem(ranks, half, lanes), vmem(ranks, half, lanes)]
        + [vmem(count, *block) for _ in range(5)]
        + [vmem(*block, dtype=F32), vmem(4, *block), vmem(*block), vmem(*block)]
        + [dma(2), dma(2), dma(3), dma(3)] + [dma(count) for _ in range(4)],
        collective=5,
        cost=cost_of(1e6, 10e6),
    )[0]


PAIR = ("dp", "ctx")


def pair_permutation(core0, core1):
    pairs = []
    for dp in range(4):
        for core in range(2):
            pairs.append((dp * 2 + core, (dp ^ (core0 if core == 0 else core1)) * 2 + core))
    return pairs


def swap_cores(value):
    return lax.ppermute(value, "ctx", [(0, 1), (1, 0)])


def share_pieces(half):
    first, second = pair_permutation(1, 2), pair_permutation(2, 1)
    a = lax.ppermute(half, PAIR, first)
    b = lax.ppermute(half, PAIR, second)
    c = lax.ppermute(a, PAIR, second)
    return [a, b, c, swap_cores(a), swap_cores(b), swap_cores(c)]


def core_half(value, axis=0):
    size = value.shape[axis] // 2
    return lax.dynamic_slice_in_dim(value, lax.axis_index("ctx") * size, size, axis)


def exchange_dp(rows):
    dp = lax.axis_index("dp")
    got = [lax.dynamic_slice_in_dim(rows, dp, 1, 0)]
    for number in (1, 2, 3):
        row = lax.dynamic_slice_in_dim(rows, dp ^ number, 1, 0)
        got.append(lax.ppermute(row, "dp", [(place, place ^ number) for place in range(4)]))
    return got


def gather_dp(row):
    dp = lax.axis_index("dp")
    table = jnp.zeros((4, row.shape[1]), row.dtype)
    table = lax.dynamic_update_slice_in_dim(table, row, dp, 0)
    for number in (1, 2, 3):
        got = lax.ppermute(row, "dp", [(place, place ^ number) for place in range(4)])
        table = lax.dynamic_update_slice_in_dim(table, got, dp ^ number, 0)
    return table


def fused_body(
    hidden,
    long_skip_input,
    condition,
    projected_text_tokens,
    sequence_adapter_index,
    skip_projection_weight,
    shift_modulation_weight,
    self_query_weight,
    self_key_weight,
    self_value_weight,
    attention_output_weight,
    cross_query_weight,
    cross_key_weight,
    cross_value_weight,
    cross_output_weight,
    feedforward_up_weight,
    feedforward_down_weight,
    skip_norm_gain,
    norm_gain_rows,
    adapter_down_factor,
    adapter_up_factor,
    cotangent,
):
    rank = lax.axis_index("tensor")
    count = lax.axis_size("tensor")
    core = lax.axis_index("ctx")
    dp = lax.axis_index("dp")
    hidden, long_skip, text, cot = hidden[0], long_skip_input[0], projected_text_tokens[0], cotangent[0]
    tokens, width = hidden.shape
    local = self_query_weight.shape[1]
    heads = local // HD
    ff = feedforward_up_weight.shape[1]
    span = skip_projection_weight.shape[0]
    share = tokens // count
    in_sizes = [2 * MODEL_WIDTH] + [MODEL_WIDTH] * 6 + [TW, TW, MODEL_WIDTH, MODEL_WIDTH, FF]
    out_sizes = [MODEL_WIDTH] * 10 + [FF, MODEL_WIDTH]
    in_at = [sum(in_sizes[:number]) for number in range(12)]
    out_at = [sum(out_sizes[:number]) for number in range(12)]
    index = sequence_adapter_index[0]
    down_table = lax.dynamic_index_in_dim(adapter_down_factor, index, 0, keepdims=False)
    up_table = lax.dynamic_index_in_dim(adapter_up_factor, index, 0, keepdims=False)

    def down_full(number):
        return down_table[:, in_at[number] : in_at[number] + in_sizes[number]]

    def up_full(number):
        return up_table[:, out_at[number] : out_at[number] + out_sizes[number]]

    def down_local(number, size):
        return lax.dynamic_slice_in_dim(down_table, in_at[number] + rank * size, size, 1)

    def up_local(number, size):
        return lax.dynamic_slice_in_dim(up_table, out_at[number] + rank * size, size, 1)

    def stack(table):
        return jnp.transpose(table.reshape(RANK, count, -1), (1, 0, 2))

    skip_t = skip_projection_weight.T
    attn_out_t = attention_output_weight.T
    cross_out_t = cross_output_weight.T
    ff_down_t = feedforward_down_weight.T

    skip_half = core_half(skip_t)
    skip_pieces = share_pieces(skip_half)

    narrow = [self_query_weight, self_key_weight, self_value_weight, attn_out_t, cross_key_weight, cross_value_weight]
    narrow_at = [sum(weight.shape[0] for weight in narrow[:number]) // 2 for number in range(6)]
    narrow_pieces = share_pieces(jnp.concatenate([core_half(weight) for weight in narrow], axis=0))

    def along_tensor(value):
        others = [
            lax.ppermute(value, "tensor", [(place, place ^ number) for place in range(count)])
            for number in range(1, count)
        ]
        return jnp.stack([value] + others)

    cross_own = along_tensor(jnp.concatenate([cross_query_weight, cross_out_t], axis=0))
    rows_q = cross_query_weight.shape[0]
    cross_half = jnp.concatenate(
        [core_half(cross_own[:, :rows_q], 1), core_half(cross_own[:, rows_q:], 1)], axis=1
    )
    cross_pieces = share_pieces(cross_half)
    cross_at = [0, rows_q // 2]
    query_stack = (cross_own[:, :rows_q], cross_pieces)
    out_stack = (cross_own[:, rows_q:], cross_pieces)

    wide_pieces = share_pieces(jnp.concatenate([core_half(feedforward_up_weight), core_half(ff_down_t)], axis=0))
    wide_at = [0, feedforward_up_weight.shape[0] // 2]

    skip_own = along_tensor(skip_t)
    skip_all_pieces = share_pieces(core_half(skip_own, 1))

    act_wide, silu_pull = jax.vjp(jax.nn.silu, condition.astype(F32))
    act_low = act_wide.astype(BF)
    tag = jnp.full((1, 128), index, jnp.int32).astype(BF)
    gathered = gather_dp(jnp.concatenate([act_low, tag], axis=1))
    indices = gathered[:, MODEL_WIDTH].astype(jnp.int32)
    mod_rows = shift_modulation_weight.shape[0]
    act_slice = lax.dynamic_slice_in_dim(gathered, dp * mod_rows, mod_rows, 1)
    shift_parts = exchange_dp(dot_nn(act_slice, shift_modulation_weight))
    mod_u = dot_nt(act_low, down_full(1))
    shift_row = sum(shift_parts) + jnp.dot(mod_u, up_full(1).astype(F32), precision=PRECISE)

    both = jnp.concatenate([hidden, long_skip], axis=1)
    part = lax.dynamic_slice_in_dim(both, rank * span, span, 1)
    part_gain = lax.dynamic_slice_in_dim(skip_norm_gain, rank * span, span, 0)[None, :]
    skip_out, attn_in = skip_forward(
        count, skip_t, skip_pieces, hidden, long_skip, part, part_gain, down_local(0, span), up_full(0),
        norm_gain_rows[0:1], shift_row,
    )
    own_text = text_forward(
        heads, text, cross_key_weight, cross_value_weight, narrow_pieces, narrow_at[4], narrow_at[5],
        jnp.concatenate([down_full(7), down_full(8)], axis=0), up_local(7, local), up_local(8, local),
    )
    text_all = jnp.zeros((count, *own_text.shape), BF)
    for number in range(count):
        got = own_text
        if number:
            got = lax.ppermute(own_text, "tensor", [(place, place ^ number) for place in range(count)])
        text_all = lax.dynamic_update_slice_in_dim(text_all, got[None], rank ^ number, 0)
    text_other = swap_cores(text_all)
    text_keys = jnp.where(core == 0, text_all, text_other)
    text_values = jnp.where(core == 0, text_other, text_all)

    qkv_down = jnp.concatenate([down_full(2), down_full(3), down_full(4)], axis=0)
    qkv_up = [up_local(number, local) for number in (2, 3, 4)]
    attn_own = [self_query_weight, self_key_weight, self_value_weight, attn_out_t]
    out_down, out_up = down_local(5, local), up_full(5)
    query, keys, values, low, logs, inv_q, inv_k, summed = attention_forward(
        count, heads, attn_in, attn_own, narrow_pieces, narrow_at[:4], qkv_down, qkv_up, out_down, out_up
    )
    cross_down, cross_up = down_full(6), stack(up_full(6))
    cout_down, cout_up = stack(down_full(9)), up_full(9)
    first, second, cross_in, mlp_in, cquery, cinv, clogs, clow, cu = cross_forward(
        count, heads, summed, skip_out, query_stack, out_stack, text_keys, text_values, norm_gain_rows, cross_down,
        cross_up, cout_down, cout_up, cross_at,
    )
    g_mlp_in, down_part, g_up_a, g_up_b, g_down_a, g_down_b = feed_forward(
        count, mlp_in, cot, second, feedforward_up_weight, ff_down_t, wide_pieces, wide_at, down_full(10),
        up_local(10, ff), down_local(11, ff), up_full(11),
    )
    block_out = lax.psum(down_part, "tensor")
    g_first, g_cq_a, g_cq_b, g_ck_a, g_ck_b, g_cv_a, g_cv_b, g_co_a, g_co_b = cross_backward(
        count, heads, g_mlp_in, cot, first, second, cross_in, cquery, cinv, clogs, clow, cu, text, query_stack,
        out_stack, text_keys, text_values, norm_gain_rows, cross_down, cross_up, cout_down, cout_up,
        jnp.concatenate([down_full(7), down_full(8)], axis=0), stack(up_full(7)), stack(up_full(8)), cross_at,
    )
    g_attn, g_first_all, g_qkv_a, g_q_b, g_k_b, g_v_b, g_o_a, g_o_b = attention_backward(
        count, heads, g_first, attn_in, query, keys, values, low, logs, inv_q, inv_k, attn_own, narrow_pieces,
        narrow_at[:4], qkv_down, qkv_up, out_down, out_up,
    )
    skip_down = jnp.transpose(down_full(0).reshape(RANK, 2, MODEL_WIDTH), (1, 0, 2))
    hidden_grad, skip_grad, g_shift, g_skip_a, g_skip_b = skip_backward(
        count, g_attn, g_first_all, skip_out, hidden, long_skip, skip_own, skip_all_pieces,
        skip_norm_gain.reshape(2, MODEL_WIDTH), skip_down, up_full(0), norm_gain_rows[0:1],
    )

    g_mod_u = dot_nt(g_shift.astype(BF), up_full(1))
    once = (rank == 0).astype(F32)
    g_mod_a = jnp.dot(g_mod_u.T, act_low.astype(F32), precision=PRECISE) * once
    g_mod_b = jnp.dot(mod_u.T, g_shift, precision=PRECISE) * once
    shift_sum = g_shift + swap_cores(g_shift)
    shift_all = gather_dp(shift_sum).astype(BF)
    act_parts = exchange_dp(dot_nt(shift_all, shift_modulation_weight))
    g_act = jnp.zeros((1, MODEL_WIDTH), F32)
    for number, piece in enumerate(act_parts):
        g_act = lax.dynamic_update_slice_in_dim(g_act, piece, (dp ^ number) * mod_rows, 1)
    shift_u = jnp.dot(shift_sum, up_full(1).astype(F32).T, precision=PRECISE)
    g_act = g_act + jnp.dot(shift_u, down_full(1).astype(F32), precision=PRECISE)
    g_condition = silu_pull(g_act)[0][0]
    size = MODEL_WIDTH // (2 * count)
    condition_gradient = lax.dynamic_slice_in_dim(g_condition, (core * count + rank) * size, size, 0)

    def unstack(value):
        return jnp.transpose(value, (1, 0, 2)).reshape(RANK, -1)

    def place_local(value, total):
        return lax.dynamic_update_slice_in_dim(jnp.zeros((RANK, total), F32), value, rank * value.shape[1], 1)

    table = jnp.concatenate(
        [
            g_skip_a[0], g_skip_a[1], g_mod_a, g_qkv_a[:RANK], g_qkv_a[RANK : 2 * RANK], g_qkv_a[2 * RANK :],
            place_local(g_o_a, MODEL_WIDTH), g_cq_a, g_ck_a, g_cv_a, unstack(g_co_a), g_up_a, place_local(g_down_a, FF),
            g_skip_b, g_mod_b, place_local(g_q_b, MODEL_WIDTH), place_local(g_k_b, MODEL_WIDTH),
            place_local(g_v_b, MODEL_WIDTH), g_o_b, unstack(g_cq_b), unstack(g_ck_b), unstack(g_cv_b), g_co_b,
            place_local(g_up_b, FF), g_down_b,
        ],
        axis=1,
    )
    wide_a, wide_b = sum(in_sizes) // 128, sum(out_sizes) // 128
    tiles = -(-(wide_a + wide_b) // 32) * 32
    table = jnp.pad(table.reshape(RANK, wide_a + wide_b, 128), ((0, 0), (0, tiles - wide_a - wide_b), (0, 0)))
    chosen = (indices[None, :] == (dp * 2 + jnp.arange(2, dtype=jnp.int32))[:, None]).astype(F32)
    chosen = jnp.broadcast_to(chosen[:, :, None, None], (2, 4, 1, 128))
    reduced = adapter_reduce(count, table, chosen)
    reduced = jnp.transpose(reduced, (1, 0, 2, 3)).reshape(RANK // count, tiles, 128)
    return (
        block_out[None],
        hidden_grad[None],
        skip_grad[None],
        condition_gradient,
        reduced[:, :wide_a].reshape(-1),
        reduced[:, wide_a : wide_a + wide_b].reshape(-1),
    )


def solution(mesh):
    in_specs = (
        P("dp", "ctx", None),
        P("dp", "ctx", None),
        P("dp", None),
        P("dp", None, None),
        P("dp"),
        P("tensor", "dp"),
        P("dp", None),
        P("dp", "tensor"),
        P("dp", "tensor"),
        P("dp", "tensor"),
        P("tensor", "dp"),
        P("dp", "tensor"),
        P("dp", "tensor"),
        P("dp", "tensor"),
        P("tensor", "dp"),
        P("dp", "tensor"),
        P("tensor", "dp"),
        P(),
        P(),
        P(),
        P(),
        P("dp", "ctx", None),
    )
    out_specs = (
        P("dp", "ctx", None),
        P("dp", "ctx", None),
        P("dp", "ctx", None),
        P(("dp", "ctx", "tensor")),
        P(("dp", "ctx", "tensor")),
        P(("dp", "ctx", "tensor")),
    )
    shape = mesh.shape
    fused = shape["dp"] == 4 and shape["ctx"] == 2 and shape["tensor"] == 4
    return jax.shard_map(fused_body if fused else body, mesh=mesh, in_specs=in_specs, out_specs=out_specs, check_vma=False)
```

```python
from functools import partial

import jax
import jax.numpy as jnp
from jax import lax
from jax.experimental import pallas as pl
from jax.experimental.pallas import tpu as pltpu
from jax.sharding import PartitionSpec as P

MODEL_WIDTH = 1408
HD = 88
FF = 6144
TW = 1024


PRECISE = lax.Precision.HIGHEST
NORM_EPS = 1e-06


def row_norm(values):
    centered = values - jnp.mean(values, axis=-1, keepdims=True)
    inverse = lax.rsqrt(jnp.mean(centered * centered, axis=-1, keepdims=True) + NORM_EPS)
    return (centered * inverse, inverse)


def head_norm(values, head_width):
    shaped = values.reshape(values.shape[:-1] + (values.shape[-1] // head_width, head_width))
    centered = shaped - jnp.mean(shaped, axis=-1, keepdims=True)
    inverse = lax.rsqrt(jnp.mean(centered * centered, axis=-1, keepdims=True) + NORM_EPS)
    return (centered * inverse, inverse)


def norm_back(normal, inverse, grad_normal):
    return inverse * (
        grad_normal
        - jnp.mean(grad_normal, axis=-1, keepdims=True)
        - normal * jnp.mean(grad_normal * normal, axis=-1, keepdims=True)
    )


def split_parts(values):
    if values.dtype == jnp.bfloat16:
        return [values]
    upper_half = values.astype(jnp.bfloat16)
    lower_half = (values - upper_half.astype(jnp.float32)).astype(jnp.bfloat16)
    return [upper_half, lower_half]


def paired_product(form, left, right):
    total = None
    for left_number, left_part in enumerate(split_parts(left)):
        for right_number, right_part in enumerate(split_parts(right)):
            if left_number + right_number < 2:
                term = jnp.einsum(form, left_part, right_part, preferred_element_type=jnp.float32)
                total = term if total is None else total + term
    return total


def lowrank_out(input_list, weight_matrix, down_piece, up_factor_piece):
    frozen_term = jnp.einsum(
        "gtb,bx->gtx", input_list, weight_matrix, preferred_element_type=jnp.float32
    )
    rank_activation = jnp.einsum(
        "snd,srd->snr", input_list, down_piece, preferred_element_type=jnp.float32
    )
    adapter_term = paired_product("dti,dip->dtp", rank_activation, up_factor_piece)
    return (frozen_term + adapter_term, rank_activation)


def lowrank_back(
    input_list,
    weight_matrix,
    down_piece,
    up_factor_piece,
    rank_activation,
    output_gradient,
    want_input,
):
    upper_gradient = paired_product("pmf,pmz->pfz", rank_activation, output_gradient)
    rank_gradient = paired_product("hzu,hlu->hzl", output_gradient, up_factor_piece)
    grad_lower = paired_product("snr,snd->srd", rank_gradient, input_list)
    if want_input:
        input_gradients = paired_product("lga,wa->lgw", output_gradient, weight_matrix)
        input_gradients = input_gradients + paired_product(
            "snr,srd->snd", rank_gradient, down_piece
        )
        return (input_gradients, grad_lower, upper_gradient)
    return (None, grad_lower, upper_gradient)


def attend_forward(query, key_rows, values_in, scale_factor):
    scores = (
        jnp.einsum("snhe,smhe->shnm", query, key_rows, preferred_element_type=jnp.float32)
        * scale_factor
    )
    row_top = jnp.max(scores, axis=-1, keepdims=True)
    exp_scores = jnp.exp(scores - row_top)
    row_total = jnp.sum(exp_scores, axis=-1, keepdims=True)
    attn_probs = (exp_scores / row_total).astype(jnp.bfloat16)
    result = jnp.einsum(
        "shnm,smhe->snhe", attn_probs, values_in, preferred_element_type=jnp.float32
    )
    return (result, row_top + jnp.log(row_total))


def attend_back(query, key_rows, values_in, log_total, grad_result, scale_factor):
    scores = (
        jnp.einsum("snhe,smhe->shnm", query, key_rows, preferred_element_type=jnp.float32)
        * scale_factor
    )
    attn_probs = jnp.exp(scores - log_total)
    grad_probs = jnp.einsum(
        "snhe,smhe->shnm", grad_result, values_in, preferred_element_type=jnp.float32
    )
    row_inner = jnp.sum(attn_probs * grad_probs, axis=-1, keepdims=True)
    grad_scores = (attn_probs * (grad_probs - row_inner)).astype(jnp.bfloat16)
    grad_query = (
        jnp.einsum("shnm,smhe->snhe", grad_scores, key_rows, preferred_element_type=jnp.float32)
        * scale_factor
    )
    grad_keys = (
        jnp.einsum("shnm,snhe->smhe", grad_scores, query, preferred_element_type=jnp.float32)
        * scale_factor
    )
    grad_values = jnp.einsum(
        "shnm,snhe->smhe",
        attn_probs.astype(jnp.bfloat16),
        grad_result,
        preferred_element_type=jnp.float32,
    )
    return (grad_query, grad_keys, grad_values)


def body(
    hidden,
    long_skip_input,
    condition,
    projected_text_tokens,
    sequence_adapter_index,
    skip_projection_weight,
    shift_modulation_weight,
    self_query_weight,
    self_key_weight,
    self_value_weight,
    attention_output_weight,
    cross_query_weight,
    cross_key_weight,
    cross_value_weight,
    cross_output_weight,
    feedforward_up_weight,
    feedforward_down_weight,
    skip_norm_gain,
    norm_gain_rows,
    adapter_down_factor,
    adapter_up_factor,
    cotangent,
):
    (
        skip_projection_weight,
        shift_modulation_weight,
        self_query_weight,
        self_key_weight,
        self_value_weight,
        attention_output_weight,
        cross_query_weight,
        cross_key_weight,
        cross_value_weight,
        cross_output_weight,
        feedforward_up_weight,
        feedforward_down_weight,
    ) = (
        lax.all_gather(skip_projection_weight, "dp", axis=1, tiled=True),
        lax.all_gather(shift_modulation_weight, "dp", axis=0, tiled=True),
        lax.all_gather(self_query_weight, "dp", axis=0, tiled=True),
        lax.all_gather(self_key_weight, "dp", axis=0, tiled=True),
        lax.all_gather(self_value_weight, "dp", axis=0, tiled=True),
        lax.all_gather(attention_output_weight, "dp", axis=1, tiled=True),
        lax.all_gather(cross_query_weight, "dp", axis=0, tiled=True),
        lax.all_gather(cross_key_weight, "dp", axis=0, tiled=True),
        lax.all_gather(cross_value_weight, "dp", axis=0, tiled=True),
        lax.all_gather(cross_output_weight, "dp", axis=1, tiled=True),
        lax.all_gather(feedforward_up_weight, "dp", axis=0, tiled=True),
        lax.all_gather(feedforward_down_weight, "dp", axis=1, tiled=True),
    )
    tensor_rank = lax.axis_index("tensor")
    tensor_count = lax.axis_size("tensor")
    seqs_local = hidden.shape[0]
    tokens_local = hidden.shape[1]
    local_width = self_query_weight.shape[1]
    heads_local = local_width // HD
    ff_local = feedforward_up_weight.shape[1]
    skip_width = skip_projection_weight.shape[0]
    scale_factor = HD ** (-0.5)
    in_sizes = [
        2 * MODEL_WIDTH,
        MODEL_WIDTH,
        MODEL_WIDTH,
        MODEL_WIDTH,
        MODEL_WIDTH,
        MODEL_WIDTH,
        MODEL_WIDTH,
        TW,
        TW,
        MODEL_WIDTH,
        MODEL_WIDTH,
        FF,
    ]
    out_sizes = [MODEL_WIDTH] * 10 + [FF, MODEL_WIDTH]
    input_offsets = [sum(in_sizes[:number]) for number in range(12)]
    output_offsets = [sum(out_sizes[:number]) for number in range(12)]
    select_adapter = (
        sequence_adapter_index[:, None]
        == jnp.arange(adapter_down_factor.shape[0], dtype=jnp.int32)[None, :]
    )
    choose_wide = select_adapter.astype(jnp.float32)
    down_seq = jnp.einsum(
        "fn,nge->fge",
        select_adapter.astype(jnp.bfloat16),
        adapter_down_factor,
        preferred_element_type=jnp.float32,
    ).astype(jnp.bfloat16)
    up_seq = jnp.einsum(
        "fn,nge->fge",
        select_adapter.astype(jnp.bfloat16),
        adapter_up_factor,
        preferred_element_type=jnp.float32,
    ).astype(jnp.bfloat16)

    def down_full(number):
        return down_seq[:, :, input_offsets[number] : input_offsets[number] + in_sizes[number]]

    def up_full(number):
        return up_seq[:, :, output_offsets[number] : output_offsets[number] + out_sizes[number]]

    def down_local(number, span_width):
        return lax.dynamic_slice_in_dim(
            down_seq, input_offsets[number] + tensor_rank * span_width, span_width, 2
        )

    def up_local(number, span_width):
        return lax.dynamic_slice_in_dim(
            up_seq, output_offsets[number] + tensor_rank * span_width, span_width, 2
        )

    def to_slots(grad_piece):
        return jnp.einsum("si,srd->ird", choose_wide, grad_piece, precision=PRECISE)

    joined = jnp.concatenate([hidden, long_skip_input], axis=-1).astype(jnp.float32)
    joined_normal, joined_inverse = row_norm(joined)
    joined_low = (joined_normal * skip_norm_gain).astype(jnp.bfloat16)
    joined_part = lax.dynamic_slice_in_dim(joined_low, tensor_rank * skip_width, skip_width, 2)
    skip_partial, skip_rank = lowrank_out(
        joined_part, skip_projection_weight, down_local(0, skip_width), up_full(0)
    )
    skip_out = lax.psum(skip_partial.astype(jnp.bfloat16), "tensor").astype(jnp.float32)
    act_wide, silu_pull = jax.vjp(jax.nn.silu, condition.astype(jnp.float32))
    act_low = act_wide.astype(jnp.bfloat16)[:, None, :]
    shift_row, mod_rank = lowrank_out(act_low, shift_modulation_weight, down_full(1), up_full(1))
    first_normal, first_inverse = row_norm(skip_out)
    attn_in = (first_normal * norm_gain_rows[0] + shift_row).astype(jnp.bfloat16)
    query_proj, query_rank = lowrank_out(
        attn_in, self_query_weight, down_full(2), up_local(2, local_width)
    )
    key_proj, key_rank = lowrank_out(
        attn_in, self_key_weight, down_full(3), up_local(3, local_width)
    )
    value_proj, value_rank = lowrank_out(
        attn_in, self_value_weight, down_full(4), up_local(4, local_width)
    )
    query_normal, query_inverse = head_norm(query_proj, HD)
    key_normal, key_inverse = head_norm(key_proj, HD)
    query_low = query_normal.astype(jnp.bfloat16)
    key_low = key_normal.astype(jnp.bfloat16).reshape(seqs_local, tokens_local, local_width)
    value_low = value_proj.astype(jnp.bfloat16)
    keys_all, values_all = (
        lax.all_gather(key_low, "ctx", axis=1, tiled=True),
        lax.all_gather(value_low, "ctx", axis=1, tiled=True),
    )
    keys_four = keys_all.reshape(seqs_local, -1, heads_local, HD)
    values_four = values_all.reshape(seqs_local, -1, heads_local, HD)
    attn_result, attn_log = attend_forward(query_low, keys_four, values_four, scale_factor)
    attn_low = attn_result.reshape(seqs_local, tokens_local, local_width).astype(jnp.bfloat16)
    attn_partial, out_rank = lowrank_out(
        attn_low, attention_output_weight, down_local(5, local_width), up_full(5)
    )
    first_res = skip_out + lax.psum(attn_partial.astype(jnp.bfloat16), "tensor").astype(jnp.float32)
    second_normal, second_inverse = row_norm(first_res)
    cross_in = (second_normal * norm_gain_rows[1]).astype(jnp.bfloat16)
    cquery_proj, cquery_rank = lowrank_out(
        cross_in, cross_query_weight, down_full(6), up_local(6, local_width)
    )
    ckey_proj, ckey_rank = lowrank_out(
        projected_text_tokens, cross_key_weight, down_full(7), up_local(7, local_width)
    )
    cvalue_proj, cvalue_rank = lowrank_out(
        projected_text_tokens, cross_value_weight, down_full(8), up_local(8, local_width)
    )
    cquery_normal, cquery_inverse = head_norm(cquery_proj, HD)
    ckey_normal, ckey_inverse = head_norm(ckey_proj, HD)
    cquery_low = cquery_normal.astype(jnp.bfloat16)
    ckey_low = ckey_normal.astype(jnp.bfloat16)
    cvalue_low = cvalue_proj.astype(jnp.bfloat16).reshape(seqs_local, -1, heads_local, HD)
    cross_result, cross_log = attend_forward(cquery_low, ckey_low, cvalue_low, scale_factor)
    cross_low = cross_result.reshape(seqs_local, tokens_local, local_width).astype(jnp.bfloat16)
    cross_partial, cout_rank = lowrank_out(
        cross_low, cross_output_weight, down_local(9, local_width), up_full(9)
    )
    second_res = first_res + lax.psum(cross_partial.astype(jnp.bfloat16), "tensor").astype(
        jnp.float32
    )
    third_normal, third_inverse = row_norm(second_res)
    mlp_in = (third_normal * norm_gain_rows[2]).astype(jnp.bfloat16)
    up_proj, up_rank = lowrank_out(
        mlp_in, feedforward_up_weight, down_full(10), up_local(10, ff_local)
    )
    activated, gelu_pull = jax.vjp(partial(jax.nn.gelu, approximate=True), up_proj)
    activated_low = activated.astype(jnp.bfloat16)
    down_partial, down_rank = lowrank_out(
        activated_low, feedforward_down_weight, down_local(11, ff_local), up_full(11)
    )
    block_out = second_res + lax.psum(down_partial.astype(jnp.bfloat16), "tensor").astype(
        jnp.float32
    )
    grad_act, grad_down_lower, grad_down_upper = lowrank_back(
        activated_low,
        feedforward_down_weight,
        down_local(11, ff_local),
        up_full(11),
        down_rank,
        cotangent,
        True,
    )
    grad_pre = gelu_pull(grad_act)[0].astype(jnp.bfloat16)
    grad_mlp_in, grad_up_lower, grad_up_upper = lowrank_back(
        mlp_in,
        feedforward_up_weight,
        down_full(10),
        up_local(10, ff_local),
        up_rank,
        grad_pre,
        True,
    )
    grad_mlp_in = lax.psum(grad_mlp_in.astype(jnp.bfloat16), "tensor").astype(jnp.float32)
    grad_second = cotangent.astype(jnp.float32) + norm_back(
        third_normal, third_inverse, grad_mlp_in * norm_gain_rows[2]
    )
    grad_cross_low, grad_cout_lower, grad_cout_upper = lowrank_back(
        cross_low,
        cross_output_weight,
        down_local(9, local_width),
        up_full(9),
        cout_rank,
        grad_second.astype(jnp.bfloat16),
        True,
    )
    grad_cross_result = grad_cross_low.astype(jnp.bfloat16).reshape(
        seqs_local, tokens_local, heads_local, HD
    )
    grad_cquery, grad_ckey, grad_cvalue = attend_back(
        cquery_low, ckey_low, cvalue_low, cross_log, grad_cross_result, scale_factor
    )
    grad_cquery_proj = (
        norm_back(cquery_normal, cquery_inverse, grad_cquery)
        .reshape(seqs_local, tokens_local, local_width)
        .astype(jnp.bfloat16)
    )
    grad_ckey_proj = norm_back(ckey_normal, ckey_inverse, grad_ckey).reshape(
        seqs_local, -1, local_width
    )
    none_first, grad_ckey_lower, grad_ckey_upper = lowrank_back(
        projected_text_tokens,
        cross_key_weight,
        down_full(7),
        up_local(7, local_width),
        ckey_rank,
        grad_ckey_proj,
        False,
    )
    none_second, grad_cvalue_lower, grad_cvalue_upper = lowrank_back(
        projected_text_tokens,
        cross_value_weight,
        down_full(8),
        up_local(8, local_width),
        cvalue_rank,
        grad_cvalue.reshape(seqs_local, -1, local_width),
        False,
    )
    grad_cross_in, grad_cquery_lower, grad_cquery_upper = lowrank_back(
        cross_in,
        cross_query_weight,
        down_full(6),
        up_local(6, local_width),
        cquery_rank,
        grad_cquery_proj,
        True,
    )
    grad_cross_in = lax.psum(grad_cross_in.astype(jnp.bfloat16), "tensor").astype(jnp.float32)
    grad_first = grad_second + norm_back(
        second_normal, second_inverse, grad_cross_in * norm_gain_rows[1]
    )
    grad_attn_low, grad_aout_lower, grad_aout_upper = lowrank_back(
        attn_low,
        attention_output_weight,
        down_local(5, local_width),
        up_full(5),
        out_rank,
        grad_first.astype(jnp.bfloat16),
        True,
    )
    grad_attn_result = grad_attn_low.astype(jnp.bfloat16).reshape(
        seqs_local, tokens_local, heads_local, HD
    )
    grad_query, grad_keys_all, grad_values_all = attend_back(
        query_low, keys_four, values_four, attn_log, grad_attn_result, scale_factor
    )
    grad_keys, grad_values = (
        lax.psum_scatter(
            grad_keys_all.reshape(seqs_local, -1, local_width).astype(jnp.bfloat16),
            "ctx",
            scatter_dimension=1,
            tiled=True,
        ).astype(jnp.float32),
        lax.psum_scatter(
            grad_values_all.reshape(seqs_local, -1, local_width).astype(jnp.bfloat16),
            "ctx",
            scatter_dimension=1,
            tiled=True,
        ).astype(jnp.float32),
    )
    grad_query_proj = (
        norm_back(query_normal, query_inverse, grad_query)
        .reshape(seqs_local, tokens_local, local_width)
        .astype(jnp.bfloat16)
    )
    grad_key_proj = (
        norm_back(
            key_normal, key_inverse, grad_keys.reshape(seqs_local, tokens_local, heads_local, HD)
        )
        .reshape(seqs_local, tokens_local, local_width)
        .astype(jnp.bfloat16)
    )
    grad_value_proj = grad_values.astype(jnp.bfloat16)
    grad_in_query, grad_query_lower, grad_query_upper = lowrank_back(
        attn_in,
        self_query_weight,
        down_full(2),
        up_local(2, local_width),
        query_rank,
        grad_query_proj,
        True,
    )
    grad_in_key, grad_key_lower, grad_key_upper = lowrank_back(
        attn_in,
        self_key_weight,
        down_full(3),
        up_local(3, local_width),
        key_rank,
        grad_key_proj,
        True,
    )
    grad_in_value, grad_value_lower, grad_value_upper = lowrank_back(
        attn_in,
        self_value_weight,
        down_full(4),
        up_local(4, local_width),
        value_rank,
        grad_value_proj,
        True,
    )
    grad_attn_in = lax.psum(
        (grad_in_query + grad_in_key + grad_in_value).astype(jnp.bfloat16), "tensor"
    ).astype(jnp.float32)
    grad_shift = jnp.sum(grad_attn_in, axis=1, keepdims=True) / tensor_count
    grad_act_low, grad_mod_lower, grad_mod_upper = lowrank_back(
        act_low, shift_modulation_weight, down_full(1), up_full(1), mod_rank, grad_shift, True
    )
    grad_condition = silu_pull(grad_act_low[:, 0, :])[0]
    grad_skip_out = grad_first + norm_back(
        first_normal, first_inverse, grad_attn_in * norm_gain_rows[0]
    )
    grad_joined_part, grad_skip_lower, grad_skip_upper = lowrank_back(
        joined_part,
        skip_projection_weight,
        down_local(0, skip_width),
        up_full(0),
        skip_rank,
        grad_skip_out.astype(jnp.bfloat16),
        True,
    )
    grad_joined = lax.all_gather(
        grad_joined_part.astype(jnp.bfloat16), "tensor", axis=2, tiled=True
    ).astype(grad_joined_part.dtype)
    grad_joined_full = norm_back(joined_normal, joined_inverse, grad_joined * skip_norm_gain)
    hidden_grad = grad_joined_full[:, :, :MODEL_WIDTH]
    skip_grad = grad_joined_full[:, :, MODEL_WIDTH:]
    lower_factor_parts = [
        (0, grad_skip_lower, True),
        (1, grad_mod_lower, False),
        (2, grad_query_lower, False),
        (3, grad_key_lower, False),
        (4, grad_value_lower, False),
        (5, grad_aout_lower, True),
        (6, grad_cquery_lower, False),
        (7, grad_ckey_lower, False),
        (8, grad_cvalue_lower, False),
        (9, grad_cout_lower, True),
        (10, grad_up_lower, False),
        (11, grad_down_lower, True),
    ]
    upper_factor_parts = [
        (0, grad_skip_upper, False),
        (1, grad_mod_upper, False),
        (2, grad_query_upper, True),
        (3, grad_key_upper, True),
        (4, grad_value_upper, True),
        (5, grad_aout_upper, False),
        (6, grad_cquery_upper, True),
        (7, grad_ckey_upper, True),
        (8, grad_cvalue_upper, True),
        (9, grad_cout_upper, False),
        (10, grad_up_upper, True),
        (11, grad_down_upper, False),
    ]
    slot_total = adapter_down_factor.shape[0]
    rank_total = adapter_down_factor.shape[1]
    cond_buffer = jnp.zeros((lax.axis_size("dp") * seqs_local, MODEL_WIDTH), jnp.float32)
    cond_buffer = lax.dynamic_update_slice_in_dim(
        cond_buffer, grad_condition, lax.axis_index("dp") * seqs_local, 0
    )
    cond_flat = cond_buffer.reshape(-1)

    def dense_table(parts_list, starts, total_width, row_count, slot_pieces):
        table = jnp.zeros((row_count, total_width), jnp.float32)
        for position, (number, grad_piece, is_local) in enumerate(parts_list):
            span_width = grad_piece.shape[2]
            column_start = starts[number] + tensor_rank * span_width if is_local else starts[number]
            table = lax.dynamic_update_slice_in_dim(table, slot_pieces[position], column_start, 1)
        return table

    down_factor_slots = [
        to_slots(grad_piece).reshape(slot_total * rank_total, -1)
        for number, grad_piece, is_local in lower_factor_parts
    ]
    up_factor_slots = [
        to_slots(grad_piece).reshape(slot_total * rank_total, -1)
        for number, grad_piece, is_local in upper_factor_parts
    ]
    down_compact = jnp.concatenate(down_factor_slots, axis=1)
    up_compact = jnp.concatenate(up_factor_slots, axis=1)
    cond_rows, down_rows, up_rows = (
        lax.psum_scatter(
            cond_flat.astype(jnp.bfloat16), ("dp", "ctx"), scatter_dimension=0, tiled=True
        ).astype(jnp.float32),
        lax.psum_scatter(
            down_compact.astype(jnp.bfloat16), ("dp", "ctx"), scatter_dimension=0, tiled=True
        ).astype(jnp.float32),
        lax.psum_scatter(
            up_compact.astype(jnp.bfloat16), ("dp", "ctx"), scatter_dimension=0, tiled=True
        ).astype(jnp.float32),
    )
    row_count = down_rows.shape[0]
    down_widths = [grad_piece.shape[2] for number, grad_piece, is_local in lower_factor_parts]
    up_widths = [grad_piece.shape[2] for number, grad_piece, is_local in upper_factor_parts]
    down_pieces = [
        down_rows[:, sum(down_widths[:position]) : sum(down_widths[: position + 1])]
        for position in range(12)
    ]
    up_pieces = [
        up_rows[:, sum(up_widths[:position]) : sum(up_widths[: position + 1])]
        for position in range(12)
    ]
    down_block = dense_table(
        lower_factor_parts, input_offsets, adapter_down_factor.shape[2], row_count, down_pieces
    ).reshape(-1)
    up_block = dense_table(
        upper_factor_parts, output_offsets, adapter_up_factor.shape[2], row_count, up_pieces
    ).reshape(-1)
    condition_gradient, adapter_down_gradient, adapter_up_gradient = (
        lax.psum_scatter(
            cond_rows.astype(jnp.bfloat16), "tensor", scatter_dimension=0, tiled=True
        ).astype(jnp.float32),
        lax.psum_scatter(
            down_block.astype(jnp.bfloat16), "tensor", scatter_dimension=0, tiled=True
        ).astype(jnp.float32),
        lax.psum_scatter(
            up_block.astype(jnp.bfloat16), "tensor", scatter_dimension=0, tiled=True
        ).astype(jnp.float32),
    )
    return (
        block_out.astype(jnp.bfloat16),
        hidden_grad,
        skip_grad,
        condition_gradient,
        adapter_down_gradient,
        adapter_up_gradient,
    )


BF = jnp.bfloat16
F32 = jnp.float32
MESH_ID = pl.DeviceIdType.MESH
RANK = 16
VMEM_BYTES = 60 << 20


def dot_nn(left, right):
    return jnp.dot(left, right, preferred_element_type=F32)


def dot_nt(left, right):
    return lax.dot_general(left, right, (((1,), (1,)), ((), ())), preferred_element_type=F32)


def dot_tn(left, right):
    return lax.dot_general(left, right, (((0,), (0,)), ((), ())), preferred_element_type=F32)


def stats(values):
    centered = values - jnp.mean(values, axis=-1, keepdims=True)
    inverse = lax.rsqrt(jnp.mean(centered * centered, axis=-1, keepdims=True) + NORM_EPS)
    return centered * inverse, inverse


def greet(partners):
    barrier = pltpu.get_barrier_semaphore()
    for condition, device in partners:
        @pl.when(condition)
        def _(device=device):
            pl.semaphore_signal(barrier, inc=1, device_id=device, device_id_type=MESH_ID)
    expected = sum(jnp.where(condition, 1, 0) for condition, _ in partners)
    pl.semaphore_wait(barrier, expected)


def line_partners(me, count):
    return [(me > 0, {"tensor": lax.max(me - 1, 0)}), (me < count - 1, {"tensor": lax.min(me + 1, count - 1)})]


def push(source, target, send_sem, recv_sem, device):
    return pltpu.make_async_remote_copy(
        src_ref=source,
        dst_ref=target,
        send_sem=send_sem,
        recv_sem=recv_sem,
        device_id=device,
        device_id_type=MESH_ID,
    )


class Line:
    def __init__(self, me, count, send_right, recv_left, send_left, recv_right):
        self.me, self.count = me, count
        self.sems = (send_right, recv_left, send_left, recv_right)
        self.left = {"tensor": lax.max(me - 1, 0)}
        self.right = {"tensor": lax.min(me + 1, count - 1)}
        self.has_left, self.has_right = me > 0, me < count - 1

    def to_right(self, source, target, slot):
        return push(source, target, self.sems[0].at[slot], self.sems[1].at[slot], self.right)

    def to_left(self, source, target, slot):
        return push(source, target, self.sems[2].at[slot], self.sems[3].at[slot], self.left)


def line_reduce_all(line, steps, compute, partial_ref, from_left, from_right, stage_right, stage_left, finish, beside=None):
    me, count = line.me, line.count
    far = count - 1 - me

    def step(number, carry):
        @pl.when(number < steps)
        def _():
            compute(number)

        slot_r = number - me

        @pl.when((slot_r >= 0) & (slot_r < steps))
        def _():
            slot = lax.clamp(0, slot_r, steps - 1)

            @pl.when(line.has_left)
            def _():
                line.to_right(stage_right.at[slot], from_left.at[slot], slot).wait_recv()

            @pl.when(line.has_right)
            def _():
                @pl.when(line.has_left)
                def _():
                    total = partial_ref[slot].astype(F32) + from_left[slot].astype(F32)
                    stage_right[slot] = total.astype(BF)

                @pl.when(jnp.logical_not(line.has_left))
                def _():
                    stage_right[slot] = partial_ref[slot]

                line.to_right(stage_right.at[slot], from_left.at[slot], slot).start()

        slot_l = number - far

        @pl.when((slot_l >= 0) & (slot_l < steps))
        def _():
            slot = lax.clamp(0, slot_l, steps - 1)

            @pl.when(line.has_right)
            def _():
                line.to_left(stage_left.at[slot], from_right.at[slot], slot).wait_recv()

            @pl.when(line.has_left)
            def _():
                @pl.when(line.has_right)
                def _():
                    total = partial_ref[slot].astype(F32) + from_right[slot].astype(F32)
                    stage_left[slot] = total.astype(BF)

                @pl.when(jnp.logical_not(line.has_right))
                def _():
                    stage_left[slot] = partial_ref[slot]

                line.to_left(stage_left.at[slot], from_right.at[slot], slot).start()

        if beside is not None:
            beside(number)
        slot_f = number - lax.max(me, far)

        @pl.when((slot_f >= 0) & (slot_f < steps))
        def _():
            slot = lax.clamp(0, slot_f, steps - 1)

            @pl.when(jnp.logical_not(line.has_left))
            def _():
                finish(slot, partial_ref[slot].astype(F32) + from_right[slot].astype(F32))

            @pl.when(line.has_left)
            def _():
                @pl.when(line.has_right)
                def _():
                    finish(
                        slot,
                        partial_ref[slot].astype(F32)
                        + from_left[slot].astype(F32)
                        + from_right[slot].astype(F32),
                    )

                @pl.when(jnp.logical_not(line.has_right))
                def _():
                    finish(slot, partial_ref[slot].astype(F32) + from_left[slot].astype(F32))

        return carry

    lax.fori_loop(0, steps + count - 1, step, 0)

    def drain(slot, carry):
        @pl.when(line.has_right)
        def _():
            line.to_right(stage_right.at[slot], from_left.at[slot], slot).wait_send()

        @pl.when(line.has_left)
        def _():
            line.to_left(stage_left.at[slot], from_right.at[slot], slot).wait_send()

        return carry

    lax.fori_loop(0, steps, drain, 0)


def scatter_order(me, count, place):
    near = lax.min(me, count - 1 - me)
    base = count - 1 - 2 * near
    index = place - base
    block = jnp.where(
        place < base,
        count - 1 - place,
        jnp.where(index % 2 == 0, 2 * near - index // 2, index // 2),
    )
    return jnp.where(2 * me > count - 1, count - 1 - block, block)


def line_scatter_step(line, number, partial_ref, from_left, from_right, stage_right, stage_left):
    me, count = line.me, line.count
    block_r = count - 1 - number + me

    @pl.when((number >= me) & line.has_right & (block_r > me))
    def _():
        block = lax.clamp(0, block_r, count - 1)

        @pl.when(line.has_left)
        def _():
            line.to_right(stage_right.at[block], from_left.at[block], block).wait_recv()
            total = partial_ref[block].astype(F32) + from_left[block].astype(F32)
            stage_right[block] = total.astype(BF)

        @pl.when(jnp.logical_not(line.has_left))
        def _():
            stage_right[block] = partial_ref[block]

        line.to_right(stage_right.at[block], from_left.at[block], block).start()

    block_l = number - (count - 1 - me)

    @pl.when((block_l >= 0) & line.has_left & (block_l < me))
    def _():
        block = lax.clamp(0, block_l, count - 1)

        @pl.when(line.has_right)
        def _():
            line.to_left(stage_left.at[block], from_right.at[block], block).wait_recv()
            total = partial_ref[block].astype(F32) + from_right[block].astype(F32)
            stage_left[block] = total.astype(BF)

        @pl.when(jnp.logical_not(line.has_right))
        def _():
            stage_left[block] = partial_ref[block]

        line.to_left(stage_left.at[block], from_right.at[block], block).start()


def line_scatter_finish(line, partial_ref, from_left, from_right, stage_right, stage_left, total_ref):
    me, count = line.me, line.count
    total_ref[...] = partial_ref[me].astype(F32)

    @pl.when(line.has_left)
    def _():
        line.to_right(stage_right.at[me], from_left.at[me], me).wait_recv()
        total_ref[...] += from_left[me].astype(F32)

    @pl.when(line.has_right)
    def _():
        line.to_left(stage_left.at[me], from_right.at[me], me).wait_recv()
        total_ref[...] += from_right[me].astype(F32)

    def drain(block, carry):
        @pl.when(block > me)
        def _():
            line.to_right(stage_right.at[block], from_left.at[block], block).wait_send()

        @pl.when(block < me)
        def _():
            line.to_left(stage_left.at[block], from_right.at[block], block).wait_send()

        return carry

    lax.fori_loop(0, count, drain, 0)


def line_gather_step(line, number, slots):
    me, count = line.me, line.count
    block_l = lax.clamp(0, me - number, count - 1)
    block_r = lax.clamp(0, me + number, count - 1)

    @pl.when(number <= me)
    def _():
        @pl.when(number > 0)
        def _():
            line.to_right(slots.at[block_l], slots.at[block_l], block_l).wait_recv()

        @pl.when(line.has_right)
        def _():
            line.to_right(slots.at[block_l], slots.at[block_l], block_l).start()

    @pl.when(me + number <= count - 1)
    def _():
        @pl.when(number > 0)
        def _():
            line.to_left(slots.at[block_r], slots.at[block_r], block_r).wait_recv()

        @pl.when(line.has_left)
        def _():
            line.to_left(slots.at[block_r], slots.at[block_r], block_r).start()


def line_gather_drain(line, slots):
    me, count = line.me, line.count

    def drain(block, carry):
        @pl.when((block <= me) & line.has_right)
        def _():
            line.to_right(slots.at[block], slots.at[block], block).wait_send()

        @pl.when((block >= me) & line.has_left)
        def _():
            line.to_left(slots.at[block], slots.at[block], block).wait_send()

        return carry

    lax.fori_loop(0, count, drain, 0)


def line_gather(line, slots, compute):
    me, count = line.me, line.count

    def step(number, carry):
        line_gather_step(line, number, slots)

        def side(which, inner):
            block = me + (2 * which - 1) * number

            @pl.when((block >= 0) & (block < count) & ((number > 0) | (which == 0)))
            def _():
                compute(lax.clamp(0, block, count - 1))

            return inner

        return lax.fori_loop(0, 2, side, carry)

    lax.fori_loop(0, count, step, 0)
    line_gather_drain(line, slots)


def xor_place(place, number):
    if number == 0:
        return place
    if number == 1:
        return place + 1 - 2 * (place % 2)
    if number == 2:
        return place + 2 - 4 * (place // 2)
    return 3 - place


def call(kernel, inputs, outs, scratch, collective=None, cost=None):
    space = {True: pltpu.VMEM, False: pl.ANY}
    return pl.pallas_call(
        kernel,
        out_shape=[jax.ShapeDtypeStruct(shape, dtype) for shape, dtype, _ in outs],
        in_specs=[pl.BlockSpec(memory_space=space[where]) for _, where in inputs],
        out_specs=[pl.BlockSpec(memory_space=space[where]) for _, _, where in outs],
        scratch_shapes=scratch,
        cost_estimate=cost,
        compiler_params=pltpu.CompilerParams(
            collective_id=collective,
            has_side_effects=collective is not None,
            vmem_limit_bytes=VMEM_BYTES,
        ),
    )(*[array for array, _ in inputs])


def cost_of(flops, moved):
    return pl.CostEstimate(flops=int(flops), bytes_accessed=int(moved), transcendentals=0)


def vmem(*shape, dtype=BF):
    return pltpu.VMEM(shape, dtype)


def dma(*shape):
    return pltpu.SemaphoreType.DMA(shape)


def whole_wait(target, sem):
    pltpu.make_async_copy(target, target, sem).wait()


def rows_of(index, size):
    return pl.ds(pl.multiple_of(index * size, size), size)


def cross_forward(count, heads, summed, skip_out, query_weight, out_weight, skip_piece, text_kv, gains, down, up,
                  out_down, out_up):
    share, width = summed.shape
    local = query_weight.shape[-1]
    scale = HD ** (-0.5)
    rows, span = skip_piece.shape

    def kernel(sum_ref, skip_ref, hbm_q, hbm_o, piece, kv, gain, a_ref, b_ref, ao, bo, first_out, second_out, in_out,
               mlp_out, q_out, inv_out, log_out, low_out, uo_out, skip_half, wq, wo, wsem, zsend, zrecv):
        me = lax.axis_index("tensor")
        core = lax.axis_index("ctx")
        loads = [
            pltpu.make_async_copy(source, target, wsem.at[number])
            for number, (source, target) in enumerate(((hbm_q, wq), (hbm_o, wo)))
        ]
        for load in loads:
            load.start()
        half = pl.ds(pl.multiple_of(core * (rows // 2), 16), rows // 2)
        own = pltpu.make_async_copy(piece.at[half, :], skip_half.at[me], wsem.at[2])
        own.start()
        z_peers = [{"tensor": xor_place(me, number)} for number in range(1, count)]
        greet([(core >= 0, device) for device in z_peers])
        sends = [
            push(piece.at[half, :], skip_half.at[me], zsend.at[number], zrecv.at[number], device)
            for number, device in enumerate(z_peers)
        ]
        for send in sends:
            send.start()
        first = skip_ref[rows_of(me, share), :] + sum_ref[...]
        first_out[...] = first
        normal, _ = stats(first)
        x = (normal * gain[1:2, :]).astype(BF)
        in_out[...] = x
        u = dot_nt(x, a_ref[...]).astype(BF)
        second_out[...] = first
        for load in loads:
            load.wait()

        def chunk(place, u_low):
            y = dot_nn(x, wq[place]) + dot_nn(u, b_ref[place])
            outs = []
            for head in range(heads):
                normal, inverse = stats(y[:, head * HD : (head + 1) * HD])
                q = normal.astype(BF)
                q_out[place, head] = q
                inv_out[place, head] = inverse
                s = dot_nt(q, kv[0, place, head, :, :HD]) * scale
                top = jnp.max(s, axis=-1, keepdims=True)
                e = jnp.exp(s - top)
                total = jnp.sum(e, axis=-1, keepdims=True)
                p = (e * (1.0 / total)).astype(BF)
                outs.append(dot_nn(p, kv[1, place, head, :, :HD]))
                log_out[place, head] = top + jnp.log(total)
            low = jnp.concatenate(outs, axis=1).astype(BF)
            low_out[place] = low
            second_out[...] += dot_nt(low, wo[place])
            return u_low + dot_nt(low, ao[place])

        u_low = lax.fori_loop(0, count, chunk, jnp.zeros((share, RANK), F32)).astype(BF)
        uo_out[...] = u_low
        second = second_out[...] + dot_nn(u_low, bo[...])
        second_out[...] = second
        normal, _ = stats(second)
        mlp_out[...] = (normal * gain[2:3, :]).astype(BF)
        own.wait()
        for number in range(count - 1):
            arrived = skip_half.at[xor_place(me, number + 1)]
            push(arrived, arrived, zsend.at[number], zrecv.at[number], z_peers[number]).wait_recv()
        for send in sends:
            send.wait_send()

    return call(
        kernel,
        [(summed, True), (skip_out, True), (query_weight, False), (out_weight, False), (skip_piece, False)]
        + [(array, True) for array in (text_kv, gains, down, up, out_down, out_up)],
        [
            ((share, width), F32, True),
            ((share, width), F32, True),
            ((share, width), BF, True),
            ((share, width), BF, True),
            ((count, heads, share, HD), BF, True),
            ((count, heads, share, 1), F32, True),
            ((count, heads, share, 1), F32, True),
            ((count, share, local), BF, True),
            ((share, RANK), BF, True),
            ((count, rows // 2, span), BF, False),
        ],
        [vmem(count, width, local), vmem(count, width, local), dma(3), dma(count), dma(count)],
        collective=6,
        cost=cost_of(4 * share * width * width, 20e6),
    )


def feed_forward(count, block_in, cotangent, second, up_weight, down_weight, skip_half, up_a, up_b, down_a, down_b):
    share, width = block_in.shape
    tokens = cotangent.shape[0]
    hidden_units = up_weight.shape[1]
    rows = 2 * skip_half.shape[1]
    span = skip_half.shape[2]

    def kernel(x_ref, cot, sec, hbm_u, hbm_d, shalf, ua, ub, da, db, summed, down_out, g_ua, g_ub, g_da, g_db, skip_all,
               slots, wu, wd, partial_ref, from_left, from_right, stage_right, stage_left, wsem, wsend, wrecv, *sems):
        me = lax.axis_index("tensor")
        core = lax.axis_index("ctx")
        dp = lax.axis_index("dp")
        gather_line = Line(me, count, *sems[:4])
        scatter_line = Line(me, count, *sems[4:])
        loads = [
            pltpu.make_async_copy(source, target, wsem.at[number])
            for number, (source, target) in enumerate(((hbm_u, wu), (hbm_d, wd)))
        ]
        for load in loads:
            load.start()
        skip = Shared(skip_all, rows, (wsend, wrecv, 0), stacked=True)
        own = pltpu.make_async_copy(shalf, skip.view(dp, core), wsem.at[2])
        own.start()
        slots[me] = x_ref[...]
        for ref in (g_ua, g_ub, g_da, g_db):
            ref[...] = jnp.zeros_like(ref)
        peers = [{"dp": xor_place(dp, 1)}, {"dp": xor_place(dp, 2)}, {"ctx": 1 - core}]
        greet(line_partners(me, count) + [(core >= 0, device) for device in peers])
        line_gather_step(gather_line, 0, slots)
        skip.send_own(shalf)
        for load in loads:
            load.wait()

        def compute(block):
            rows = rows_of(block, share)
            x = slots[block]
            ct = cot[rows, :]
            u = dot_nt(x, ua[...]).astype(BF)
            up = dot_nn(x, wu[...]) + dot_nn(u, ub[...])
            square = up * up
            curve = jnp.tanh(0.7978845608028654 * (up + 0.044715 * square * up))
            half = 0.5 * (1.0 + curve)
            active = (up * half).astype(BF)
            slope = half + 0.5 * up * (1.0 - curve * curve) * (0.7978845608028654 * (1.0 + 0.134145 * square))
            ud = dot_nt(active, da[...]).astype(BF)
            down = dot_nt(active, wd[...]) + dot_nn(ud, db[...])
            down_out[rows, :] = down.astype(BF)

            @pl.when(block == me)
            def _():
                down_out[rows, :] = (down + sec[...]).astype(BF)

            gd = dot_nt(ct, db[...]).astype(BF)
            g_active = dot_nn(ct, wd[...]) + dot_nn(gd, da[...])
            g_up = (g_active * slope).astype(BF)
            gu = dot_nt(g_up, ub[...]).astype(BF)
            partial_ref[block] = (dot_nt(g_up, wu[...]) + dot_nn(gu, ua[...])).astype(BF)
            g_ub[...] += dot_tn(u, g_up)
            g_ua[...] += dot_tn(gu, x)
            g_db[...] += dot_tn(ud, ct)
            g_da[...] += dot_tn(gd, active)

        compute(me)

        def step(number, carry):
            line_gather_step(gather_line, number, slots)

            def side(which, inner):
                block = me + (2 * which - 1) * number

                @pl.when((block >= 0) & (block < count))
                def _():
                    compute(lax.clamp(0, block, count - 1))

                return inner

            return lax.fori_loop(0, 2, side, carry)

        lax.fori_loop(1, count, step, 0)
        own.wait()
        skip.wait(0)
        skip.forward()
        skip.swap(0)
        skip.swap(3)

        def scatter(number, carry):
            line_scatter_step(scatter_line, number, partial_ref, from_left, from_right, stage_right, stage_left)
            return carry

        lax.fori_loop(0, count - 1, scatter, 0)
        skip.wait(1)
        skip.swap(1)
        line_gather_drain(gather_line, slots)
        line_scatter_finish(scatter_line, partial_ref, from_left, from_right, stage_right, stage_left, summed)
        skip.wait(2)
        skip.swap(2)
        skip.wait_swaps()
        skip.drain()

    buffers = [vmem(count, share, width) for _ in range(5)]
    return call(
        kernel,
        [(block_in, True), (cotangent, True), (second, True), (up_weight, False), (down_weight, False), (skip_half, False)]
        + [(array, True) for array in (up_a, up_b, down_a, down_b)],
        [
            ((share, width), F32, True),
            ((tokens, width), BF, True),
            ((RANK, width), F32, True),
            ((RANK, hidden_units), F32, True),
            ((RANK, hidden_units), F32, True),
            ((RANK, width), F32, True),
            ((count, 4 * rows, span), BF, False),
        ],
        [vmem(count, share, width), vmem(width, hidden_units), vmem(width, hidden_units)]
        + buffers + [dma(3), dma(1, 7), dma(1, 7)] + [dma(count) for _ in range(8)],
        collective=3,
        cost=cost_of(8 * tokens * width * hidden_units, 60e6),
    )


class Shared:
    def __init__(self, target, rows, sems, stacked=False, split=True):
        self.target, self.rows, self.stacked, self.split = target, rows, stacked, split
        self.send_sem, self.recv_sem, self.index = sems
        dp, core = lax.axis_index("dp"), lax.axis_index("ctx")
        self.dp, self.core = dp, core
        self.first = jnp.where(core == 0, xor_place(dp, 1), xor_place(dp, 2))
        self.second = jnp.where(core == 0, xor_place(dp, 2), xor_place(dp, 1))
        self.third = xor_place(dp, 3)

    def view(self, block, which):
        size = self.rows // 2 if self.split else self.rows
        start = block * self.rows + (which * size if self.split else 0)
        rows = pl.ds(pl.multiple_of(start, 16), size)
        return self.target.at[:, rows, :] if self.stacked else self.target.at[rows, :]

    def copy(self, number, source, block, which, device):
        target = self.view(block, which)
        source = target if source is None else source
        return push(source, target, self.send_sem.at[self.index, number], self.recv_sem.at[self.index, number], device)

    def send_own(self, source=None):
        self.copy(0, source, self.dp, self.core, {"dp": self.first}).start()
        self.copy(1, source, self.dp, self.core, {"dp": self.second}).start()

    def blocks(self):
        return [self.first, self.second, self.third] + ([self.dp] if self.stacked else [])

    def wait(self, number):
        self.copy(number, None, self.blocks()[number], self.core, {"dp": self.first}).wait_recv()

    def forward(self):
        self.copy(2, None, self.first, self.core, {"dp": self.second}).start()

    def swap(self, number):
        self.copy(3 + number, None, self.blocks()[number], self.core, {"ctx": 1 - self.core}).start()

    def wait_swaps(self):
        other = [self.second, self.first, self.third, self.dp]
        for number in range(len(self.blocks())):
            self.copy(3 + number, None, other[number], 1 - self.core, {"ctx": 1 - self.core}).wait_recv()

    def drain(self):
        for number in range(3 + (len(self.blocks()) if self.split else 0)):
            self.copy(number, None, self.dp, self.core, {"dp": self.first}).wait_send()


def front(count, heads, act, tag, hidden, long_skip, part, part_gain, text, weights, mods, gain_row, skip_ab, text_ab,
          qkv_ab, out_ab):
    tokens, width = hidden.shape
    span = part.shape[1]
    words, text_width = text.shape
    local = weights["q"].shape[1]
    units = weights["up"].shape[1]
    share = tokens // count
    block = min(128, tokens)
    chunk = min(64, tokens)
    steps = tokens // chunk
    each = block // chunk
    scale = HD ** (-0.5)
    rows = weights["q"].shape[0]
    text_rows = weights["ck"].shape[0]
    mod_rows = mods[0].shape[0]

    def kernel(skip_own, q_own, k_own, v_own, o_own, ck_own, cv_own, cq_own, co_own, up_own, dn_own,
               act_ref, tag_ref, hid, lsk, par, pgain, t_ref, wm, ma, mb, gain, sa, sb, ta, tk, tv, qa, qb, kb, vb, oa, ob,
               skip_out, attn_in, q_out, keys, values, low_out, log_out, inv_q, inv_k, summed, act_all, text_kv,
               wq, wk, wv, wo, wcq, wco, wup, wdn,
               wskip, wtext, mod_in, mod_slice, mod_out, partial_a, left_a, right_a, sr_a, sl_a,
               partial_b, left_b, right_b, sr_b, sl_b, wsend, wrecv, local_sem, zsend, zrecv, msend, mrecv, tsend, trecv,
               xsend, xrecv, *sems):
        me = lax.axis_index("tensor")
        core = lax.axis_index("ctx")
        dp = lax.axis_index("dp")
        always = core >= 0
        peer = {"ctx": 1 - core}
        dp_peers = [{"dp": xor_place(dp, number)} for number in (1, 2, 3)]
        z_peers = [{"tensor": xor_place(me, number)} for number in range(1, count)]
        reduce_line = Line(me, count, *sems[:4])
        scatter_line = Line(me, count, *sems[4:])

        def sems_of(number):
            return (wsend, wrecv, number)

        skip = Shared(wskip, rows, sems_of(0))
        shared = {
            name: Shared(target, rows, sems_of(number))
            for name, target, number in (("q", wq, 1), ("k", wk, 2), ("v", wv, 3), ("o", wo, 4))
        }
        words_w = Shared(wtext, text_rows, sems_of(5), split=False)
        cross = [Shared(wcq, rows, sems_of(6), stacked=True), Shared(wco, rows, sems_of(7), stacked=True)]
        wide = [Shared(wup, rows, sems_of(8)), Shared(wdn, rows, sems_of(9))]
        owns = {"q": q_own, "k": k_own, "v": v_own, "o": o_own}
        half = pl.ds(pl.multiple_of(core * (rows // 2), 16), rows // 2)
        mine = pl.ds(pl.multiple_of(dp * rows, 16), rows)
        my_half = pl.ds(pl.multiple_of(dp * rows + core * (rows // 2), 16), rows // 2)

        places = [
            pltpu.make_async_copy(source, target.at[mine, :], local_sem.at[number])
            for number, (source, target) in enumerate(
                ((skip_own, wskip), (q_own, wq), (k_own, wk), (v_own, wv), (o_own, wo), (up_own, wup), (dn_own, wdn))
            )
        ]
        for place in places:
            place.start()
        crossing = [
            pltpu.make_async_copy(source.at[half, :], target.at[me, my_half, :], local_sem.at[7 + number])
            for number, (source, target) in enumerate(((cq_own, wcq), (co_own, wco)))
        ]
        text_mine = pl.ds(pl.multiple_of(dp * text_rows, 16), text_rows)

        def text_place(source):
            return pltpu.make_async_copy(source, wtext.at[text_mine, :], local_sem.at[9])

        @pl.when(core == 0)
        def _():
            text_place(ck_own).start()

        @pl.when(core == 1)
        def _():
            text_place(cv_own).start()

        for place in crossing:
            place.start()
        act_all[dp] = jnp.concatenate([act_ref[...].astype(F32), tag_ref[...]], axis=1)
        greet([(always, device) for device in dp_peers + z_peers + [peer]])
        skip.send_own(skip_own.at[half, :])

        def z_copies(number):
            return [
                push(source.at[half, :], target.at[me, my_half, :], zsend.at[which, number], zrecv.at[which, number],
                     z_peers[number])
                for which, (source, target) in enumerate(((cq_own, wcq), (co_own, wco)))
            ]

        for number in range(count - 1):
            for copy in z_copies(number):
                copy.start()
        spread = [
            push(act_all.at[dp], act_all.at[dp], msend.at[0, number], mrecv.at[0, number], device)
            for number, device in enumerate(dp_peers)
        ]
        for copy in spread:
            copy.start()
        skip.wait(0)
        skip.forward()
        for name in ("q", "k", "v", "o"):
            shared[name].send_own(owns[name].at[half, :])

        @pl.when(core == 0)
        def _():
            words_w.send_own(ck_own)

        @pl.when(core == 1)
        def _():
            words_w.send_own(cv_own)

        skip.swap(0)

        for number in (1, 2, 3):
            source = act_all.at[xor_place(dp, number)]
            push(source, source, msend.at[0, number - 1], mrecv.at[0, number - 1], dp_peers[number - 1]).wait_recv()
        for owner in range(4):
            @pl.when(dp == owner)
            def _(owner=owner):
                span_of = slice(owner * mod_rows, (owner + 1) * mod_rows)
                for sequence in range(4):
                    mod_slice[sequence : sequence + 1, :] = act_all[sequence, :, span_of]

        products = dot_nn(mod_slice[...].astype(BF), wm[...])
        for sequence in range(4):
            mod_out[sequence] = products[sequence : sequence + 1]
        backs = [
            push(mod_out.at[xor_place(dp, number)], mod_in.at[dp], msend.at[1, number - 1], mrecv.at[1, number - 1],
                 dp_peers[number - 1])
            for number in (1, 2, 3)
        ]
        for copy in backs:
            copy.start()
        skip.wait(1)
        skip.swap(1)
        mod_in[dp] = mod_out[dp]
        mod_u = dot_nt(act_ref[...], ma[...]).astype(BF)
        mod_low = dot_nn(mod_u, mb[...])
        for number in (1, 2, 3):
            target = mod_in.at[xor_place(dp, number)]
            push(target, target, msend.at[1, number - 1], mrecv.at[1, number - 1], dp_peers[number - 1]).wait_recv()
        shift = mod_in[0] + mod_in[1] + mod_in[2] + mod_in[3] + mod_low
        skip.wait(2)
        skip.swap(2)
        places[0].wait()
        skip.wait_swaps()

        def compute(number):
            @pl.when(number % each == 0)
            def _():
                here = rows_of(number // each, block)
                left = hid[here, :].astype(F32)
                right = lsk[here, :].astype(F32)
                mean = (jnp.sum(left, axis=-1, keepdims=True) + jnp.sum(right, axis=-1, keepdims=True)) / (2 * width)
                spread = jnp.sum((left - mean) ** 2, axis=-1, keepdims=True)
                spread += jnp.sum((right - mean) ** 2, axis=-1, keepdims=True)
                inverse = lax.rsqrt(spread / (2 * width) + NORM_EPS)
                x = ((par[here, :].astype(F32) - mean) * inverse * pgain[...]).astype(BF)
                u = dot_nt(x, sa[...]).astype(BF)
                y = (dot_nt(x, wskip[...]) + dot_nn(u, sb[...])).astype(BF)
                for piece in range(each):
                    partial_a[number + piece] = y[piece * chunk : (piece + 1) * chunk]

        def finish(slot, total):
            here = rows_of(slot, chunk)
            skip_out[here, :] = total
            normal, _ = stats(total)
            attn_in[here, :] = (normal * gain[...] + shift).astype(BF)

        def beside(number):
            @pl.when(number == 3)
            def _():
                for weight in (*shared.values(), words_w):
                    weight.wait(0)
                    weight.forward()
                for weight in shared.values():
                    weight.swap(0)

            @pl.when(number == 4)
            def _():
                for weight in (*shared.values(), words_w):
                    weight.wait(1)
                for weight in shared.values():
                    weight.swap(1)

            @pl.when(number == 6)
            def _():
                for place in crossing:
                    place.wait()
                for other in range(count - 1):
                    for which, target in enumerate((wcq, wco)):
                        block_in = target.at[xor_place(me, other + 1), my_half, :]
                        push(block_in, block_in, zsend.at[which, other], zrecv.at[which, other], z_peers[other]).wait_recv()
                for weight in cross:
                    weight.send_own()

            @pl.when(number == 7)
            def _():
                for weight in (*shared.values(), words_w):
                    weight.wait(2)
                for weight in shared.values():
                    weight.swap(2)

        line_reduce_all(reduce_line, steps, compute, partial_a, left_a, right_a, sr_a, sl_a, finish, beside)

        @pl.when(core == 0)
        def _():
            text_place(ck_own).wait()

        @pl.when(core == 1)
        def _():
            text_place(cv_own).wait()

        x = t_ref[...]
        u = dot_nt(x, ta[...]).astype(BF)
        y = dot_nn(x, wtext[...])

        @pl.when(core == 0)
        def _():
            z = y + dot_nn(u[:, :RANK], tk[...])
            for head in range(heads):
                normal, inverse = stats(z[:, head * HD : (head + 1) * HD])
                upper = inverse.astype(BF)
                lower = (inverse - upper.astype(F32)).astype(BF)
                text_kv[0, me, head] = jnp.concatenate([normal.astype(BF), upper, lower], axis=1)

        @pl.when(core == 1)
        def _():
            z = (y + dot_nn(u[:, RANK:], tv[...])).astype(BF)
            filler = jnp.zeros((words, 2), BF)
            for head in range(heads):
                text_kv[1, me, head] = jnp.concatenate([z[:, head * HD : (head + 1) * HD], filler], axis=1)

        texts = [
            push(text_kv.at[core, me], text_kv.at[core, me], tsend.at[number], trecv.at[number], z_peers[number])
            for number in range(count - 1)
        ]
        for copy in texts:
            copy.start()

        for number in range(1, 5):
            places[number].wait()
        for weight in shared.values():
            weight.wait_swaps()

        def project(number, carry):
            here = rows_of(number, block)
            x = attn_in[here, :]
            u = dot_nt(x, qa[...]).astype(BF)
            yq = dot_nn(x, wq[...]) + dot_nn(u[:, :RANK], qb[...])
            yk = dot_nn(x, wk[...]) + dot_nn(u[:, RANK : 2 * RANK], kb[...])
            yv = (dot_nn(x, wv[...]) + dot_nn(u[:, 2 * RANK :], vb[...])).astype(BF)
            for head in range(heads):
                span_of = slice(head * HD, (head + 1) * HD)
                normal, inverse = stats(yq[:, span_of])
                q_out[head, here, :] = normal.astype(BF)
                inv_q[head, here, :] = inverse
                normal, inverse = stats(yk[:, span_of])
                keys[core, head, here, :] = normal.astype(BF)
                inv_k[head, here, :] = inverse
                values[core, head, here, :] = yv[:, span_of]
            return carry

        lax.fori_loop(0, tokens // block, project, 0)
        swaps = [
            push(ref.at[core], ref.at[core], xsend.at[number], xrecv.at[number], peer)
            for number, ref in enumerate((keys, values))
        ]
        for swap in swaps:
            swap.start()
        for weight in cross:
            weight.wait(0)
            weight.forward()
            weight.swap(0)
            weight.swap(3)
        for weight, own in zip(wide, (up_own, dn_own)):
            weight.send_own(own.at[half, :])
        for number, ref in enumerate((keys, values)):
            push(ref.at[1 - core], ref.at[1 - core], xsend.at[number], xrecv.at[number], peer).wait_recv()

        def attend(place, carry):
            dest = scatter_order(me, count, place)
            here = rows_of(dest, share)
            outs = []
            for head in range(heads):
                q = q_out[head, here, :]
                s0 = dot_nt(q, keys[0, head]) * scale
                s1 = dot_nt(q, keys[1, head]) * scale
                top = jnp.maximum(jnp.max(s0, axis=-1, keepdims=True), jnp.max(s1, axis=-1, keepdims=True))
                e0 = jnp.exp(s0 - top)
                e1 = jnp.exp(s1 - top)
                total = jnp.sum(e0, axis=-1, keepdims=True) + jnp.sum(e1, axis=-1, keepdims=True)
                share_of = 1.0 / total
                p0 = (e0 * share_of).astype(BF)
                p1 = (e1 * share_of).astype(BF)
                outs.append(dot_nn(p0, values[0, head]) + dot_nn(p1, values[1, head]))
                log_out[head, here, :] = top + jnp.log(total)
            low = jnp.concatenate(outs, axis=1).astype(BF)
            low_out[here, :] = low
            u = dot_nt(low, oa[...]).astype(BF)
            partial_b[dest] = (dot_nt(low, wo[...]) + dot_nn(u, ob[...])).astype(BF)

            @pl.when(place < count - 1)
            def _():
                line_scatter_step(scatter_line, place, partial_b, left_b, right_b, sr_b, sl_b)

            @pl.when(place == 1)
            def _():
                for weight in cross:
                    weight.wait(1)
                    weight.swap(1)
                for number in range(count - 1):
                    arrived = text_kv.at[core, xor_place(me, number + 1)]
                    push(arrived, arrived, tsend.at[number], trecv.at[number], z_peers[number]).wait_recv()
                push(text_kv.at[core], text_kv.at[core], tsend.at[count - 1], trecv.at[count - 1], peer).start()

            @pl.when(place == 2)
            def _():
                for weight in cross:
                    weight.wait(2)
                    weight.swap(2)

            return carry

        lax.fori_loop(0, count, attend, 0)
        for weight in wide:
            weight.wait(0)
            weight.forward()
            weight.swap(0)
        for weight in wide:
            weight.wait(1)
            weight.swap(1)
        line_scatter_finish(scatter_line, partial_b, left_b, right_b, sr_b, sl_b, summed)
        for weight in wide:
            weight.wait(2)
            weight.swap(2)
        others = text_kv.at[1 - core]
        push(others, others, tsend.at[count - 1], trecv.at[count - 1], peer).wait_recv()
        for weight in cross + wide:
            weight.wait_swaps()
        places[5].wait()
        places[6].wait()
        for weight in (skip, *shared.values(), words_w, *cross, *wide):
            weight.drain()
        for number in range(count - 1):
            for copy in z_copies(number):
                copy.wait_send()
        for copy in spread + backs + texts:
            copy.wait_send()
        push(text_kv.at[core], text_kv.at[core], tsend.at[count - 1], trecv.at[count - 1], peer).wait_send()
        for swap in swaps:
            swap.wait_send()

    names = ("skip", "q", "k", "v", "o", "ck", "cv", "cq", "co", "up", "dn")
    return call(
        kernel,
        [(weights[name], False) for name in names]
        + [(array, True) for array in (act, tag, hidden, long_skip, part, part_gain, text, *mods, gain_row, *skip_ab,
                                       *text_ab, *qkv_ab, *out_ab)],
        [
            ((tokens, width), F32, True),
            ((tokens, width), BF, True),
            ((heads, tokens, HD), BF, True),
            ((2, heads, tokens, HD), BF, True),
            ((2, heads, tokens, HD), BF, True),
            ((tokens, local), BF, True),
            ((heads, tokens, 1), F32, True),
            ((heads, tokens, 1), F32, True),
            ((heads, tokens, 1), F32, True),
            ((share, width), F32, True),
            ((4, 1, width + 128), F32, True),
            ((2, count, heads, words, HD + 2), BF, True),
        ]
        + [((width, local), BF, True) for _ in range(4)]
        + [((count, width, local), BF, False) for _ in range(2)]
        + [((width, units), BF, False) for _ in range(2)],
        [vmem(width, span), vmem(text_width, local), vmem(4, 1, width, dtype=F32), vmem(4, mod_rows, dtype=F32),
         vmem(4, 1, width, dtype=F32)]
        + [vmem(steps, chunk, width) for _ in range(5)] + [vmem(count, share, width) for _ in range(5)]
        + [dma(10, 7), dma(10, 7), dma(10), dma(2, count), dma(2, count), dma(2, 3), dma(2, 3), dma(count), dma(count),
           dma(2), dma(2)]
        + [dma(steps) for _ in range(4)] + [dma(count) for _ in range(4)],
        collective=1,
        cost=cost_of(8 * tokens * width * local, 60e6),
    )


def norm_backward(normal, inverse, grad):
    return inverse * (
        grad
        - jnp.mean(grad, axis=-1, keepdims=True)
        - normal * jnp.mean(grad * normal, axis=-1, keepdims=True)
    )


def cross_backward(count, heads, g_in, cotangent, first, second, block_in, query, inverses, logs, low, u_low, text,
                   query_weight, out_weight, text_kv, gains, down, up, out_down, out_up, text_down, up_key, up_value):
    share, width = g_in.shape
    local = query_weight.shape[-1]
    words, text_width = text.shape
    scale = HD ** (-0.5)

    def kernel(g_ref, cot, first_ref, second_ref, x_ref, q_ref, inv_ref, log_ref, low_ref, uo_ref, t_ref, hbm_q, hbm_o,
               kv, gain, a_ref, b_ref, ao, bo, at, bk, bv, g_first, ga_q, gb_q, ga_k, gb_k, ga_v, gb_v, ga_o, gb_o,
               acc, wq, wo, wsem):
        me = lax.axis_index("tensor")
        loads = [
            pltpu.make_async_copy(source, target, wsem.at[number])
            for number, (source, target) in enumerate(((hbm_q, wq), (hbm_o, wo)))
        ]
        for load in loads:
            load.start()
        normal, inverse = stats(second_ref[...])
        g_second = cot[rows_of(me, share), :].astype(F32) + norm_backward(normal, inverse, g_ref[...] * gain[2:3, :])
        g_low = g_second.astype(BF)
        go = dot_nt(g_low, bo[...]).astype(BF)
        gb_o[...] = dot_tn(uo_ref[...], g_low)
        x = x_ref[...]
        uq = dot_nt(x, a_ref[...]).astype(BF)
        words_in = t_ref[...]
        ut = dot_nt(words_in, at[...]).astype(BF)
        uk, uv = ut[:, :RANK], ut[:, RANK:]
        acc[...] = jnp.zeros_like(acc)
        for load in loads:
            load.wait()

        def chunk(place, carry):
            gq_sum, gk_sum, gv_sum = carry
            g_attn = (dot_nn(g_low, wo[place]) + dot_nn(go, ao[place])).astype(BF)
            ga_o[place] = dot_tn(go, low_ref[place])
            gq_parts, gk_parts, gv_parts = [], [], []
            for head in range(heads):
                gh = g_attn[:, head * HD : (head + 1) * HD]
                q = q_ref[place, head]
                kfull = kv[0, place, head]
                k = kfull[:, :HD]
                v = kv[1, place, head, :, :HD]
                p = jnp.exp(dot_nt(q, k) * scale - log_ref[place, head])
                dp = dot_nt(gh, v)
                inner = jnp.sum(p * dp, axis=-1, keepdims=True)
                ds = (p * (dp - inner)).astype(BF)
                dq = dot_nn(ds, k) * scale
                dk = dot_tn(ds, q) * scale
                dv = dot_tn(p.astype(BF), gh)
                gq_parts.append(norm_backward(q.astype(F32), inv_ref[place, head], dq))
                inv_k = kfull[:, HD : HD + 1].astype(F32) + kfull[:, HD + 1 : HD + 2].astype(F32)
                gk_parts.append(norm_backward(k.astype(F32), inv_k, dk))
                gv_parts.append(dv)
            gq = jnp.concatenate(gq_parts, axis=1).astype(BF)
            gk = jnp.concatenate(gk_parts, axis=1).astype(BF)
            gv = jnp.concatenate(gv_parts, axis=1).astype(BF)
            acc[...] += dot_nt(gq, wq[place])
            gb_q[place] = dot_tn(uq, gq)
            gb_k[place] = dot_tn(uk, gk)
            gb_v[place] = dot_tn(uv, gv)
            return (
                gq_sum + dot_nt(gq, b_ref[place]),
                gk_sum + dot_nt(gk, bk[place]),
                gv_sum + dot_nt(gv, bv[place]),
            )

        start = (jnp.zeros((share, RANK), F32), jnp.zeros((words, RANK), F32), jnp.zeros((words, RANK), F32))
        gq_sum, gk_sum, gv_sum = lax.fori_loop(0, count, chunk, start)
        gq_sum = gq_sum.astype(BF)
        ga_q[...] = dot_tn(gq_sum, x)
        ga_k[...] = dot_tn(gk_sum.astype(BF), words_in)
        ga_v[...] = dot_tn(gv_sum.astype(BF), words_in)
        g_x = acc[...] + dot_nn(gq_sum, a_ref[...])
        normal, inverse = stats(first_ref[...])
        g_first[...] = (g_second + norm_backward(normal, inverse, g_x * gain[1:2, :])).astype(BF)

    return call(
        kernel,
        [(array, True) for array in (g_in, cotangent, first, second, block_in, query, inverses, logs, low, u_low, text)]
        + [(query_weight, False), (out_weight, False)]
        + [(array, True) for array in (text_kv, gains, down, up, out_down, out_up, text_down, up_key, up_value)],
        [
            ((share, width), BF, True),
            ((RANK, width), F32, True),
            ((count, RANK, local), F32, True),
            ((RANK, text_width), F32, True),
            ((count, RANK, local), F32, True),
            ((RANK, text_width), F32, True),
            ((count, RANK, local), F32, True),
            ((count, RANK, local), F32, True),
            ((RANK, width), F32, True),
        ],
        [vmem(share, width, dtype=F32), vmem(count, width, local), vmem(count, width, local), dma(2)],
        cost=cost_of(8 * share * width * width, 20e6),
    )


def attention_backward(count, heads, g_first, attn_in, query, keys, values, low, logs, inv_q, inv_k, weights, down, ups,
                       out_down, out_up):
    share, width = g_first.shape
    tokens = attn_in.shape[0]
    local = weights[0].shape[1]
    block = min(128, tokens)
    chunk = min(64, tokens)
    steps = tokens // chunk
    each = block // chunk
    scale = HD ** (-0.5)

    def kernel(g_ref, x_ref, q_ref, k_ref, v_ref, low_ref, log_ref, iq_ref, ik_ref, *refs):
        (wq, wk, wv, wo, a_ref, bq, bk, bv, ao, bo, total_out, gall, ga_in, gb_q, gb_k, gb_v, ga_o, gb_o, gq_low, gk_acc,
         gv_acc, swap_out, swap_in, partial_ref, from_left, from_right, stage_right, stage_left, xsend, xrecv,
         *sems) = refs
        me = lax.axis_index("tensor")
        core = lax.axis_index("ctx")
        peer = {"ctx": 1 - core}
        gather_line = Line(me, count, *sems[:4])
        reduce_line = Line(me, count, *sems[4:])
        gall[me] = g_ref[...]
        for ref in (ga_in, gb_q, gb_k, gb_v, ga_o, gb_o, gk_acc, gv_acc):
            ref[...] = jnp.zeros_like(ref)
        greet(line_partners(me, count) + [(core >= 0, peer)])
        line_gather_step(gather_line, 0, gall)

        def attend(place):
            rows = rows_of(place, share)
            g = gall[place]
            go = dot_nt(g, bo[...]).astype(BF)
            g_attn = (dot_nn(g, wo[...]) + dot_nn(go, ao[...])).astype(BF)
            low = low_ref[rows, :]
            uo = dot_nt(low, ao[...]).astype(BF)
            gb_o[...] += dot_tn(uo, g)
            ga_o[...] += dot_tn(go, low)
            parts = []
            for head in range(heads):
                gh = g_attn[:, head * HD : (head + 1) * HD]
                q = q_ref[head, rows, :]
                probs, grads = [], []
                inner = 0.0
                for half in range(2):
                    p = jnp.exp(dot_nt(q, k_ref[half, head]) * scale - log_ref[head, rows, :])
                    dp = dot_nt(gh, v_ref[half, head])
                    inner = inner + jnp.sum(p * dp, axis=-1, keepdims=True)
                    probs.append(p)
                    grads.append(dp)
                dq = 0.0
                for half in range(2):
                    ds = (probs[half] * (grads[half] - inner)).astype(BF)
                    dq = dq + dot_nn(ds, k_ref[half, head])
                    gk_acc[half, head] += dot_tn(ds, q)
                    gv_acc[half, head] += dot_tn(probs[half].astype(BF), gh)
                parts.append(norm_backward(q.astype(F32), iq_ref[head, rows, :], dq * scale))
            gq_low[rows, :] = jnp.concatenate(parts, axis=1).astype(BF)

        attend(me)

        def gather(number, carry):
            line_gather_step(gather_line, number, gall)

            def side(which, inner):
                place = me + (2 * which - 1) * number

                @pl.when((place >= 0) & (place < count))
                def _():
                    attend(lax.clamp(0, place, count - 1))

                return inner

            return lax.fori_loop(0, 2, side, carry)

        lax.fori_loop(1, count, gather, 0)
        swap_out[0] = (gk_acc[1 - core] * scale).astype(BF)
        swap_out[1] = gv_acc[1 - core].astype(BF)
        swap = push(swap_out, swap_in, xsend, xrecv, peer)
        swap.start()
        line_gather_drain(gather_line, gall)
        swap.wait()

        def compute(number):
            @pl.when(number % each == 0)
            def _():
                rows = rows_of(number // each, block)
                x = x_ref[rows, :]
                u = dot_nt(x, a_ref[...]).astype(BF)
                parts_k, parts_v = [], []
                for head in range(heads):
                    dk = gk_acc[core, head, rows, :] * scale + swap_in[0, head, rows, :].astype(F32)
                    normal = k_ref[core, head, rows, :].astype(F32)
                    parts_k.append(norm_backward(normal, ik_ref[head, rows, :], dk))
                    parts_v.append(gv_acc[core, head, rows, :] + swap_in[1, head, rows, :].astype(F32))
                gq = gq_low[rows, :]
                gk = jnp.concatenate(parts_k, axis=1).astype(BF)
                gv = jnp.concatenate(parts_v, axis=1).astype(BF)
                gu = jnp.concatenate([dot_nt(gq, bq[...]), dot_nt(gk, bk[...]), dot_nt(gv, bv[...])], axis=1).astype(BF)
                y = dot_nt(gq, wq[...]) + dot_nt(gk, wk[...]) + dot_nt(gv, wv[...]) + dot_nn(gu, a_ref[...])
                y = y.astype(BF)
                for piece in range(each):
                    partial_ref[number + piece] = y[piece * chunk : (piece + 1) * chunk]
                ga_in[...] += dot_tn(gu, x)
                gb_q[...] += dot_tn(u[:, :RANK], gq)
                gb_k[...] += dot_tn(u[:, RANK : 2 * RANK], gk)
                gb_v[...] += dot_tn(u[:, 2 * RANK :], gv)

        def finish(slot, total):
            total_out[rows_of(slot, chunk), :] = total

        line_reduce_all(
            reduce_line, steps, compute, partial_ref, from_left, from_right, stage_right, stage_left, finish
        )

    buffers = [vmem(steps, chunk, width) for _ in range(5)]
    return call(
        kernel,
        [(array, True) for array in (g_first, attn_in, query, keys, values, low, logs, inv_q, inv_k)]
        + [(array, True) for array in (*weights, down, *ups, out_down, out_up)],
        [
            ((tokens, width), F32, True),
            ((count, share, width), BF, True),
            ((3 * RANK, width), F32, True),
            ((RANK, local), F32, True),
            ((RANK, local), F32, True),
            ((RANK, local), F32, True),
            ((RANK, local), F32, True),
            ((RANK, width), F32, True),
        ],
        [vmem(tokens, local), vmem(2, heads, tokens, HD, dtype=F32), vmem(2, heads, tokens, HD, dtype=F32)]
        + [vmem(2, heads, tokens, HD), vmem(2, heads, tokens, HD)]
        + buffers + [dma(), dma()] + [dma(count) for _ in range(4)] + [dma(steps) for _ in range(4)],
        collective=4,
        cost=cost_of(16 * tokens * width * local, 60e6),
    )


def skip_backward(count, g_attn, g_first, skip_out, hidden, long_skip, weight, gain_halves, down, up, gain_row):
    tokens, width = hidden.shape
    span = weight.shape[-1]
    share = tokens // count
    block = share

    def kernel(g_ref, gf_ref, skip_ref, hid, lsk, hbm_w, gains, a_ref, b_ref, gain, out_h, out_l, g_shift,
               ga, gb, w, buf_h, buf_l, low, wsem, osem):
        me = lax.axis_index("tensor")
        load = pltpu.make_async_copy(hbm_w, w, wsem)
        load.start()
        g_shift[...] = jnp.zeros_like(g_shift)
        load.wait()

        def step(number, carry):
            rows = rows_of(number, block)
            ga_in = g_ref[rows, :]
            g_shift[...] += jnp.sum(ga_in, axis=0, keepdims=True)
            normal, inverse = stats(skip_ref[rows, :])
            g_low = (
                gf_ref[number].astype(F32) + norm_backward(normal, inverse, ga_in * gain[...])
            ).astype(BF)
            left = hid[rows, :].astype(F32)
            right = lsk[rows, :].astype(F32)
            mean = (jnp.sum(left, axis=-1, keepdims=True) + jnp.sum(right, axis=-1, keepdims=True)) / (2 * width)
            left = left - mean
            right = right - mean
            spread = jnp.sum(left * left, axis=-1, keepdims=True) + jnp.sum(right * right, axis=-1, keepdims=True)
            inverse = lax.rsqrt(spread / (2 * width) + NORM_EPS)
            left = left * inverse
            right = right * inverse
            gu = dot_nt(g_low, b_ref[...]).astype(BF)

            @pl.when(number == me)
            def _():
                low_l = (left * gains[0:1, :]).astype(BF)
                low_r = (right * gains[1:2, :]).astype(BF)
                u = (dot_nt(low_l, a_ref[0]) + dot_nt(low_r, a_ref[1])).astype(BF)
                ga[0] = dot_tn(gu, low_l)
                ga[1] = dot_tn(gu, low_r)
                gb[...] = dot_tn(u, g_low)

            for place in range(count):
                low[:, place * span : (place + 1) * span] = dot_nn(g_low, w[place])
            gl = (low[:, :width] + dot_nn(gu, a_ref[0])) * gains[0:1, :]
            gr = (low[:, width:] + dot_nn(gu, a_ref[1])) * gains[1:2, :]
            mean = (jnp.sum(gl, axis=-1, keepdims=True) + jnp.sum(gr, axis=-1, keepdims=True)) / (2 * width)
            inner = (
                jnp.sum(gl * left, axis=-1, keepdims=True) + jnp.sum(gr * right, axis=-1, keepdims=True)
            ) / (2 * width)
            buf_h[number] = inverse * (gl - mean - left * inner)
            buf_l[number] = inverse * (gr - mean - right * inner)
            pltpu.make_async_copy(buf_h.at[number], out_h.at[rows, :], osem.at[0, number]).start()
            pltpu.make_async_copy(buf_l.at[number], out_l.at[rows, :], osem.at[1, number]).start()
            return carry

        lax.fori_loop(0, tokens // block, step, 0)

        def drain(number, carry):
            rows = rows_of(number, block)
            pltpu.make_async_copy(buf_h.at[number], out_h.at[rows, :], osem.at[0, number]).wait()
            pltpu.make_async_copy(buf_l.at[number], out_l.at[rows, :], osem.at[1, number]).wait()
            return carry

        lax.fori_loop(0, tokens // block, drain, 0)

    blocks = tokens // block
    return call(
        kernel,
        [(array, True) for array in (g_attn, g_first, skip_out, hidden, long_skip)]
        + [(weight, False)]
        + [(array, True) for array in (gain_halves, down, up, gain_row)],
        [
            ((tokens, width), F32, False),
            ((tokens, width), F32, False),
            ((1, width), F32, True),
            ((2, RANK, width), F32, True),
            ((RANK, width), F32, True),
        ],
        [
            vmem(count, width, span),
            vmem(blocks, block, width, dtype=F32),
            vmem(blocks, block, width, dtype=F32),
            vmem(block, 2 * width, dtype=F32),
            dma(),
            dma(2, blocks),
        ],
        cost=cost_of(4 * tokens * width * width, 30e6),
    )


def adapter_reduce(count, table, chosen):
    ranks, tiles, lanes = table.shape
    half = tiles // 2
    own_rows = ranks // count

    def kernel(t_ref, sel, out, swap_out, swap_in, partial_ref, from_left, from_right, stage_right, stage_left, summed,
               slots, other_out, other_in, ssem, rsem, dsend, drecv, *sems):
        me = lax.axis_index("tensor")
        core = lax.axis_index("ctx")
        dp = lax.axis_index("dp")
        peer = {"ctx": 1 - core}
        line = Line(me, count, *sems)
        peers = [{"dp": xor_place(dp, number)} for number in (1, 2, 3)]
        greet(line_partners(me, count) + [(core >= 0, peer)] + [(core >= 0, device) for device in peers])
        swap_out[...] = t_ref[:, pl.ds(pl.multiple_of((1 - core) * half, 16), half), :].astype(BF)
        swap = push(swap_out, swap_in, ssem.at[0], rsem.at[0], peer)
        swap.start()
        swap.wait()
        for number in range(count):
            part = slice(number * own_rows, (number + 1) * own_rows)
            mine = t_ref[part, pl.ds(pl.multiple_of(core * half, 16), half), :]
            partial_ref[number] = (mine + swap_in[part].astype(F32)).astype(BF)

        def scatter(number, carry):
            line_scatter_step(line, number, partial_ref, from_left, from_right, stage_right, stage_left)
            return carry

        lax.fori_loop(0, count - 1, scatter, 0)
        line_scatter_finish(line, partial_ref, from_left, from_right, stage_right, stage_left, summed)
        slots[dp] = summed[...].astype(BF)
        sends = [
            push(slots.at[dp], slots.at[dp], dsend.at[number], drecv.at[number], device)
            for number, device in enumerate(peers)
        ]
        for send in sends:
            send.start()
        for number in (1, 2, 3):
            source = slots.at[xor_place(dp, number)]
            push(source, source, dsend.at[number - 1], drecv.at[number - 1], peers[number - 1]).wait_recv()

        def total(which):
            result = jnp.zeros((own_rows, half, lanes), F32)
            for sequence in range(4):
                result = result + slots[sequence].astype(F32) * sel[which, sequence]
            return result

        other_out[...] = total(1 - core).astype(BF)
        swap = push(other_out, other_in, ssem.at[1], rsem.at[1], peer)
        swap.start()
        out[core] = total(core)
        for send in sends:
            send.wait_send()
        swap.wait()
        out[1 - core] = other_in[...].astype(F32)

    block = (own_rows, half, lanes)
    return call(
        kernel,
        [(table, True), (chosen, True)],
        [((2, *block), F32, True)],
        [vmem(ranks, half, lanes), vmem(ranks, half, lanes)]
        + [vmem(count, *block) for _ in range(5)]
        + [vmem(*block, dtype=F32), vmem(4, *block), vmem(*block), vmem(*block)]
        + [dma(2), dma(2), dma(3), dma(3)] + [dma(count) for _ in range(4)],
        collective=5,
        cost=cost_of(1e6, 10e6),
    )[0]


def swap_cores(value):
    return lax.ppermute(value, "ctx", [(0, 1), (1, 0)])


def exchange_dp(rows):
    dp = lax.axis_index("dp")
    got = [lax.dynamic_slice_in_dim(rows, dp, 1, 0)]
    for number in (1, 2, 3):
        row = lax.dynamic_slice_in_dim(rows, dp ^ number, 1, 0)
        got.append(lax.ppermute(row, "dp", [(place, place ^ number) for place in range(4)]))
    return got


def gather_dp(row):
    dp = lax.axis_index("dp")
    table = jnp.zeros((4, row.shape[1]), row.dtype)
    table = lax.dynamic_update_slice_in_dim(table, row, dp, 0)
    for number in (1, 2, 3):
        got = lax.ppermute(row, "dp", [(place, place ^ number) for place in range(4)])
        table = lax.dynamic_update_slice_in_dim(table, got, dp ^ number, 0)
    return table


def fused_body(
    hidden,
    long_skip_input,
    condition,
    projected_text_tokens,
    sequence_adapter_index,
    skip_projection_weight,
    shift_modulation_weight,
    self_query_weight,
    self_key_weight,
    self_value_weight,
    attention_output_weight,
    cross_query_weight,
    cross_key_weight,
    cross_value_weight,
    cross_output_weight,
    feedforward_up_weight,
    feedforward_down_weight,
    skip_norm_gain,
    norm_gain_rows,
    adapter_down_factor,
    adapter_up_factor,
    cotangent,
):
    rank = lax.axis_index("tensor")
    count = lax.axis_size("tensor")
    core = lax.axis_index("ctx")
    dp = lax.axis_index("dp")
    hidden, long_skip, text, cot = hidden[0], long_skip_input[0], projected_text_tokens[0], cotangent[0]
    tokens, width = hidden.shape
    local = self_query_weight.shape[1]
    heads = local // HD
    ff = feedforward_up_weight.shape[1]
    span = skip_projection_weight.shape[0]
    share = tokens // count
    in_sizes = [2 * MODEL_WIDTH] + [MODEL_WIDTH] * 6 + [TW, TW, MODEL_WIDTH, MODEL_WIDTH, FF]
    out_sizes = [MODEL_WIDTH] * 10 + [FF, MODEL_WIDTH]
    in_at = [sum(in_sizes[:number]) for number in range(12)]
    out_at = [sum(out_sizes[:number]) for number in range(12)]
    index = sequence_adapter_index[0]
    down_table = lax.dynamic_index_in_dim(adapter_down_factor, index, 0, keepdims=False)
    up_table = lax.dynamic_index_in_dim(adapter_up_factor, index, 0, keepdims=False)

    def down_full(number):
        return down_table[:, in_at[number] : in_at[number] + in_sizes[number]]

    def up_full(number):
        return up_table[:, out_at[number] : out_at[number] + out_sizes[number]]

    def down_local(number, size):
        return lax.dynamic_slice_in_dim(down_table, in_at[number] + rank * size, size, 1)

    def up_local(number, size):
        return lax.dynamic_slice_in_dim(up_table, out_at[number] + rank * size, size, 1)

    def stack(table):
        return jnp.transpose(table.reshape(RANK, count, -1), (1, 0, 2))

    weights = {
        "skip": skip_projection_weight.T,
        "q": self_query_weight,
        "k": self_key_weight,
        "v": self_value_weight,
        "o": attention_output_weight.T,
        "ck": cross_key_weight,
        "cv": cross_value_weight,
        "cq": cross_query_weight,
        "co": cross_output_weight.T,
        "up": feedforward_up_weight,
        "dn": feedforward_down_weight.T,
    }
    mod_rows = shift_modulation_weight.shape[0]
    act_wide, silu_pull = jax.vjp(jax.nn.silu, condition.astype(F32))
    act_low = act_wide.astype(BF)
    mod_u = dot_nt(act_low, down_full(1))
    tag = jnp.full((1, 128), index, jnp.int32).astype(F32)

    both = jnp.concatenate([hidden, long_skip], axis=1)
    part = lax.dynamic_slice_in_dim(both, rank * span, span, 1)
    part_gain = lax.dynamic_slice_in_dim(skip_norm_gain, rank * span, span, 0)[None, :]
    text_down = jnp.concatenate([down_full(7), down_full(8)], axis=0)
    qkv_down = jnp.concatenate([down_full(2), down_full(3), down_full(4)], axis=0)
    qkv_up = [up_local(number, local) for number in (2, 3, 4)]
    out_down, out_up = down_local(5, local), up_full(5)
    (skip_out, attn_in, query, keys, values, low, logs, inv_q, inv_k, summed, act_all, text_kv, wq, wk, wv, wo, wcq, wco,
     wup, wdn) = front(
        count, heads, act_low, tag, hidden, long_skip, part, part_gain, text, weights,
        (shift_modulation_weight, down_full(1), up_full(1)), norm_gain_rows[0:1],
        (down_local(0, span), up_full(0)), (text_down, up_local(7, local), up_local(8, local)), (qkv_down, *qkv_up),
        (out_down, out_up),
    )
    indices = act_all[:, 0, MODEL_WIDTH].astype(jnp.int32)
    cross_down, cross_up = down_full(6), stack(up_full(6))
    cout_down, cout_up = stack(down_full(9)), up_full(9)
    first, second, cross_in, mlp_in, cquery, cinv, clogs, clow, cu, skip_half = cross_forward(
        count, heads, summed, skip_out, wcq, wco, weights["skip"], text_kv, norm_gain_rows, cross_down, cross_up,
        cout_down, cout_up,
    )
    g_mlp_in, down_part, g_up_a, g_up_b, g_down_a, g_down_b, skip_all = feed_forward(
        count, mlp_in, cot, second, wup, wdn, skip_half, down_full(10), up_local(10, ff), down_local(11, ff), up_full(11),
    )
    block_out = lax.psum(down_part, "tensor")
    g_first, g_cq_a, g_cq_b, g_ck_a, g_ck_b, g_cv_a, g_cv_b, g_co_a, g_co_b = cross_backward(
        count, heads, g_mlp_in, cot, first, second, cross_in, cquery, cinv, clogs, clow, cu, text, wcq, wco,
        text_kv, norm_gain_rows, cross_down, cross_up, cout_down, cout_up, text_down, stack(up_full(7)),
        stack(up_full(8)),
    )
    g_attn, g_first_all, g_qkv_a, g_q_b, g_k_b, g_v_b, g_o_a, g_o_b = attention_backward(
        count, heads, g_first, attn_in, query, keys, values, low, logs, inv_q, inv_k, (wq, wk, wv, wo), qkv_down,
        qkv_up, out_down, out_up,
    )
    skip_down = jnp.transpose(down_full(0).reshape(RANK, 2, MODEL_WIDTH), (1, 0, 2))
    hidden_grad, skip_grad, g_shift, g_skip_a, g_skip_b = skip_backward(
        count, g_attn, g_first_all, skip_out, hidden, long_skip, skip_all,
        skip_norm_gain.reshape(2, MODEL_WIDTH), skip_down, up_full(0), norm_gain_rows[0:1],
    )

    g_mod_u = dot_nt(g_shift.astype(BF), up_full(1))
    once = (rank == 0).astype(F32)
    g_mod_a = jnp.dot(g_mod_u.T, act_low.astype(F32), precision=PRECISE) * once
    g_mod_b = jnp.dot(mod_u.T, g_shift, precision=PRECISE) * once
    shift_sum = g_shift + swap_cores(g_shift)
    shift_all = gather_dp(shift_sum).astype(BF)
    act_parts = exchange_dp(dot_nt(shift_all, shift_modulation_weight))
    g_act = jnp.zeros((1, MODEL_WIDTH), F32)
    for number, piece in enumerate(act_parts):
        g_act = lax.dynamic_update_slice_in_dim(g_act, piece, (dp ^ number) * mod_rows, 1)
    shift_u = jnp.dot(shift_sum, up_full(1).astype(F32).T, precision=PRECISE)
    g_act = g_act + jnp.dot(shift_u, down_full(1).astype(F32), precision=PRECISE)
    g_condition = silu_pull(g_act)[0][0]
    size = MODEL_WIDTH // (2 * count)
    condition_gradient = lax.dynamic_slice_in_dim(g_condition, (core * count + rank) * size, size, 0)

    def unstack(value):
        return jnp.transpose(value, (1, 0, 2)).reshape(RANK, -1)

    def place_local(value, total):
        return lax.dynamic_update_slice_in_dim(jnp.zeros((RANK, total), F32), value, rank * value.shape[1], 1)

    table = jnp.concatenate(
        [
            g_skip_a[0], g_skip_a[1], g_mod_a, g_qkv_a[:RANK], g_qkv_a[RANK : 2 * RANK], g_qkv_a[2 * RANK :],
            place_local(g_o_a, MODEL_WIDTH), g_cq_a, g_ck_a, g_cv_a, unstack(g_co_a), g_up_a, place_local(g_down_a, FF),
            g_skip_b, g_mod_b, place_local(g_q_b, MODEL_WIDTH), place_local(g_k_b, MODEL_WIDTH),
            place_local(g_v_b, MODEL_WIDTH), g_o_b, unstack(g_cq_b), unstack(g_ck_b), unstack(g_cv_b), g_co_b,
            place_local(g_up_b, FF), g_down_b,
        ],
        axis=1,
    )
    wide_a, wide_b = sum(in_sizes) // 128, sum(out_sizes) // 128
    tiles = -(-(wide_a + wide_b) // 32) * 32
    table = jnp.pad(table.reshape(RANK, wide_a + wide_b, 128), ((0, 0), (0, tiles - wide_a - wide_b), (0, 0)))
    chosen = (indices[None, :] == (dp * 2 + jnp.arange(2, dtype=jnp.int32))[:, None]).astype(F32)
    chosen = jnp.broadcast_to(chosen[:, :, None, None], (2, 4, 1, 128))
    reduced = adapter_reduce(count, table, chosen)
    reduced = jnp.transpose(reduced, (1, 0, 2, 3)).reshape(RANK // count, tiles, 128)
    return (
        block_out[None],
        hidden_grad[None],
        skip_grad[None],
        condition_gradient,
        reduced[:, :wide_a].reshape(-1),
        reduced[:, wide_a : wide_a + wide_b].reshape(-1),
    )


def solution(mesh):
    in_specs = (
        P("dp", "ctx", None),
        P("dp", "ctx", None),
        P("dp", None),
        P("dp", None, None),
        P("dp"),
        P("tensor", "dp"),
        P("dp", None),
        P("dp", "tensor"),
        P("dp", "tensor"),
        P("dp", "tensor"),
        P("tensor", "dp"),
        P("dp", "tensor"),
        P("dp", "tensor"),
        P("dp", "tensor"),
        P("tensor", "dp"),
        P("dp", "tensor"),
        P("tensor", "dp"),
        P(),
        P(),
        P(),
        P(),
        P("dp", "ctx", None),
    )
    out_specs = (
        P("dp", "ctx", None),
        P("dp", "ctx", None),
        P("dp", "ctx", None),
        P(("dp", "ctx", "tensor")),
        P(("dp", "ctx", "tensor")),
        P(("dp", "ctx", "tensor")),
    )
    shape = mesh.shape
    fused = shape["dp"] == 4 and shape["ctx"] == 2 and shape["tensor"] == 4
    return jax.shard_map(fused_body if fused else body, mesh=mesh, in_specs=in_specs, out_specs=out_specs, check_vma=False)
```

```python
from functools import partial

import jax
import jax.numpy as jnp
from jax import lax
from jax.experimental import pallas as pl
from jax.experimental.pallas import tpu as pltpu
from jax.sharding import PartitionSpec as P

MODEL_WIDTH = 1408
HD = 88
FF = 6144
TW = 1024


PRECISE = lax.Precision.HIGHEST
NORM_EPS = 1e-06


def row_norm(values):
    centered = values - jnp.mean(values, axis=-1, keepdims=True)
    inverse = lax.rsqrt(jnp.mean(centered * centered, axis=-1, keepdims=True) + NORM_EPS)
    return (centered * inverse, inverse)


def head_norm(values, head_width):
    shaped = values.reshape(values.shape[:-1] + (values.shape[-1] // head_width, head_width))
    centered = shaped - jnp.mean(shaped, axis=-1, keepdims=True)
    inverse = lax.rsqrt(jnp.mean(centered * centered, axis=-1, keepdims=True) + NORM_EPS)
    return (centered * inverse, inverse)


def norm_back(normal, inverse, grad_normal):
    return inverse * (
        grad_normal
        - jnp.mean(grad_normal, axis=-1, keepdims=True)
        - normal * jnp.mean(grad_normal * normal, axis=-1, keepdims=True)
    )


def split_parts(values):
    if values.dtype == jnp.bfloat16:
        return [values]
    upper_half = values.astype(jnp.bfloat16)
    lower_half = (values - upper_half.astype(jnp.float32)).astype(jnp.bfloat16)
    return [upper_half, lower_half]


def paired_product(form, left, right):
    total = None
    for left_number, left_part in enumerate(split_parts(left)):
        for right_number, right_part in enumerate(split_parts(right)):
            if left_number + right_number < 2:
                term = jnp.einsum(form, left_part, right_part, preferred_element_type=jnp.float32)
                total = term if total is None else total + term
    return total


def lowrank_out(input_list, weight_matrix, down_piece, up_factor_piece):
    frozen_term = jnp.einsum(
        "gtb,bx->gtx", input_list, weight_matrix, preferred_element_type=jnp.float32
    )
    rank_activation = jnp.einsum(
        "snd,srd->snr", input_list, down_piece, preferred_element_type=jnp.float32
    )
    adapter_term = paired_product("dti,dip->dtp", rank_activation, up_factor_piece)
    return (frozen_term + adapter_term, rank_activation)


def lowrank_back(
    input_list,
    weight_matrix,
    down_piece,
    up_factor_piece,
    rank_activation,
    output_gradient,
    want_input,
):
    upper_gradient = paired_product("pmf,pmz->pfz", rank_activation, output_gradient)
    rank_gradient = paired_product("hzu,hlu->hzl", output_gradient, up_factor_piece)
    grad_lower = paired_product("snr,snd->srd", rank_gradient, input_list)
    if want_input:
        input_gradients = paired_product("lga,wa->lgw", output_gradient, weight_matrix)
        input_gradients = input_gradients + paired_product(
            "snr,srd->snd", rank_gradient, down_piece
        )
        return (input_gradients, grad_lower, upper_gradient)
    return (None, grad_lower, upper_gradient)


def attend_forward(query, key_rows, values_in, scale_factor):
    scores = (
        jnp.einsum("snhe,smhe->shnm", query, key_rows, preferred_element_type=jnp.float32)
        * scale_factor
    )
    row_top = jnp.max(scores, axis=-1, keepdims=True)
    exp_scores = jnp.exp(scores - row_top)
    row_total = jnp.sum(exp_scores, axis=-1, keepdims=True)
    attn_probs = (exp_scores / row_total).astype(jnp.bfloat16)
    result = jnp.einsum(
        "shnm,smhe->snhe", attn_probs, values_in, preferred_element_type=jnp.float32
    )
    return (result, row_top + jnp.log(row_total))


def attend_back(query, key_rows, values_in, log_total, grad_result, scale_factor):
    scores = (
        jnp.einsum("snhe,smhe->shnm", query, key_rows, preferred_element_type=jnp.float32)
        * scale_factor
    )
    attn_probs = jnp.exp(scores - log_total)
    grad_probs = jnp.einsum(
        "snhe,smhe->shnm", grad_result, values_in, preferred_element_type=jnp.float32
    )
    row_inner = jnp.sum(attn_probs * grad_probs, axis=-1, keepdims=True)
    grad_scores = (attn_probs * (grad_probs - row_inner)).astype(jnp.bfloat16)
    grad_query = (
        jnp.einsum("shnm,smhe->snhe", grad_scores, key_rows, preferred_element_type=jnp.float32)
        * scale_factor
    )
    grad_keys = (
        jnp.einsum("shnm,snhe->smhe", grad_scores, query, preferred_element_type=jnp.float32)
        * scale_factor
    )
    grad_values = jnp.einsum(
        "shnm,snhe->smhe",
        attn_probs.astype(jnp.bfloat16),
        grad_result,
        preferred_element_type=jnp.float32,
    )
    return (grad_query, grad_keys, grad_values)


def body(
    hidden,
    long_skip_input,
    condition,
    projected_text_tokens,
    sequence_adapter_index,
    skip_projection_weight,
    shift_modulation_weight,
    self_query_weight,
    self_key_weight,
    self_value_weight,
    attention_output_weight,
    cross_query_weight,
    cross_key_weight,
    cross_value_weight,
    cross_output_weight,
    feedforward_up_weight,
    feedforward_down_weight,
    skip_norm_gain,
    norm_gain_rows,
    adapter_down_factor,
    adapter_up_factor,
    cotangent,
):
    (
        skip_projection_weight,
        shift_modulation_weight,
        self_query_weight,
        self_key_weight,
        self_value_weight,
        attention_output_weight,
        cross_query_weight,
        cross_key_weight,
        cross_value_weight,
        cross_output_weight,
        feedforward_up_weight,
        feedforward_down_weight,
    ) = (
        lax.all_gather(skip_projection_weight, "dp", axis=1, tiled=True),
        lax.all_gather(shift_modulation_weight, "dp", axis=0, tiled=True),
        lax.all_gather(self_query_weight, "dp", axis=0, tiled=True),
        lax.all_gather(self_key_weight, "dp", axis=0, tiled=True),
        lax.all_gather(self_value_weight, "dp", axis=0, tiled=True),
        lax.all_gather(attention_output_weight, "dp", axis=1, tiled=True),
        lax.all_gather(cross_query_weight, "dp", axis=0, tiled=True),
        lax.all_gather(cross_key_weight, "dp", axis=0, tiled=True),
        lax.all_gather(cross_value_weight, "dp", axis=0, tiled=True),
        lax.all_gather(cross_output_weight, "dp", axis=1, tiled=True),
        lax.all_gather(feedforward_up_weight, "dp", axis=0, tiled=True),
        lax.all_gather(feedforward_down_weight, "dp", axis=1, tiled=True),
    )
    tensor_rank = lax.axis_index("tensor")
    tensor_count = lax.axis_size("tensor")
    seqs_local = hidden.shape[0]
    tokens_local = hidden.shape[1]
    local_width = self_query_weight.shape[1]
    heads_local = local_width // HD
    ff_local = feedforward_up_weight.shape[1]
    skip_width = skip_projection_weight.shape[0]
    scale_factor = HD ** (-0.5)
    in_sizes = [
        2 * MODEL_WIDTH,
        MODEL_WIDTH,
        MODEL_WIDTH,
        MODEL_WIDTH,
        MODEL_WIDTH,
        MODEL_WIDTH,
        MODEL_WIDTH,
        TW,
        TW,
        MODEL_WIDTH,
        MODEL_WIDTH,
        FF,
    ]
    out_sizes = [MODEL_WIDTH] * 10 + [FF, MODEL_WIDTH]
    input_offsets = [sum(in_sizes[:number]) for number in range(12)]
    output_offsets = [sum(out_sizes[:number]) for number in range(12)]
    select_adapter = (
        sequence_adapter_index[:, None]
        == jnp.arange(adapter_down_factor.shape[0], dtype=jnp.int32)[None, :]
    )
    choose_wide = select_adapter.astype(jnp.float32)
    down_seq = jnp.einsum(
        "fn,nge->fge",
        select_adapter.astype(jnp.bfloat16),
        adapter_down_factor,
        preferred_element_type=jnp.float32,
    ).astype(jnp.bfloat16)
    up_seq = jnp.einsum(
        "fn,nge->fge",
        select_adapter.astype(jnp.bfloat16),
        adapter_up_factor,
        preferred_element_type=jnp.float32,
    ).astype(jnp.bfloat16)

    def down_full(number):
        return down_seq[:, :, input_offsets[number] : input_offsets[number] + in_sizes[number]]

    def up_full(number):
        return up_seq[:, :, output_offsets[number] : output_offsets[number] + out_sizes[number]]

    def down_local(number, span_width):
        return lax.dynamic_slice_in_dim(
            down_seq, input_offsets[number] + tensor_rank * span_width, span_width, 2
        )

    def up_local(number, span_width):
        return lax.dynamic_slice_in_dim(
            up_seq, output_offsets[number] + tensor_rank * span_width, span_width, 2
        )

    def to_slots(grad_piece):
        return jnp.einsum("si,srd->ird", choose_wide, grad_piece, precision=PRECISE)

    joined = jnp.concatenate([hidden, long_skip_input], axis=-1).astype(jnp.float32)
    joined_normal, joined_inverse = row_norm(joined)
    joined_low = (joined_normal * skip_norm_gain).astype(jnp.bfloat16)
    joined_part = lax.dynamic_slice_in_dim(joined_low, tensor_rank * skip_width, skip_width, 2)
    skip_partial, skip_rank = lowrank_out(
        joined_part, skip_projection_weight, down_local(0, skip_width), up_full(0)
    )
    skip_out = lax.psum(skip_partial.astype(jnp.bfloat16), "tensor").astype(jnp.float32)
    act_wide, silu_pull = jax.vjp(jax.nn.silu, condition.astype(jnp.float32))
    act_low = act_wide.astype(jnp.bfloat16)[:, None, :]
    shift_row, mod_rank = lowrank_out(act_low, shift_modulation_weight, down_full(1), up_full(1))
    first_normal, first_inverse = row_norm(skip_out)
    attn_in = (first_normal * norm_gain_rows[0] + shift_row).astype(jnp.bfloat16)
    query_proj, query_rank = lowrank_out(
        attn_in, self_query_weight, down_full(2), up_local(2, local_width)
    )
    key_proj, key_rank = lowrank_out(
        attn_in, self_key_weight, down_full(3), up_local(3, local_width)
    )
    value_proj, value_rank = lowrank_out(
        attn_in, self_value_weight, down_full(4), up_local(4, local_width)
    )
    query_normal, query_inverse = head_norm(query_proj, HD)
    key_normal, key_inverse = head_norm(key_proj, HD)
    query_low = query_normal.astype(jnp.bfloat16)
    key_low = key_normal.astype(jnp.bfloat16).reshape(seqs_local, tokens_local, local_width)
    value_low = value_proj.astype(jnp.bfloat16)
    keys_all, values_all = (
        lax.all_gather(key_low, "ctx", axis=1, tiled=True),
        lax.all_gather(value_low, "ctx", axis=1, tiled=True),
    )
    keys_four = keys_all.reshape(seqs_local, -1, heads_local, HD)
    values_four = values_all.reshape(seqs_local, -1, heads_local, HD)
    attn_result, attn_log = attend_forward(query_low, keys_four, values_four, scale_factor)
    attn_low = attn_result.reshape(seqs_local, tokens_local, local_width).astype(jnp.bfloat16)
    attn_partial, out_rank = lowrank_out(
        attn_low, attention_output_weight, down_local(5, local_width), up_full(5)
    )
    first_res = skip_out + lax.psum(attn_partial.astype(jnp.bfloat16), "tensor").astype(jnp.float32)
    second_normal, second_inverse = row_norm(first_res)
    cross_in = (second_normal * norm_gain_rows[1]).astype(jnp.bfloat16)
    cquery_proj, cquery_rank = lowrank_out(
        cross_in, cross_query_weight, down_full(6), up_local(6, local_width)
    )
    ckey_proj, ckey_rank = lowrank_out(
        projected_text_tokens, cross_key_weight, down_full(7), up_local(7, local_width)
    )
    cvalue_proj, cvalue_rank = lowrank_out(
        projected_text_tokens, cross_value_weight, down_full(8), up_local(8, local_width)
    )
    cquery_normal, cquery_inverse = head_norm(cquery_proj, HD)
    ckey_normal, ckey_inverse = head_norm(ckey_proj, HD)
    cquery_low = cquery_normal.astype(jnp.bfloat16)
    ckey_low = ckey_normal.astype(jnp.bfloat16)
    cvalue_low = cvalue_proj.astype(jnp.bfloat16).reshape(seqs_local, -1, heads_local, HD)
    cross_result, cross_log = attend_forward(cquery_low, ckey_low, cvalue_low, scale_factor)
    cross_low = cross_result.reshape(seqs_local, tokens_local, local_width).astype(jnp.bfloat16)
    cross_partial, cout_rank = lowrank_out(
        cross_low, cross_output_weight, down_local(9, local_width), up_full(9)
    )
    second_res = first_res + lax.psum(cross_partial.astype(jnp.bfloat16), "tensor").astype(
        jnp.float32
    )
    third_normal, third_inverse = row_norm(second_res)
    mlp_in = (third_normal * norm_gain_rows[2]).astype(jnp.bfloat16)
    up_proj, up_rank = lowrank_out(
        mlp_in, feedforward_up_weight, down_full(10), up_local(10, ff_local)
    )
    activated, gelu_pull = jax.vjp(partial(jax.nn.gelu, approximate=True), up_proj)
    activated_low = activated.astype(jnp.bfloat16)
    down_partial, down_rank = lowrank_out(
        activated_low, feedforward_down_weight, down_local(11, ff_local), up_full(11)
    )
    block_out = second_res + lax.psum(down_partial.astype(jnp.bfloat16), "tensor").astype(
        jnp.float32
    )
    grad_act, grad_down_lower, grad_down_upper = lowrank_back(
        activated_low,
        feedforward_down_weight,
        down_local(11, ff_local),
        up_full(11),
        down_rank,
        cotangent,
        True,
    )
    grad_pre = gelu_pull(grad_act)[0].astype(jnp.bfloat16)
    grad_mlp_in, grad_up_lower, grad_up_upper = lowrank_back(
        mlp_in,
        feedforward_up_weight,
        down_full(10),
        up_local(10, ff_local),
        up_rank,
        grad_pre,
        True,
    )
    grad_mlp_in = lax.psum(grad_mlp_in.astype(jnp.bfloat16), "tensor").astype(jnp.float32)
    grad_second = cotangent.astype(jnp.float32) + norm_back(
        third_normal, third_inverse, grad_mlp_in * norm_gain_rows[2]
    )
    grad_cross_low, grad_cout_lower, grad_cout_upper = lowrank_back(
        cross_low,
        cross_output_weight,
        down_local(9, local_width),
        up_full(9),
        cout_rank,
        grad_second.astype(jnp.bfloat16),
        True,
    )
    grad_cross_result = grad_cross_low.astype(jnp.bfloat16).reshape(
        seqs_local, tokens_local, heads_local, HD
    )
    grad_cquery, grad_ckey, grad_cvalue = attend_back(
        cquery_low, ckey_low, cvalue_low, cross_log, grad_cross_result, scale_factor
    )
    grad_cquery_proj = (
        norm_back(cquery_normal, cquery_inverse, grad_cquery)
        .reshape(seqs_local, tokens_local, local_width)
        .astype(jnp.bfloat16)
    )
    grad_ckey_proj = norm_back(ckey_normal, ckey_inverse, grad_ckey).reshape(
        seqs_local, -1, local_width
    )
    none_first, grad_ckey_lower, grad_ckey_upper = lowrank_back(
        projected_text_tokens,
        cross_key_weight,
        down_full(7),
        up_local(7, local_width),
        ckey_rank,
        grad_ckey_proj,
        False,
    )
    none_second, grad_cvalue_lower, grad_cvalue_upper = lowrank_back(
        projected_text_tokens,
        cross_value_weight,
        down_full(8),
        up_local(8, local_width),
        cvalue_rank,
        grad_cvalue.reshape(seqs_local, -1, local_width),
        False,
    )
    grad_cross_in, grad_cquery_lower, grad_cquery_upper = lowrank_back(
        cross_in,
        cross_query_weight,
        down_full(6),
        up_local(6, local_width),
        cquery_rank,
        grad_cquery_proj,
        True,
    )
    grad_cross_in = lax.psum(grad_cross_in.astype(jnp.bfloat16), "tensor").astype(jnp.float32)
    grad_first = grad_second + norm_back(
        second_normal, second_inverse, grad_cross_in * norm_gain_rows[1]
    )
    grad_attn_low, grad_aout_lower, grad_aout_upper = lowrank_back(
        attn_low,
        attention_output_weight,
        down_local(5, local_width),
        up_full(5),
        out_rank,
        grad_first.astype(jnp.bfloat16),
        True,
    )
    grad_attn_result = grad_attn_low.astype(jnp.bfloat16).reshape(
        seqs_local, tokens_local, heads_local, HD
    )
    grad_query, grad_keys_all, grad_values_all = attend_back(
        query_low, keys_four, values_four, attn_log, grad_attn_result, scale_factor
    )
    grad_keys, grad_values = (
        lax.psum_scatter(
            grad_keys_all.reshape(seqs_local, -1, local_width).astype(jnp.bfloat16),
            "ctx",
            scatter_dimension=1,
            tiled=True,
        ).astype(jnp.float32),
        lax.psum_scatter(
            grad_values_all.reshape(seqs_local, -1, local_width).astype(jnp.bfloat16),
            "ctx",
            scatter_dimension=1,
            tiled=True,
        ).astype(jnp.float32),
    )
    grad_query_proj = (
        norm_back(query_normal, query_inverse, grad_query)
        .reshape(seqs_local, tokens_local, local_width)
        .astype(jnp.bfloat16)
    )
    grad_key_proj = (
        norm_back(
            key_normal, key_inverse, grad_keys.reshape(seqs_local, tokens_local, heads_local, HD)
        )
        .reshape(seqs_local, tokens_local, local_width)
        .astype(jnp.bfloat16)
    )
    grad_value_proj = grad_values.astype(jnp.bfloat16)
    grad_in_query, grad_query_lower, grad_query_upper = lowrank_back(
        attn_in,
        self_query_weight,
        down_full(2),
        up_local(2, local_width),
        query_rank,
        grad_query_proj,
        True,
    )
    grad_in_key, grad_key_lower, grad_key_upper = lowrank_back(
        attn_in,
        self_key_weight,
        down_full(3),
        up_local(3, local_width),
        key_rank,
        grad_key_proj,
        True,
    )
    grad_in_value, grad_value_lower, grad_value_upper = lowrank_back(
        attn_in,
        self_value_weight,
        down_full(4),
        up_local(4, local_width),
        value_rank,
        grad_value_proj,
        True,
    )
    grad_attn_in = lax.psum(
        (grad_in_query + grad_in_key + grad_in_value).astype(jnp.bfloat16), "tensor"
    ).astype(jnp.float32)
    grad_shift = jnp.sum(grad_attn_in, axis=1, keepdims=True) / tensor_count
    grad_act_low, grad_mod_lower, grad_mod_upper = lowrank_back(
        act_low, shift_modulation_weight, down_full(1), up_full(1), mod_rank, grad_shift, True
    )
    grad_condition = silu_pull(grad_act_low[:, 0, :])[0]
    grad_skip_out = grad_first + norm_back(
        first_normal, first_inverse, grad_attn_in * norm_gain_rows[0]
    )
    grad_joined_part, grad_skip_lower, grad_skip_upper = lowrank_back(
        joined_part,
        skip_projection_weight,
        down_local(0, skip_width),
        up_full(0),
        skip_rank,
        grad_skip_out.astype(jnp.bfloat16),
        True,
    )
    grad_joined = lax.all_gather(
        grad_joined_part.astype(jnp.bfloat16), "tensor", axis=2, tiled=True
    ).astype(grad_joined_part.dtype)
    grad_joined_full = norm_back(joined_normal, joined_inverse, grad_joined * skip_norm_gain)
    hidden_grad = grad_joined_full[:, :, :MODEL_WIDTH]
    skip_grad = grad_joined_full[:, :, MODEL_WIDTH:]
    lower_factor_parts = [
        (0, grad_skip_lower, True),
        (1, grad_mod_lower, False),
        (2, grad_query_lower, False),
        (3, grad_key_lower, False),
        (4, grad_value_lower, False),
        (5, grad_aout_lower, True),
        (6, grad_cquery_lower, False),
        (7, grad_ckey_lower, False),
        (8, grad_cvalue_lower, False),
        (9, grad_cout_lower, True),
        (10, grad_up_lower, False),
        (11, grad_down_lower, True),
    ]
    upper_factor_parts = [
        (0, grad_skip_upper, False),
        (1, grad_mod_upper, False),
        (2, grad_query_upper, True),
        (3, grad_key_upper, True),
        (4, grad_value_upper, True),
        (5, grad_aout_upper, False),
        (6, grad_cquery_upper, True),
        (7, grad_ckey_upper, True),
        (8, grad_cvalue_upper, True),
        (9, grad_cout_upper, False),
        (10, grad_up_upper, True),
        (11, grad_down_upper, False),
    ]
    slot_total = adapter_down_factor.shape[0]
    rank_total = adapter_down_factor.shape[1]
    cond_buffer = jnp.zeros((lax.axis_size("dp") * seqs_local, MODEL_WIDTH), jnp.float32)
    cond_buffer = lax.dynamic_update_slice_in_dim(
        cond_buffer, grad_condition, lax.axis_index("dp") * seqs_local, 0
    )
    cond_flat = cond_buffer.reshape(-1)

    def dense_table(parts_list, starts, total_width, row_count, slot_pieces):
        table = jnp.zeros((row_count, total_width), jnp.float32)
        for position, (number, grad_piece, is_local) in enumerate(parts_list):
            span_width = grad_piece.shape[2]
            column_start = starts[number] + tensor_rank * span_width if is_local else starts[number]
            table = lax.dynamic_update_slice_in_dim(table, slot_pieces[position], column_start, 1)
        return table

    down_factor_slots = [
        to_slots(grad_piece).reshape(slot_total * rank_total, -1)
        for number, grad_piece, is_local in lower_factor_parts
    ]
    up_factor_slots = [
        to_slots(grad_piece).reshape(slot_total * rank_total, -1)
        for number, grad_piece, is_local in upper_factor_parts
    ]
    down_compact = jnp.concatenate(down_factor_slots, axis=1)
    up_compact = jnp.concatenate(up_factor_slots, axis=1)
    cond_rows, down_rows, up_rows = (
        lax.psum_scatter(
            cond_flat.astype(jnp.bfloat16), ("dp", "ctx"), scatter_dimension=0, tiled=True
        ).astype(jnp.float32),
        lax.psum_scatter(
            down_compact.astype(jnp.bfloat16), ("dp", "ctx"), scatter_dimension=0, tiled=True
        ).astype(jnp.float32),
        lax.psum_scatter(
            up_compact.astype(jnp.bfloat16), ("dp", "ctx"), scatter_dimension=0, tiled=True
        ).astype(jnp.float32),
    )
    row_count = down_rows.shape[0]
    down_widths = [grad_piece.shape[2] for number, grad_piece, is_local in lower_factor_parts]
    up_widths = [grad_piece.shape[2] for number, grad_piece, is_local in upper_factor_parts]
    down_pieces = [
        down_rows[:, sum(down_widths[:position]) : sum(down_widths[: position + 1])]
        for position in range(12)
    ]
    up_pieces = [
        up_rows[:, sum(up_widths[:position]) : sum(up_widths[: position + 1])]
        for position in range(12)
    ]
    down_block = dense_table(
        lower_factor_parts, input_offsets, adapter_down_factor.shape[2], row_count, down_pieces
    ).reshape(-1)
    up_block = dense_table(
        upper_factor_parts, output_offsets, adapter_up_factor.shape[2], row_count, up_pieces
    ).reshape(-1)
    condition_gradient, adapter_down_gradient, adapter_up_gradient = (
        lax.psum_scatter(
            cond_rows.astype(jnp.bfloat16), "tensor", scatter_dimension=0, tiled=True
        ).astype(jnp.float32),
        lax.psum_scatter(
            down_block.astype(jnp.bfloat16), "tensor", scatter_dimension=0, tiled=True
        ).astype(jnp.float32),
        lax.psum_scatter(
            up_block.astype(jnp.bfloat16), "tensor", scatter_dimension=0, tiled=True
        ).astype(jnp.float32),
    )
    return (
        block_out.astype(jnp.bfloat16),
        hidden_grad,
        skip_grad,
        condition_gradient,
        adapter_down_gradient,
        adapter_up_gradient,
    )


BF = jnp.bfloat16
F32 = jnp.float32
MESH_ID = pl.DeviceIdType.MESH
RANK = 16
VMEM_BYTES = 60 << 20


def dot_nn(left, right):
    return jnp.dot(left, right, preferred_element_type=F32)


def dot_nt(left, right):
    return lax.dot_general(left, right, (((1,), (1,)), ((), ())), preferred_element_type=F32)


def dot_tn(left, right):
    return lax.dot_general(left, right, (((0,), (0,)), ((), ())), preferred_element_type=F32)


def stats(values):
    centered = values - jnp.mean(values, axis=-1, keepdims=True)
    inverse = lax.rsqrt(jnp.mean(centered * centered, axis=-1, keepdims=True) + NORM_EPS)
    return centered * inverse, inverse


def greet(partners):
    barrier = pltpu.get_barrier_semaphore()
    for condition, device in partners:
        @pl.when(condition)
        def _(device=device):
            pl.semaphore_signal(barrier, inc=1, device_id=device, device_id_type=MESH_ID)
    expected = sum(jnp.where(condition, 1, 0) for condition, _ in partners)
    pl.semaphore_wait(barrier, expected)


def line_partners(me, count):
    return [(me > 0, {"tensor": lax.max(me - 1, 0)}), (me < count - 1, {"tensor": lax.min(me + 1, count - 1)})]


def push(source, target, send_sem, recv_sem, device):
    return pltpu.make_async_remote_copy(
        src_ref=source,
        dst_ref=target,
        send_sem=send_sem,
        recv_sem=recv_sem,
        device_id=device,
        device_id_type=MESH_ID,
    )


class Line:
    def __init__(self, me, count, send_right, recv_left, send_left, recv_right):
        self.me, self.count = me, count
        self.sems = (send_right, recv_left, send_left, recv_right)
        self.left = {"tensor": lax.max(me - 1, 0)}
        self.right = {"tensor": lax.min(me + 1, count - 1)}
        self.has_left, self.has_right = me > 0, me < count - 1

    def to_right(self, source, target, slot):
        return push(source, target, self.sems[0].at[slot], self.sems[1].at[slot], self.right)

    def to_left(self, source, target, slot):
        return push(source, target, self.sems[2].at[slot], self.sems[3].at[slot], self.left)


def line_reduce_all(line, steps, compute, partial_ref, from_left, from_right, stage_right, stage_left, finish, beside=None):
    me, count = line.me, line.count
    far = count - 1 - me

    def step(number, carry):
        @pl.when(number < steps)
        def _():
            compute(number)

        slot_r = number - me

        @pl.when((slot_r >= 0) & (slot_r < steps))
        def _():
            slot = lax.clamp(0, slot_r, steps - 1)

            @pl.when(line.has_left)
            def _():
                line.to_right(stage_right.at[slot], from_left.at[slot], slot).wait_recv()

            @pl.when(line.has_right)
            def _():
                @pl.when(line.has_left)
                def _():
                    total = partial_ref[slot].astype(F32) + from_left[slot].astype(F32)
                    stage_right[slot] = total.astype(BF)

                @pl.when(jnp.logical_not(line.has_left))
                def _():
                    stage_right[slot] = partial_ref[slot]

                line.to_right(stage_right.at[slot], from_left.at[slot], slot).start()

        slot_l = number - far

        @pl.when((slot_l >= 0) & (slot_l < steps))
        def _():
            slot = lax.clamp(0, slot_l, steps - 1)

            @pl.when(line.has_right)
            def _():
                line.to_left(stage_left.at[slot], from_right.at[slot], slot).wait_recv()

            @pl.when(line.has_left)
            def _():
                @pl.when(line.has_right)
                def _():
                    total = partial_ref[slot].astype(F32) + from_right[slot].astype(F32)
                    stage_left[slot] = total.astype(BF)

                @pl.when(jnp.logical_not(line.has_right))
                def _():
                    stage_left[slot] = partial_ref[slot]

                line.to_left(stage_left.at[slot], from_right.at[slot], slot).start()

        if beside is not None:
            beside(number)
        slot_f = number - lax.max(me, far)

        @pl.when((slot_f >= 0) & (slot_f < steps))
        def _():
            slot = lax.clamp(0, slot_f, steps - 1)

            @pl.when(jnp.logical_not(line.has_left))
            def _():
                finish(slot, partial_ref[slot].astype(F32) + from_right[slot].astype(F32))

            @pl.when(line.has_left)
            def _():
                @pl.when(line.has_right)
                def _():
                    finish(
                        slot,
                        partial_ref[slot].astype(F32)
                        + from_left[slot].astype(F32)
                        + from_right[slot].astype(F32),
                    )

                @pl.when(jnp.logical_not(line.has_right))
                def _():
                    finish(slot, partial_ref[slot].astype(F32) + from_left[slot].astype(F32))

        return carry

    lax.fori_loop(0, steps + count - 1, step, 0)

    def drain(slot, carry):
        @pl.when(line.has_right)
        def _():
            line.to_right(stage_right.at[slot], from_left.at[slot], slot).wait_send()

        @pl.when(line.has_left)
        def _():
            line.to_left(stage_left.at[slot], from_right.at[slot], slot).wait_send()

        return carry

    lax.fori_loop(0, steps, drain, 0)


def scatter_order(me, count, place):
    near = lax.min(me, count - 1 - me)
    base = count - 1 - 2 * near
    index = place - base
    block = jnp.where(
        place < base,
        count - 1 - place,
        jnp.where(index % 2 == 0, 2 * near - index // 2, index // 2),
    )
    return jnp.where(2 * me > count - 1, count - 1 - block, block)


def line_scatter_step(line, number, partial_ref, from_left, from_right, stage_right, stage_left):
    me, count = line.me, line.count
    block_r = count - 1 - number + me

    @pl.when((number >= me) & line.has_right & (block_r > me))
    def _():
        block = lax.clamp(0, block_r, count - 1)

        @pl.when(line.has_left)
        def _():
            line.to_right(stage_right.at[block], from_left.at[block], block).wait_recv()
            total = partial_ref[block].astype(F32) + from_left[block].astype(F32)
            stage_right[block] = total.astype(BF)

        @pl.when(jnp.logical_not(line.has_left))
        def _():
            stage_right[block] = partial_ref[block]

        line.to_right(stage_right.at[block], from_left.at[block], block).start()

    block_l = number - (count - 1 - me)

    @pl.when((block_l >= 0) & line.has_left & (block_l < me))
    def _():
        block = lax.clamp(0, block_l, count - 1)

        @pl.when(line.has_right)
        def _():
            line.to_left(stage_left.at[block], from_right.at[block], block).wait_recv()
            total = partial_ref[block].astype(F32) + from_right[block].astype(F32)
            stage_left[block] = total.astype(BF)

        @pl.when(jnp.logical_not(line.has_right))
        def _():
            stage_left[block] = partial_ref[block]

        line.to_left(stage_left.at[block], from_right.at[block], block).start()


def line_scatter_finish(line, partial_ref, from_left, from_right, stage_right, stage_left, total_ref):
    me, count = line.me, line.count
    total_ref[...] = partial_ref[me].astype(F32)

    @pl.when(line.has_left)
    def _():
        line.to_right(stage_right.at[me], from_left.at[me], me).wait_recv()
        total_ref[...] += from_left[me].astype(F32)

    @pl.when(line.has_right)
    def _():
        line.to_left(stage_left.at[me], from_right.at[me], me).wait_recv()
        total_ref[...] += from_right[me].astype(F32)

    def drain(block, carry):
        @pl.when(block > me)
        def _():
            line.to_right(stage_right.at[block], from_left.at[block], block).wait_send()

        @pl.when(block < me)
        def _():
            line.to_left(stage_left.at[block], from_right.at[block], block).wait_send()

        return carry

    lax.fori_loop(0, count, drain, 0)


def line_gather_step(line, number, slots):
    me, count = line.me, line.count
    block_l = lax.clamp(0, me - number, count - 1)
    block_r = lax.clamp(0, me + number, count - 1)

    @pl.when(number <= me)
    def _():
        @pl.when(number > 0)
        def _():
            line.to_right(slots.at[block_l], slots.at[block_l], block_l).wait_recv()

        @pl.when(line.has_right)
        def _():
            line.to_right(slots.at[block_l], slots.at[block_l], block_l).start()

    @pl.when(me + number <= count - 1)
    def _():
        @pl.when(number > 0)
        def _():
            line.to_left(slots.at[block_r], slots.at[block_r], block_r).wait_recv()

        @pl.when(line.has_left)
        def _():
            line.to_left(slots.at[block_r], slots.at[block_r], block_r).start()


def line_gather_drain(line, slots):
    me, count = line.me, line.count

    def drain(block, carry):
        @pl.when((block <= me) & line.has_right)
        def _():
            line.to_right(slots.at[block], slots.at[block], block).wait_send()

        @pl.when((block >= me) & line.has_left)
        def _():
            line.to_left(slots.at[block], slots.at[block], block).wait_send()

        return carry

    lax.fori_loop(0, count, drain, 0)


def line_gather(line, slots, compute):
    me, count = line.me, line.count

    def step(number, carry):
        line_gather_step(line, number, slots)

        def side(which, inner):
            block = me + (2 * which - 1) * number

            @pl.when((block >= 0) & (block < count) & ((number > 0) | (which == 0)))
            def _():
                compute(lax.clamp(0, block, count - 1))

            return inner

        return lax.fori_loop(0, 2, side, carry)

    lax.fori_loop(0, count, step, 0)
    line_gather_drain(line, slots)


def xor_place(place, number):
    if number == 0:
        return place
    if number == 1:
        return place + 1 - 2 * (place % 2)
    if number == 2:
        return place + 2 - 4 * (place // 2)
    return 3 - place


def call(kernel, inputs, outs, scratch, collective=None, cost=None):
    space = {True: pltpu.VMEM, False: pl.ANY, None: pltpu.SMEM}
    return pl.pallas_call(
        kernel,
        out_shape=[jax.ShapeDtypeStruct(shape, dtype) for shape, dtype, _ in outs],
        in_specs=[pl.BlockSpec(memory_space=space[where]) for _, where in inputs],
        out_specs=[pl.BlockSpec(memory_space=space[where]) for _, _, where in outs],
        scratch_shapes=scratch,
        cost_estimate=cost,
        compiler_params=pltpu.CompilerParams(
            collective_id=collective,
            has_side_effects=collective is not None,
            vmem_limit_bytes=VMEM_BYTES,
        ),
    )(*[array for array, _ in inputs])


def cost_of(flops, moved):
    return pl.CostEstimate(flops=int(flops), bytes_accessed=int(moved), transcendentals=0)


def vmem(*shape, dtype=BF):
    return pltpu.VMEM(shape, dtype)


def dma(*shape):
    return pltpu.SemaphoreType.DMA(shape)


def whole_wait(target, sem):
    pltpu.make_async_copy(target, target, sem).wait()


def rows_of(index, size):
    return pl.ds(pl.multiple_of(index * size, size), size)


IN_SIZES = [2 * MODEL_WIDTH] + [MODEL_WIDTH] * 6 + [TW, TW, MODEL_WIDTH, MODEL_WIDTH, FF]
OUT_SIZES = [MODEL_WIDTH] * 10 + [FF, MODEL_WIDTH]
IN_AT = [sum(IN_SIZES[:number]) for number in range(13)]
OUT_AT = [sum(OUT_SIZES[:number]) for number in range(13)]


def down_of(table, number):
    return table[:, IN_AT[number] : IN_AT[number + 1]]


def up_of(table, number):
    return table[:, OUT_AT[number] : OUT_AT[number + 1]]


def take_local(target, table, start, me, count):
    size = target.shape[-1]
    for place in range(count):
        @pl.when(me == place)
        def _(place=place):
            target[...] = table[:, start + place * size : start + (place + 1) * size]


def take_stack(target, table, start, count):
    size = target.shape[-1]
    for place in range(count):
        target[place] = table[:, start + place * size : start + (place + 1) * size]


def cross_forward(count, heads, summed, skip_out, query_weight, out_weight, skip_piece, text_kv, gains, tables):
    share, width = summed.shape
    local = query_weight.shape[-1]
    scale = HD ** (-0.5)
    rows, span = skip_piece.shape

    def kernel(sum_ref, skip_ref, hbm_q, hbm_o, piece, kv, gain, dtab, utab, first_out, second_out, in_out,
               mlp_out, q_out, inv_out, log_out, low_out, uo_out, skip_half, wq, wo, b_ref, ao, wsem, zsend, zrecv):
        me = lax.axis_index("tensor")
        core = lax.axis_index("ctx")
        loads = [
            pltpu.make_async_copy(source, target, wsem.at[number])
            for number, (source, target) in enumerate(((hbm_q, wq), (hbm_o, wo)))
        ]
        for load in loads:
            load.start()
        half = pl.ds(pl.multiple_of(core * (rows // 2), 16), rows // 2)
        own = pltpu.make_async_copy(piece.at[half, :], skip_half.at[me], wsem.at[2])
        own.start()
        z_peers = [{"tensor": xor_place(me, number)} for number in range(1, count)]
        greet([(core >= 0, device) for device in z_peers])
        sends = [
            push(piece.at[half, :], skip_half.at[me], zsend.at[number], zrecv.at[number], device)
            for number, device in enumerate(z_peers)
        ]
        for send in sends:
            send.start()
        take_stack(b_ref, utab, OUT_AT[6], count)
        take_stack(ao, dtab, IN_AT[9], count)
        first = skip_ref[rows_of(me, share), :] + sum_ref[...]
        first_out[...] = first
        normal, _ = stats(first)
        x = (normal * gain[1:2, :]).astype(BF)
        in_out[...] = x
        u = dot_nt(x, down_of(dtab, 6)).astype(BF)
        second_out[...] = first
        for load in loads:
            load.wait()

        def chunk(place, u_low):
            y = dot_nn(x, wq[place]) + dot_nn(u, b_ref[place])
            outs = []
            for head in range(heads):
                normal, inverse = stats(y[:, head * HD : (head + 1) * HD])
                q = normal.astype(BF)
                q_out[place, head] = q
                inv_out[place, head] = inverse
                s = dot_nt(q, kv[0, place, head, :, :HD]) * scale
                top = jnp.max(s, axis=-1, keepdims=True)
                e = jnp.exp(s - top)
                total = jnp.sum(e, axis=-1, keepdims=True)
                p = (e * (1.0 / total)).astype(BF)
                outs.append(dot_nn(p, kv[1, place, head, :, :HD]))
                log_out[place, head] = top + jnp.log(total)
            low = jnp.concatenate(outs, axis=1).astype(BF)
            low_out[place] = low
            second_out[...] += dot_nt(low, wo[place])
            return u_low + dot_nt(low, ao[place])

        u_low = lax.fori_loop(0, count, chunk, jnp.zeros((share, RANK), F32)).astype(BF)
        uo_out[...] = u_low
        second = second_out[...] + dot_nn(u_low, up_of(utab, 9))
        second_out[...] = second
        normal, _ = stats(second)
        mlp_out[...] = (normal * gain[2:3, :]).astype(BF)
        own.wait()
        for number in range(count - 1):
            arrived = skip_half.at[xor_place(me, number + 1)]
            push(arrived, arrived, zsend.at[number], zrecv.at[number], z_peers[number]).wait_recv()
        for send in sends:
            send.wait_send()

    return call(
        kernel,
        [(summed, True), (skip_out, True), (query_weight, False), (out_weight, False), (skip_piece, False)]
        + [(array, True) for array in (text_kv, gains, *tables)],
        [
            ((share, width), F32, True),
            ((share, width), F32, True),
            ((share, width), BF, True),
            ((share, width), BF, True),
            ((count, heads, share, HD), BF, True),
            ((count, heads, share, 1), F32, True),
            ((count, heads, share, 1), F32, True),
            ((count, share, local), BF, True),
            ((share, RANK), BF, True),
            ((count, rows // 2, span), BF, False),
        ],
        [vmem(count, width, local), vmem(count, width, local), vmem(count, RANK, local), vmem(count, RANK, local),
         dma(3), dma(count), dma(count)],
        collective=6,
        cost=cost_of(4 * share * width * width, 20e6),
    )


def feed_forward(count, block_in, cotangent, second, up_weight, down_weight, skip_half, tables):
    share, width = block_in.shape
    tokens = cotangent.shape[0]
    hidden_units = up_weight.shape[1]
    rows = 2 * skip_half.shape[1]
    span = skip_half.shape[2]

    def kernel(x_ref, cot, sec, hbm_u, hbm_d, shalf, dtab, utab, summed, down_out, g_ua, g_ub, g_da, g_db, skip_all,
               slots, wu, wd, ub, da, partial_ref, from_left, from_right, stage_right, stage_left, wsem, wsend, wrecv, *sems):
        me = lax.axis_index("tensor")
        core = lax.axis_index("ctx")
        dp = lax.axis_index("dp")
        gather_line = Line(me, count, *sems[:4])
        scatter_line = Line(me, count, *sems[4:])
        loads = [
            pltpu.make_async_copy(source, target, wsem.at[number])
            for number, (source, target) in enumerate(((hbm_u, wu), (hbm_d, wd)))
        ]
        for load in loads:
            load.start()
        skip = Shared(skip_all, rows, (wsend, wrecv, 0), stacked=True)
        own = pltpu.make_async_copy(shalf, skip.view(dp, core), wsem.at[2])
        own.start()
        slots[me] = x_ref[...]
        for ref in (g_ua, g_ub, g_da, g_db):
            ref[...] = jnp.zeros_like(ref)
        peers = [{"dp": xor_place(dp, 1)}, {"dp": xor_place(dp, 2)}, {"ctx": 1 - core}]
        greet(line_partners(me, count) + [(core >= 0, device) for device in peers])
        line_gather_step(gather_line, 0, slots)
        skip.send_own(shalf)
        take_local(ub, utab, OUT_AT[10], me, count)
        take_local(da, dtab, IN_AT[11], me, count)
        for load in loads:
            load.wait()

        def compute(block):
            rows = rows_of(block, share)
            x = slots[block]
            ct = cot[rows, :]
            ua, db = down_of(dtab, 10), up_of(utab, 11)
            u = dot_nt(x, ua).astype(BF)
            up = dot_nn(x, wu[...]) + dot_nn(u, ub[...])
            square = up * up
            curve = jnp.tanh(0.7978845608028654 * (up + 0.044715 * square * up))
            half = 0.5 * (1.0 + curve)
            active = (up * half).astype(BF)
            slope = half + 0.5 * up * (1.0 - curve * curve) * (0.7978845608028654 * (1.0 + 0.134145 * square))
            ud = dot_nt(active, da[...]).astype(BF)
            down = dot_nt(active, wd[...]) + dot_nn(ud, db)
            down_out[rows, :] = down.astype(BF)

            @pl.when(block == me)
            def _():
                down_out[rows, :] = (down + sec[...]).astype(BF)

            gd = dot_nt(ct, db).astype(BF)
            g_active = dot_nn(ct, wd[...]) + dot_nn(gd, da[...])
            g_up = (g_active * slope).astype(BF)
            gu = dot_nt(g_up, ub[...]).astype(BF)
            partial_ref[block] = (dot_nt(g_up, wu[...]) + dot_nn(gu, ua)).astype(BF)
            g_ub[...] += dot_tn(u, g_up)
            g_ua[...] += dot_tn(gu, x)
            g_db[...] += dot_tn(ud, ct)
            g_da[...] += dot_tn(gd, active)

        def step(number, carry):
            @pl.when(number > 0)
            def _():
                line_gather_step(gather_line, number, slots)

            def side(which, inner):
                block = me + (2 * which - 1) * number

                @pl.when((block >= 0) & (block < count) & ((number > 0) | (which == 0)))
                def _():
                    compute(lax.clamp(0, block, count - 1))

                return inner

            return lax.fori_loop(0, 2, side, carry)

        lax.fori_loop(0, count, step, 0)
        own.wait()
        skip.wait(0)
        skip.forward()
        skip.swap(0)
        skip.swap(3)

        def scatter(number, carry):
            line_scatter_step(scatter_line, number, partial_ref, from_left, from_right, stage_right, stage_left)
            return carry

        lax.fori_loop(0, count - 1, scatter, 0)
        skip.wait(1)
        skip.swap(1)
        line_gather_drain(gather_line, slots)
        line_scatter_finish(scatter_line, partial_ref, from_left, from_right, stage_right, stage_left, summed)
        skip.wait(2)
        skip.swap(2)
        skip.wait_swaps()
        skip.drain()

    buffers = [vmem(count, share, width) for _ in range(5)]
    return call(
        kernel,
        [(block_in, True), (cotangent, True), (second, True), (up_weight, False), (down_weight, False), (skip_half, False)]
        + [(array, True) for array in tables],
        [
            ((share, width), F32, True),
            ((tokens, width), BF, True),
            ((RANK, width), F32, True),
            ((RANK, hidden_units), F32, True),
            ((RANK, hidden_units), F32, True),
            ((RANK, width), F32, True),
            ((count, 4 * rows, span), BF, False),
        ],
        [vmem(count, share, width), vmem(width, hidden_units), vmem(width, hidden_units), vmem(RANK, hidden_units),
         vmem(RANK, hidden_units)]
        + buffers + [dma(3), dma(1, 7), dma(1, 7)] + [dma(count) for _ in range(8)],
        collective=3,
        cost=cost_of(8 * tokens * width * hidden_units, 60e6),
    )


class Shared:
    def __init__(self, target, rows, sems, stacked=False, split=True, columns=False):
        self.target, self.rows, self.stacked, self.split, self.columns = target, rows, stacked, split, columns
        self.send_sem, self.recv_sem, self.index = sems
        dp, core = lax.axis_index("dp"), lax.axis_index("ctx")
        self.dp, self.core = dp, core
        self.first = jnp.where(core == 0, xor_place(dp, 1), xor_place(dp, 2))
        self.second = jnp.where(core == 0, xor_place(dp, 2), xor_place(dp, 1))
        self.third = xor_place(dp, 3)

    def view(self, block, which):
        if self.columns:
            return self.target.at[:, pl.ds(pl.multiple_of(block * self.rows, 128), self.rows)]
        size = self.rows // 2 if self.split else self.rows
        start = block * self.rows + (which * size if self.split else 0)
        rows = pl.ds(pl.multiple_of(start, 16), size)
        return self.target.at[:, rows, :] if self.stacked else self.target.at[rows, :]

    def copy(self, number, source, block, which, device):
        target = self.view(block, which)
        source = target if source is None else source
        return push(source, target, self.send_sem.at[self.index, number], self.recv_sem.at[self.index, number], device)

    def send_own(self, source=None):
        self.copy(0, source, self.dp, self.core, {"dp": self.first}).start()
        self.copy(1, source, self.dp, self.core, {"dp": self.second}).start()

    def blocks(self):
        return [self.first, self.second, self.third] + ([self.dp] if self.stacked else [])

    def wait(self, number):
        self.copy(number, None, self.blocks()[number], self.core, {"dp": self.first}).wait_recv()

    def forward(self):
        self.copy(2, None, self.first, self.core, {"dp": self.second}).start()

    def swap(self, number):
        self.copy(3 + number, None, self.blocks()[number], self.core, {"ctx": 1 - self.core}).start()

    def wait_swaps(self):
        other = [self.second, self.first, self.third, self.dp]
        for number in range(len(self.blocks())):
            self.copy(3 + number, None, other[number], 1 - self.core, {"ctx": 1 - self.core}).wait_recv()

    def drain(self):
        for number in range(3 + (len(self.blocks()) if self.split else 0)):
            self.copy(number, None, self.dp, self.core, {"dp": self.first}).wait_send()


def front(count, heads, condition, index, hidden, long_skip, text, weights, mod_weight, gain_halves, gain_rows, tables):
    tokens, width = hidden.shape
    span = weights["skip"].shape[1]
    words, text_width = text.shape
    local = weights["q"].shape[1]
    units = weights["up"].shape[1]
    share = tokens // count
    block = min(128, tokens)
    chunk = min(64, tokens)
    steps = tokens // chunk
    each = block // chunk
    scale = HD ** (-0.5)
    rows = weights["q"].shape[0]
    text_rows = weights["ck"].shape[1]
    mod_rows = mod_weight.shape[0]

    def kernel(skip_own, q_own, k_own, v_own, o_own, ck_own, cv_own, cq_own, co_own, up_own, dn_own,
               index_ref, cond, hid, lsk, t_ref, wm, halves, gain, dtab, utab,
               skip_out, attn_in, q_out, keys, values, low_out, log_out, inv_q, inv_k, summed, act_all, text_kv,
               wq, wk, wv, wo, wcq, wco, wup, wdn,
               wskip, wtext, part_x, pgain, sa, tk, tv, qa, qb, kb, vb, oa, mod_in, mod_slice, mod_out, partial_a, left_a, right_a, sr_a, sl_a,
               partial_b, left_b, right_b, sr_b, sl_b, wsend, wrecv, local_sem, zsend, zrecv, msend, mrecv, tsend, trecv,
               xsend, xrecv, *sems):
        me = lax.axis_index("tensor")
        core = lax.axis_index("ctx")
        dp = lax.axis_index("dp")
        always = core >= 0
        peer = {"ctx": 1 - core}
        dp_peers = [{"dp": xor_place(dp, number)} for number in (1, 2, 3)]
        z_peers = [{"tensor": xor_place(me, number)} for number in range(1, count)]
        reduce_line = Line(me, count, *sems[:4])
        scatter_line = Line(me, count, *sems[4:])

        def sems_of(number):
            return (wsend, wrecv, number)

        skip = Shared(wskip, rows, sems_of(0))
        shared = {
            name: Shared(target, rows, sems_of(number))
            for name, target, number in (("q", wq, 1), ("k", wk, 2), ("v", wv, 3), ("o", wo, 4))
        }
        words_w = Shared(wtext, text_rows, sems_of(5), split=False, columns=True)
        cross = [Shared(wcq, rows, sems_of(6), stacked=True), Shared(wco, rows, sems_of(7), stacked=True)]
        wide = [Shared(wup, rows, sems_of(8)), Shared(wdn, rows, sems_of(9))]
        owns = {"q": q_own, "k": k_own, "v": v_own, "o": o_own}
        half = pl.ds(pl.multiple_of(core * (rows // 2), 16), rows // 2)
        mine = pl.ds(pl.multiple_of(dp * rows, 16), rows)
        my_half = pl.ds(pl.multiple_of(dp * rows + core * (rows // 2), 16), rows // 2)

        places = [
            pltpu.make_async_copy(source, target.at[mine, :], local_sem.at[number])
            for number, (source, target) in enumerate(
                ((skip_own, wskip), (q_own, wq), (k_own, wk), (v_own, wv), (o_own, wo), (up_own, wup), (dn_own, wdn))
            )
        ]
        for place in places:
            place.start()
        crossing = [
            pltpu.make_async_copy(source.at[half, :], target.at[me, my_half, :], local_sem.at[7 + number])
            for number, (source, target) in enumerate(((cq_own, wcq), (co_own, wco)))
        ]
        text_mine = pl.ds(pl.multiple_of(dp * text_rows, 128), text_rows)

        def text_place(source):
            return pltpu.make_async_copy(source, wtext.at[:, text_mine], local_sem.at[9])

        @pl.when(core == 0)
        def _():
            text_place(ck_own).start()

        @pl.when(core == 1)
        def _():
            text_place(cv_own).start()

        for place in crossing:
            place.start()
        value = cond[...].astype(F32)
        act_low = (value / (1.0 + jnp.exp(-value))).astype(BF)
        tag = jnp.full((1, 128), index_ref[0], jnp.int32).astype(F32)
        act_all[dp] = jnp.concatenate([act_low.astype(F32), tag], axis=1)
        greet([(always, device) for device in dp_peers + z_peers + [peer]])
        skip.send_own(skip_own.at[half, :])

        def z_copies(number):
            return [
                push(source.at[half, :], target.at[me, my_half, :], zsend.at[which, number], zrecv.at[which, number],
                     z_peers[number])
                for which, (source, target) in enumerate(((cq_own, wcq), (co_own, wco)))
            ]

        for number in range(count - 1):
            for copy in z_copies(number):
                copy.start()
        spread = [
            push(act_all.at[dp], act_all.at[dp], msend.at[0, number], mrecv.at[0, number], device)
            for number, device in enumerate(dp_peers)
        ]
        for copy in spread:
            copy.start()
        for place in range(count):
            @pl.when(me == place)
            def _(place=place):
                side = place * span // width
                start = place * span % width
                pgain[...] = halves[side : side + 1, start : start + span]
        take_local(sa, dtab, 0, me, count)
        take_local(tk, utab, OUT_AT[7], me, count)
        take_local(tv, utab, OUT_AT[8], me, count)
        for number, target in enumerate((qb, kb, vb)):
            qa[number * RANK : (number + 1) * RANK, :] = down_of(dtab, 2 + number)
            take_local(target, utab, OUT_AT[2 + number], me, count)
        take_local(oa, dtab, IN_AT[5], me, count)
        skip.wait(0)
        skip.forward()
        for name in ("q", "k", "v", "o"):
            shared[name].send_own(owns[name].at[half, :])

        @pl.when(core == 0)
        def _():
            words_w.send_own(ck_own)

        @pl.when(core == 1)
        def _():
            words_w.send_own(cv_own)

        skip.swap(0)

        for number in (1, 2, 3):
            source = act_all.at[xor_place(dp, number)]
            push(source, source, msend.at[0, number - 1], mrecv.at[0, number - 1], dp_peers[number - 1]).wait_recv()
        for owner in range(4):
            @pl.when(dp == owner)
            def _(owner=owner):
                span_of = slice(owner * mod_rows, (owner + 1) * mod_rows)
                for sequence in range(4):
                    mod_slice[sequence : sequence + 1, :] = act_all[sequence, :, span_of]

        products = dot_nn(mod_slice[...].astype(BF), wm[...])
        for sequence in range(4):
            mod_out[sequence] = products[sequence : sequence + 1]
        backs = [
            push(mod_out.at[xor_place(dp, number)], mod_in.at[dp], msend.at[1, number - 1], mrecv.at[1, number - 1],
                 dp_peers[number - 1])
            for number in (1, 2, 3)
        ]
        for copy in backs:
            copy.start()
        skip.wait(1)
        skip.swap(1)
        mod_in[dp] = mod_out[dp]
        mod_u = dot_nt(act_low, down_of(dtab, 1)).astype(BF)
        mod_low = dot_nn(mod_u, up_of(utab, 1))
        for number in (1, 2, 3):
            target = mod_in.at[xor_place(dp, number)]
            push(target, target, msend.at[1, number - 1], mrecv.at[1, number - 1], dp_peers[number - 1]).wait_recv()
        shift = mod_in[0] + mod_in[1] + mod_in[2] + mod_in[3] + mod_low
        skip.wait(2)
        skip.swap(2)
        places[0].wait()
        skip.wait_swaps()

        def compute(number):
            @pl.when(number % each == 0)
            def _():
                here = rows_of(number // each, block)
                left = hid[here, :].astype(F32)
                right = lsk[here, :].astype(F32)
                mean = (jnp.sum(left, axis=-1, keepdims=True) + jnp.sum(right, axis=-1, keepdims=True)) / (2 * width)
                spread = jnp.sum((left - mean) ** 2, axis=-1, keepdims=True)
                spread += jnp.sum((right - mean) ** 2, axis=-1, keepdims=True)
                inverse = lax.rsqrt(spread / (2 * width) + NORM_EPS)
                for place in range(count):
                    @pl.when(me == place)
                    def _(place=place):
                        source = hid if place * span < width else lsk
                        start = place * span % width
                        part_x[...] = source[here, start : start + span].astype(F32)
                x = ((part_x[...] - mean) * inverse * pgain[...]).astype(BF)
                u = dot_nt(x, sa[...]).astype(BF)
                y = (dot_nt(x, wskip[...]) + dot_nn(u, up_of(utab, 0))).astype(BF)
                for piece in range(each):
                    partial_a[number + piece] = y[piece * chunk : (piece + 1) * chunk]

        def finish(slot, total):
            here = rows_of(slot, chunk)
            skip_out[here, :] = total
            normal, _ = stats(total)
            attn_in[here, :] = (normal * gain[0:1, :] + shift).astype(BF)

        def beside(number):
            @pl.when(number == 3)
            def _():
                for weight in (*shared.values(), words_w):
                    weight.wait(0)
                    weight.forward()
                for weight in shared.values():
                    weight.swap(0)

            @pl.when(number == 4)
            def _():
                for weight in (*shared.values(), words_w):
                    weight.wait(1)
                for weight in shared.values():
                    weight.swap(1)

            @pl.when(number == 6)
            def _():
                for place in crossing:
                    place.wait()
                for other in range(count - 1):
                    for which, target in enumerate((wcq, wco)):
                        block_in = target.at[xor_place(me, other + 1), my_half, :]
                        push(block_in, block_in, zsend.at[which, other], zrecv.at[which, other], z_peers[other]).wait_recv()
                for weight in cross:
                    weight.send_own()

            @pl.when(number == 7)
            def _():
                for weight in (*shared.values(), words_w):
                    weight.wait(2)
                for weight in shared.values():
                    weight.swap(2)

        line_reduce_all(reduce_line, steps, compute, partial_a, left_a, right_a, sr_a, sl_a, finish, beside)

        @pl.when(core == 0)
        def _():
            text_place(ck_own).wait()

        @pl.when(core == 1)
        def _():
            text_place(cv_own).wait()

        x = t_ref[...]
        y = dot_nt(x, wtext[...])

        @pl.when(core == 0)
        def _():
            z = y + dot_nn(dot_nt(x, down_of(dtab, 7)).astype(BF), tk[...])
            for head in range(heads):
                normal, inverse = stats(z[:, head * HD : (head + 1) * HD])
                upper = inverse.astype(BF)
                lower = (inverse - upper.astype(F32)).astype(BF)
                text_kv[0, me, head] = jnp.concatenate([normal.astype(BF), upper, lower], axis=1)

        @pl.when(core == 1)
        def _():
            z = (y + dot_nn(dot_nt(x, down_of(dtab, 8)).astype(BF), tv[...])).astype(BF)
            filler = jnp.zeros((words, 2), BF)
            for head in range(heads):
                text_kv[1, me, head] = jnp.concatenate([z[:, head * HD : (head + 1) * HD], filler], axis=1)

        texts = [
            push(text_kv.at[core, me], text_kv.at[core, me], tsend.at[number], trecv.at[number], z_peers[number])
            for number in range(count - 1)
        ]
        for copy in texts:
            copy.start()

        for number in range(1, 5):
            places[number].wait()
        for weight in shared.values():
            weight.wait_swaps()

        def project(number, carry):
            here = rows_of(number, block)
            x = attn_in[here, :]
            u = dot_nt(x, qa[...]).astype(BF)
            yq = dot_nn(x, wq[...]) + dot_nn(u[:, :RANK], qb[...])
            yk = dot_nn(x, wk[...]) + dot_nn(u[:, RANK : 2 * RANK], kb[...])
            yv = (dot_nn(x, wv[...]) + dot_nn(u[:, 2 * RANK :], vb[...])).astype(BF)
            for head in range(heads):
                span_of = slice(head * HD, (head + 1) * HD)
                normal, inverse = stats(yq[:, span_of])
                q_out[head, here, :] = normal.astype(BF)
                inv_q[head, here, :] = inverse
                normal, inverse = stats(yk[:, span_of])
                keys[core, head, here, :] = normal.astype(BF)
                inv_k[head, here, :] = inverse
                values[core, head, here, :] = yv[:, span_of]
            return carry

        lax.fori_loop(0, tokens // block, project, 0)
        swaps = [
            push(ref.at[core], ref.at[core], xsend.at[number], xrecv.at[number], peer)
            for number, ref in enumerate((keys, values))
        ]
        for swap in swaps:
            swap.start()
        for weight in cross:
            weight.wait(0)
            weight.forward()
            weight.swap(0)
            weight.swap(3)
        for weight, own in zip(wide, (up_own, dn_own)):
            weight.send_own(own.at[half, :])
        for number, ref in enumerate((keys, values)):
            push(ref.at[1 - core], ref.at[1 - core], xsend.at[number], xrecv.at[number], peer).wait_recv()

        def attend(place, carry):
            dest = scatter_order(me, count, place)
            here = rows_of(dest, share)
            outs = []
            for head in range(heads):
                q = q_out[head, here, :]
                s0 = dot_nt(q, keys[0, head]) * scale
                s1 = dot_nt(q, keys[1, head]) * scale
                top = jnp.maximum(jnp.max(s0, axis=-1, keepdims=True), jnp.max(s1, axis=-1, keepdims=True))
                e0 = jnp.exp(s0 - top)
                e1 = jnp.exp(s1 - top)
                total = jnp.sum(e0, axis=-1, keepdims=True) + jnp.sum(e1, axis=-1, keepdims=True)
                share_of = 1.0 / total
                p0 = (e0 * share_of).astype(BF)
                p1 = (e1 * share_of).astype(BF)
                outs.append(dot_nn(p0, values[0, head]) + dot_nn(p1, values[1, head]))
                log_out[head, here, :] = top + jnp.log(total)
            low = jnp.concatenate(outs, axis=1).astype(BF)
            low_out[here, :] = low
            u = dot_nt(low, oa[...]).astype(BF)
            partial_b[dest] = (dot_nt(low, wo[...]) + dot_nn(u, up_of(utab, 5))).astype(BF)

            @pl.when(place < count - 1)
            def _():
                line_scatter_step(scatter_line, place, partial_b, left_b, right_b, sr_b, sl_b)

            @pl.when(place == 1)
            def _():
                for weight in cross:
                    weight.wait(1)
                    weight.swap(1)
                for number in range(count - 1):
                    arrived = text_kv.at[core, xor_place(me, number + 1)]
                    push(arrived, arrived, tsend.at[number], trecv.at[number], z_peers[number]).wait_recv()
                push(text_kv.at[core], text_kv.at[core], tsend.at[count - 1], trecv.at[count - 1], peer).start()

            @pl.when(place == 2)
            def _():
                for weight in cross:
                    weight.wait(2)
                    weight.swap(2)

            return carry

        lax.fori_loop(0, count, attend, 0)
        for weight in wide:
            weight.wait(0)
            weight.forward()
            weight.swap(0)
        for weight in wide:
            weight.wait(1)
            weight.swap(1)
        line_scatter_finish(scatter_line, partial_b, left_b, right_b, sr_b, sl_b, summed)
        for weight in wide:
            weight.wait(2)
            weight.swap(2)
        others = text_kv.at[1 - core]
        push(others, others, tsend.at[count - 1], trecv.at[count - 1], peer).wait_recv()
        for weight in cross + wide:
            weight.wait_swaps()
        places[5].wait()
        places[6].wait()
        for weight in (skip, *shared.values(), words_w, *cross, *wide):
            weight.drain()
        for number in range(count - 1):
            for copy in z_copies(number):
                copy.wait_send()
        for copy in spread + backs + texts:
            copy.wait_send()
        push(text_kv.at[core], text_kv.at[core], tsend.at[count - 1], trecv.at[count - 1], peer).wait_send()
        for swap in swaps:
            swap.wait_send()

    names = ("skip", "q", "k", "v", "o", "ck", "cv", "cq", "co", "up", "dn")
    return call(
        kernel,
        [(weights[name], False) for name in names] + [(index, None)]
        + [(array, True) for array in (condition, hidden, long_skip, text, mod_weight, gain_halves, gain_rows, *tables)],
        [
            ((tokens, width), F32, True),
            ((tokens, width), BF, True),
            ((heads, tokens, HD), BF, True),
            ((2, heads, tokens, HD), BF, True),
            ((2, heads, tokens, HD), BF, True),
            ((tokens, local), BF, True),
            ((heads, tokens, 1), F32, True),
            ((heads, tokens, 1), F32, True),
            ((heads, tokens, 1), F32, True),
            ((share, width), F32, True),
            ((4, 1, width + 128), F32, True),
            ((2, count, heads, words, HD + 2), BF, True),
        ]
        + [((width, local), BF, True) for _ in range(4)]
        + [((count, width, local), BF, False) for _ in range(2)]
        + [((width, units), BF, False) for _ in range(2)],
        [vmem(width, span), vmem(local, text_width), vmem(block, span, dtype=F32), vmem(1, span, dtype=F32),
         vmem(RANK, span), vmem(RANK, local), vmem(RANK, local), vmem(3 * RANK, width)]
        + [vmem(RANK, local) for _ in range(4)]
        + [vmem(4, 1, width, dtype=F32), vmem(4, mod_rows, dtype=F32),
         vmem(4, 1, width, dtype=F32)]
        + [vmem(steps, chunk, width) for _ in range(5)] + [vmem(count, share, width) for _ in range(5)]
        + [dma(10, 7), dma(10, 7), dma(10), dma(2, count), dma(2, count), dma(2, 3), dma(2, 3), dma(count), dma(count),
           dma(2), dma(2)]
        + [dma(steps) for _ in range(4)] + [dma(count) for _ in range(4)],
        collective=1,
        cost=cost_of(8 * tokens * width * local, 60e6),
    )


def norm_backward(normal, inverse, grad):
    return inverse * (
        grad
        - jnp.mean(grad, axis=-1, keepdims=True)
        - normal * jnp.mean(grad * normal, axis=-1, keepdims=True)
    )


def cross_backward(count, heads, g_in, cotangent, first, second, block_in, query, inverses, logs, low, u_low, text,
                   query_weight, out_weight, text_kv, gains, tables):
    share, width = g_in.shape
    local = query_weight.shape[-1]
    words, text_width = text.shape
    scale = HD ** (-0.5)

    def kernel(g_ref, cot, first_ref, second_ref, x_ref, q_ref, inv_ref, log_ref, low_ref, uo_ref, t_ref, hbm_q, hbm_o,
               kv, gain, dtab, utab, g_first, ga_q, gb_q, ga_k, gb_k, ga_v, gb_v, ga_o, gb_o,
               acc, wq, wo, b_ref, ao, bk, bv, wsem):
        me = lax.axis_index("tensor")
        loads = [
            pltpu.make_async_copy(source, target, wsem.at[number])
            for number, (source, target) in enumerate(((hbm_q, wq), (hbm_o, wo)))
        ]
        for load in loads:
            load.start()
        normal, inverse = stats(second_ref[...])
        g_second = cot[rows_of(me, share), :].astype(F32) + norm_backward(normal, inverse, g_ref[...] * gain[2:3, :])
        g_low = g_second.astype(BF)
        take_stack(b_ref, utab, OUT_AT[6], count)
        take_stack(ao, dtab, IN_AT[9], count)
        take_stack(bk, utab, OUT_AT[7], count)
        take_stack(bv, utab, OUT_AT[8], count)
        go = dot_nt(g_low, up_of(utab, 9)).astype(BF)
        gb_o[...] = dot_tn(uo_ref[...], g_low)
        x = x_ref[...]
        uq = dot_nt(x, down_of(dtab, 6)).astype(BF)
        words_in = t_ref[...]
        uk = dot_nt(words_in, down_of(dtab, 7)).astype(BF)
        uv = dot_nt(words_in, down_of(dtab, 8)).astype(BF)
        acc[...] = jnp.zeros_like(acc)
        for load in loads:
            load.wait()

        def chunk(place, carry):
            gq_sum, gk_sum, gv_sum = carry
            g_attn = (dot_nn(g_low, wo[place]) + dot_nn(go, ao[place])).astype(BF)
            ga_o[place] = dot_tn(go, low_ref[place])
            gq_parts, gk_parts, gv_parts = [], [], []
            for head in range(heads):
                gh = g_attn[:, head * HD : (head + 1) * HD]
                q = q_ref[place, head]
                kfull = kv[0, place, head]
                k = kfull[:, :HD]
                v = kv[1, place, head, :, :HD]
                p = jnp.exp(dot_nt(q, k) * scale - log_ref[place, head])
                dp = dot_nt(gh, v)
                inner = jnp.sum(p * dp, axis=-1, keepdims=True)
                ds = (p * (dp - inner)).astype(BF)
                dq = dot_nn(ds, k) * scale
                dk = dot_tn(ds, q) * scale
                dv = dot_tn(p.astype(BF), gh)
                gq_parts.append(norm_backward(q.astype(F32), inv_ref[place, head], dq))
                inv_k = kfull[:, HD : HD + 1].astype(F32) + kfull[:, HD + 1 : HD + 2].astype(F32)
                gk_parts.append(norm_backward(k.astype(F32), inv_k, dk))
                gv_parts.append(dv)
            gq = jnp.concatenate(gq_parts, axis=1).astype(BF)
            gk = jnp.concatenate(gk_parts, axis=1).astype(BF)
            gv = jnp.concatenate(gv_parts, axis=1).astype(BF)
            acc[...] += dot_nt(gq, wq[place])
            gb_q[place] = dot_tn(uq, gq)
            gb_k[place] = dot_tn(uk, gk)
            gb_v[place] = dot_tn(uv, gv)
            return (
                gq_sum + dot_nt(gq, b_ref[place]),
                gk_sum + dot_nt(gk, bk[place]),
                gv_sum + dot_nt(gv, bv[place]),
            )

        start = (jnp.zeros((share, RANK), F32), jnp.zeros((words, RANK), F32), jnp.zeros((words, RANK), F32))
        gq_sum, gk_sum, gv_sum = lax.fori_loop(0, count, chunk, start)
        gq_sum = gq_sum.astype(BF)
        ga_q[...] = dot_tn(gq_sum, x)
        ga_k[...] = dot_tn(gk_sum.astype(BF), words_in)
        ga_v[...] = dot_tn(gv_sum.astype(BF), words_in)
        g_x = acc[...] + dot_nn(gq_sum, down_of(dtab, 6))
        normal, inverse = stats(first_ref[...])
        g_first[...] = (g_second + norm_backward(normal, inverse, g_x * gain[1:2, :])).astype(BF)

    return call(
        kernel,
        [(array, True) for array in (g_in, cotangent, first, second, block_in, query, inverses, logs, low, u_low, text)]
        + [(query_weight, False), (out_weight, False)]
        + [(array, True) for array in (text_kv, gains, *tables)],
        [
            ((share, width), BF, True),
            ((RANK, width), F32, True),
            ((count, RANK, local), F32, True),
            ((RANK, text_width), F32, True),
            ((count, RANK, local), F32, True),
            ((RANK, text_width), F32, True),
            ((count, RANK, local), F32, True),
            ((count, RANK, local), F32, True),
            ((RANK, width), F32, True),
        ],
        [vmem(share, width, dtype=F32), vmem(count, width, local), vmem(count, width, local)]
        + [vmem(count, RANK, local) for _ in range(4)] + [dma(2)],
        cost=cost_of(8 * share * width * width, 20e6),
    )


def attention_backward(count, heads, g_first, attn_in, query, keys, values, low, logs, inv_q, inv_k, weights, tables):
    share, width = g_first.shape
    tokens = attn_in.shape[0]
    local = weights[0].shape[1]
    block = min(128, tokens)
    chunk = min(64, tokens)
    steps = tokens // chunk
    each = block // chunk
    scale = HD ** (-0.5)

    def kernel(g_ref, x_ref, q_ref, k_ref, v_ref, low_ref, log_ref, iq_ref, ik_ref, *refs):
        (wq, wk, wv, wo, dtab, utab, total_out, gall, ga_in, gb_q, gb_k, gb_v, ga_o, gb_o, gq_low, gk_acc,
         gv_acc, swap_out, swap_in, partial_ref, from_left, from_right, stage_right, stage_left, a_ref, bq, bk,
         bv, ao, xsend, xrecv, *sems) = refs
        me = lax.axis_index("tensor")
        core = lax.axis_index("ctx")
        peer = {"ctx": 1 - core}
        gather_line = Line(me, count, *sems[:4])
        reduce_line = Line(me, count, *sems[4:])
        gall[me] = g_ref[...]
        for ref in (ga_in, gb_q, gb_k, gb_v, ga_o, gb_o, gk_acc, gv_acc):
            ref[...] = jnp.zeros_like(ref)
        greet(line_partners(me, count) + [(core >= 0, peer)])
        line_gather_step(gather_line, 0, gall)
        for number, target in enumerate((bq, bk, bv)):
            a_ref[number * RANK : (number + 1) * RANK, :] = down_of(dtab, 2 + number)
            take_local(target, utab, OUT_AT[2 + number], me, count)
        take_local(ao, dtab, IN_AT[5], me, count)

        def attend(place):
            rows = rows_of(place, share)
            g = gall[place]
            go = dot_nt(g, up_of(utab, 5)).astype(BF)
            g_attn = (dot_nn(g, wo[...]) + dot_nn(go, ao[...])).astype(BF)
            low = low_ref[rows, :]
            uo = dot_nt(low, ao[...]).astype(BF)
            gb_o[...] += dot_tn(uo, g)
            ga_o[...] += dot_tn(go, low)
            parts = []
            for head in range(heads):
                gh = g_attn[:, head * HD : (head + 1) * HD]
                q = q_ref[head, rows, :]
                probs, grads = [], []
                inner = 0.0
                for half in range(2):
                    p = jnp.exp(dot_nt(q, k_ref[half, head]) * scale - log_ref[head, rows, :])
                    dp = dot_nt(gh, v_ref[half, head])
                    inner = inner + jnp.sum(p * dp, axis=-1, keepdims=True)
                    probs.append(p)
                    grads.append(dp)
                dq = 0.0
                for half in range(2):
                    ds = (probs[half] * (grads[half] - inner)).astype(BF)
                    dq = dq + dot_nn(ds, k_ref[half, head])
                    gk_acc[half, head] += dot_tn(ds, q)
                    gv_acc[half, head] += dot_tn(probs[half].astype(BF), gh)
                parts.append(norm_backward(q.astype(F32), iq_ref[head, rows, :], dq * scale))
            gq_low[rows, :] = jnp.concatenate(parts, axis=1).astype(BF)

        def gather(number, carry):
            @pl.when(number > 0)
            def _():
                line_gather_step(gather_line, number, gall)

            def side(which, inner):
                place = me + (2 * which - 1) * number

                @pl.when((place >= 0) & (place < count) & ((number > 0) | (which == 0)))
                def _():
                    attend(lax.clamp(0, place, count - 1))

                return inner

            return lax.fori_loop(0, 2, side, carry)

        lax.fori_loop(0, count, gather, 0)
        swap_out[0] = (gk_acc[1 - core] * scale).astype(BF)
        swap_out[1] = gv_acc[1 - core].astype(BF)
        swap = push(swap_out, swap_in, xsend, xrecv, peer)
        swap.start()
        line_gather_drain(gather_line, gall)
        swap.wait()

        def compute(number):
            @pl.when(number % each == 0)
            def _():
                rows = rows_of(number // each, block)
                x = x_ref[rows, :]
                u = dot_nt(x, a_ref[...]).astype(BF)
                parts_k, parts_v = [], []
                for head in range(heads):
                    dk = gk_acc[core, head, rows, :] * scale + swap_in[0, head, rows, :].astype(F32)
                    normal = k_ref[core, head, rows, :].astype(F32)
                    parts_k.append(norm_backward(normal, ik_ref[head, rows, :], dk))
                    parts_v.append(gv_acc[core, head, rows, :] + swap_in[1, head, rows, :].astype(F32))
                gq = gq_low[rows, :]
                gk = jnp.concatenate(parts_k, axis=1).astype(BF)
                gv = jnp.concatenate(parts_v, axis=1).astype(BF)
                gu = jnp.concatenate([dot_nt(gq, bq[...]), dot_nt(gk, bk[...]), dot_nt(gv, bv[...])], axis=1).astype(BF)
                y = dot_nt(gq, wq[...]) + dot_nt(gk, wk[...]) + dot_nt(gv, wv[...]) + dot_nn(gu, a_ref[...])
                y = y.astype(BF)
                for piece in range(each):
                    partial_ref[number + piece] = y[piece * chunk : (piece + 1) * chunk]
                ga_in[...] += dot_tn(gu, x)
                gb_q[...] += dot_tn(u[:, :RANK], gq)
                gb_k[...] += dot_tn(u[:, RANK : 2 * RANK], gk)
                gb_v[...] += dot_tn(u[:, 2 * RANK :], gv)

        def finish(slot, total):
            total_out[rows_of(slot, chunk), :] = total

        line_reduce_all(
            reduce_line, steps, compute, partial_ref, from_left, from_right, stage_right, stage_left, finish
        )

    buffers = [vmem(steps, chunk, width) for _ in range(5)]
    return call(
        kernel,
        [(array, True) for array in (g_first, attn_in, query, keys, values, low, logs, inv_q, inv_k)]
        + [(array, True) for array in (*weights, *tables)],
        [
            ((tokens, width), F32, True),
            ((count, share, width), BF, True),
            ((3 * RANK, width), F32, True),
            ((RANK, local), F32, True),
            ((RANK, local), F32, True),
            ((RANK, local), F32, True),
            ((RANK, local), F32, True),
            ((RANK, width), F32, True),
        ],
        [vmem(tokens, local), vmem(2, heads, tokens, HD, dtype=F32), vmem(2, heads, tokens, HD, dtype=F32)]
        + [vmem(2, heads, tokens, HD), vmem(2, heads, tokens, HD)]
        + buffers + [vmem(3 * RANK, width)] + [vmem(RANK, local) for _ in range(4)] + [dma(), dma()] + [dma(count) for _ in range(4)] + [dma(steps) for _ in range(4)],
        collective=4,
        cost=cost_of(16 * tokens * width * local, 60e6),
    )


def back_end(count, g_attn, g_first, skip_out, hidden, long_skip, weight, mod_weight, gain_halves, gain_rows, tables,
             condition, act_all, wide_grads, local_down, local_up, stacked):
    tokens, width = hidden.shape
    span = weight.shape[-1]
    block = tokens // count
    own_rows = RANK // count
    columns = IN_AT[12] + OUT_AT[12]
    half = -(-columns // 256) * 128
    mod_rows = mod_weight.shape[0]
    wide_at, wide = list(wide_grads), list(wide_grads.values())
    local_at = [number for number in local_down] + [IN_AT[12] + number for number in local_up]
    local = list(local_down.values()) + list(local_up.values())
    stacked_at, stack = list(stacked), list(stacked.values())

    def kernel(g_ref, gf_ref, skip_ref, hid, lsk, hbm_w, wm, gains, gain, dtab, utab, cond, act_ref, *refs):
        wide_refs, refs = refs[: len(wide)], refs[len(wide) :]
        local_refs, refs = refs[: len(local)], refs[len(local) :]
        stack_refs, refs = refs[: len(stack)], refs[len(stack) :]
        (out_h, out_l, out_a, out_b, out_c, w, buf_h, buf_l, low, table, swap_out, swap_in, partial_ref, from_left,
         from_right, stage_right, stage_left, summed, slots, other_out, other_in, shifts, shift_in, act_out, act_in, g_act,
         wsem, osem, ssem, rsem, dsend, drecv, msend, mrecv, *sems) = refs
        me = lax.axis_index("tensor")
        core = lax.axis_index("ctx")
        dp = lax.axis_index("dp")
        peer = {"ctx": 1 - core}
        line = Line(me, count, *sems)
        peers = [{"dp": xor_place(dp, number)} for number in (1, 2, 3)]
        load = pltpu.make_async_copy(hbm_w, w, wsem)
        load.start()
        greet(line_partners(me, count) + [(core >= 0, peer)] + [(core >= 0, device) for device in peers])

        g_shift = jnp.sum(g_ref[...], axis=0, keepdims=True)
        shift_in[0] = g_shift
        swap_shift = push(shift_in.at[0], shift_in.at[1], ssem.at[2], rsem.at[2], peer)
        swap_shift.start()
        act = act_ref[dp, :, :width]
        act_low = act.astype(BF)
        mod_u = dot_nt(act_low, down_of(dtab, 1))
        once = jnp.where(me == 0, 1.0, 0.0)
        shift_u = dot_nt(g_shift.astype(BF), up_of(utab, 1))
        mod_a = jnp.concatenate([shift_u * once, jnp.zeros((7, RANK), F32)], axis=0).astype(BF)
        mod_b = jnp.concatenate([mod_u * once, jnp.zeros((7, RANK), F32)], axis=0).astype(BF)
        act_pad = jnp.concatenate([act_low.astype(F32), jnp.zeros((7, width), F32)], axis=0).astype(BF)
        shift_pad = jnp.concatenate([g_shift, jnp.zeros((7, width), F32)], axis=0).astype(BF)

        table[...] = jnp.zeros_like(table)
        table[:, IN_AT[1] : IN_AT[2]] = dot_tn(mod_a, act_pad)
        table[:, IN_AT[12] + OUT_AT[1] : IN_AT[12] + OUT_AT[2]] = dot_tn(mod_b, shift_pad)
        for start, ref in zip(wide_at, wide_refs):
            table[:, start : start + ref.shape[1]] = ref[...]
        for start, ref in zip(stacked_at, stack_refs):
            size = ref.shape[2]
            for place in range(count):
                table[:, start + place * size : start + (place + 1) * size] = ref[place]
        for place in range(count):
            @pl.when(me == place)
            def _(place=place):
                for start, ref in zip(local_at, local_refs):
                    size = ref.shape[1]
                    table[:, start + place * size : start + (place + 1) * size] = ref[...]

        load.wait()

        def skip_block(number, own):
            rows = rows_of(number, block)
            ga_in = g_ref[rows, :]
            normal, inverse = stats(skip_ref[rows, :])
            g_low = (
                gf_ref[number].astype(F32) + norm_backward(normal, inverse, ga_in * gain[0:1, :])
            ).astype(BF)
            left = hid[rows, :].astype(F32)
            right = lsk[rows, :].astype(F32)
            mean = (jnp.sum(left, axis=-1, keepdims=True) + jnp.sum(right, axis=-1, keepdims=True)) / (2 * width)
            left = left - mean
            right = right - mean
            spread = jnp.sum(left * left, axis=-1, keepdims=True) + jnp.sum(right * right, axis=-1, keepdims=True)
            inverse = lax.rsqrt(spread / (2 * width) + NORM_EPS)
            left = left * inverse
            right = right * inverse
            gu = dot_nt(g_low, up_of(utab, 0)).astype(BF)
            a_left, a_right = dtab[:, :width], dtab[:, width : 2 * width]

            @pl.when(own)
            def _():
                low_l = (left * gains[0:1, :]).astype(BF)
                low_r = (right * gains[1:2, :]).astype(BF)
                u = (dot_nt(low_l, a_left) + dot_nt(low_r, a_right)).astype(BF)
                table[:, :width] = dot_tn(gu, low_l)
                table[:, width : 2 * width] = dot_tn(gu, low_r)
                table[:, IN_AT[12] : IN_AT[12] + width] = dot_tn(u, g_low)

            for place in range(count):
                low[:, place * span : (place + 1) * span] = dot_nn(g_low, w[place])
            gl = (low[:, :width] + dot_nn(gu, a_left)) * gains[0:1, :]
            gr = (low[:, width:] + dot_nn(gu, a_right)) * gains[1:2, :]
            mean = (jnp.sum(gl, axis=-1, keepdims=True) + jnp.sum(gr, axis=-1, keepdims=True)) / (2 * width)
            inner = (
                jnp.sum(gl * left, axis=-1, keepdims=True) + jnp.sum(gr * right, axis=-1, keepdims=True)
            ) / (2 * width)
            buf_h[number] = inverse * (gl - mean - left * inner)
            buf_l[number] = inverse * (gr - mean - right * inner)
            pltpu.make_async_copy(buf_h.at[number], out_h.at[rows, :], osem.at[0, number]).start()
            pltpu.make_async_copy(buf_l.at[number], out_l.at[rows, :], osem.at[1, number]).start()

        swap = push(swap_out, swap_in, ssem.at[0], rsem.at[0], peer)
        shift_sends = [
            push(shifts.at[dp], shifts.at[dp], msend.at[0, number], mrecv.at[0, number], device)
            for number, device in enumerate(peers)
        ]
        act_sends = [
            push(act_out.at[xor_place(dp, number)], act_in.at[dp], msend.at[1, number - 1], mrecv.at[1, number - 1],
                 peers[number - 1])
            for number in (1, 2, 3)
        ]

        def step(number, carry):
            place = lax.rem(me + number, count)
            skip_block(place, number == 0)

            @pl.when(number == 0)
            def _():
                for which in range(2):
                    @pl.when(core == which)
                    def _(which=which):
                        swap_out[...] = table[:, (1 - which) * half : (2 - which) * half].astype(BF)

                swap.start()
                swap_shift.wait()
                shifts[dp] = shift_in[0] + shift_in[1]
                for send in shift_sends:
                    send.start()

            @pl.when(number == 1)
            def _():
                swap.wait()
                for which in range(2):
                    @pl.when(core == which)
                    def _(which=which):
                        for part in range(count):
                            at = slice(part * own_rows, (part + 1) * own_rows)
                            mine = table[at, which * half : (which + 1) * half]
                            partial_ref[part] = (mine + swap_in[at, :].astype(F32)).astype(BF)

                for other in (1, 2, 3):
                    source = shifts.at[xor_place(dp, other)]
                    push(source, source, msend.at[0, other - 1], mrecv.at[0, other - 1], peers[other - 1]).wait_recv()
                every = jnp.concatenate([shifts[sequence] for sequence in range(4)], axis=0).astype(BF)
                products = dot_nt(every, wm[...])
                for sequence in range(4):
                    act_out[sequence] = products[sequence : sequence + 1]
                for send in act_sends:
                    send.start()

            @pl.when((number >= 1) & (number < count))
            def _():
                line_scatter_step(line, number - 1, partial_ref, from_left, from_right, stage_right, stage_left)

            return carry

        lax.fori_loop(0, count, step, 0)
        line_scatter_finish(line, partial_ref, from_left, from_right, stage_right, stage_left, summed)
        slots[dp] = summed[...].astype(BF)
        sends = [
            push(slots.at[dp], slots.at[dp], dsend.at[number], drecv.at[number], device)
            for number, device in enumerate(peers)
        ]
        for send in sends:
            send.start()

        act_in[dp] = act_out[dp]
        for number in (1, 2, 3):
            source = act_in.at[xor_place(dp, number)]
            push(source, source, msend.at[1, number - 1], mrecv.at[1, number - 1], peers[number - 1]).wait_recv()
        for place in range(4):
            g_act[:, place * mod_rows : (place + 1) * mod_rows] = act_in[place]
        full_u = dot_nt(shifts[dp].astype(BF), up_of(utab, 1)).astype(BF)
        grad = g_act[...] + dot_nn(full_u, down_of(dtab, 1))
        value = cond[...].astype(F32)
        gate = 1.0 / (1.0 + jnp.exp(-value))
        out_c[...] = grad * gate * (1.0 + value * (1.0 - gate))

        for number in (1, 2, 3):
            source = slots.at[xor_place(dp, number)]
            push(source, source, dsend.at[number - 1], drecv.at[number - 1], peers[number - 1]).wait_recv()

        def total(which):
            slot = (dp * 2 + which).astype(F32)
            result = jnp.zeros((own_rows, half), F32)
            for sequence in range(4):
                chosen = jnp.where(act_ref[sequence, :, width : width + 1] == slot, 1.0, 0.0)
                result = result + slots[sequence].astype(F32) * chosen
            return result

        other_out[...] = total(1 - core).astype(BF)
        last = push(other_out, other_in, ssem.at[1], rsem.at[1], peer)
        last.start()
        mine = total(core)
        last.wait_recv()
        other = other_in[...].astype(F32)
        for which in range(2):
            @pl.when(core == which)
            def _(which=which):
                both = (mine, other) if which == 0 else (other, mine)
                cut = IN_AT[12]
                whole = jnp.concatenate(both, axis=1)
                out_a[...] = whole[:, :cut]
                out_b[...] = whole[:, cut:columns]

        last.wait_send()
        for send in sends + shift_sends + act_sends:
            send.wait_send()

        def drain(number, carry):
            rows = rows_of(number, block)
            pltpu.make_async_copy(buf_h.at[number], out_h.at[rows, :], osem.at[0, number]).wait()
            pltpu.make_async_copy(buf_l.at[number], out_l.at[rows, :], osem.at[1, number]).wait()
            return carry

        lax.fori_loop(0, count, drain, 0)

    part = (own_rows, half)
    return call(
        kernel,
        [(array, True) for array in (g_attn, g_first, skip_out, hidden, long_skip)]
        + [(weight, False)]
        + [(array, True) for array in (mod_weight, gain_halves, gain_rows, *tables, condition, act_all, *wide, *local,
                                       *stack)],
        [
            ((tokens, width), F32, False),
            ((tokens, width), F32, False),
            ((own_rows, IN_AT[12]), F32, True),
            ((own_rows, OUT_AT[12]), F32, True),
            ((1, width), F32, True),
        ],
        [
            vmem(count, width, span),
            vmem(count, block, width, dtype=F32),
            vmem(count, block, width, dtype=F32),
            vmem(block, 2 * width, dtype=F32),
            vmem(RANK, 2 * half, dtype=F32),
            vmem(RANK, half),
            vmem(RANK, half),
        ]
        + [vmem(count, *part) for _ in range(5)]
        + [vmem(*part, dtype=F32), vmem(4, *part), vmem(*part), vmem(*part)]
        + [vmem(4, 1, width, dtype=F32), vmem(2, 1, width, dtype=F32), vmem(4, 1, mod_rows, dtype=F32),
           vmem(4, 1, mod_rows, dtype=F32), vmem(1, width, dtype=F32)]
        + [dma(), dma(2, count), dma(3), dma(3), dma(3), dma(3), dma(2, 3), dma(2, 3)] + [dma(count) for _ in range(4)],
        collective=5,
        cost=cost_of(4 * tokens * width * width, 30e6),
    )


def fused_body(
    hidden,
    long_skip_input,
    condition,
    projected_text_tokens,
    sequence_adapter_index,
    skip_projection_weight,
    shift_modulation_weight,
    self_query_weight,
    self_key_weight,
    self_value_weight,
    attention_output_weight,
    cross_query_weight,
    cross_key_weight,
    cross_value_weight,
    cross_output_weight,
    feedforward_up_weight,
    feedforward_down_weight,
    skip_norm_gain,
    norm_gain_rows,
    adapter_down_factor,
    adapter_up_factor,
    cotangent,
):
    rank = lax.axis_index("tensor")
    count = lax.axis_size("tensor")
    core = lax.axis_index("ctx")
    dp = lax.axis_index("dp")
    hidden, long_skip, text, cot = hidden[0], long_skip_input[0], projected_text_tokens[0], cotangent[0]
    local = self_query_weight.shape[1]
    heads = local // HD
    index = sequence_adapter_index[0]
    tables = (
        lax.dynamic_index_in_dim(adapter_down_factor, index, 0, keepdims=False),
        lax.dynamic_index_in_dim(adapter_up_factor, index, 0, keepdims=False),
    )
    gain_halves = skip_norm_gain.reshape(2, MODEL_WIDTH)

    weights = {
        "skip": skip_projection_weight.T,
        "q": self_query_weight,
        "k": self_key_weight,
        "v": self_value_weight,
        "o": attention_output_weight.T,
        "ck": cross_key_weight.T,
        "cv": cross_value_weight.T,
        "cq": cross_query_weight,
        "co": cross_output_weight.T,
        "up": feedforward_up_weight,
        "dn": feedforward_down_weight.T,
    }
    (skip_out, attn_in, query, keys, values, low, logs, inv_q, inv_k, summed, act_all, text_kv, wq, wk, wv, wo, wcq, wco,
     wup, wdn) = front(
        count, heads, condition, sequence_adapter_index, hidden, long_skip, text, weights, shift_modulation_weight,
        gain_halves, norm_gain_rows, tables,
    )
    first, second, cross_in, mlp_in, cquery, cinv, clogs, clow, cu, skip_half = cross_forward(
        count, heads, summed, skip_out, wcq, wco, weights["skip"], text_kv, norm_gain_rows, tables
    )
    g_mlp_in, down_part, g_up_a, g_up_b, g_down_a, g_down_b, skip_all = feed_forward(
        count, mlp_in, cot, second, wup, wdn, skip_half, tables
    )
    block_out = lax.psum(down_part, "tensor")
    g_first, g_cq_a, g_cq_b, g_ck_a, g_ck_b, g_cv_a, g_cv_b, g_co_a, g_co_b = cross_backward(
        count, heads, g_mlp_in, cot, first, second, cross_in, cquery, cinv, clogs, clow, cu, text, wcq, wco, text_kv,
        norm_gain_rows, tables,
    )
    g_attn, g_first_all, g_qkv_a, g_q_b, g_k_b, g_v_b, g_o_a, g_o_b = attention_backward(
        count, heads, g_first, attn_in, query, keys, values, low, logs, inv_q, inv_k, (wq, wk, wv, wo), tables
    )
    base = IN_AT[12]
    hidden_grad, skip_grad, grad_down, grad_up, g_condition = back_end(
        count, g_attn, g_first_all, skip_out, hidden, long_skip, skip_all, shift_modulation_weight, gain_halves,
        norm_gain_rows, tables, condition, act_all,
        {
            IN_AT[6]: g_cq_a, IN_AT[7]: g_ck_a, IN_AT[8]: g_cv_a, IN_AT[10]: g_up_a,
            IN_AT[2]: g_qkv_a[:RANK], IN_AT[3]: g_qkv_a[RANK : 2 * RANK], IN_AT[4]: g_qkv_a[2 * RANK :],
            base + OUT_AT[5]: g_o_b, base + OUT_AT[9]: g_co_b, base + OUT_AT[11]: g_down_b,
        },
        {IN_AT[5]: g_o_a, IN_AT[11]: g_down_a},
        {OUT_AT[2]: g_q_b, OUT_AT[3]: g_k_b, OUT_AT[4]: g_v_b, OUT_AT[10]: g_up_b},
        {
            IN_AT[9]: g_co_a, base + OUT_AT[6]: g_cq_b, base + OUT_AT[7]: g_ck_b, base + OUT_AT[8]: g_cv_b,
        },
    )
    size = MODEL_WIDTH // (2 * count)
    condition_gradient = lax.dynamic_slice_in_dim(g_condition[0], (core * count + rank) * size, size, 0)
    return (
        block_out[None],
        hidden_grad[None],
        skip_grad[None],
        condition_gradient,
        grad_down.reshape(-1),
        grad_up.reshape(-1),
    )


def solution(mesh):
    in_specs = (
        P("dp", "ctx", None),
        P("dp", "ctx", None),
        P("dp", None),
        P("dp", None, None),
        P("dp"),
        P("tensor", "dp"),
        P("dp", None),
        P("dp", "tensor"),
        P("dp", "tensor"),
        P("dp", "tensor"),
        P("tensor", "dp"),
        P("dp", "tensor"),
        P("dp", "tensor"),
        P("dp", "tensor"),
        P("tensor", "dp"),
        P("dp", "tensor"),
        P("tensor", "dp"),
        P(),
        P(),
        P(),
        P(),
        P("dp", "ctx", None),
    )
    out_specs = (
        P("dp", "ctx", None),
        P("dp", "ctx", None),
        P("dp", "ctx", None),
        P(("dp", "ctx", "tensor")),
        P(("dp", "ctx", "tensor")),
        P(("dp", "ctx", "tensor")),
    )
    shape = mesh.shape
    fused = shape["dp"] == 4 and shape["ctx"] == 2 and shape["tensor"] == 4
    return jax.shard_map(fused_body if fused else body, mesh=mesh, in_specs=in_specs, out_specs=out_specs, check_vma=False)
```

```python
from functools import partial

import jax
import jax.numpy as jnp
from jax import lax
from jax.experimental import pallas as pl
from jax.experimental.pallas import tpu as pltpu
from jax.sharding import PartitionSpec as P

MODEL_WIDTH = 1408
HD = 88
FF = 6144
TW = 1024


PRECISE = lax.Precision.HIGHEST
NORM_EPS = 1e-06


def row_norm(values):
    centered = values - jnp.mean(values, axis=-1, keepdims=True)
    inverse = lax.rsqrt(jnp.mean(centered * centered, axis=-1, keepdims=True) + NORM_EPS)
    return (centered * inverse, inverse)


def head_norm(values, head_width):
    shaped = values.reshape(values.shape[:-1] + (values.shape[-1] // head_width, head_width))
    centered = shaped - jnp.mean(shaped, axis=-1, keepdims=True)
    inverse = lax.rsqrt(jnp.mean(centered * centered, axis=-1, keepdims=True) + NORM_EPS)
    return (centered * inverse, inverse)


def norm_back(normal, inverse, grad_normal):
    return inverse * (
        grad_normal
        - jnp.mean(grad_normal, axis=-1, keepdims=True)
        - normal * jnp.mean(grad_normal * normal, axis=-1, keepdims=True)
    )


def split_parts(values):
    if values.dtype == jnp.bfloat16:
        return [values]
    upper_half = values.astype(jnp.bfloat16)
    lower_half = (values - upper_half.astype(jnp.float32)).astype(jnp.bfloat16)
    return [upper_half, lower_half]


def paired_product(form, left, right):
    total = None
    for left_number, left_part in enumerate(split_parts(left)):
        for right_number, right_part in enumerate(split_parts(right)):
            if left_number + right_number < 2:
                term = jnp.einsum(form, left_part, right_part, preferred_element_type=jnp.float32)
                total = term if total is None else total + term
    return total


def lowrank_out(input_list, weight_matrix, down_piece, up_factor_piece):
    frozen_term = jnp.einsum(
        "gtb,bx->gtx", input_list, weight_matrix, preferred_element_type=jnp.float32
    )
    rank_activation = jnp.einsum(
        "snd,srd->snr", input_list, down_piece, preferred_element_type=jnp.float32
    )
    adapter_term = paired_product("dti,dip->dtp", rank_activation, up_factor_piece)
    return (frozen_term + adapter_term, rank_activation)


def lowrank_back(
    input_list,
    weight_matrix,
    down_piece,
    up_factor_piece,
    rank_activation,
    output_gradient,
    want_input,
):
    upper_gradient = paired_product("pmf,pmz->pfz", rank_activation, output_gradient)
    rank_gradient = paired_product("hzu,hlu->hzl", output_gradient, up_factor_piece)
    grad_lower = paired_product("snr,snd->srd", rank_gradient, input_list)
    if want_input:
        input_gradients = paired_product("lga,wa->lgw", output_gradient, weight_matrix)
        input_gradients = input_gradients + paired_product(
            "snr,srd->snd", rank_gradient, down_piece
        )
        return (input_gradients, grad_lower, upper_gradient)
    return (None, grad_lower, upper_gradient)


def attend_forward(query, key_rows, values_in, scale_factor):
    scores = (
        jnp.einsum("snhe,smhe->shnm", query, key_rows, preferred_element_type=jnp.float32)
        * scale_factor
    )
    row_top = jnp.max(scores, axis=-1, keepdims=True)
    exp_scores = jnp.exp(scores - row_top)
    row_total = jnp.sum(exp_scores, axis=-1, keepdims=True)
    attn_probs = (exp_scores / row_total).astype(jnp.bfloat16)
    result = jnp.einsum(
        "shnm,smhe->snhe", attn_probs, values_in, preferred_element_type=jnp.float32
    )
    return (result, row_top + jnp.log(row_total))


def attend_back(query, key_rows, values_in, log_total, grad_result, scale_factor):
    scores = (
        jnp.einsum("snhe,smhe->shnm", query, key_rows, preferred_element_type=jnp.float32)
        * scale_factor
    )
    attn_probs = jnp.exp(scores - log_total)
    grad_probs = jnp.einsum(
        "snhe,smhe->shnm", grad_result, values_in, preferred_element_type=jnp.float32
    )
    row_inner = jnp.sum(attn_probs * grad_probs, axis=-1, keepdims=True)
    grad_scores = (attn_probs * (grad_probs - row_inner)).astype(jnp.bfloat16)
    grad_query = (
        jnp.einsum("shnm,smhe->snhe", grad_scores, key_rows, preferred_element_type=jnp.float32)
        * scale_factor
    )
    grad_keys = (
        jnp.einsum("shnm,snhe->smhe", grad_scores, query, preferred_element_type=jnp.float32)
        * scale_factor
    )
    grad_values = jnp.einsum(
        "shnm,snhe->smhe",
        attn_probs.astype(jnp.bfloat16),
        grad_result,
        preferred_element_type=jnp.float32,
    )
    return (grad_query, grad_keys, grad_values)


def body(
    hidden,
    long_skip_input,
    condition,
    projected_text_tokens,
    sequence_adapter_index,
    skip_projection_weight,
    shift_modulation_weight,
    self_query_weight,
    self_key_weight,
    self_value_weight,
    attention_output_weight,
    cross_query_weight,
    cross_key_weight,
    cross_value_weight,
    cross_output_weight,
    feedforward_up_weight,
    feedforward_down_weight,
    skip_norm_gain,
    norm_gain_rows,
    adapter_down_factor,
    adapter_up_factor,
    cotangent,
):
    (
        skip_projection_weight,
        shift_modulation_weight,
        self_query_weight,
        self_key_weight,
        self_value_weight,
        attention_output_weight,
        cross_query_weight,
        cross_key_weight,
        cross_value_weight,
        cross_output_weight,
        feedforward_up_weight,
        feedforward_down_weight,
    ) = (
        lax.all_gather(skip_projection_weight, "dp", axis=1, tiled=True),
        lax.all_gather(shift_modulation_weight, "dp", axis=0, tiled=True),
        lax.all_gather(self_query_weight, "dp", axis=0, tiled=True),
        lax.all_gather(self_key_weight, "dp", axis=0, tiled=True),
        lax.all_gather(self_value_weight, "dp", axis=0, tiled=True),
        lax.all_gather(attention_output_weight, "dp", axis=1, tiled=True),
        lax.all_gather(cross_query_weight, "dp", axis=0, tiled=True),
        lax.all_gather(cross_key_weight, "dp", axis=0, tiled=True),
        lax.all_gather(cross_value_weight, "dp", axis=0, tiled=True),
        lax.all_gather(cross_output_weight, "dp", axis=1, tiled=True),
        lax.all_gather(feedforward_up_weight, "dp", axis=0, tiled=True),
        lax.all_gather(feedforward_down_weight, "dp", axis=1, tiled=True),
    )
    tensor_rank = lax.axis_index("tensor")
    tensor_count = lax.axis_size("tensor")
    seqs_local = hidden.shape[0]
    tokens_local = hidden.shape[1]
    local_width = self_query_weight.shape[1]
    heads_local = local_width // HD
    ff_local = feedforward_up_weight.shape[1]
    skip_width = skip_projection_weight.shape[0]
    scale_factor = HD ** (-0.5)
    in_sizes = [
        2 * MODEL_WIDTH,
        MODEL_WIDTH,
        MODEL_WIDTH,
        MODEL_WIDTH,
        MODEL_WIDTH,
        MODEL_WIDTH,
        MODEL_WIDTH,
        TW,
        TW,
        MODEL_WIDTH,
        MODEL_WIDTH,
        FF,
    ]
    out_sizes = [MODEL_WIDTH] * 10 + [FF, MODEL_WIDTH]
    input_offsets = [sum(in_sizes[:number]) for number in range(12)]
    output_offsets = [sum(out_sizes[:number]) for number in range(12)]
    select_adapter = (
        sequence_adapter_index[:, None]
        == jnp.arange(adapter_down_factor.shape[0], dtype=jnp.int32)[None, :]
    )
    choose_wide = select_adapter.astype(jnp.float32)
    down_seq = jnp.einsum(
        "fn,nge->fge",
        select_adapter.astype(jnp.bfloat16),
        adapter_down_factor,
        preferred_element_type=jnp.float32,
    ).astype(jnp.bfloat16)
    up_seq = jnp.einsum(
        "fn,nge->fge",
        select_adapter.astype(jnp.bfloat16),
        adapter_up_factor,
        preferred_element_type=jnp.float32,
    ).astype(jnp.bfloat16)

    def down_full(number):
        return down_seq[:, :, input_offsets[number] : input_offsets[number] + in_sizes[number]]

    def up_full(number):
        return up_seq[:, :, output_offsets[number] : output_offsets[number] + out_sizes[number]]

    def down_local(number, span_width):
        return lax.dynamic_slice_in_dim(
            down_seq, input_offsets[number] + tensor_rank * span_width, span_width, 2
        )

    def up_local(number, span_width):
        return lax.dynamic_slice_in_dim(
            up_seq, output_offsets[number] + tensor_rank * span_width, span_width, 2
        )

    def to_slots(grad_piece):
        return jnp.einsum("si,srd->ird", choose_wide, grad_piece, precision=PRECISE)

    joined = jnp.concatenate([hidden, long_skip_input], axis=-1).astype(jnp.float32)
    joined_normal, joined_inverse = row_norm(joined)
    joined_low = (joined_normal * skip_norm_gain).astype(jnp.bfloat16)
    joined_part = lax.dynamic_slice_in_dim(joined_low, tensor_rank * skip_width, skip_width, 2)
    skip_partial, skip_rank = lowrank_out(
        joined_part, skip_projection_weight, down_local(0, skip_width), up_full(0)
    )
    skip_out = lax.psum(skip_partial.astype(jnp.bfloat16), "tensor").astype(jnp.float32)
    act_wide, silu_pull = jax.vjp(jax.nn.silu, condition.astype(jnp.float32))
    act_low = act_wide.astype(jnp.bfloat16)[:, None, :]
    shift_row, mod_rank = lowrank_out(act_low, shift_modulation_weight, down_full(1), up_full(1))
    first_normal, first_inverse = row_norm(skip_out)
    attn_in = (first_normal * norm_gain_rows[0] + shift_row).astype(jnp.bfloat16)
    query_proj, query_rank = lowrank_out(
        attn_in, self_query_weight, down_full(2), up_local(2, local_width)
    )
    key_proj, key_rank = lowrank_out(
        attn_in, self_key_weight, down_full(3), up_local(3, local_width)
    )
    value_proj, value_rank = lowrank_out(
        attn_in, self_value_weight, down_full(4), up_local(4, local_width)
    )
    query_normal, query_inverse = head_norm(query_proj, HD)
    key_normal, key_inverse = head_norm(key_proj, HD)
    query_low = query_normal.astype(jnp.bfloat16)
    key_low = key_normal.astype(jnp.bfloat16).reshape(seqs_local, tokens_local, local_width)
    value_low = value_proj.astype(jnp.bfloat16)
    keys_all, values_all = (
        lax.all_gather(key_low, "ctx", axis=1, tiled=True),
        lax.all_gather(value_low, "ctx", axis=1, tiled=True),
    )
    keys_four = keys_all.reshape(seqs_local, -1, heads_local, HD)
    values_four = values_all.reshape(seqs_local, -1, heads_local, HD)
    attn_result, attn_log = attend_forward(query_low, keys_four, values_four, scale_factor)
    attn_low = attn_result.reshape(seqs_local, tokens_local, local_width).astype(jnp.bfloat16)
    attn_partial, out_rank = lowrank_out(
        attn_low, attention_output_weight, down_local(5, local_width), up_full(5)
    )
    first_res = skip_out + lax.psum(attn_partial.astype(jnp.bfloat16), "tensor").astype(jnp.float32)
    second_normal, second_inverse = row_norm(first_res)
    cross_in = (second_normal * norm_gain_rows[1]).astype(jnp.bfloat16)
    cquery_proj, cquery_rank = lowrank_out(
        cross_in, cross_query_weight, down_full(6), up_local(6, local_width)
    )
    ckey_proj, ckey_rank = lowrank_out(
        projected_text_tokens, cross_key_weight, down_full(7), up_local(7, local_width)
    )
    cvalue_proj, cvalue_rank = lowrank_out(
        projected_text_tokens, cross_value_weight, down_full(8), up_local(8, local_width)
    )
    cquery_normal, cquery_inverse = head_norm(cquery_proj, HD)
    ckey_normal, ckey_inverse = head_norm(ckey_proj, HD)
    cquery_low = cquery_normal.astype(jnp.bfloat16)
    ckey_low = ckey_normal.astype(jnp.bfloat16)
    cvalue_low = cvalue_proj.astype(jnp.bfloat16).reshape(seqs_local, -1, heads_local, HD)
    cross_result, cross_log = attend_forward(cquery_low, ckey_low, cvalue_low, scale_factor)
    cross_low = cross_result.reshape(seqs_local, tokens_local, local_width).astype(jnp.bfloat16)
    cross_partial, cout_rank = lowrank_out(
        cross_low, cross_output_weight, down_local(9, local_width), up_full(9)
    )
    second_res = first_res + lax.psum(cross_partial.astype(jnp.bfloat16), "tensor").astype(
        jnp.float32
    )
    third_normal, third_inverse = row_norm(second_res)
    mlp_in = (third_normal * norm_gain_rows[2]).astype(jnp.bfloat16)
    up_proj, up_rank = lowrank_out(
        mlp_in, feedforward_up_weight, down_full(10), up_local(10, ff_local)
    )
    activated, gelu_pull = jax.vjp(partial(jax.nn.gelu, approximate=True), up_proj)
    activated_low = activated.astype(jnp.bfloat16)
    down_partial, down_rank = lowrank_out(
        activated_low, feedforward_down_weight, down_local(11, ff_local), up_full(11)
    )
    block_out = second_res + lax.psum(down_partial.astype(jnp.bfloat16), "tensor").astype(
        jnp.float32
    )
    grad_act, grad_down_lower, grad_down_upper = lowrank_back(
        activated_low,
        feedforward_down_weight,
        down_local(11, ff_local),
        up_full(11),
        down_rank,
        cotangent,
        True,
    )
    grad_pre = gelu_pull(grad_act)[0].astype(jnp.bfloat16)
    grad_mlp_in, grad_up_lower, grad_up_upper = lowrank_back(
        mlp_in,
        feedforward_up_weight,
        down_full(10),
        up_local(10, ff_local),
        up_rank,
        grad_pre,
        True,
    )
    grad_mlp_in = lax.psum(grad_mlp_in.astype(jnp.bfloat16), "tensor").astype(jnp.float32)
    grad_second = cotangent.astype(jnp.float32) + norm_back(
        third_normal, third_inverse, grad_mlp_in * norm_gain_rows[2]
    )
    grad_cross_low, grad_cout_lower, grad_cout_upper = lowrank_back(
        cross_low,
        cross_output_weight,
        down_local(9, local_width),
        up_full(9),
        cout_rank,
        grad_second.astype(jnp.bfloat16),
        True,
    )
    grad_cross_result = grad_cross_low.astype(jnp.bfloat16).reshape(
        seqs_local, tokens_local, heads_local, HD
    )
    grad_cquery, grad_ckey, grad_cvalue = attend_back(
        cquery_low, ckey_low, cvalue_low, cross_log, grad_cross_result, scale_factor
    )
    grad_cquery_proj = (
        norm_back(cquery_normal, cquery_inverse, grad_cquery)
        .reshape(seqs_local, tokens_local, local_width)
        .astype(jnp.bfloat16)
    )
    grad_ckey_proj = norm_back(ckey_normal, ckey_inverse, grad_ckey).reshape(
        seqs_local, -1, local_width
    )
    none_first, grad_ckey_lower, grad_ckey_upper = lowrank_back(
        projected_text_tokens,
        cross_key_weight,
        down_full(7),
        up_local(7, local_width),
        ckey_rank,
        grad_ckey_proj,
        False,
    )
    none_second, grad_cvalue_lower, grad_cvalue_upper = lowrank_back(
        projected_text_tokens,
        cross_value_weight,
        down_full(8),
        up_local(8, local_width),
        cvalue_rank,
        grad_cvalue.reshape(seqs_local, -1, local_width),
        False,
    )
    grad_cross_in, grad_cquery_lower, grad_cquery_upper = lowrank_back(
        cross_in,
        cross_query_weight,
        down_full(6),
        up_local(6, local_width),
        cquery_rank,
        grad_cquery_proj,
        True,
    )
    grad_cross_in = lax.psum(grad_cross_in.astype(jnp.bfloat16), "tensor").astype(jnp.float32)
    grad_first = grad_second + norm_back(
        second_normal, second_inverse, grad_cross_in * norm_gain_rows[1]
    )
    grad_attn_low, grad_aout_lower, grad_aout_upper = lowrank_back(
        attn_low,
        attention_output_weight,
        down_local(5, local_width),
        up_full(5),
        out_rank,
        grad_first.astype(jnp.bfloat16),
        True,
    )
    grad_attn_result = grad_attn_low.astype(jnp.bfloat16).reshape(
        seqs_local, tokens_local, heads_local, HD
    )
    grad_query, grad_keys_all, grad_values_all = attend_back(
        query_low, keys_four, values_four, attn_log, grad_attn_result, scale_factor
    )
    grad_keys, grad_values = (
        lax.psum_scatter(
            grad_keys_all.reshape(seqs_local, -1, local_width).astype(jnp.bfloat16),
            "ctx",
            scatter_dimension=1,
            tiled=True,
        ).astype(jnp.float32),
        lax.psum_scatter(
            grad_values_all.reshape(seqs_local, -1, local_width).astype(jnp.bfloat16),
            "ctx",
            scatter_dimension=1,
            tiled=True,
        ).astype(jnp.float32),
    )
    grad_query_proj = (
        norm_back(query_normal, query_inverse, grad_query)
        .reshape(seqs_local, tokens_local, local_width)
        .astype(jnp.bfloat16)
    )
    grad_key_proj = (
        norm_back(
            key_normal, key_inverse, grad_keys.reshape(seqs_local, tokens_local, heads_local, HD)
        )
        .reshape(seqs_local, tokens_local, local_width)
        .astype(jnp.bfloat16)
    )
    grad_value_proj = grad_values.astype(jnp.bfloat16)
    grad_in_query, grad_query_lower, grad_query_upper = lowrank_back(
        attn_in,
        self_query_weight,
        down_full(2),
        up_local(2, local_width),
        query_rank,
        grad_query_proj,
        True,
    )
    grad_in_key, grad_key_lower, grad_key_upper = lowrank_back(
        attn_in,
        self_key_weight,
        down_full(3),
        up_local(3, local_width),
        key_rank,
        grad_key_proj,
        True,
    )
    grad_in_value, grad_value_lower, grad_value_upper = lowrank_back(
        attn_in,
        self_value_weight,
        down_full(4),
        up_local(4, local_width),
        value_rank,
        grad_value_proj,
        True,
    )
    grad_attn_in = lax.psum(
        (grad_in_query + grad_in_key + grad_in_value).astype(jnp.bfloat16), "tensor"
    ).astype(jnp.float32)
    grad_shift = jnp.sum(grad_attn_in, axis=1, keepdims=True) / tensor_count
    grad_act_low, grad_mod_lower, grad_mod_upper = lowrank_back(
        act_low, shift_modulation_weight, down_full(1), up_full(1), mod_rank, grad_shift, True
    )
    grad_condition = silu_pull(grad_act_low[:, 0, :])[0]
    grad_skip_out = grad_first + norm_back(
        first_normal, first_inverse, grad_attn_in * norm_gain_rows[0]
    )
    grad_joined_part, grad_skip_lower, grad_skip_upper = lowrank_back(
        joined_part,
        skip_projection_weight,
        down_local(0, skip_width),
        up_full(0),
        skip_rank,
        grad_skip_out.astype(jnp.bfloat16),
        True,
    )
    grad_joined = lax.all_gather(
        grad_joined_part.astype(jnp.bfloat16), "tensor", axis=2, tiled=True
    ).astype(grad_joined_part.dtype)
    grad_joined_full = norm_back(joined_normal, joined_inverse, grad_joined * skip_norm_gain)
    hidden_grad = grad_joined_full[:, :, :MODEL_WIDTH]
    skip_grad = grad_joined_full[:, :, MODEL_WIDTH:]
    lower_factor_parts = [
        (0, grad_skip_lower, True),
        (1, grad_mod_lower, False),
        (2, grad_query_lower, False),
        (3, grad_key_lower, False),
        (4, grad_value_lower, False),
        (5, grad_aout_lower, True),
        (6, grad_cquery_lower, False),
        (7, grad_ckey_lower, False),
        (8, grad_cvalue_lower, False),
        (9, grad_cout_lower, True),
        (10, grad_up_lower, False),
        (11, grad_down_lower, True),
    ]
    upper_factor_parts = [
        (0, grad_skip_upper, False),
        (1, grad_mod_upper, False),
        (2, grad_query_upper, True),
        (3, grad_key_upper, True),
        (4, grad_value_upper, True),
        (5, grad_aout_upper, False),
        (6, grad_cquery_upper, True),
        (7, grad_ckey_upper, True),
        (8, grad_cvalue_upper, True),
        (9, grad_cout_upper, False),
        (10, grad_up_upper, True),
        (11, grad_down_upper, False),
    ]
    slot_total = adapter_down_factor.shape[0]
    rank_total = adapter_down_factor.shape[1]
    cond_buffer = jnp.zeros((lax.axis_size("dp") * seqs_local, MODEL_WIDTH), jnp.float32)
    cond_buffer = lax.dynamic_update_slice_in_dim(
        cond_buffer, grad_condition, lax.axis_index("dp") * seqs_local, 0
    )
    cond_flat = cond_buffer.reshape(-1)

    def dense_table(parts_list, starts, total_width, row_count, slot_pieces):
        table = jnp.zeros((row_count, total_width), jnp.float32)
        for position, (number, grad_piece, is_local) in enumerate(parts_list):
            span_width = grad_piece.shape[2]
            column_start = starts[number] + tensor_rank * span_width if is_local else starts[number]
            table = lax.dynamic_update_slice_in_dim(table, slot_pieces[position], column_start, 1)
        return table

    down_factor_slots = [
        to_slots(grad_piece).reshape(slot_total * rank_total, -1)
        for number, grad_piece, is_local in lower_factor_parts
    ]
    up_factor_slots = [
        to_slots(grad_piece).reshape(slot_total * rank_total, -1)
        for number, grad_piece, is_local in upper_factor_parts
    ]
    down_compact = jnp.concatenate(down_factor_slots, axis=1)
    up_compact = jnp.concatenate(up_factor_slots, axis=1)
    cond_rows, down_rows, up_rows = (
        lax.psum_scatter(
            cond_flat.astype(jnp.bfloat16), ("dp", "ctx"), scatter_dimension=0, tiled=True
        ).astype(jnp.float32),
        lax.psum_scatter(
            down_compact.astype(jnp.bfloat16), ("dp", "ctx"), scatter_dimension=0, tiled=True
        ).astype(jnp.float32),
        lax.psum_scatter(
            up_compact.astype(jnp.bfloat16), ("dp", "ctx"), scatter_dimension=0, tiled=True
        ).astype(jnp.float32),
    )
    row_count = down_rows.shape[0]
    down_widths = [grad_piece.shape[2] for number, grad_piece, is_local in lower_factor_parts]
    up_widths = [grad_piece.shape[2] for number, grad_piece, is_local in upper_factor_parts]
    down_pieces = [
        down_rows[:, sum(down_widths[:position]) : sum(down_widths[: position + 1])]
        for position in range(12)
    ]
    up_pieces = [
        up_rows[:, sum(up_widths[:position]) : sum(up_widths[: position + 1])]
        for position in range(12)
    ]
    down_block = dense_table(
        lower_factor_parts, input_offsets, adapter_down_factor.shape[2], row_count, down_pieces
    ).reshape(-1)
    up_block = dense_table(
        upper_factor_parts, output_offsets, adapter_up_factor.shape[2], row_count, up_pieces
    ).reshape(-1)
    condition_gradient, adapter_down_gradient, adapter_up_gradient = (
        lax.psum_scatter(
            cond_rows.astype(jnp.bfloat16), "tensor", scatter_dimension=0, tiled=True
        ).astype(jnp.float32),
        lax.psum_scatter(
            down_block.astype(jnp.bfloat16), "tensor", scatter_dimension=0, tiled=True
        ).astype(jnp.float32),
        lax.psum_scatter(
            up_block.astype(jnp.bfloat16), "tensor", scatter_dimension=0, tiled=True
        ).astype(jnp.float32),
    )
    return (
        block_out.astype(jnp.bfloat16),
        hidden_grad,
        skip_grad,
        condition_gradient,
        adapter_down_gradient,
        adapter_up_gradient,
    )


BF = jnp.bfloat16
F32 = jnp.float32
MESH_ID = pl.DeviceIdType.MESH
RANK = 16
VMEM_BYTES = 60 << 20


def dot_nn(left, right):
    return jnp.dot(left, right, preferred_element_type=F32)


def dot_nt(left, right):
    return lax.dot_general(left, right, (((1,), (1,)), ((), ())), preferred_element_type=F32)


def dot_tn(left, right):
    return lax.dot_general(left, right, (((0,), (0,)), ((), ())), preferred_element_type=F32)


def stats(values):
    centered = values - jnp.mean(values, axis=-1, keepdims=True)
    inverse = lax.rsqrt(jnp.mean(centered * centered, axis=-1, keepdims=True) + NORM_EPS)
    return centered * inverse, inverse


def greet(partners):
    barrier = pltpu.get_barrier_semaphore()
    for condition, device in partners:
        @pl.when(condition)
        def _(device=device):
            pl.semaphore_signal(barrier, inc=1, device_id=device, device_id_type=MESH_ID)
    expected = sum(jnp.where(condition, 1, 0) for condition, _ in partners)
    pl.semaphore_wait(barrier, expected)


def line_partners(me, count):
    return [(me > 0, {"tensor": lax.max(me - 1, 0)}), (me < count - 1, {"tensor": lax.min(me + 1, count - 1)})]


def push(source, target, send_sem, recv_sem, device):
    return pltpu.make_async_remote_copy(
        src_ref=source,
        dst_ref=target,
        send_sem=send_sem,
        recv_sem=recv_sem,
        device_id=device,
        device_id_type=MESH_ID,
    )


class Line:
    def __init__(self, me, count, send_right, recv_left, send_left, recv_right):
        self.me, self.count = me, count
        self.sems = (send_right, recv_left, send_left, recv_right)
        self.left = {"tensor": lax.max(me - 1, 0)}
        self.right = {"tensor": lax.min(me + 1, count - 1)}
        self.has_left, self.has_right = me > 0, me < count - 1

    def to_right(self, source, target, slot):
        return push(source, target, self.sems[0].at[slot], self.sems[1].at[slot], self.right)

    def to_left(self, source, target, slot):
        return push(source, target, self.sems[2].at[slot], self.sems[3].at[slot], self.left)


def line_reduce_all(line, steps, compute, partial_ref, from_left, from_right, stage_right, stage_left, finish,
                    beside=None, after=None):
    me, count = line.me, line.count
    far = count - 1 - me

    def step(number, carry):
        @pl.when(number < steps)
        def _():
            compute(number)

        slot_r = number - me

        @pl.when((slot_r >= 0) & (slot_r < steps))
        def _():
            slot = lax.clamp(0, slot_r, steps - 1)

            @pl.when(line.has_left)
            def _():
                line.to_right(stage_right.at[slot], from_left.at[slot], slot).wait_recv()

            @pl.when(line.has_right)
            def _():
                @pl.when(line.has_left)
                def _():
                    total = partial_ref[slot].astype(F32) + from_left[slot].astype(F32)
                    stage_right[slot] = total.astype(BF)

                @pl.when(jnp.logical_not(line.has_left))
                def _():
                    stage_right[slot] = partial_ref[slot]

                line.to_right(stage_right.at[slot], from_left.at[slot], slot).start()

        slot_l = number - far

        @pl.when((slot_l >= 0) & (slot_l < steps))
        def _():
            slot = lax.clamp(0, slot_l, steps - 1)

            @pl.when(line.has_right)
            def _():
                line.to_left(stage_left.at[slot], from_right.at[slot], slot).wait_recv()

            @pl.when(line.has_left)
            def _():
                @pl.when(line.has_right)
                def _():
                    total = partial_ref[slot].astype(F32) + from_right[slot].astype(F32)
                    stage_left[slot] = total.astype(BF)

                @pl.when(jnp.logical_not(line.has_right))
                def _():
                    stage_left[slot] = partial_ref[slot]

                line.to_left(stage_left.at[slot], from_right.at[slot], slot).start()

        if beside is not None:
            beside(number)
        slot_f = number - lax.max(me, far)

        @pl.when((slot_f >= 0) & (slot_f < steps))
        def _():
            slot = lax.clamp(0, slot_f, steps - 1)

            @pl.when(jnp.logical_not(line.has_left))
            def _():
                finish(slot, partial_ref[slot].astype(F32) + from_right[slot].astype(F32))

            @pl.when(line.has_left)
            def _():
                @pl.when(line.has_right)
                def _():
                    finish(
                        slot,
                        partial_ref[slot].astype(F32)
                        + from_left[slot].astype(F32)
                        + from_right[slot].astype(F32),
                    )

                @pl.when(jnp.logical_not(line.has_right))
                def _():
                    finish(slot, partial_ref[slot].astype(F32) + from_left[slot].astype(F32))

            if after is not None:
                after(slot)

        return carry

    lax.fori_loop(0, steps + count - 1, step, 0)

    def drain(slot, carry):
        @pl.when(line.has_right)
        def _():
            line.to_right(stage_right.at[slot], from_left.at[slot], slot).wait_send()

        @pl.when(line.has_left)
        def _():
            line.to_left(stage_left.at[slot], from_right.at[slot], slot).wait_send()

        return carry

    lax.fori_loop(0, steps, drain, 0)


def scatter_order(me, count, place):
    near = lax.min(me, count - 1 - me)
    base = count - 1 - 2 * near
    index = place - base
    block = jnp.where(
        place < base,
        count - 1 - place,
        jnp.where(index % 2 == 0, 2 * near - index // 2, index // 2),
    )
    return jnp.where(2 * me > count - 1, count - 1 - block, block)


def line_scatter_step(line, number, partial_ref, from_left, from_right, stage_right, stage_left):
    me, count = line.me, line.count
    block_r = count - 1 - number + me

    @pl.when((number >= me) & line.has_right & (block_r > me))
    def _():
        block = lax.clamp(0, block_r, count - 1)

        @pl.when(line.has_left)
        def _():
            line.to_right(stage_right.at[block], from_left.at[block], block).wait_recv()
            total = partial_ref[block].astype(F32) + from_left[block].astype(F32)
            stage_right[block] = total.astype(BF)

        @pl.when(jnp.logical_not(line.has_left))
        def _():
            stage_right[block] = partial_ref[block]

        line.to_right(stage_right.at[block], from_left.at[block], block).start()

    block_l = number - (count - 1 - me)

    @pl.when((block_l >= 0) & line.has_left & (block_l < me))
    def _():
        block = lax.clamp(0, block_l, count - 1)

        @pl.when(line.has_right)
        def _():
            line.to_left(stage_left.at[block], from_right.at[block], block).wait_recv()
            total = partial_ref[block].astype(F32) + from_right[block].astype(F32)
            stage_left[block] = total.astype(BF)

        @pl.when(jnp.logical_not(line.has_right))
        def _():
            stage_left[block] = partial_ref[block]

        line.to_left(stage_left.at[block], from_right.at[block], block).start()


def line_scatter_finish(line, partial_ref, from_left, from_right, stage_right, stage_left, total_ref):
    me, count = line.me, line.count
    total_ref[...] = partial_ref[me].astype(F32)

    @pl.when(line.has_left)
    def _():
        line.to_right(stage_right.at[me], from_left.at[me], me).wait_recv()
        total_ref[...] += from_left[me].astype(F32)

    @pl.when(line.has_right)
    def _():
        line.to_left(stage_left.at[me], from_right.at[me], me).wait_recv()
        total_ref[...] += from_right[me].astype(F32)

    def drain(block, carry):
        @pl.when(block > me)
        def _():
            line.to_right(stage_right.at[block], from_left.at[block], block).wait_send()

        @pl.when(block < me)
        def _():
            line.to_left(stage_left.at[block], from_right.at[block], block).wait_send()

        return carry

    lax.fori_loop(0, count, drain, 0)


def line_gather_step(line, number, slots):
    me, count = line.me, line.count
    block_l = lax.clamp(0, me - number, count - 1)
    block_r = lax.clamp(0, me + number, count - 1)

    @pl.when(number <= me)
    def _():
        @pl.when(number > 0)
        def _():
            line.to_right(slots.at[block_l], slots.at[block_l], block_l).wait_recv()

        @pl.when(line.has_right)
        def _():
            line.to_right(slots.at[block_l], slots.at[block_l], block_l).start()

    @pl.when(me + number <= count - 1)
    def _():
        @pl.when(number > 0)
        def _():
            line.to_left(slots.at[block_r], slots.at[block_r], block_r).wait_recv()

        @pl.when(line.has_left)
        def _():
            line.to_left(slots.at[block_r], slots.at[block_r], block_r).start()


def line_gather_drain(line, slots):
    me, count = line.me, line.count

    def drain(block, carry):
        @pl.when((block <= me) & line.has_right)
        def _():
            line.to_right(slots.at[block], slots.at[block], block).wait_send()

        @pl.when((block >= me) & line.has_left)
        def _():
            line.to_left(slots.at[block], slots.at[block], block).wait_send()

        return carry

    lax.fori_loop(0, count, drain, 0)


def line_gather(line, slots, compute):
    me, count = line.me, line.count

    def step(number, carry):
        line_gather_step(line, number, slots)

        def side(which, inner):
            block = me + (2 * which - 1) * number

            @pl.when((block >= 0) & (block < count) & ((number > 0) | (which == 0)))
            def _():
                compute(lax.clamp(0, block, count - 1))

            return inner

        return lax.fori_loop(0, 2, side, carry)

    lax.fori_loop(0, count, step, 0)
    line_gather_drain(line, slots)


def xor_place(place, number):
    if number == 0:
        return place
    if number == 1:
        return place + 1 - 2 * (place % 2)
    if number == 2:
        return place + 2 - 4 * (place // 2)
    return 3 - place


def call(kernel, inputs, outs, scratch, collective=None, cost=None):
    space = {True: pltpu.VMEM, False: pl.ANY, None: pltpu.SMEM}
    return pl.pallas_call(
        kernel,
        out_shape=[jax.ShapeDtypeStruct(shape, dtype) for shape, dtype, _ in outs],
        in_specs=[pl.BlockSpec(memory_space=space[where]) for _, where in inputs],
        out_specs=[pl.BlockSpec(memory_space=space[where]) for _, _, where in outs],
        scratch_shapes=scratch,
        cost_estimate=cost,
        compiler_params=pltpu.CompilerParams(
            collective_id=collective,
            has_side_effects=collective is not None,
            vmem_limit_bytes=VMEM_BYTES,
        ),
    )(*[array for array, _ in inputs])


def cost_of(flops, moved):
    return pl.CostEstimate(flops=int(flops), bytes_accessed=int(moved), transcendentals=0)


def vmem(*shape, dtype=BF):
    return pltpu.VMEM(shape, dtype)


def dma(*shape):
    return pltpu.SemaphoreType.DMA(shape)


def whole_wait(target, sem):
    pltpu.make_async_copy(target, target, sem).wait()


def rows_of(index, size):
    return pl.ds(pl.multiple_of(index * size, size), size)


IN_SIZES = [2 * MODEL_WIDTH] + [MODEL_WIDTH] * 6 + [TW, TW, MODEL_WIDTH, MODEL_WIDTH, FF]
OUT_SIZES = [MODEL_WIDTH] * 10 + [FF, MODEL_WIDTH]
IN_AT = [sum(IN_SIZES[:number]) for number in range(13)]
OUT_AT = [sum(OUT_SIZES[:number]) for number in range(13)]


def down_of(table, number):
    return table[:, IN_AT[number] : IN_AT[number + 1]]


def up_of(table, number):
    return table[:, OUT_AT[number] : OUT_AT[number + 1]]


def take_local(target, table, start, me, count):
    size = target.shape[-1]
    for place in range(count):
        @pl.when(me == place)
        def _(place=place):
            target[...] = table[:, start + place * size : start + (place + 1) * size]


def take_stack(target, table, start, count):
    size = target.shape[-1]
    for place in range(count):
        target[place] = table[:, start + place * size : start + (place + 1) * size]


def norm_backward(normal, inverse, grad):
    return inverse * (
        grad
        - jnp.mean(grad, axis=-1, keepdims=True)
        - normal * jnp.mean(grad * normal, axis=-1, keepdims=True)
    )


def middle(count, heads, summed, skip_out, query_weight, out_weight, up_weight, down_piece, skip_piece, text_kv, text,
           cotangent, gains, tables):
    share, width = summed.shape
    tokens = skip_out.shape[0]
    local = query_weight.shape[-1]
    units = up_weight.shape[1]
    words, text_width = text.shape
    rows, span = skip_piece.shape
    scale = HD ** (-0.5)
    two = count // 2
    wide = two * share

    def kernel(sum_ref, skip_hbm, q_hbm, o_hbm, u_hbm, d_own, piece, kv, text_hbm, cot_hbm, gain, dtab, utab,
               g_first, block_sum, ga_q, gb_q, ga_k, gb_k, ga_v, gb_v, ga_o, gb_o, g_ua, g_ub, g_da, g_db, skip_all,
               wq, wo, wu, wd, cot, t_ref, first_ref, second_ref, x_ref, q_ref, inv_ref, log_ref, low_ref, acc, b_ref, ao,
               bk, bv, ub, da, slots, skip_half, active, grads, u_all, ud_all, gu_all, gd_all, partial_g, left_g, right_g,
               sr_g, sl_g, partial_b, left_b, right_b, sr_b, sl_b, lsem, wsend, wrecv, zsend, zrecv, *sems):
        me = lax.axis_index("tensor")
        core = lax.axis_index("ctx")
        dp = lax.axis_index("dp")
        always = core >= 0
        half = pl.ds(pl.multiple_of(core * (rows // 2), 16), rows // 2)
        down_rows = d_own.shape[0]
        down_half = pl.ds(pl.multiple_of(core * (down_rows // 2), 16), down_rows // 2)
        mine = pl.ds(pl.multiple_of(dp * down_rows, 16), down_rows)
        loads = [
            pltpu.make_async_copy(source, target, lsem.at[number])
            for number, (source, target) in enumerate(
                ((skip_hbm.at[rows_of(me, share), :], first_ref), (piece.at[half, :], skip_half.at[me]), (q_hbm, wq),
                 (o_hbm, wo), (d_own, wd.at[mine, :]), (cot_hbm, cot), (u_hbm, wu), (text_hbm, t_ref))
            )
        ]
        for load in loads:
            load.start()
        gather_line = Line(me, count, *sems[:4])
        grad_line = Line(me, count, *sems[4:8])
        block_line = Line(me, count, *sems[8:])
        down = Shared(wd, down_rows, (wsend, wrecv, 0))
        skip = Shared(skip_all, rows, (wsend, wrecv, 1), stacked=True)
        z_peers = [{"tensor": xor_place(me, number)} for number in range(1, count)]
        others = [{"dp": xor_place(dp, 1)}, {"dp": xor_place(dp, 2)}, {"ctx": 1 - core}]
        greet([(always, device) for device in z_peers + others])
        down.send_own(d_own.at[down_half, :])
        z_sends = [
            push(piece.at[half, :], skip_half.at[me], zsend.at[number], zrecv.at[number], device)
            for number, device in enumerate(z_peers)
        ]
        for send in z_sends:
            send.start()
        take_stack(b_ref, utab, OUT_AT[6], count)
        take_stack(ao, dtab, IN_AT[9], count)
        take_stack(bk, utab, OUT_AT[7], count)
        take_stack(bv, utab, OUT_AT[8], count)
        take_local(ub, utab, OUT_AT[10], me, count)
        take_local(da, dtab, IN_AT[11], me, count)

        loads[0].wait()
        first = first_ref[...] + sum_ref[...]
        first_ref[...] = first
        second_ref[...] = first
        normal, _ = stats(first)
        x = (normal * gain[1:2, :]).astype(BF)
        x_ref[...] = x
        u = dot_nt(x, down_of(dtab, 6)).astype(BF)
        loads[2].wait()
        loads[3].wait()

        def cross(place, u_low):
            y = dot_nn(x_ref[...], wq[place]) + dot_nn(u, b_ref[place])
            outs, inverses, logs = [], [], []
            for head in range(heads):
                at = slice(head * HD, (head + 1) * HD)
                normal, inverse = stats(y[:, at])
                q = normal.astype(BF)
                q_ref[place, head] = q
                inverses.append(inverse)
                s = dot_nt(q, kv[0, place, :, at]) * scale
                top = jnp.max(s, axis=-1, keepdims=True)
                e = jnp.exp(s - top)
                total = jnp.sum(e, axis=-1, keepdims=True)
                p = (e * (1.0 / total)).astype(BF)
                outs.append(dot_nn(p, kv[1, place, :, at]))
                logs.append(top + jnp.log(total))
            inv_ref[place] = jnp.concatenate(inverses, axis=1)
            log_ref[place] = jnp.concatenate(logs, axis=1)
            low = jnp.concatenate(outs, axis=1).astype(BF)
            low_ref[place] = low
            second_ref[...] += dot_nt(low, wo[place])
            return u_low + dot_nt(low, ao[place])

        u_low = lax.fori_loop(0, count, cross, jnp.zeros((share, RANK), F32)).astype(BF)
        second = second_ref[...] + dot_nn(u_low, up_of(utab, 9))
        second_ref[...] = second
        normal, _ = stats(second)
        slots[me] = (normal * gain[2:3, :]).astype(BF)

        line_gather_step(gather_line, 0, slots)
        down.wait(0)
        down.forward()
        down.swap(0)
        down.wait(1)
        down.swap(1)
        loads[1].wait()
        for number in range(count - 1):
            arrived = skip_half.at[xor_place(me, number + 1)]
            push(arrived, arrived, zsend.at[number], zrecv.at[number], z_peers[number]).wait_recv()
        skip_place = pltpu.make_async_copy(skip_half, skip.view(dp, core), lsem.at[8])
        skip_place.start()
        skip.send_own(skip_half)
        line_gather_step(gather_line, 1, slots)
        down.wait(2)
        down.swap(2)
        loads[4].wait()
        loads[5].wait()
        loads[6].wait()
        ua, db = down_of(dtab, 10), up_of(utab, 11)
        down.wait_swaps()
        line_gather_step(gather_line, 2, slots)

        def part(number):
            return pl.ds(pl.multiple_of(number * wide, wide), wide)

        def first_grads(number, carry):
            ct = cot[part(number), :]
            gd = dot_nt(ct, db).astype(BF)
            gd_all[part(number), :] = gd
            grads[part(number), :] = (dot_nn(ct, wd[...]) + dot_nn(gd, da[...])).astype(BF)
            return carry

        lax.fori_loop(0, 2, first_grads, 0)
        line_gather_step(gather_line, 3, slots)
        lead = jnp.where(2 * me < count, 1, 0)

        def forward_half(turn, carry):
            number = jnp.where(turn == 0, lead, 1 - lead)
            here = part(number)
            x = slots[pl.ds(number * two, two)].reshape(wide, width)
            u = dot_nt(x, ua).astype(BF)
            u_all[here, :] = u
            up = dot_nn(x, wu[...]) + dot_nn(u, ub[...])
            square = up * up
            curve = jnp.tanh(0.7978845608028654 * (up + 0.044715 * square * up))
            flat = 0.5 * (1.0 + curve)
            active[here, :] = (up * flat).astype(BF)
            slope = flat + 0.5 * up * (1.0 - curve * curve) * (0.7978845608028654 * (1.0 + 0.134145 * square))
            g_up = (grads[here, :].astype(F32) * slope).astype(BF)
            grads[here, :] = g_up
            gu = dot_nt(g_up, ub[...]).astype(BF)
            gu_all[here, :] = gu
            g_x = (dot_nt(g_up, wu[...]) + dot_nn(gu, ua)).astype(BF)
            partial_g[pl.ds(number * two, two)] = g_x.reshape(two, share, width)
            line_scatter_step(grad_line, turn, partial_g, left_g, right_g, sr_g, sl_g)
            return carry

        lax.fori_loop(0, 2, forward_half, 0)
        skip.wait(0)
        skip.forward()
        skip.wait(1)

        def down_half_product(turn, carry):
            number = jnp.where(turn == 0, lead, 1 - lead)
            here = part(number)
            act = active[here, :]
            ud = dot_nt(act, da[...]).astype(BF)
            ud_all[here, :] = ud
            y = dot_nt(act, wd[...]) + dot_nn(ud, db)
            for piece_of in range(two):
                block = number * two + piece_of
                own = jnp.where(block == me, 1.0, 0.0)
                one = y[piece_of * share : (piece_of + 1) * share] + second_ref[...] * own
                partial_b[block] = one.astype(BF)

            @pl.when(turn == 0)
            def _():
                line_scatter_step(grad_line, 2, partial_g, left_g, right_g, sr_g, sl_g)

            return carry

        lax.fori_loop(0, 2, down_half_product, 0)
        skip_place.wait()
        skip.swap(0)
        skip.swap(1)
        skip.swap(3)
        line_scatter_step(block_line, 0, partial_b, left_b, right_b, sr_b, sl_b)
        g_ub[...] = dot_tn(u_all[...], grads[...])
        g_ua[...] = dot_tn(gu_all[...], slots[...].reshape(tokens, width))
        g_db[...] = dot_tn(ud_all[...], cot[...])
        g_da[...] = dot_tn(gd_all[...], active[...])
        loads[7].wait()
        uq = dot_nt(x_ref[...], down_of(dtab, 6)).astype(BF)
        words_in = t_ref[...]
        uk = dot_nt(words_in, down_of(dtab, 7)).astype(BF)
        uv = dot_nt(words_in, down_of(dtab, 8)).astype(BF)
        line_gather_drain(gather_line, slots)
        line_scatter_finish(grad_line, partial_g, left_g, right_g, sr_g, sl_g, acc)
        skip.wait(2)
        skip.swap(2)

        normal, inverse = stats(second_ref[...])
        g_second = cot[rows_of(me, share), :].astype(F32) + norm_backward(normal, inverse, acc[...] * gain[2:3, :])
        second_ref[...] = g_second
        g_low = g_second.astype(BF)
        slots[me] = g_low
        go = dot_nt(g_low, up_of(utab, 9)).astype(BF)
        gb_o[...] = dot_tn(u_low, g_low)
        acc[...] = jnp.zeros_like(acc)

        def cross_grads(place, carry):
            gq_sum, gk_sum, gv_sum = carry

            @pl.when((place > 0) & (place < count - 1))
            def _():
                line_scatter_step(block_line, place, partial_b, left_b, right_b, sr_b, sl_b)

            g_attn = (dot_nn(slots[me], wo[place]) + dot_nn(go, ao[place])).astype(BF)
            ga_o[place] = dot_tn(go, low_ref[place])
            gq_parts, gk_parts, gv_parts = [], [], []
            for head in range(heads):
                at = slice(head * HD, (head + 1) * HD)
                gh = g_attn[:, at]
                q = q_ref[place, head]
                k = kv[0, place, :, at]
                v = kv[1, place, :, at]
                p = jnp.exp(dot_nt(q, k) * scale - log_ref[place, :, head : head + 1])
                dp_ = dot_nt(gh, v)
                inner = jnp.sum(p * dp_, axis=-1, keepdims=True)
                ds = (p * (dp_ - inner)).astype(BF)
                dq = dot_nn(ds, k) * scale
                dk = dot_tn(ds, q) * scale
                gq_parts.append(norm_backward(q.astype(F32), inv_ref[place, :, head : head + 1], dq))
                side = kv[0, place, :, local + 2 * head : local + 2 * head + 2].astype(F32)
                gk_parts.append(norm_backward(k.astype(F32), side[:, 0:1] + side[:, 1:2], dk))
                gv_parts.append(dot_tn(p.astype(BF), gh))
            gq = jnp.concatenate(gq_parts, axis=1).astype(BF)
            gk = jnp.concatenate(gk_parts, axis=1).astype(BF)
            gv = jnp.concatenate(gv_parts, axis=1).astype(BF)
            acc[...] += dot_nt(gq, wq[place])
            gb_q[place] = dot_tn(uq, gq)
            gb_k[place] = dot_tn(uk, gk)
            gb_v[place] = dot_tn(uv, gv)
            return (
                gq_sum + dot_nt(gq, b_ref[place]),
                gk_sum + dot_nt(gk, bk[place]),
                gv_sum + dot_nt(gv, bv[place]),
            )

        start = (jnp.zeros((share, RANK), F32), jnp.zeros((words, RANK), F32), jnp.zeros((words, RANK), F32))
        gq_sum, gk_sum, gv_sum = lax.fori_loop(0, count, cross_grads, start)
        gq_sum = gq_sum.astype(BF)
        ga_q[...] = dot_tn(gq_sum, x_ref[...])
        ga_k[...] = dot_tn(gk_sum.astype(BF), words_in)
        ga_v[...] = dot_tn(gv_sum.astype(BF), words_in)
        g_x = acc[...] + dot_nn(gq_sum, down_of(dtab, 6))
        normal, inverse = stats(first_ref[...])
        g_first[...] = (second_ref[...] + norm_backward(normal, inverse, g_x * gain[1:2, :])).astype(BF)
        line_scatter_finish(block_line, partial_b, left_b, right_b, sr_b, sl_b, acc)
        block_sum[...] = acc[...].astype(BF)
        skip.wait_swaps()
        skip.drain()
        down.drain()
        for send in z_sends:
            send.wait_send()

    buffers = [vmem(count, share, width) for _ in range(5)]
    return call(
        kernel,
        [(summed, True)]
        + [(array, False) for array in (skip_out, query_weight, out_weight, up_weight, down_piece, skip_piece)]
        + [(text_kv, True), (text, False), (cotangent, False)]
        + [(array, True) for array in (gains, *tables)],
        [
            ((share, width), BF, True),
            ((share, width), BF, True),
            ((RANK, width), F32, True),
            ((count, RANK, local), F32, True),
            ((RANK, text_width), F32, True),
            ((count, RANK, local), F32, True),
            ((RANK, text_width), F32, True),
            ((count, RANK, local), F32, True),
            ((count, RANK, local), F32, True),
            ((RANK, width), F32, True),
            ((RANK, width), F32, True),
            ((RANK, units), F32, True),
            ((RANK, units), F32, True),
            ((RANK, width), F32, True),
            ((count, 4 * rows, span), BF, False),
        ],
        [vmem(count, width, local), vmem(count, width, local), vmem(width, units), vmem(width, units),
         vmem(tokens, width), vmem(words, text_width), vmem(share, width, dtype=F32), vmem(share, width, dtype=F32),
         vmem(share, width), vmem(count, heads, share, HD), vmem(count, share, heads, dtype=F32),
         vmem(count, share, heads, dtype=F32), vmem(count, share, local), vmem(share, width, dtype=F32)]
        + [vmem(count, RANK, local) for _ in range(4)] + [vmem(RANK, units) for _ in range(2)]
        + [vmem(count, share, width), vmem(count, rows // 2, span), vmem(tokens, units), vmem(tokens, units)]
        + [vmem(tokens, RANK) for _ in range(4)] + buffers + buffers
        + [dma(9), dma(2, 7), dma(2, 7), dma(count), dma(count)] + [dma(count) for _ in range(12)],
        collective=3,
        cost=cost_of(12 * tokens * width * units, 60e6),
    )


class Shared:
    def __init__(self, target, rows, sems, stacked=False, split=True, columns=False):
        self.target, self.rows, self.stacked, self.split, self.columns = target, rows, stacked, split, columns
        self.send_sem, self.recv_sem, self.index = sems
        dp, core = lax.axis_index("dp"), lax.axis_index("ctx")
        self.dp, self.core = dp, core
        self.first = jnp.where(core == 0, xor_place(dp, 1), xor_place(dp, 2))
        self.second = jnp.where(core == 0, xor_place(dp, 2), xor_place(dp, 1))
        self.third = xor_place(dp, 3)

    def view(self, block, which):
        if self.columns:
            return self.target.at[:, pl.ds(pl.multiple_of(block * self.rows, 128), self.rows)]
        size = self.rows // 2 if self.split else self.rows
        start = block * self.rows + (which * size if self.split else 0)
        rows = pl.ds(pl.multiple_of(start, 16), size)
        return self.target.at[:, rows, :] if self.stacked else self.target.at[rows, :]

    def copy(self, number, source, block, which, device):
        target = self.view(block, which)
        source = target if source is None else source
        return push(source, target, self.send_sem.at[self.index, number], self.recv_sem.at[self.index, number], device)

    def send_own(self, source=None):
        self.copy(0, source, self.dp, self.core, {"dp": self.first}).start()
        self.copy(1, source, self.dp, self.core, {"dp": self.second}).start()

    def blocks(self):
        return [self.first, self.second, self.third] + ([self.dp] if self.stacked else [])

    def wait(self, number):
        self.copy(number, None, self.blocks()[number], self.core, {"dp": self.first}).wait_recv()

    def forward(self):
        self.copy(2, None, self.first, self.core, {"dp": self.second}).start()

    def swap(self, number):
        self.copy(3 + number, None, self.blocks()[number], self.core, {"ctx": 1 - self.core}).start()

    def wait_swaps(self):
        other = [self.second, self.first, self.third, self.dp]
        for number in range(len(self.blocks())):
            self.copy(3 + number, None, other[number], 1 - self.core, {"ctx": 1 - self.core}).wait_recv()

    def drain(self):
        for number in range(3 + (len(self.blocks()) if self.split else 0)):
            self.copy(number, None, self.dp, self.core, {"dp": self.first}).wait_send()


def front(count, heads, condition, index, hidden, long_skip, text, weights, mod_weight, gain_halves, gain_rows, tables):
    tokens, width = hidden.shape
    span = weights["skip"].shape[1]
    words, text_width = text.shape
    local = weights["q"].shape[1]
    units = weights["up"].shape[1]
    share = tokens // count
    block = min(128, tokens)
    chunk = min(64, tokens)
    steps = tokens // chunk
    each = block // chunk
    scale = HD ** (-0.5)
    rows = weights["q"].shape[0]
    text_rows = weights["ck"].shape[1]
    mod_rows = mod_weight.shape[0]

    def kernel(skip_own, q_own, k_own, v_own, o_own, ck_own, cv_own, cq_own, co_own, up_own,
               index_ref, cond, hid, lsk, t_ref, wm, halves, gain, dtab, utab,
               skip_hbm, attn_hbm, q_out, keys, values, low_out, log_out, inv_q, inv_k, summed, act_all, text_kv,
               wq_hbm, wk_hbm, wv_hbm, wo_hbm, wcq, wco, wup,
               skip_out, attn_in, wq, wk, wv, wo, out_sem, shift_row, wskip, wtext, part_x, pgain, sa, tk, tv, qa, qb, kb, vb, oa, mod_in, mod_slice, mod_out, partial_a, left_a, right_a, sr_a, sl_a,
               partial_b, left_b, right_b, sr_b, sl_b, wsend, wrecv, local_sem, zsend, zrecv, msend, mrecv, tsend, trecv,
               xsend, xrecv, *sems):
        me = lax.axis_index("tensor")
        core = lax.axis_index("ctx")
        dp = lax.axis_index("dp")
        always = core >= 0
        peer = {"ctx": 1 - core}
        dp_peers = [{"dp": xor_place(dp, number)} for number in (1, 2, 3)]
        z_peers = [{"tensor": xor_place(me, number)} for number in range(1, count)]
        reduce_line = Line(me, count, *sems[:4])
        scatter_line = Line(me, count, *sems[4:8])
        text_line = Line(me, count, *sems[8:])

        def sems_of(number):
            return (wsend, wrecv, number)

        skip = Shared(wskip, rows, sems_of(0))
        shared = {
            name: Shared(target, rows, sems_of(number))
            for name, target, number in (("q", wq, 1), ("k", wk, 2), ("v", wv, 3), ("o", wo, 4))
        }
        words_w = Shared(wtext, text_rows, sems_of(5), split=False, columns=True)
        cross = [Shared(wcq, rows, sems_of(6), stacked=True), Shared(wco, rows, sems_of(7), stacked=True)]
        wide = [Shared(wup, rows, sems_of(8))]
        owns = {"q": q_own, "k": k_own, "v": v_own, "o": o_own}
        half = pl.ds(pl.multiple_of(core * (rows // 2), 16), rows // 2)
        mine = pl.ds(pl.multiple_of(dp * rows, 16), rows)
        my_half = pl.ds(pl.multiple_of(dp * rows + core * (rows // 2), 16), rows // 2)

        for place in range(count):
            @pl.when(me == place)
            def _(place=place):
                side = place * span // width
                start = place * span % width
                pgain[...] = halves[side : side + 1, start : start + span]

        places = [
            pltpu.make_async_copy(source, target.at[mine, :], local_sem.at[number])
            for number, (source, target) in enumerate(
                ((skip_own, wskip), (q_own, wq), (k_own, wk), (v_own, wv), (o_own, wo), (up_own, wup))
            )
        ]
        for place in places:
            place.start()
        crossing = [
            pltpu.make_async_copy(source.at[half, :], target.at[me, my_half, :], local_sem.at[7 + number])
            for number, (source, target) in enumerate(((cq_own, wcq), (co_own, wco)))
        ]
        text_mine = pl.ds(pl.multiple_of(dp * text_rows, 128), text_rows)

        def text_place(source):
            return pltpu.make_async_copy(source, wtext.at[:, text_mine], local_sem.at[9])

        @pl.when(core == 0)
        def _():
            text_place(ck_own).start()

        @pl.when(core == 1)
        def _():
            text_place(cv_own).start()

        for place in crossing:
            place.start()
        value = cond[...].astype(F32)
        act_low = (value / (1.0 + jnp.exp(-value))).astype(BF)
        tag = jnp.full((1, 128), index_ref[0], jnp.int32).astype(F32)
        act_all[dp] = jnp.concatenate([act_low.astype(F32), tag], axis=1)
        greet([(always, device) for device in dp_peers + z_peers + [peer]])
        skip.send_own(skip_own.at[half, :])

        def z_copies(number):
            return [
                push(source.at[half, :], target.at[me, my_half, :], zsend.at[which, number], zrecv.at[which, number],
                     z_peers[number])
                for which, (source, target) in enumerate(((cq_own, wcq), (co_own, wco)))
            ]

        for number in range(count - 1):
            for copy in z_copies(number):
                copy.start()
        spread = [
            push(act_all.at[dp], act_all.at[dp], msend.at[0, number], mrecv.at[0, number], device)
            for number, device in enumerate(dp_peers)
        ]
        for copy in spread:
            copy.start()
        take_local(sa, dtab, 0, me, count)
        take_local(tk, utab, OUT_AT[7], me, count)
        take_local(tv, utab, OUT_AT[8], me, count)
        for number, target in enumerate((qb, kb, vb)):
            qa[number * RANK : (number + 1) * RANK, :] = down_of(dtab, 2 + number)
            take_local(target, utab, OUT_AT[2 + number], me, count)
        take_local(oa, dtab, IN_AT[5], me, count)
        skip.wait(0)
        skip.forward()
        for name in ("q", "k", "v", "o"):
            shared[name].send_own(owns[name].at[half, :])

        @pl.when(core == 0)
        def _():
            words_w.send_own(ck_own)

        @pl.when(core == 1)
        def _():
            words_w.send_own(cv_own)

        skip.swap(0)

        skip.wait(1)
        skip.swap(1)

        for number in (1, 2, 3):
            source = act_all.at[xor_place(dp, number)]
            push(source, source, msend.at[0, number - 1], mrecv.at[0, number - 1], dp_peers[number - 1]).wait_recv()
        for owner in range(4):
            @pl.when(dp == owner)
            def _(owner=owner):
                span_of = slice(owner * mod_rows, (owner + 1) * mod_rows)
                for sequence in range(4):
                    mod_slice[sequence : sequence + 1, :] = act_all[sequence, :, span_of]

        skip.wait(2)
        skip.swap(2)
        products = dot_nn(mod_slice[...].astype(BF), wm[...])
        for sequence in range(4):
            mod_out[sequence] = products[sequence : sequence + 1]
        backs = [
            push(mod_out.at[xor_place(dp, number)], mod_in.at[dp], msend.at[1, number - 1], mrecv.at[1, number - 1],
                 dp_peers[number - 1])
            for number in (1, 2, 3)
        ]
        for copy in backs:
            copy.start()
        mod_in[dp] = mod_out[dp]
        places[0].wait()
        skip.wait_swaps()

        def compute(number):
            @pl.when(number % each == 0)
            def _():
                here = rows_of(number // each, block)
                left = hid[here, :].astype(F32)
                right = lsk[here, :].astype(F32)
                mean = (jnp.sum(left, axis=-1, keepdims=True) + jnp.sum(right, axis=-1, keepdims=True)) / (2 * width)
                spread = jnp.sum((left - mean) ** 2, axis=-1, keepdims=True)
                spread += jnp.sum((right - mean) ** 2, axis=-1, keepdims=True)
                inverse = lax.rsqrt(spread / (2 * width) + NORM_EPS)
                for place in range(count):
                    @pl.when(me == place)
                    def _(place=place):
                        source = hid if place * span < width else lsk
                        start = place * span % width
                        part_x[...] = source[here, start : start + span].astype(F32)
                x = ((part_x[...] - mean) * inverse * pgain[...]).astype(BF)
                u = dot_nt(x, sa[...]).astype(BF)
                y = (dot_nt(x, wskip[...]) + dot_nn(u, up_of(utab, 0))).astype(BF)
                for piece in range(each):
                    partial_a[number + piece] = y[piece * chunk : (piece + 1) * chunk]

        def text_product():
            @pl.when(core == 0)
            def _():
                text_place(ck_own).wait()

            @pl.when(core == 1)
            def _():
                text_place(cv_own).wait()

            x = t_ref[...]
            y = dot_nt(x, wtext[...])

            @pl.when(core == 0)
            def _():
                z = y + dot_nn(dot_nt(x, down_of(dtab, 7)).astype(BF), tk[...])
                parts, sides = [], []
                for head in range(heads):
                    normal, inverse = stats(z[:, head * HD : (head + 1) * HD])
                    upper = inverse.astype(BF)
                    parts.append(normal.astype(BF))
                    sides += [upper, (inverse - upper.astype(F32)).astype(BF)]
                text_kv[0, me, :, :local] = jnp.concatenate(parts, axis=1)
                text_kv[0, me, :, local : local + 2 * heads] = jnp.concatenate(sides, axis=1)

            @pl.when(core == 1)
            def _():
                z = y + dot_nn(dot_nt(x, down_of(dtab, 8)).astype(BF), tv[...])
                text_kv[1, me, :, :local] = z.astype(BF)

        text_slots = text_kv.at[core]

        def finish(slot, total):
            here = rows_of(slot, chunk)
            skip_out[here, :] = total
            normal, _ = stats(total)
            attn_in[here, :] = (normal * gain[0:1, :] + shift_row[...]).astype(BF)

        def beside(number):
            @pl.when(number == 1)
            def _():
                for other in (1, 2, 3):
                    target = mod_in.at[xor_place(dp, other)]
                    push(target, target, msend.at[1, other - 1], mrecv.at[1, other - 1], dp_peers[other - 1]).wait_recv()
                mod_u = dot_nt(act_low, down_of(dtab, 1)).astype(BF)
                shift_row[...] = mod_in[0] + mod_in[1] + mod_in[2] + mod_in[3] + dot_nn(mod_u, up_of(utab, 1))

            @pl.when(number == 3)
            def _():
                for weight in (*shared.values(), words_w):
                    weight.wait(0)
                    weight.forward()
                for weight in (*shared.values(), words_w):
                    weight.wait(1)
                for weight in shared.values():
                    weight.swap(0)
                    weight.swap(1)

            @pl.when(number == 4)
            def _():
                for place in crossing:
                    place.wait()
                for other in range(count - 1):
                    for which, target in enumerate((wcq, wco)):
                        block_in = target.at[xor_place(me, other + 1), my_half, :]
                        push(block_in, block_in, zsend.at[which, other], zrecv.at[which, other], z_peers[other]).wait_recv()
                for weight in cross:
                    weight.send_own()

            @pl.when(number == 7)
            def _():
                for weight in (*shared.values(), words_w):
                    weight.wait(2)
                for weight in shared.values():
                    weight.swap(2)

            @pl.when(number == 8)
            def _():
                text_product()
                line_gather_step(text_line, 0, text_slots)

        line_reduce_all(reduce_line, steps, compute, partial_a, left_a, right_a, sr_a, sl_a, finish, beside)

        for number in range(1, 5):
            places[number].wait()
        for weight in shared.values():
            weight.wait_swaps()
        stores = [
            pltpu.make_async_copy(source, target, out_sem.at[number])
            for number, (source, target) in enumerate(
                ((skip_out, skip_hbm), (attn_in, attn_hbm), (wq, wq_hbm), (wk, wk_hbm), (wv, wv_hbm), (wo, wo_hbm))
            )
        ]
        for store in stores:
            store.start()

        def project(number, carry):
            here = rows_of(number, block)
            x = attn_in[here, :]
            u = dot_nt(x, qa[...]).astype(BF)
            yq = dot_nn(x, wq[...]) + dot_nn(u[:, :RANK], qb[...])
            yk = dot_nn(x, wk[...]) + dot_nn(u[:, RANK : 2 * RANK], kb[...])
            yv = (dot_nn(x, wv[...]) + dot_nn(u[:, 2 * RANK :], vb[...])).astype(BF)
            parts_q, parts_k = [], []
            for head in range(heads):
                span_of = slice(head * HD, (head + 1) * HD)
                normal, inverse = stats(yq[:, span_of])
                q_out[head, here, :] = normal.astype(BF)
                parts_q.append(inverse)
                normal, inverse = stats(yk[:, span_of])
                keys[core, head, here, :] = normal.astype(BF)
                parts_k.append(inverse)
                values[core, head, here, :] = yv[:, span_of]
            inv_q[here, :] = jnp.concatenate(parts_q, axis=1)
            inv_k[here, :] = jnp.concatenate(parts_k, axis=1)
            return carry

        lax.fori_loop(0, tokens // block, project, 0)
        swaps = [
            push(ref.at[core], ref.at[core], xsend.at[number], xrecv.at[number], peer)
            for number, ref in enumerate((keys, values))
        ]
        for swap in swaps:
            swap.start()
        line_gather_step(text_line, 1, text_slots)
        for weight in cross:
            weight.wait(0)
            weight.forward()
            weight.swap(0)
            weight.swap(3)
        for weight in wide:
            weight.send_own(up_own.at[half, :])
        for number, ref in enumerate((keys, values)):
            push(ref.at[1 - core], ref.at[1 - core], xsend.at[number], xrecv.at[number], peer).wait_recv()

        def attend(place, carry):
            dest = scatter_order(me, count, place)
            here = rows_of(dest, share)
            outs, logs = [], []
            for head in range(heads):
                q = q_out[head, here, :]
                s0 = dot_nt(q, keys[0, head]) * scale
                s1 = dot_nt(q, keys[1, head]) * scale
                top = jnp.maximum(jnp.max(s0, axis=-1, keepdims=True), jnp.max(s1, axis=-1, keepdims=True))
                e0 = jnp.exp(s0 - top)
                e1 = jnp.exp(s1 - top)
                total = jnp.sum(e0, axis=-1, keepdims=True) + jnp.sum(e1, axis=-1, keepdims=True)
                share_of = 1.0 / total
                p0 = (e0 * share_of).astype(BF)
                p1 = (e1 * share_of).astype(BF)
                outs.append(dot_nn(p0, values[0, head]) + dot_nn(p1, values[1, head]))
                logs.append(top + jnp.log(total))
            low = jnp.concatenate(outs, axis=1).astype(BF)
            low_out[here, :] = low
            log_out[here, :] = jnp.concatenate(logs, axis=1)
            u = dot_nt(low, oa[...]).astype(BF)
            partial_b[dest] = (dot_nt(low, wo[...]) + dot_nn(u, up_of(utab, 5))).astype(BF)

            @pl.when(place < count - 1)
            def _():
                line_scatter_step(scatter_line, place, partial_b, left_b, right_b, sr_b, sl_b)

            @pl.when(place == 0)
            def _():
                line_gather_step(text_line, 2, text_slots)

            @pl.when(place == 1)
            def _():
                for weight in cross:
                    weight.wait(1)
                    weight.swap(1)
                line_gather_step(text_line, 3, text_slots)
                push(text_slots, text_slots, tsend, trecv, peer).start()

            @pl.when(place == 2)
            def _():
                for weight in cross:
                    weight.wait(2)
                    weight.swap(2)

            return carry

        lax.fori_loop(0, count, attend, 0)
        for weight in wide:
            weight.wait(0)
            weight.forward()
            weight.swap(0)
        for weight in wide:
            weight.wait(1)
            weight.swap(1)
        line_scatter_finish(scatter_line, partial_b, left_b, right_b, sr_b, sl_b, summed)
        for weight in wide:
            weight.wait(2)
            weight.swap(2)
        others = text_kv.at[1 - core]
        push(others, others, tsend, trecv, peer).wait_recv()
        for weight in cross + wide:
            weight.wait_swaps()
        places[5].wait()
        for store in stores:
            store.wait()
        for weight in (skip, *shared.values(), words_w, *cross, *wide):
            weight.drain()
        for number in range(count - 1):
            for copy in z_copies(number):
                copy.wait_send()
        for copy in spread + backs:
            copy.wait_send()
        line_gather_drain(text_line, text_slots)
        push(text_slots, text_slots, tsend, trecv, peer).wait_send()
        for swap in swaps:
            swap.wait_send()

    names = ("skip", "q", "k", "v", "o", "ck", "cv", "cq", "co", "up")
    return call(
        kernel,
        [(weights[name], name in ("cq", "co", "up")) for name in names] + [(index, None)]
        + [(array, True) for array in (condition, hidden, long_skip, text, mod_weight, gain_halves, gain_rows, *tables)],
        [
            ((tokens, width), F32, False),
            ((tokens, width), BF, False),
            ((heads, tokens, HD), BF, True),
            ((2, heads, tokens, HD), BF, True),
            ((2, heads, tokens, HD), BF, True),
            ((tokens, local), BF, True),
            ((tokens, heads), F32, True),
            ((tokens, heads), F32, True),
            ((tokens, heads), F32, True),
            ((share, width), F32, True),
            ((4, 1, width + 128), F32, True),
            ((2, count, words, local + 32), BF, True),
        ]
        + [((width, local), BF, False) for _ in range(4)]
        + [((count, width, local), BF, False) for _ in range(2)]
        + [((width, units), BF, False)],
        [vmem(tokens, width, dtype=F32), vmem(tokens, width)] + [vmem(width, local) for _ in range(4)]
        + [dma(6), vmem(1, width, dtype=F32), vmem(width, span), vmem(local, text_width), vmem(block, span, dtype=F32), vmem(1, span, dtype=F32),
         vmem(RANK, span), vmem(RANK, local), vmem(RANK, local), vmem(3 * RANK, width)]
        + [vmem(RANK, local) for _ in range(4)]
        + [vmem(4, 1, width, dtype=F32), vmem(4, mod_rows, dtype=F32),
         vmem(4, 1, width, dtype=F32)]
        + [vmem(steps, chunk, width) for _ in range(5)] + [vmem(count, share, width) for _ in range(5)]
        + [dma(10, 7), dma(10, 7), dma(10), dma(2, count), dma(2, count), dma(2, 3), dma(2, 3), dma(), dma(),
           dma(2), dma(2)]
        + [dma(steps) for _ in range(4)] + [dma(count) for _ in range(8)],
        collective=1,
        cost=cost_of(8 * tokens * width * local, 60e6),
    )


def attention_backward(count, heads, g_first, block_sum, query, keys, values, low, logs, inv_q, inv_k, out_weight, tables):
    share, width = g_first.shape
    tokens = query.shape[1]
    local = low.shape[1]
    scale = HD ** (-0.5)

    def kernel(g_ref, b_in, q_ref, k_ref, v_ref, low_ref, log_ref, iq_ref, ik_ref, wo, dtab, utab, gq_low, gk_low, gv_low,
               gall, ball, ga_o, gb_o, gk_acc, gv_acc, swap_out, swap_in, ao, xsend, xrecv, *sems):
        me = lax.axis_index("tensor")
        core = lax.axis_index("ctx")
        peer = {"ctx": 1 - core}
        grad_line = Line(me, count, *sems[:4])
        block_line = Line(me, count, *sems[4:])
        gall[me] = g_ref[...]
        ball[me] = b_in[...]
        greet(line_partners(me, count) + [(core >= 0, peer)])
        line_gather_step(grad_line, 0, gall)
        for ref in (ga_o, gb_o, gk_acc, gv_acc):
            ref[...] = jnp.zeros_like(ref)
        take_local(ao, dtab, IN_AT[5], me, count)

        def attend(place):
            rows = rows_of(place, share)
            g = gall[place]
            go = dot_nt(g, up_of(utab, 5)).astype(BF)
            g_attn = (dot_nn(g, wo[...]) + dot_nn(go, ao[...])).astype(BF)
            low = low_ref[rows, :]
            uo = dot_nt(low, ao[...]).astype(BF)
            gb_o[...] += dot_tn(uo, g)
            ga_o[...] += dot_tn(go, low)
            parts = []
            for head in range(heads):
                gh = g_attn[:, head * HD : (head + 1) * HD]
                q = q_ref[head, rows, :]
                probs, grads = [], []
                inner = 0.0
                for half in range(2):
                    p = jnp.exp(dot_nt(q, k_ref[half, head]) * scale - log_ref[rows, head : head + 1])
                    dp = dot_nt(gh, v_ref[half, head])
                    inner = inner + jnp.sum(p * dp, axis=-1, keepdims=True)
                    probs.append(p)
                    grads.append(dp)
                dq = 0.0
                for half in range(2):
                    ds = (probs[half] * (grads[half] - inner)).astype(BF)
                    dq = dq + dot_nn(ds, k_ref[half, head])
                    gk_acc[half, head] += dot_tn(ds, q)
                    gv_acc[half, head] += dot_tn(probs[half].astype(BF), gh)
                parts.append(norm_backward(q.astype(F32), iq_ref[rows, head : head + 1], dq * scale))
            gq_low[rows, :] = jnp.concatenate(parts, axis=1).astype(BF)

        def gather(number, carry):
            @pl.when(number > 0)
            def _():
                line_gather_step(grad_line, number, gall)

            @pl.when(number == count - 1)
            def _():
                line_gather_step(block_line, 0, ball)

            def side(which, inner):
                place = me + (2 * which - 1) * number

                @pl.when((place >= 0) & (place < count) & ((number > 0) | (which == 0)))
                def _():
                    attend(lax.clamp(0, place, count - 1))

                return inner

            return lax.fori_loop(0, 2, side, carry)

        lax.fori_loop(0, count, gather, 0)
        swap_out[0] = (gk_acc[1 - core] * scale).astype(BF)
        swap_out[1] = gv_acc[1 - core].astype(BF)
        swap = push(swap_out, swap_in, xsend, xrecv, peer)
        swap.start()
        line_gather_step(block_line, 1, ball)
        line_gather_drain(grad_line, gall)
        swap.wait()

        def keys_back(place, carry):
            rows = rows_of(place, share)
            parts_k, parts_v = [], []
            for head in range(heads):
                dk = gk_acc[core, head, rows, :] * scale + swap_in[0, head, rows, :].astype(F32)
                normal = k_ref[core, head, rows, :].astype(F32)
                parts_k.append(norm_backward(normal, ik_ref[rows, head : head + 1], dk))
                parts_v.append(gv_acc[core, head, rows, :] + swap_in[1, head, rows, :].astype(F32))
            gk_low[rows, :] = jnp.concatenate(parts_k, axis=1).astype(BF)
            gv_low[rows, :] = jnp.concatenate(parts_v, axis=1).astype(BF)
            return carry

        lax.fori_loop(0, count, keys_back, 0)
        line_gather_step(block_line, 2, ball)
        line_gather_step(block_line, 3, ball)
        line_gather_drain(block_line, ball)

    return call(
        kernel,
        [(array, True) for array in (g_first, block_sum, query, keys, values, low, logs, inv_q, inv_k, out_weight, *tables)],
        [
            ((tokens, local), BF, True),
            ((tokens, local), BF, True),
            ((tokens, local), BF, True),
            ((count, share, width), BF, True),
            ((count, share, width), BF, True),
            ((RANK, local), F32, True),
            ((RANK, width), F32, True),
        ],
        [vmem(2, heads, tokens, HD, dtype=F32), vmem(2, heads, tokens, HD, dtype=F32), vmem(2, heads, tokens, HD),
         vmem(2, heads, tokens, HD), vmem(RANK, local), dma(), dma()]
        + [dma(count) for _ in range(8)],
        collective=4,
        cost=cost_of(16 * tokens * width * local, 60e6),
    )


EARLY_A, EARLY_B = IN_AT[2], OUT_AT[2]
EARLY = IN_AT[12] - EARLY_A + OUT_AT[12] - EARLY_B
LATE = EARLY_A + EARLY_B


def back_end(count, grads, projections, attn_in, g_first, skip_out, hidden, long_skip, weight, mod_weight, gain_halves,
             gain_rows, tables, condition, act_all, wide_grads, local_down, local_up, stacked):
    tokens, width = hidden.shape
    local = grads[0].shape[1]
    span = weight.shape[-1]
    block = tokens // count
    chunk = min(64, block)
    each = block // chunk
    steps = tokens // chunk
    own_rows = RANK // count
    half_e = -(-EARLY // 256) * 128
    half_l = -(-LATE // 256) * 128
    base = IN_AT[12] - EARLY_A
    mod_rows = mod_weight.shape[0]

    def early(column):
        return column - EARLY_A if column < IN_AT[12] else column - EARLY_A - EARLY_B

    wide_at, wide = [early(column) for column in wide_grads], list(wide_grads.values())
    local_at = [early(column) for column in local_down] + [early(IN_AT[12] + column) for column in local_up]
    own_grads = list(local_down.values()) + list(local_up.values())
    stacked_at, stack = [early(column) for column in stacked], list(stacked.values())

    def kernel(gq, gk, gv, wq, wk, wv, x_ref, gf_ref, skip_ref, hid, lsk, hbm_w, wm, gains, gain, dtab, utab, cond, act_ref,
               *refs):
        wide_refs, refs = refs[: len(wide)], refs[len(wide) :]
        own_refs, refs = refs[: len(own_grads)], refs[len(own_grads) :]
        stack_refs, refs = refs[: len(stack)], refs[len(stack) :]
        (out_h, out_l, out_a, out_b, out_c, w, buf_h, buf_l, low, g_ref, qkv_a, bq, bk, bv, partial_g, left_g, right_g,
         sr_g, sl_g, table, late, swap_out, swap_in, partial_e, left_e, right_e, sr_e, sl_e, summed, late_out, late_in,
         partial_l, slots_l, slots, other_out, other_in, shifts, shift_in, act_out, act_in, g_act, g_sum,
         wsem, osem, ssem, rsem, dsend, drecv, msend, mrecv, zsend, zrecv, *sems) = refs
        me = lax.axis_index("tensor")
        core = lax.axis_index("ctx")
        dp = lax.axis_index("dp")
        peer = {"ctx": 1 - core}
        grad_line = Line(me, count, *sems[:4])
        early_line = Line(me, count, *sems[4:])
        peers = [{"dp": xor_place(dp, number)} for number in (1, 2, 3)]
        z_peers = [{"tensor": xor_place(me, number)} for number in range(1, count)]
        load = pltpu.make_async_copy(hbm_w, w, wsem)
        load.start()
        greet([(core >= 0, device) for device in z_peers + peers + [peer]])
        for number, target in enumerate((bq, bk, bv)):
            qkv_a[number * RANK : (number + 1) * RANK, :] = down_of(dtab, 2 + number)
            take_local(target, utab, OUT_AT[2 + number], me, count)
        g_sum[...] = jnp.zeros_like(g_sum)
        act_low = act_ref[dp, :, :width].astype(BF)

        def compute(number):
            @pl.when(number % each == 0)
            def _():
                rows = rows_of(number // each, block)
                gu = jnp.concatenate(
                    [dot_nt(gq[rows, :], bq[...]), dot_nt(gk[rows, :], bk[...]), dot_nt(gv[rows, :], bv[...])], axis=1
                ).astype(BF)
                y = dot_nt(gq[rows, :], wq[...]) + dot_nt(gk[rows, :], wk[...]) + dot_nt(gv[rows, :], wv[...])
                y = (y + dot_nn(gu, qkv_a[...])).astype(BF)
                for piece in range(each):
                    partial_g[number + piece] = y[piece * chunk : (piece + 1) * chunk]

        def finish(slot, total):
            g_ref[rows_of(slot, chunk), :] = total

        def skip_block(number):
            rows = rows_of(number, block)
            ga_in = g_ref[rows, :]
            g_sum[...] += jnp.sum(ga_in, axis=0, keepdims=True)
            normal, inverse = stats(skip_ref[rows, :])
            g_low = (
                gf_ref[number].astype(F32) + norm_backward(normal, inverse, ga_in * gain[0:1, :])
            ).astype(BF)
            left = hid[rows, :].astype(F32)
            right = lsk[rows, :].astype(F32)
            mean = (jnp.sum(left, axis=-1, keepdims=True) + jnp.sum(right, axis=-1, keepdims=True)) / (2 * width)
            left = left - mean
            right = right - mean
            spread = jnp.sum(left * left, axis=-1, keepdims=True) + jnp.sum(right * right, axis=-1, keepdims=True)
            inverse = lax.rsqrt(spread / (2 * width) + NORM_EPS)
            left = left * inverse
            right = right * inverse
            gu = dot_nt(g_low, up_of(utab, 0)).astype(BF)
            a_left, a_right = dtab[:, :width], dtab[:, width : 2 * width]

            @pl.when(number == me)
            def _():
                low_l = (left * gains[0:1, :]).astype(BF)
                low_r = (right * gains[1:2, :]).astype(BF)
                u = (dot_nt(low_l, a_left) + dot_nt(low_r, a_right)).astype(BF)
                late[:, :width] = dot_tn(gu, low_l)
                late[:, width : 2 * width] = dot_tn(gu, low_r)
                late[:, EARLY_A : EARLY_A + width] = dot_tn(u, g_low)

            for place in range(count):
                low[:, place * span : (place + 1) * span] = dot_nn(g_low, w[place])
            gl = (low[:, :width] + dot_nn(gu, a_left)) * gains[0:1, :]
            gr = (low[:, width:] + dot_nn(gu, a_right)) * gains[1:2, :]
            mean = (jnp.sum(gl, axis=-1, keepdims=True) + jnp.sum(gr, axis=-1, keepdims=True)) / (2 * width)
            inner = (
                jnp.sum(gl * left, axis=-1, keepdims=True) + jnp.sum(gr * right, axis=-1, keepdims=True)
            ) / (2 * width)
            buf_h[number] = inverse * (gl - mean - left * inner)
            buf_l[number] = inverse * (gr - mean - right * inner)
            pltpu.make_async_copy(buf_h.at[number], out_h.at[rows, :], osem.at[0, number]).start()
            pltpu.make_async_copy(buf_l.at[number], out_l.at[rows, :], osem.at[1, number]).start()

        swap = push(swap_out, swap_in, ssem.at[0], rsem.at[0], peer)

        def early_step(number):
            line_scatter_step(early_line, number, partial_e, left_e, right_e, sr_e, sl_e)

        def beside(number):
            @pl.when(number == 1)
            def _():
                load.wait()
                x = x_ref[...]
                u = dot_nt(x, qkv_a[...]).astype(BF)
                table[...] = jnp.zeros_like(table)
                late[...] = jnp.zeros_like(late)
                for start, ref in zip(wide_at, wide_refs):
                    table[:, start : start + ref.shape[1]] = ref[...]
                for start, ref in zip(stacked_at, stack_refs):
                    size = ref.shape[2]
                    for place in range(count):
                        table[:, start + place * size : start + (place + 1) * size] = ref[place]
                qkv_b = []
                for which, (grad, factor) in enumerate(((gq, bq), (gk, bk), (gv, bv))):
                    gu = dot_nt(grad[...], factor[...]).astype(BF)
                    table[:, which * width : (which + 1) * width] = dot_tn(gu, x)
                    qkv_b.append(dot_tn(u[:, which * RANK : (which + 1) * RANK], grad[...]))
                for place in range(count):
                    @pl.when(me == place)
                    def _(place=place):
                        for which, piece in enumerate(qkv_b):
                            start = base + which * width + place * local
                            table[:, start : start + local] = piece
                        for start, ref in zip(local_at, own_refs):
                            size = ref.shape[1]
                            table[:, start + place * size : start + (place + 1) * size] = ref[...]
                for which in range(2):
                    @pl.when(core == which)
                    def _(which=which):
                        swap_out[...] = table[:, (1 - which) * half_e : (2 - which) * half_e].astype(BF)

                swap.start()

            @pl.when(number == 3)
            def _():
                swap.wait()
                for which in range(2):
                    @pl.when(core == which)
                    def _(which=which):
                        for part in range(count):
                            at = slice(part * own_rows, (part + 1) * own_rows)
                            mine = table[at, which * half_e : (which + 1) * half_e]
                            partial_e[part] = (mine + swap_in[at, :].astype(F32)).astype(BF)

            @pl.when((number >= steps) & (number < steps + count - 1))
            def _():
                early_step(number - steps)

        def after(slot):
            @pl.when(slot % each == each - 1)
            def _():
                skip_block(slot // each)

        line_reduce_all(
            grad_line, steps, compute, partial_g, left_g, right_g, sr_g, sl_g, finish, beside, after
        )

        g_shift = g_sum[...]
        shift_in[0] = g_shift
        swap_shift = push(shift_in.at[0], shift_in.at[1], ssem.at[2], rsem.at[2], peer)
        swap_shift.start()
        mod_u = dot_nt(act_low, down_of(dtab, 1))
        once = jnp.where(me == 0, 1.0, 0.0)
        shift_u = dot_nt(g_shift.astype(BF), up_of(utab, 1))
        zeros_u, zeros_w = jnp.zeros((7, RANK), F32), jnp.zeros((7, width), F32)
        mod_a = jnp.concatenate([shift_u * once, zeros_u], axis=0).astype(BF)
        mod_b = jnp.concatenate([mod_u * once, zeros_u], axis=0).astype(BF)
        act_pad = jnp.concatenate([act_low.astype(F32), zeros_w], axis=0).astype(BF)
        shift_pad = jnp.concatenate([g_shift, zeros_w], axis=0).astype(BF)
        late[:, IN_AT[1] : IN_AT[2]] = dot_tn(mod_a, act_pad)
        late[:, EARLY_A + OUT_AT[1] : EARLY_A + OUT_AT[2]] = dot_tn(mod_b, shift_pad)
        for which in range(2):
            @pl.when(core == which)
            def _(which=which):
                late_out[...] = late[:, (1 - which) * half_l : (2 - which) * half_l].astype(BF)

        swap_late = push(late_out, late_in, ssem.at[1], rsem.at[1], peer)
        swap_late.start()
        swap_shift.wait()
        shifts[dp] = shift_in[0] + shift_in[1]
        shift_sends = [
            push(shifts.at[dp], shifts.at[dp], msend.at[0, number], mrecv.at[0, number], device)
            for number, device in enumerate(peers)
        ]
        for send in shift_sends:
            send.start()
        swap_late.wait()
        for which in range(2):
            @pl.when(core == which)
            def _(which=which):
                for part in range(count):
                    at = slice(part * own_rows, (part + 1) * own_rows)
                    mine = late[at, which * half_l : (which + 1) * half_l]
                    partial_l[part] = (mine + late_in[at, :].astype(F32)).astype(BF)

        late_sends = [
            push(partial_l.at[xor_place(me, number + 1)], slots_l.at[me], zsend.at[number], zrecv.at[number], device)
            for number, device in enumerate(z_peers)
        ]
        for send in late_sends:
            send.start()
        slots_l[me] = partial_l[me]
        for number in (1, 2, 3):
            source = shifts.at[xor_place(dp, number)]
            push(source, source, msend.at[0, number - 1], mrecv.at[0, number - 1], peers[number - 1]).wait_recv()
        every = jnp.concatenate([shifts[sequence] for sequence in range(4)], axis=0).astype(BF)
        products = dot_nt(every, wm[...])
        for sequence in range(4):
            act_out[sequence] = products[sequence : sequence + 1]
        act_sends = [
            push(act_out.at[xor_place(dp, number)], act_in.at[dp], msend.at[1, number - 1], mrecv.at[1, number - 1],
                 peers[number - 1])
            for number in (1, 2, 3)
        ]
        for send in act_sends:
            send.start()
        line_scatter_finish(early_line, partial_e, left_e, right_e, sr_e, sl_e, summed)
        slots[dp, :, :half_e] = summed[...].astype(BF)
        for number in range(count - 1):
            arrived = slots_l.at[xor_place(me, number + 1)]
            push(arrived, arrived, zsend.at[number], zrecv.at[number], z_peers[number]).wait_recv()
        late_sum = slots_l[0].astype(F32)
        for place in range(1, count):
            late_sum = late_sum + slots_l[place].astype(F32)
        slots[dp, :, half_e:] = late_sum.astype(BF)
        sends = [
            push(slots.at[dp], slots.at[dp], dsend.at[number], drecv.at[number], device)
            for number, device in enumerate(peers)
        ]
        for send in sends:
            send.start()

        act_in[dp] = act_out[dp]
        for number in (1, 2, 3):
            source = act_in.at[xor_place(dp, number)]
            push(source, source, msend.at[1, number - 1], mrecv.at[1, number - 1], peers[number - 1]).wait_recv()
        for place in range(4):
            g_act[:, place * mod_rows : (place + 1) * mod_rows] = act_in[place]
        full_u = dot_nt(shifts[dp].astype(BF), up_of(utab, 1)).astype(BF)
        grad = g_act[...] + dot_nn(full_u, down_of(dtab, 1))
        value = cond[...].astype(F32)
        gate = 1.0 / (1.0 + jnp.exp(-value))
        out_c[...] = grad * gate * (1.0 + value * (1.0 - gate))

        for number in (1, 2, 3):
            source = slots.at[xor_place(dp, number)]
            push(source, source, dsend.at[number - 1], drecv.at[number - 1], peers[number - 1]).wait_recv()

        def total(which):
            slot = (dp * 2 + which).astype(F32)
            result = jnp.zeros((own_rows, half_e + half_l), F32)
            for sequence in range(4):
                chosen = jnp.where(act_ref[sequence, :, width : width + 1] == slot, 1.0, 0.0)
                result = result + slots[sequence].astype(F32) * chosen
            return result

        other_out[...] = total(1 - core).astype(BF)
        last = push(other_out, other_in, ssem.at[3], rsem.at[3], peer)
        last.start()
        mine = total(core)
        last.wait_recv()
        other = other_in[...].astype(F32)
        for which in range(2):
            @pl.when(core == which)
            def _(which=which):
                both = (mine, other) if which == 0 else (other, mine)
                first = jnp.concatenate([piece[:, :half_e] for piece in both], axis=1)
                second = jnp.concatenate([piece[:, half_e:] for piece in both], axis=1)
                out_a[:, :EARLY_A] = second[:, :EARLY_A]
                out_a[:, EARLY_A:] = first[:, :base]
                out_b[:, :EARLY_B] = second[:, EARLY_A:LATE]
                out_b[:, EARLY_B:] = first[:, base:EARLY]

        last.wait_send()
        for send in sends + shift_sends + act_sends + late_sends:
            send.wait_send()

        def drain(number, carry):
            rows = rows_of(number, block)
            pltpu.make_async_copy(buf_h.at[number], out_h.at[rows, :], osem.at[0, number]).wait()
            pltpu.make_async_copy(buf_l.at[number], out_l.at[rows, :], osem.at[1, number]).wait()
            return carry

        lax.fori_loop(0, count, drain, 0)

    part_e = (own_rows, half_e)
    part_l = (own_rows, half_l)
    part = (own_rows, half_e + half_l)
    return call(
        kernel,
        [(array, True) for array in (*grads, *projections, attn_in, g_first, skip_out, hidden, long_skip)]
        + [(weight, False)]
        + [(array, True) for array in (mod_weight, gain_halves, gain_rows, *tables, condition, act_all, *wide, *own_grads,
                                       *stack)],
        [
            ((tokens, width), F32, False),
            ((tokens, width), F32, False),
            ((own_rows, IN_AT[12]), F32, True),
            ((own_rows, OUT_AT[12]), F32, True),
            ((1, width), F32, True),
        ],
        [
            vmem(count, width, span),
            vmem(count, block, width, dtype=F32),
            vmem(count, block, width, dtype=F32),
            vmem(block, 2 * width, dtype=F32),
            vmem(tokens, width, dtype=F32),
            vmem(3 * RANK, width),
            vmem(RANK, local), vmem(RANK, local), vmem(RANK, local),
        ]
        + [vmem(steps, chunk, width) for _ in range(5)]
        + [vmem(RANK, 2 * half_e, dtype=F32), vmem(RANK, 2 * half_l, dtype=F32), vmem(RANK, half_e), vmem(RANK, half_e)]
        + [vmem(count, *part_e) for _ in range(5)]
        + [vmem(*part_e, dtype=F32), vmem(RANK, half_l), vmem(RANK, half_l), vmem(count, *part_l), vmem(count, *part_l)]
        + [vmem(4, *part), vmem(*part), vmem(*part)]
        + [vmem(4, 1, width, dtype=F32), vmem(2, 1, width, dtype=F32), vmem(4, 1, mod_rows, dtype=F32),
           vmem(4, 1, mod_rows, dtype=F32), vmem(1, width, dtype=F32), vmem(1, width, dtype=F32)]
        + [dma(), dma(2, count), dma(4), dma(4), dma(3), dma(3), dma(2, 3), dma(2, 3), dma(count), dma(count)]
        + [dma(steps) for _ in range(4)] + [dma(count) for _ in range(4)],
        collective=5,
        cost=cost_of(4 * tokens * width * width, 30e6),
    )


def fused_body(
    hidden,
    long_skip_input,
    condition,
    projected_text_tokens,
    sequence_adapter_index,
    skip_projection_weight,
    shift_modulation_weight,
    self_query_weight,
    self_key_weight,
    self_value_weight,
    attention_output_weight,
    cross_query_weight,
    cross_key_weight,
    cross_value_weight,
    cross_output_weight,
    feedforward_up_weight,
    feedforward_down_weight,
    skip_norm_gain,
    norm_gain_rows,
    adapter_down_factor,
    adapter_up_factor,
    cotangent,
):
    rank = lax.axis_index("tensor")
    count = lax.axis_size("tensor")
    core = lax.axis_index("ctx")
    dp = lax.axis_index("dp")
    hidden, long_skip, text, cot = hidden[0], long_skip_input[0], projected_text_tokens[0], cotangent[0]
    local = self_query_weight.shape[1]
    heads = local // HD
    index = sequence_adapter_index[0]
    tables = (
        lax.dynamic_index_in_dim(adapter_down_factor, index, 0, keepdims=False),
        lax.dynamic_index_in_dim(adapter_up_factor, index, 0, keepdims=False),
    )
    gain_halves = skip_norm_gain.reshape(2, MODEL_WIDTH)

    weights = {
        "skip": skip_projection_weight.T,
        "q": self_query_weight,
        "k": self_key_weight,
        "v": self_value_weight,
        "o": attention_output_weight.T,
        "ck": cross_key_weight.T,
        "cv": cross_value_weight.T,
        "cq": cross_query_weight,
        "co": cross_output_weight.T,
        "up": feedforward_up_weight,
        "dn": feedforward_down_weight.T,
    }
    (skip_out, attn_in, query, keys, values, low, logs, inv_q, inv_k, summed, act_all, text_kv, wq, wk, wv, wo, wcq, wco,
     wup) = front(
        count, heads, condition, sequence_adapter_index, hidden, long_skip, text, weights, shift_modulation_weight,
        gain_halves, norm_gain_rows, tables,
    )
    (g_first, block_sum, g_cq_a, g_cq_b, g_ck_a, g_ck_b, g_cv_a, g_cv_b, g_co_a, g_co_b, g_up_a, g_up_b, g_down_a, g_down_b,
     skip_all) = middle(
        count, heads, summed, skip_out, wcq, wco, wup, weights["dn"], weights["skip"], text_kv, text, cot, norm_gain_rows,
        tables,
    )
    gq, gk, gv, g_first_all, block_all, g_o_a, g_o_b = attention_backward(
        count, heads, g_first, block_sum, query, keys, values, low, logs, inv_q, inv_k, wo, tables
    )
    block_out = block_all.reshape(hidden.shape)
    base = IN_AT[12]
    hidden_grad, skip_grad, grad_down, grad_up, g_condition = back_end(
        count, (gq, gk, gv), (wq, wk, wv), attn_in, g_first_all, skip_out, hidden, long_skip, skip_all,
        shift_modulation_weight, gain_halves, norm_gain_rows, tables, condition, act_all,
        {
            IN_AT[6]: g_cq_a, IN_AT[7]: g_ck_a, IN_AT[8]: g_cv_a, IN_AT[10]: g_up_a,
            base + OUT_AT[5]: g_o_b, base + OUT_AT[9]: g_co_b, base + OUT_AT[11]: g_down_b,
        },
        {IN_AT[5]: g_o_a, IN_AT[11]: g_down_a},
        {OUT_AT[10]: g_up_b},
        {
            IN_AT[9]: g_co_a, base + OUT_AT[6]: g_cq_b, base + OUT_AT[7]: g_ck_b, base + OUT_AT[8]: g_cv_b,
        },
    )
    size = MODEL_WIDTH // (2 * count)
    condition_gradient = lax.dynamic_slice_in_dim(g_condition[0], (core * count + rank) * size, size, 0)
    return (
        block_out[None],
        hidden_grad[None],
        skip_grad[None],
        condition_gradient,
        grad_down.reshape(-1),
        grad_up.reshape(-1),
    )


def solution(mesh):
    in_specs = (
        P("dp", "ctx", None),
        P("dp", "ctx", None),
        P("dp", None),
        P("dp", None, None),
        P("dp"),
        P("tensor", "dp"),
        P("dp", None),
        P("dp", "tensor"),
        P("dp", "tensor"),
        P("dp", "tensor"),
        P("tensor", "dp"),
        P("dp", "tensor"),
        P("dp", "tensor"),
        P("dp", "tensor"),
        P("tensor", "dp"),
        P("dp", "tensor"),
        P("tensor", "dp"),
        P(),
        P(),
        P(),
        P(),
        P("dp", "ctx", None),
    )
    out_specs = (
        P("dp", "ctx", None),
        P("dp", "ctx", None),
        P("dp", "ctx", None),
        P(("dp", "ctx", "tensor")),
        P(("dp", "ctx", "tensor")),
        P(("dp", "ctx", "tensor")),
    )
    shape = mesh.shape
    fused = shape["dp"] == 4 and shape["ctx"] == 2 and shape["tensor"] == 4
    return jax.shard_map(fused_body if fused else body, mesh=mesh, in_specs=in_specs, out_specs=out_specs, check_vma=False)
```

```python
from functools import partial

import jax
import jax.numpy as jnp
from jax import lax
from jax.experimental import pallas as pl
from jax.experimental.pallas import tpu as pltpu
from jax.sharding import PartitionSpec as P

MODEL_WIDTH = 1408
HD = 88
FF = 6144
TW = 1024


PRECISE = lax.Precision.HIGHEST
NORM_EPS = 1e-06


def row_norm(values):
    centered = values - jnp.mean(values, axis=-1, keepdims=True)
    inverse = lax.rsqrt(jnp.mean(centered * centered, axis=-1, keepdims=True) + NORM_EPS)
    return (centered * inverse, inverse)


def head_norm(values, head_width):
    shaped = values.reshape(values.shape[:-1] + (values.shape[-1] // head_width, head_width))
    centered = shaped - jnp.mean(shaped, axis=-1, keepdims=True)
    inverse = lax.rsqrt(jnp.mean(centered * centered, axis=-1, keepdims=True) + NORM_EPS)
    return (centered * inverse, inverse)


def norm_back(normal, inverse, grad_normal):
    return inverse * (
        grad_normal
        - jnp.mean(grad_normal, axis=-1, keepdims=True)
        - normal * jnp.mean(grad_normal * normal, axis=-1, keepdims=True)
    )


def split_parts(values):
    if values.dtype == jnp.bfloat16:
        return [values]
    upper_half = values.astype(jnp.bfloat16)
    lower_half = (values - upper_half.astype(jnp.float32)).astype(jnp.bfloat16)
    return [upper_half, lower_half]


def paired_product(form, left, right):
    total = None
    for left_number, left_part in enumerate(split_parts(left)):
        for right_number, right_part in enumerate(split_parts(right)):
            if left_number + right_number < 2:
                term = jnp.einsum(form, left_part, right_part, preferred_element_type=jnp.float32)
                total = term if total is None else total + term
    return total


def lowrank_out(input_list, weight_matrix, down_piece, up_factor_piece):
    frozen_term = jnp.einsum(
        "gtb,bx->gtx", input_list, weight_matrix, preferred_element_type=jnp.float32
    )
    rank_activation = jnp.einsum(
        "snd,srd->snr", input_list, down_piece, preferred_element_type=jnp.float32
    )
    adapter_term = paired_product("dti,dip->dtp", rank_activation, up_factor_piece)
    return (frozen_term + adapter_term, rank_activation)


def lowrank_back(
    input_list,
    weight_matrix,
    down_piece,
    up_factor_piece,
    rank_activation,
    output_gradient,
    want_input,
):
    upper_gradient = paired_product("pmf,pmz->pfz", rank_activation, output_gradient)
    rank_gradient = paired_product("hzu,hlu->hzl", output_gradient, up_factor_piece)
    grad_lower = paired_product("snr,snd->srd", rank_gradient, input_list)
    if want_input:
        input_gradients = paired_product("lga,wa->lgw", output_gradient, weight_matrix)
        input_gradients = input_gradients + paired_product(
            "snr,srd->snd", rank_gradient, down_piece
        )
        return (input_gradients, grad_lower, upper_gradient)
    return (None, grad_lower, upper_gradient)


def attend_forward(query, key_rows, values_in, scale_factor):
    scores = (
        jnp.einsum("snhe,smhe->shnm", query, key_rows, preferred_element_type=jnp.float32)
        * scale_factor
    )
    row_top = jnp.max(scores, axis=-1, keepdims=True)
    exp_scores = jnp.exp(scores - row_top)
    row_total = jnp.sum(exp_scores, axis=-1, keepdims=True)
    attn_probs = (exp_scores / row_total).astype(jnp.bfloat16)
    result = jnp.einsum(
        "shnm,smhe->snhe", attn_probs, values_in, preferred_element_type=jnp.float32
    )
    return (result, row_top + jnp.log(row_total))


def attend_back(query, key_rows, values_in, log_total, grad_result, scale_factor):
    scores = (
        jnp.einsum("snhe,smhe->shnm", query, key_rows, preferred_element_type=jnp.float32)
        * scale_factor
    )
    attn_probs = jnp.exp(scores - log_total)
    grad_probs = jnp.einsum(
        "snhe,smhe->shnm", grad_result, values_in, preferred_element_type=jnp.float32
    )
    row_inner = jnp.sum(attn_probs * grad_probs, axis=-1, keepdims=True)
    grad_scores = (attn_probs * (grad_probs - row_inner)).astype(jnp.bfloat16)
    grad_query = (
        jnp.einsum("shnm,smhe->snhe", grad_scores, key_rows, preferred_element_type=jnp.float32)
        * scale_factor
    )
    grad_keys = (
        jnp.einsum("shnm,snhe->smhe", grad_scores, query, preferred_element_type=jnp.float32)
        * scale_factor
    )
    grad_values = jnp.einsum(
        "shnm,snhe->smhe",
        attn_probs.astype(jnp.bfloat16),
        grad_result,
        preferred_element_type=jnp.float32,
    )
    return (grad_query, grad_keys, grad_values)


def body(
    hidden,
    long_skip_input,
    condition,
    projected_text_tokens,
    sequence_adapter_index,
    skip_projection_weight,
    shift_modulation_weight,
    self_query_weight,
    self_key_weight,
    self_value_weight,
    attention_output_weight,
    cross_query_weight,
    cross_key_weight,
    cross_value_weight,
    cross_output_weight,
    feedforward_up_weight,
    feedforward_down_weight,
    skip_norm_gain,
    norm_gain_rows,
    adapter_down_factor,
    adapter_up_factor,
    cotangent,
):
    (
        skip_projection_weight,
        shift_modulation_weight,
        self_query_weight,
        self_key_weight,
        self_value_weight,
        attention_output_weight,
        cross_query_weight,
        cross_key_weight,
        cross_value_weight,
        cross_output_weight,
        feedforward_up_weight,
        feedforward_down_weight,
    ) = (
        lax.all_gather(skip_projection_weight, "dp", axis=1, tiled=True),
        lax.all_gather(shift_modulation_weight, "dp", axis=0, tiled=True),
        lax.all_gather(self_query_weight, "dp", axis=0, tiled=True),
        lax.all_gather(self_key_weight, "dp", axis=0, tiled=True),
        lax.all_gather(self_value_weight, "dp", axis=0, tiled=True),
        lax.all_gather(attention_output_weight, "dp", axis=1, tiled=True),
        lax.all_gather(cross_query_weight, "dp", axis=0, tiled=True),
        lax.all_gather(cross_key_weight, "dp", axis=0, tiled=True),
        lax.all_gather(cross_value_weight, "dp", axis=0, tiled=True),
        lax.all_gather(cross_output_weight, "dp", axis=1, tiled=True),
        lax.all_gather(feedforward_up_weight, "dp", axis=0, tiled=True),
        lax.all_gather(feedforward_down_weight, "dp", axis=1, tiled=True),
    )
    tensor_rank = lax.axis_index("tensor")
    tensor_count = lax.axis_size("tensor")
    seqs_local = hidden.shape[0]
    tokens_local = hidden.shape[1]
    local_width = self_query_weight.shape[1]
    heads_local = local_width // HD
    ff_local = feedforward_up_weight.shape[1]
    skip_width = skip_projection_weight.shape[0]
    scale_factor = HD ** (-0.5)
    in_sizes = [
        2 * MODEL_WIDTH,
        MODEL_WIDTH,
        MODEL_WIDTH,
        MODEL_WIDTH,
        MODEL_WIDTH,
        MODEL_WIDTH,
        MODEL_WIDTH,
        TW,
        TW,
        MODEL_WIDTH,
        MODEL_WIDTH,
        FF,
    ]
    out_sizes = [MODEL_WIDTH] * 10 + [FF, MODEL_WIDTH]
    input_offsets = [sum(in_sizes[:number]) for number in range(12)]
    output_offsets = [sum(out_sizes[:number]) for number in range(12)]
    select_adapter = (
        sequence_adapter_index[:, None]
        == jnp.arange(adapter_down_factor.shape[0], dtype=jnp.int32)[None, :]
    )
    choose_wide = select_adapter.astype(jnp.float32)
    down_seq = jnp.einsum(
        "fn,nge->fge",
        select_adapter.astype(jnp.bfloat16),
        adapter_down_factor,
        preferred_element_type=jnp.float32,
    ).astype(jnp.bfloat16)
    up_seq = jnp.einsum(
        "fn,nge->fge",
        select_adapter.astype(jnp.bfloat16),
        adapter_up_factor,
        preferred_element_type=jnp.float32,
    ).astype(jnp.bfloat16)

    def down_full(number):
        return down_seq[:, :, input_offsets[number] : input_offsets[number] + in_sizes[number]]

    def up_full(number):
        return up_seq[:, :, output_offsets[number] : output_offsets[number] + out_sizes[number]]

    def down_local(number, span_width):
        return lax.dynamic_slice_in_dim(
            down_seq, input_offsets[number] + tensor_rank * span_width, span_width, 2
        )

    def up_local(number, span_width):
        return lax.dynamic_slice_in_dim(
            up_seq, output_offsets[number] + tensor_rank * span_width, span_width, 2
        )

    def to_slots(grad_piece):
        return jnp.einsum("si,srd->ird", choose_wide, grad_piece, precision=PRECISE)

    joined = jnp.concatenate([hidden, long_skip_input], axis=-1).astype(jnp.float32)
    joined_normal, joined_inverse = row_norm(joined)
    joined_low = (joined_normal * skip_norm_gain).astype(jnp.bfloat16)
    joined_part = lax.dynamic_slice_in_dim(joined_low, tensor_rank * skip_width, skip_width, 2)
    skip_partial, skip_rank = lowrank_out(
        joined_part, skip_projection_weight, down_local(0, skip_width), up_full(0)
    )
    skip_out = lax.psum(skip_partial.astype(jnp.bfloat16), "tensor").astype(jnp.float32)
    act_wide, silu_pull = jax.vjp(jax.nn.silu, condition.astype(jnp.float32))
    act_low = act_wide.astype(jnp.bfloat16)[:, None, :]
    shift_row, mod_rank = lowrank_out(act_low, shift_modulation_weight, down_full(1), up_full(1))
    first_normal, first_inverse = row_norm(skip_out)
    attn_in = (first_normal * norm_gain_rows[0] + shift_row).astype(jnp.bfloat16)
    query_proj, query_rank = lowrank_out(
        attn_in, self_query_weight, down_full(2), up_local(2, local_width)
    )
    key_proj, key_rank = lowrank_out(
        attn_in, self_key_weight, down_full(3), up_local(3, local_width)
    )
    value_proj, value_rank = lowrank_out(
        attn_in, self_value_weight, down_full(4), up_local(4, local_width)
    )
    query_normal, query_inverse = head_norm(query_proj, HD)
    key_normal, key_inverse = head_norm(key_proj, HD)
    query_low = query_normal.astype(jnp.bfloat16)
    key_low = key_normal.astype(jnp.bfloat16).reshape(seqs_local, tokens_local, local_width)
    value_low = value_proj.astype(jnp.bfloat16)
    keys_all, values_all = (
        lax.all_gather(key_low, "ctx", axis=1, tiled=True),
        lax.all_gather(value_low, "ctx", axis=1, tiled=True),
    )
    keys_four = keys_all.reshape(seqs_local, -1, heads_local, HD)
    values_four = values_all.reshape(seqs_local, -1, heads_local, HD)
    attn_result, attn_log = attend_forward(query_low, keys_four, values_four, scale_factor)
    attn_low = attn_result.reshape(seqs_local, tokens_local, local_width).astype(jnp.bfloat16)
    attn_partial, out_rank = lowrank_out(
        attn_low, attention_output_weight, down_local(5, local_width), up_full(5)
    )
    first_res = skip_out + lax.psum(attn_partial.astype(jnp.bfloat16), "tensor").astype(jnp.float32)
    second_normal, second_inverse = row_norm(first_res)
    cross_in = (second_normal * norm_gain_rows[1]).astype(jnp.bfloat16)
    cquery_proj, cquery_rank = lowrank_out(
        cross_in, cross_query_weight, down_full(6), up_local(6, local_width)
    )
    ckey_proj, ckey_rank = lowrank_out(
        projected_text_tokens, cross_key_weight, down_full(7), up_local(7, local_width)
    )
    cvalue_proj, cvalue_rank = lowrank_out(
        projected_text_tokens, cross_value_weight, down_full(8), up_local(8, local_width)
    )
    cquery_normal, cquery_inverse = head_norm(cquery_proj, HD)
    ckey_normal, ckey_inverse = head_norm(ckey_proj, HD)
    cquery_low = cquery_normal.astype(jnp.bfloat16)
    ckey_low = ckey_normal.astype(jnp.bfloat16)
    cvalue_low = cvalue_proj.astype(jnp.bfloat16).reshape(seqs_local, -1, heads_local, HD)
    cross_result, cross_log = attend_forward(cquery_low, ckey_low, cvalue_low, scale_factor)
    cross_low = cross_result.reshape(seqs_local, tokens_local, local_width).astype(jnp.bfloat16)
    cross_partial, cout_rank = lowrank_out(
        cross_low, cross_output_weight, down_local(9, local_width), up_full(9)
    )
    second_res = first_res + lax.psum(cross_partial.astype(jnp.bfloat16), "tensor").astype(
        jnp.float32
    )
    third_normal, third_inverse = row_norm(second_res)
    mlp_in = (third_normal * norm_gain_rows[2]).astype(jnp.bfloat16)
    up_proj, up_rank = lowrank_out(
        mlp_in, feedforward_up_weight, down_full(10), up_local(10, ff_local)
    )
    activated, gelu_pull = jax.vjp(partial(jax.nn.gelu, approximate=True), up_proj)
    activated_low = activated.astype(jnp.bfloat16)
    down_partial, down_rank = lowrank_out(
        activated_low, feedforward_down_weight, down_local(11, ff_local), up_full(11)
    )
    block_out = second_res + lax.psum(down_partial.astype(jnp.bfloat16), "tensor").astype(
        jnp.float32
    )
    grad_act, grad_down_lower, grad_down_upper = lowrank_back(
        activated_low,
        feedforward_down_weight,
        down_local(11, ff_local),
        up_full(11),
        down_rank,
        cotangent,
        True,
    )
    grad_pre = gelu_pull(grad_act)[0].astype(jnp.bfloat16)
    grad_mlp_in, grad_up_lower, grad_up_upper = lowrank_back(
        mlp_in,
        feedforward_up_weight,
        down_full(10),
        up_local(10, ff_local),
        up_rank,
        grad_pre,
        True,
    )
    grad_mlp_in = lax.psum(grad_mlp_in.astype(jnp.bfloat16), "tensor").astype(jnp.float32)
    grad_second = cotangent.astype(jnp.float32) + norm_back(
        third_normal, third_inverse, grad_mlp_in * norm_gain_rows[2]
    )
    grad_cross_low, grad_cout_lower, grad_cout_upper = lowrank_back(
        cross_low,
        cross_output_weight,
        down_local(9, local_width),
        up_full(9),
        cout_rank,
        grad_second.astype(jnp.bfloat16),
        True,
    )
    grad_cross_result = grad_cross_low.astype(jnp.bfloat16).reshape(
        seqs_local, tokens_local, heads_local, HD
    )
    grad_cquery, grad_ckey, grad_cvalue = attend_back(
        cquery_low, ckey_low, cvalue_low, cross_log, grad_cross_result, scale_factor
    )
    grad_cquery_proj = (
        norm_back(cquery_normal, cquery_inverse, grad_cquery)
        .reshape(seqs_local, tokens_local, local_width)
        .astype(jnp.bfloat16)
    )
    grad_ckey_proj = norm_back(ckey_normal, ckey_inverse, grad_ckey).reshape(
        seqs_local, -1, local_width
    )
    none_first, grad_ckey_lower, grad_ckey_upper = lowrank_back(
        projected_text_tokens,
        cross_key_weight,
        down_full(7),
        up_local(7, local_width),
        ckey_rank,
        grad_ckey_proj,
        False,
    )
    none_second, grad_cvalue_lower, grad_cvalue_upper = lowrank_back(
        projected_text_tokens,
        cross_value_weight,
        down_full(8),
        up_local(8, local_width),
        cvalue_rank,
        grad_cvalue.reshape(seqs_local, -1, local_width),
        False,
    )
    grad_cross_in, grad_cquery_lower, grad_cquery_upper = lowrank_back(
        cross_in,
        cross_query_weight,
        down_full(6),
        up_local(6, local_width),
        cquery_rank,
        grad_cquery_proj,
        True,
    )
    grad_cross_in = lax.psum(grad_cross_in.astype(jnp.bfloat16), "tensor").astype(jnp.float32)
    grad_first = grad_second + norm_back(
        second_normal, second_inverse, grad_cross_in * norm_gain_rows[1]
    )
    grad_attn_low, grad_aout_lower, grad_aout_upper = lowrank_back(
        attn_low,
        attention_output_weight,
        down_local(5, local_width),
        up_full(5),
        out_rank,
        grad_first.astype(jnp.bfloat16),
        True,
    )
    grad_attn_result = grad_attn_low.astype(jnp.bfloat16).reshape(
        seqs_local, tokens_local, heads_local, HD
    )
    grad_query, grad_keys_all, grad_values_all = attend_back(
        query_low, keys_four, values_four, attn_log, grad_attn_result, scale_factor
    )
    grad_keys, grad_values = (
        lax.psum_scatter(
            grad_keys_all.reshape(seqs_local, -1, local_width).astype(jnp.bfloat16),
            "ctx",
            scatter_dimension=1,
            tiled=True,
        ).astype(jnp.float32),
        lax.psum_scatter(
            grad_values_all.reshape(seqs_local, -1, local_width).astype(jnp.bfloat16),
            "ctx",
            scatter_dimension=1,
            tiled=True,
        ).astype(jnp.float32),
    )
    grad_query_proj = (
        norm_back(query_normal, query_inverse, grad_query)
        .reshape(seqs_local, tokens_local, local_width)
        .astype(jnp.bfloat16)
    )
    grad_key_proj = (
        norm_back(
            key_normal, key_inverse, grad_keys.reshape(seqs_local, tokens_local, heads_local, HD)
        )
        .reshape(seqs_local, tokens_local, local_width)
        .astype(jnp.bfloat16)
    )
    grad_value_proj = grad_values.astype(jnp.bfloat16)
    grad_in_query, grad_query_lower, grad_query_upper = lowrank_back(
        attn_in,
        self_query_weight,
        down_full(2),
        up_local(2, local_width),
        query_rank,
        grad_query_proj,
        True,
    )
    grad_in_key, grad_key_lower, grad_key_upper = lowrank_back(
        attn_in,
        self_key_weight,
        down_full(3),
        up_local(3, local_width),
        key_rank,
        grad_key_proj,
        True,
    )
    grad_in_value, grad_value_lower, grad_value_upper = lowrank_back(
        attn_in,
        self_value_weight,
        down_full(4),
        up_local(4, local_width),
        value_rank,
        grad_value_proj,
        True,
    )
    grad_attn_in = lax.psum(
        (grad_in_query + grad_in_key + grad_in_value).astype(jnp.bfloat16), "tensor"
    ).astype(jnp.float32)
    grad_shift = jnp.sum(grad_attn_in, axis=1, keepdims=True) / tensor_count
    grad_act_low, grad_mod_lower, grad_mod_upper = lowrank_back(
        act_low, shift_modulation_weight, down_full(1), up_full(1), mod_rank, grad_shift, True
    )
    grad_condition = silu_pull(grad_act_low[:, 0, :])[0]
    grad_skip_out = grad_first + norm_back(
        first_normal, first_inverse, grad_attn_in * norm_gain_rows[0]
    )
    grad_joined_part, grad_skip_lower, grad_skip_upper = lowrank_back(
        joined_part,
        skip_projection_weight,
        down_local(0, skip_width),
        up_full(0),
        skip_rank,
        grad_skip_out.astype(jnp.bfloat16),
        True,
    )
    grad_joined = lax.all_gather(
        grad_joined_part.astype(jnp.bfloat16), "tensor", axis=2, tiled=True
    ).astype(grad_joined_part.dtype)
    grad_joined_full = norm_back(joined_normal, joined_inverse, grad_joined * skip_norm_gain)
    hidden_grad = grad_joined_full[:, :, :MODEL_WIDTH]
    skip_grad = grad_joined_full[:, :, MODEL_WIDTH:]
    lower_factor_parts = [
        (0, grad_skip_lower, True),
        (1, grad_mod_lower, False),
        (2, grad_query_lower, False),
        (3, grad_key_lower, False),
        (4, grad_value_lower, False),
        (5, grad_aout_lower, True),
        (6, grad_cquery_lower, False),
        (7, grad_ckey_lower, False),
        (8, grad_cvalue_lower, False),
        (9, grad_cout_lower, True),
        (10, grad_up_lower, False),
        (11, grad_down_lower, True),
    ]
    upper_factor_parts = [
        (0, grad_skip_upper, False),
        (1, grad_mod_upper, False),
        (2, grad_query_upper, True),
        (3, grad_key_upper, True),
        (4, grad_value_upper, True),
        (5, grad_aout_upper, False),
        (6, grad_cquery_upper, True),
        (7, grad_ckey_upper, True),
        (8, grad_cvalue_upper, True),
        (9, grad_cout_upper, False),
        (10, grad_up_upper, True),
        (11, grad_down_upper, False),
    ]
    slot_total = adapter_down_factor.shape[0]
    rank_total = adapter_down_factor.shape[1]
    cond_buffer = jnp.zeros((lax.axis_size("dp") * seqs_local, MODEL_WIDTH), jnp.float32)
    cond_buffer = lax.dynamic_update_slice_in_dim(
        cond_buffer, grad_condition, lax.axis_index("dp") * seqs_local, 0
    )
    cond_flat = cond_buffer.reshape(-1)

    def dense_table(parts_list, starts, total_width, row_count, slot_pieces):
        table = jnp.zeros((row_count, total_width), jnp.float32)
        for position, (number, grad_piece, is_local) in enumerate(parts_list):
            span_width = grad_piece.shape[2]
            column_start = starts[number] + tensor_rank * span_width if is_local else starts[number]
            table = lax.dynamic_update_slice_in_dim(table, slot_pieces[position], column_start, 1)
        return table

    down_factor_slots = [
        to_slots(grad_piece).reshape(slot_total * rank_total, -1)
        for number, grad_piece, is_local in lower_factor_parts
    ]
    up_factor_slots = [
        to_slots(grad_piece).reshape(slot_total * rank_total, -1)
        for number, grad_piece, is_local in upper_factor_parts
    ]
    down_compact = jnp.concatenate(down_factor_slots, axis=1)
    up_compact = jnp.concatenate(up_factor_slots, axis=1)
    cond_rows, down_rows, up_rows = (
        lax.psum_scatter(
            cond_flat.astype(jnp.bfloat16), ("dp", "ctx"), scatter_dimension=0, tiled=True
        ).astype(jnp.float32),
        lax.psum_scatter(
            down_compact.astype(jnp.bfloat16), ("dp", "ctx"), scatter_dimension=0, tiled=True
        ).astype(jnp.float32),
        lax.psum_scatter(
            up_compact.astype(jnp.bfloat16), ("dp", "ctx"), scatter_dimension=0, tiled=True
        ).astype(jnp.float32),
    )
    row_count = down_rows.shape[0]
    down_widths = [grad_piece.shape[2] for number, grad_piece, is_local in lower_factor_parts]
    up_widths = [grad_piece.shape[2] for number, grad_piece, is_local in upper_factor_parts]
    down_pieces = [
        down_rows[:, sum(down_widths[:position]) : sum(down_widths[: position + 1])]
        for position in range(12)
    ]
    up_pieces = [
        up_rows[:, sum(up_widths[:position]) : sum(up_widths[: position + 1])]
        for position in range(12)
    ]
    down_block = dense_table(
        lower_factor_parts, input_offsets, adapter_down_factor.shape[2], row_count, down_pieces
    ).reshape(-1)
    up_block = dense_table(
        upper_factor_parts, output_offsets, adapter_up_factor.shape[2], row_count, up_pieces
    ).reshape(-1)
    condition_gradient, adapter_down_gradient, adapter_up_gradient = (
        lax.psum_scatter(
            cond_rows.astype(jnp.bfloat16), "tensor", scatter_dimension=0, tiled=True
        ).astype(jnp.float32),
        lax.psum_scatter(
            down_block.astype(jnp.bfloat16), "tensor", scatter_dimension=0, tiled=True
        ).astype(jnp.float32),
        lax.psum_scatter(
            up_block.astype(jnp.bfloat16), "tensor", scatter_dimension=0, tiled=True
        ).astype(jnp.float32),
    )
    return (
        block_out.astype(jnp.bfloat16),
        hidden_grad,
        skip_grad,
        condition_gradient,
        adapter_down_gradient,
        adapter_up_gradient,
    )


BF = jnp.bfloat16
F32 = jnp.float32
MESH_ID = pl.DeviceIdType.MESH
RANK = 16
CHUNK = 64
VMEM_BYTES = 60 << 20


def dot_nn(left, right):
    return jnp.dot(left, right, preferred_element_type=F32)


def dot_nt(left, right):
    return lax.dot_general(left, right, (((1,), (1,)), ((), ())), preferred_element_type=F32)


def dot_tn(left, right):
    return lax.dot_general(left, right, (((0,), (0,)), ((), ())), preferred_element_type=F32)


def stats(values):
    centered = values - jnp.mean(values, axis=-1, keepdims=True)
    inverse = lax.rsqrt(jnp.mean(centered * centered, axis=-1, keepdims=True) + NORM_EPS)
    return centered * inverse, inverse


def greet(partners):
    barrier = pltpu.get_barrier_semaphore()
    for condition, device in partners:
        @pl.when(condition)
        def _(device=device):
            pl.semaphore_signal(barrier, inc=1, device_id=device, device_id_type=MESH_ID)
    expected = sum(jnp.where(condition, 1, 0) for condition, _ in partners)
    pl.semaphore_wait(barrier, expected)


def line_partners(me, count):
    return [(me > 0, {"tensor": lax.max(me - 1, 0)}), (me < count - 1, {"tensor": lax.min(me + 1, count - 1)})]


def push(source, target, send_sem, recv_sem, device):
    return pltpu.make_async_remote_copy(
        src_ref=source,
        dst_ref=target,
        send_sem=send_sem,
        recv_sem=recv_sem,
        device_id=device,
        device_id_type=MESH_ID,
    )


class Line:
    def __init__(self, me, count, send_right, recv_left, send_left, recv_right):
        self.me, self.count = me, count
        self.sems = (send_right, recv_left, send_left, recv_right)
        self.left = {"tensor": lax.max(me - 1, 0)}
        self.right = {"tensor": lax.min(me + 1, count - 1)}
        self.has_left, self.has_right = me > 0, me < count - 1

    def to_right(self, source, target, slot):
        return push(source, target, self.sems[0].at[slot], self.sems[1].at[slot], self.right)

    def to_left(self, source, target, slot):
        return push(source, target, self.sems[2].at[slot], self.sems[3].at[slot], self.left)


def line_reduce_all(line, steps, compute, partial_ref, from_left, from_right, stage_right, stage_left, finish,
                    beside=None, after=None):
    me, count = line.me, line.count
    far = count - 1 - me

    def step(number, carry):
        @pl.when(number < steps)
        def _():
            compute(number)

        slot_r = number - me

        @pl.when((slot_r >= 0) & (slot_r < steps))
        def _():
            slot = lax.clamp(0, slot_r, steps - 1)

            @pl.when(line.has_left)
            def _():
                line.to_right(stage_right.at[slot], from_left.at[slot], slot).wait_recv()

            @pl.when(line.has_right)
            def _():
                @pl.when(line.has_left)
                def _():
                    total = partial_ref[slot].astype(F32) + from_left[slot].astype(F32)
                    stage_right[slot] = total.astype(BF)

                @pl.when(jnp.logical_not(line.has_left))
                def _():
                    stage_right[slot] = partial_ref[slot]

                line.to_right(stage_right.at[slot], from_left.at[slot], slot).start()

        slot_l = number - far

        @pl.when((slot_l >= 0) & (slot_l < steps))
        def _():
            slot = lax.clamp(0, slot_l, steps - 1)

            @pl.when(line.has_right)
            def _():
                line.to_left(stage_left.at[slot], from_right.at[slot], slot).wait_recv()

            @pl.when(line.has_left)
            def _():
                @pl.when(line.has_right)
                def _():
                    total = partial_ref[slot].astype(F32) + from_right[slot].astype(F32)
                    stage_left[slot] = total.astype(BF)

                @pl.when(jnp.logical_not(line.has_right))
                def _():
                    stage_left[slot] = partial_ref[slot]

                line.to_left(stage_left.at[slot], from_right.at[slot], slot).start()

        if beside is not None:
            beside(number)
        slot_f = number - lax.max(me, far)

        @pl.when((slot_f >= 0) & (slot_f < steps))
        def _():
            slot = lax.clamp(0, slot_f, steps - 1)

            @pl.when(jnp.logical_not(line.has_left))
            def _():
                finish(slot, partial_ref[slot].astype(F32) + from_right[slot].astype(F32))

            @pl.when(line.has_left)
            def _():
                @pl.when(line.has_right)
                def _():
                    finish(
                        slot,
                        partial_ref[slot].astype(F32)
                        + from_left[slot].astype(F32)
                        + from_right[slot].astype(F32),
                    )

                @pl.when(jnp.logical_not(line.has_right))
                def _():
                    finish(slot, partial_ref[slot].astype(F32) + from_left[slot].astype(F32))

            if after is not None:
                after(slot)

        return carry

    lax.fori_loop(0, steps + count - 1, step, 0)

    def drain(slot, carry):
        @pl.when(line.has_right)
        def _():
            line.to_right(stage_right.at[slot], from_left.at[slot], slot).wait_send()

        @pl.when(line.has_left)
        def _():
            line.to_left(stage_left.at[slot], from_right.at[slot], slot).wait_send()

        return carry

    lax.fori_loop(0, steps, drain, 0)


def scatter_order(me, count, place):
    near = lax.min(me, count - 1 - me)
    base = count - 1 - 2 * near
    index = place - base
    block = jnp.where(
        place < base,
        count - 1 - place,
        jnp.where(index % 2 == 0, 2 * near - index // 2, index // 2),
    )
    return jnp.where(2 * me > count - 1, count - 1 - block, block)


def line_scatter_step(line, number, partial_ref, from_left, from_right, stage_right, stage_left):
    me, count = line.me, line.count
    block_r = count - 1 - number + me

    @pl.when((number >= me) & line.has_right & (block_r > me))
    def _():
        block = lax.clamp(0, block_r, count - 1)

        @pl.when(line.has_left)
        def _():
            line.to_right(stage_right.at[block], from_left.at[block], block).wait_recv()
            total = partial_ref[block].astype(F32) + from_left[block].astype(F32)
            stage_right[block] = total.astype(BF)

        @pl.when(jnp.logical_not(line.has_left))
        def _():
            stage_right[block] = partial_ref[block]

        line.to_right(stage_right.at[block], from_left.at[block], block).start()

    block_l = number - (count - 1 - me)

    @pl.when((block_l >= 0) & line.has_left & (block_l < me))
    def _():
        block = lax.clamp(0, block_l, count - 1)

        @pl.when(line.has_right)
        def _():
            line.to_left(stage_left.at[block], from_right.at[block], block).wait_recv()
            total = partial_ref[block].astype(F32) + from_right[block].astype(F32)
            stage_left[block] = total.astype(BF)

        @pl.when(jnp.logical_not(line.has_right))
        def _():
            stage_left[block] = partial_ref[block]

        line.to_left(stage_left.at[block], from_right.at[block], block).start()


def line_scatter_finish(line, partial_ref, from_left, from_right, stage_right, stage_left, total_ref):
    me, count = line.me, line.count
    total_ref[...] = partial_ref[me].astype(F32)

    @pl.when(line.has_left)
    def _():
        line.to_right(stage_right.at[me], from_left.at[me], me).wait_recv()
        total_ref[...] += from_left[me].astype(F32)

    @pl.when(line.has_right)
    def _():
        line.to_left(stage_left.at[me], from_right.at[me], me).wait_recv()
        total_ref[...] += from_right[me].astype(F32)

    def drain(block, carry):
        @pl.when(block > me)
        def _():
            line.to_right(stage_right.at[block], from_left.at[block], block).wait_send()

        @pl.when(block < me)
        def _():
            line.to_left(stage_left.at[block], from_right.at[block], block).wait_send()

        return carry

    lax.fori_loop(0, count, drain, 0)


def line_gather_step(line, number, slots):
    me, count = line.me, line.count
    block_l = lax.clamp(0, me - number, count - 1)
    block_r = lax.clamp(0, me + number, count - 1)
    view = slots if callable(slots) else lambda block: slots.at[block]

    @pl.when(number <= me)
    def _():
        @pl.when(number > 0)
        def _():
            line.to_right(view(block_l), view(block_l), block_l).wait_recv()

        @pl.when(line.has_right)
        def _():
            line.to_right(view(block_l), view(block_l), block_l).start()

    @pl.when(me + number <= count - 1)
    def _():
        @pl.when(number > 0)
        def _():
            line.to_left(view(block_r), view(block_r), block_r).wait_recv()

        @pl.when(line.has_left)
        def _():
            line.to_left(view(block_r), view(block_r), block_r).start()


def line_gather_drain(line, slots):
    me, count = line.me, line.count
    view = slots if callable(slots) else lambda block: slots.at[block]

    def drain(block, carry):
        @pl.when((block <= me) & line.has_right)
        def _():
            line.to_right(view(block), view(block), block).wait_send()

        @pl.when((block >= me) & line.has_left)
        def _():
            line.to_left(view(block), view(block), block).wait_send()

        return carry

    lax.fori_loop(0, count, drain, 0)


def xor_place(place, number):
    if number == 0:
        return place
    if number == 1:
        return place + 1 - 2 * (place % 2)
    if number == 2:
        return place + 2 - 4 * (place // 2)
    return 3 - place


def call(kernel, inputs, outs, scratch, collective=None, cost=None):
    space = {True: pltpu.VMEM, False: pl.ANY, None: pltpu.SMEM}
    return pl.pallas_call(
        kernel,
        out_shape=[jax.ShapeDtypeStruct(shape, dtype) for shape, dtype, _ in outs],
        in_specs=[pl.BlockSpec(memory_space=space[where]) for _, where in inputs],
        out_specs=[pl.BlockSpec(memory_space=space[where]) for _, _, where in outs],
        scratch_shapes=scratch,
        cost_estimate=cost,
        compiler_params=pltpu.CompilerParams(
            collective_id=collective,
            has_side_effects=collective is not None,
            vmem_limit_bytes=VMEM_BYTES,
        ),
    )(*[array for array, _ in inputs])


def cost_of(flops, moved):
    return pl.CostEstimate(flops=int(flops), bytes_accessed=int(moved), transcendentals=0)


def vmem(*shape, dtype=BF):
    return pltpu.VMEM(shape, dtype)


def dma(*shape):
    return pltpu.SemaphoreType.DMA(shape)


def whole_wait(target, sem):
    pltpu.make_async_copy(target, target, sem).wait()


def rows_of(index, size):
    return pl.ds(pl.multiple_of(index * size, size), size)


IN_SIZES = [2 * MODEL_WIDTH] + [MODEL_WIDTH] * 6 + [TW, TW, MODEL_WIDTH, MODEL_WIDTH, FF]
OUT_SIZES = [MODEL_WIDTH] * 10 + [FF, MODEL_WIDTH]
IN_AT = [sum(IN_SIZES[:number]) for number in range(13)]
OUT_AT = [sum(OUT_SIZES[:number]) for number in range(13)]


def down_of(table, number):
    return table[:, IN_AT[number] : IN_AT[number + 1]]


def up_of(table, number):
    return table[:, OUT_AT[number] : OUT_AT[number + 1]]


def take_local(target, table, start, me, count):
    size = target.shape[-1]
    for place in range(count):
        @pl.when(me == place)
        def _(place=place):
            target[...] = table[:, start + place * size : start + (place + 1) * size]


def take_stack(target, table, start, count):
    size = target.shape[-1]
    for place in range(count):
        target[place] = table[:, start + place * size : start + (place + 1) * size]


def norm_backward(normal, inverse, grad):
    return inverse * (
        grad
        - jnp.mean(grad, axis=-1, keepdims=True)
        - normal * jnp.mean(grad * normal, axis=-1, keepdims=True)
    )


def middle(count, heads, summed, skip_out, query_weight, out_weight, up_weight, down_piece, skip_piece, text_kv, text,
           cotangent, gains, tables):
    share, width = summed.shape
    tokens = skip_out.shape[0]
    local = query_weight.shape[-1]
    units = up_weight.shape[1]
    words, text_width = text.shape
    rows, span = skip_piece.shape
    scale = HD ** (-0.5)
    part_rows = share // 2
    wide = count * part_rows

    def kernel(sum_ref, skip_hbm, q_hbm, o_hbm, u_hbm, d_own, piece, kv, text_hbm, cot_hbm, gain, dtab, utab,
               g_first, block_sum, ga_q, gb_q, ga_k, gb_k, ga_v, gb_v, ga_o, gb_o, g_ua, g_ub, g_da, g_db, skip_all,
               wq, wo, wu, wd, cot, t_ref, first_ref, second_ref, x_ref, x_low, q_ref, inv_ref, log_ref, low_ref, acc, b_ref, ao,
               bk, bv, ub, da, slots, skip_half, active, grads, u_all, ud_all, gu_all, gd_all, partial_g, left_g, right_g,
               sr_g, sl_g, partial_b, left_b, right_b, sr_b, sl_b, lsem, wsend, wrecv, zsend, zrecv, *sems):
        me = lax.axis_index("tensor")
        core = lax.axis_index("ctx")
        dp = lax.axis_index("dp")
        always = core >= 0
        half = pl.ds(pl.multiple_of(core * (rows // 2), 16), rows // 2)
        down_rows = d_own.shape[0]
        down_half = pl.ds(pl.multiple_of(core * (down_rows // 2), 16), down_rows // 2)
        mine = pl.ds(pl.multiple_of(dp * down_rows, 16), down_rows)
        loads = [
            pltpu.make_async_copy(source, target, lsem.at[number])
            for number, (source, target) in enumerate(
                ((skip_hbm.at[rows_of(me, share), :], first_ref), (piece.at[half, :], skip_half.at[me]), (q_hbm, wq),
                 (o_hbm, wo), (d_own, wd.at[mine, :]), (cot_hbm.at[:, 0], cot.at[0]), (u_hbm, wu), (text_hbm, t_ref),
                 (cot_hbm.at[:, 1], cot.at[1]))
            )
        ]
        for load in loads:
            load.start()
        gather_lines = [Line(me, count, *sems[:4]), Line(me, count, *sems[4:8])]
        grad_lines = [Line(me, count, *sems[8:12]), Line(me, count, *sems[12:16])]
        block_line = Line(me, count, *sems[16:])

        def gather(which, number):
            line_gather_step(gather_lines[which], number, slots.at[which])

        def scatter(which, number):
            line_scatter_step(
                grad_lines[which], number, partial_g.at[which], left_g.at[which], right_g.at[which], sr_g.at[which],
                sl_g.at[which],
            )

        down = Shared(wd, down_rows, (wsend, wrecv, 0))
        skip = Shared(skip_all, rows, (wsend, wrecv, 1), stacked=True)
        z_peers = [{"tensor": xor_place(me, number)} for number in range(1, count)]
        others = [{"dp": xor_place(dp, 1)}, {"dp": xor_place(dp, 2)}, {"ctx": 1 - core}]
        greet([(always, device) for device in z_peers + others])
        down.send_own(d_own.at[down_half, :])
        z_sends = [
            push(piece.at[half, :], skip_half.at[me], zsend.at[number], zrecv.at[number], device)
            for number, device in enumerate(z_peers)
        ]
        for send in z_sends:
            send.start()
        take_stack(b_ref, utab, OUT_AT[6], count)
        take_stack(ao, dtab, IN_AT[9], count)
        take_stack(bk, utab, OUT_AT[7], count)
        take_stack(bv, utab, OUT_AT[8], count)
        take_local(ub, utab, OUT_AT[10], me, count)
        take_local(da, dtab, IN_AT[11], me, count)

        loads[0].wait()
        first = first_ref[...] + sum_ref[...]
        first_ref[...] = first
        second_ref[...] = first
        normal, _ = stats(first)
        x = (normal * gain[1:2, :]).astype(BF)
        x_ref[...] = x
        u = dot_nt(x, down_of(dtab, 6)).astype(BF)
        loads[2].wait()
        loads[3].wait()

        def cross(place, u_low):
            y = dot_nn(x_ref[...], wq[place]) + dot_nn(u, b_ref[place])
            outs, inverses, logs = [], [], []
            for head in range(heads):
                at = slice(head * HD, (head + 1) * HD)
                normal, inverse = stats(y[:, at])
                q = normal.astype(BF)
                q_ref[place, head] = q
                inverses.append(inverse)
                s = dot_nt(q, kv[0, place, :, at]) * scale
                top = jnp.max(s, axis=-1, keepdims=True)
                e = jnp.exp(s - top)
                total = jnp.sum(e, axis=-1, keepdims=True)
                p = (e * (1.0 / total)).astype(BF)
                outs.append(dot_nn(p, kv[1, place, :, at]))
                logs.append(top + jnp.log(total))
            inv_ref[place] = jnp.concatenate(inverses, axis=1)
            log_ref[place] = jnp.concatenate(logs, axis=1)
            low = jnp.concatenate(outs, axis=1).astype(BF)
            low_ref[place] = low
            second_ref[...] += dot_nt(low, wo[place])
            return u_low + dot_nt(low, ao[place])

        u_low = lax.fori_loop(0, count, cross, jnp.zeros((share, RANK), F32)).astype(BF)
        second = second_ref[...] + dot_nn(u_low, up_of(utab, 9))
        second_ref[...] = second
        normal, _ = stats(second)
        x_mlp = (normal * gain[2:3, :]).astype(BF)
        slots[0, me] = x_mlp[:part_rows]
        slots[1, me] = x_mlp[part_rows:]

        gather(0, 0)
        down.wait(0)
        down.forward()
        down.swap(0)
        down.wait(1)
        down.swap(1)
        gather(0, 1)
        gather(1, 0)
        loads[1].wait()
        for number in range(count - 1):
            arrived = skip_half.at[xor_place(me, number + 1)]
            push(arrived, arrived, zsend.at[number], zrecv.at[number], z_peers[number]).wait_recv()
        skip_place = pltpu.make_async_copy(skip_half, skip.view(dp, core), lsem.at[9])
        skip_place.start()
        skip.send_own(skip_half)
        down.wait(2)
        down.swap(2)
        for number in (4, 5, 6, 8):
            loads[number].wait()
        ua, db = down_of(dtab, 10), up_of(utab, 11)
        gather(0, 2)
        gather(1, 1)
        down.wait_swaps()

        def part(number):
            return pl.ds(pl.multiple_of(number * wide, wide), wide)

        def first_grads(number, carry):
            ct = cot[number].reshape(wide, width)
            gd = dot_nt(ct, db).astype(BF)
            gd_all[part(number), :] = gd
            grads[part(number), :] = (dot_nn(ct, wd[...]) + dot_nn(gd, da[...])).astype(BF)
            return carry

        lax.fori_loop(0, 1, first_grads, 0)
        gather(0, 3)

        def forward_part(number, carry):
            here = part(number)

            @pl.when(number == 1)
            def _():
                first_grads(1, 0)
                gather(1, 3)
                scatter(0, 1)

            x = slots[number].reshape(wide, width)
            u = dot_nt(x, ua).astype(BF)
            u_all[here, :] = u
            up = dot_nn(x, wu[...]) + dot_nn(u, ub[...])
            square = up * up
            curve = jnp.tanh(0.7978845608028654 * (up + 0.044715 * square * up))
            flat = 0.5 * (1.0 + curve)
            active[here, :] = (up * flat).astype(BF)
            slope = flat + 0.5 * up * (1.0 - curve * curve) * (0.7978845608028654 * (1.0 + 0.134145 * square))
            g_up = (grads[here, :].astype(F32) * slope).astype(BF)
            grads[here, :] = g_up
            gu = dot_nt(g_up, ub[...]).astype(BF)
            gu_all[here, :] = gu
            g_x = (dot_nt(g_up, wu[...]) + dot_nn(gu, ua)).astype(BF)
            partial_g[number] = g_x.reshape(count, part_rows, width)

            @pl.when(number == 0)
            def _():
                scatter(0, 0)
                gather(1, 2)

            return carry

        lax.fori_loop(0, 2, forward_part, 0)
        scatter(0, 2)
        scatter(1, 0)
        skip.wait(0)
        skip.forward()
        skip.wait(1)

        def down_product(number, carry):
            here = part(number)
            act = active[here, :]
            ud = dot_nt(act, da[...]).astype(BF)
            ud_all[here, :] = ud
            y = dot_nt(act, wd[...]) + dot_nn(ud, db)
            piece_rows = rows_of(number, part_rows)
            for block in range(count):
                own = jnp.where(block == me, 1.0, 0.0)
                one = y[block * part_rows : (block + 1) * part_rows] + second_ref[piece_rows, :] * own
                partial_b[block, piece_rows, :] = one.astype(BF)

            @pl.when(number == 0)
            def _():
                scatter(1, 1)

            return carry

        lax.fori_loop(0, 2, down_product, 0)
        scatter(1, 2)
        skip_place.wait()
        skip.swap(0)
        skip.swap(1)
        skip.swap(3)
        line_scatter_step(block_line, 0, partial_b, left_b, right_b, sr_b, sl_b)
        g_ub[...] = dot_tn(u_all[...], grads[...])
        g_ua[...] = dot_tn(gu_all[...], slots[...].reshape(tokens, width))
        g_db[...] = dot_tn(ud_all[...], cot[...].reshape(tokens, width))
        g_da[...] = dot_tn(gd_all[...], active[...])
        loads[7].wait()
        uq = dot_nt(x_ref[...], down_of(dtab, 6)).astype(BF)
        words_in = t_ref[...]
        uk = dot_nt(words_in, down_of(dtab, 7)).astype(BF)
        uv = dot_nt(words_in, down_of(dtab, 8)).astype(BF)
        for which in range(2):
            line_gather_drain(gather_lines[which], slots.at[which])
            line_scatter_finish(
                grad_lines[which], partial_g.at[which], left_g.at[which], right_g.at[which], sr_g.at[which],
                sl_g.at[which], acc.at[which * part_rows : (which + 1) * part_rows, :],
            )
        skip.wait(2)
        skip.swap(2)

        normal, inverse = stats(second_ref[...])
        own_cot = jnp.concatenate([cot[0, me], cot[1, me]], axis=0).astype(F32)
        g_second = own_cot + norm_backward(normal, inverse, acc[...] * gain[2:3, :])
        second_ref[...] = g_second
        g_low = g_second.astype(BF)
        x_low[...] = g_low
        go = dot_nt(g_low, up_of(utab, 9)).astype(BF)
        gb_o[...] = dot_tn(u_low, g_low)
        acc[...] = jnp.zeros_like(acc)

        def cross_grads(place, carry):
            gq_sum, gk_sum, gv_sum = carry

            @pl.when((place > 0) & (place < count - 1))
            def _():
                line_scatter_step(block_line, place, partial_b, left_b, right_b, sr_b, sl_b)

            g_attn = (dot_nn(x_low[...], wo[place]) + dot_nn(go, ao[place])).astype(BF)
            ga_o[place] = dot_tn(go, low_ref[place])
            gq_parts, gk_parts, gv_parts = [], [], []
            for head in range(heads):
                at = slice(head * HD, (head + 1) * HD)
                gh = g_attn[:, at]
                q = q_ref[place, head]
                k = kv[0, place, :, at]
                v = kv[1, place, :, at]
                p = jnp.exp(dot_nt(q, k) * scale - log_ref[place, :, head : head + 1])
                dp_ = dot_nt(gh, v)
                inner = jnp.sum(p * dp_, axis=-1, keepdims=True)
                ds = (p * (dp_ - inner)).astype(BF)
                dq = dot_nn(ds, k) * scale
                dk = dot_tn(ds, q) * scale
                gq_parts.append(norm_backward(q.astype(F32), inv_ref[place, :, head : head + 1], dq))
                side = kv[0, place, :, local + 2 * head : local + 2 * head + 2].astype(F32)
                gk_parts.append(norm_backward(k.astype(F32), side[:, 0:1] + side[:, 1:2], dk))
                gv_parts.append(dot_tn(p.astype(BF), gh))
            gq = jnp.concatenate(gq_parts, axis=1).astype(BF)
            gk = jnp.concatenate(gk_parts, axis=1).astype(BF)
            gv = jnp.concatenate(gv_parts, axis=1).astype(BF)
            acc[...] += dot_nt(gq, wq[place])
            gb_q[place] = dot_tn(uq, gq)
            gb_k[place] = dot_tn(uk, gk)
            gb_v[place] = dot_tn(uv, gv)
            return (
                gq_sum + dot_nt(gq, b_ref[place]),
                gk_sum + dot_nt(gk, bk[place]),
                gv_sum + dot_nt(gv, bv[place]),
            )

        start = (jnp.zeros((share, RANK), F32), jnp.zeros((words, RANK), F32), jnp.zeros((words, RANK), F32))
        gq_sum, gk_sum, gv_sum = lax.fori_loop(0, count, cross_grads, start)
        gq_sum = gq_sum.astype(BF)
        ga_q[...] = dot_tn(gq_sum, x_ref[...])
        ga_k[...] = dot_tn(gk_sum.astype(BF), words_in)
        ga_v[...] = dot_tn(gv_sum.astype(BF), words_in)
        g_x = acc[...] + dot_nn(gq_sum, down_of(dtab, 6))
        normal, inverse = stats(first_ref[...])
        g_first[...] = (second_ref[...] + norm_backward(normal, inverse, g_x * gain[1:2, :])).astype(BF)
        line_scatter_finish(block_line, partial_b, left_b, right_b, sr_b, sl_b, acc)
        block_sum[...] = acc[...].astype(BF)
        skip.wait_swaps()
        skip.drain()
        down.drain()
        for send in z_sends:
            send.wait_send()

    buffers = [vmem(count, share, width) for _ in range(5)]
    return call(
        kernel,
        [(summed, True)]
        + [(array, False) for array in (skip_out, query_weight, out_weight, up_weight, down_piece, skip_piece)]
        + [(text_kv, True), (text, False), (cotangent, False)]
        + [(array, True) for array in (gains, *tables)],
        [
            ((share, width), BF, True),
            ((share, width), BF, True),
            ((RANK, width), F32, True),
            ((count, RANK, local), F32, True),
            ((RANK, text_width), F32, True),
            ((count, RANK, local), F32, True),
            ((RANK, text_width), F32, True),
            ((count, RANK, local), F32, True),
            ((count, RANK, local), F32, True),
            ((RANK, width), F32, True),
            ((RANK, width), F32, True),
            ((RANK, units), F32, True),
            ((RANK, units), F32, True),
            ((RANK, width), F32, True),
            ((count, 4 * rows, span), BF, False),
        ],
        [vmem(count, width, local), vmem(count, width, local), vmem(width, units), vmem(width, units),
         vmem(2, count, part_rows, width), vmem(words, text_width), vmem(share, width, dtype=F32),
         vmem(share, width, dtype=F32), vmem(share, width), vmem(share, width), vmem(count, heads, share, HD), vmem(count, share, heads, dtype=F32),
         vmem(count, share, heads, dtype=F32), vmem(count, share, local), vmem(share, width, dtype=F32)]
        + [vmem(count, RANK, local) for _ in range(4)] + [vmem(RANK, units) for _ in range(2)]
        + [vmem(2, count, part_rows, width), vmem(count, rows // 2, span), vmem(tokens, units), vmem(tokens, units)]
        + [vmem(tokens, RANK) for _ in range(4)] + [vmem(2, count, part_rows, width) for _ in range(5)] + buffers
        + [dma(10), dma(2, 7), dma(2, 7), dma(count), dma(count)] + [dma(count) for _ in range(20)],
        collective=3,
        cost=cost_of(12 * tokens * width * units, 60e6),
    )


class Shared:
    def __init__(self, target, rows, sems, stacked=False, split=True, columns=False):
        self.target, self.rows, self.stacked, self.split, self.columns = target, rows, stacked, split, columns
        self.send_sem, self.recv_sem, self.index = sems
        dp, core = lax.axis_index("dp"), lax.axis_index("ctx")
        self.dp, self.core = dp, core
        self.first = jnp.where(core == 0, xor_place(dp, 1), xor_place(dp, 2))
        self.second = jnp.where(core == 0, xor_place(dp, 2), xor_place(dp, 1))
        self.third = xor_place(dp, 3)

    def view(self, block, which):
        if self.columns:
            return self.target.at[:, pl.ds(pl.multiple_of(block * self.rows, 128), self.rows)]
        size = self.rows // 2 if self.split else self.rows
        start = block * self.rows + (which * size if self.split else 0)
        rows = pl.ds(pl.multiple_of(start, 16), size)
        return self.target.at[:, rows, :] if self.stacked else self.target.at[rows, :]

    def copy(self, number, source, block, which, device):
        target = self.view(block, which)
        source = target if source is None else source
        return push(source, target, self.send_sem.at[self.index, number], self.recv_sem.at[self.index, number], device)

    def send_own(self, source=None):
        self.copy(0, source, self.dp, self.core, {"dp": self.first}).start()
        self.copy(1, source, self.dp, self.core, {"dp": self.second}).start()

    def blocks(self):
        return [self.first, self.second, self.third] + ([self.dp] if self.stacked else [])

    def wait(self, number):
        self.copy(number, None, self.blocks()[number], self.core, {"dp": self.first}).wait_recv()

    def forward(self):
        self.copy(2, None, self.first, self.core, {"dp": self.second}).start()

    def swap(self, number):
        self.copy(3 + number, None, self.blocks()[number], self.core, {"ctx": 1 - self.core}).start()

    def wait_swaps(self):
        other = [self.second, self.first, self.third, self.dp]
        for number in range(len(self.blocks())):
            self.copy(3 + number, None, other[number], 1 - self.core, {"ctx": 1 - self.core}).wait_recv()

    def drain(self):
        for number in range(3 + (len(self.blocks()) if self.split else 0)):
            self.copy(number, None, self.dp, self.core, {"dp": self.first}).wait_send()


def front(count, heads, condition, index, hidden, long_skip, text, weights, mod_weight, gain_halves, gain_rows, tables):
    tokens, width = hidden.shape
    span = weights["skip"].shape[1]
    words, text_width = text.shape
    local = weights["q"].shape[1]
    units = weights["up"].shape[1]
    share = tokens // count
    block = min(128, tokens)
    chunk = min(CHUNK, tokens)
    pace = max(1, 64 // chunk)
    steps = tokens // chunk
    each = block // chunk
    scale = HD ** (-0.5)
    rows = weights["q"].shape[0]
    text_rows = weights["ck"].shape[1]
    mod_rows = mod_weight.shape[0]

    def kernel(skip_own, q_own, k_own, v_own, o_own, ck_own, cv_own, cq_own, co_own, up_own,
               index_ref, cond, hid, lsk, t_ref, wm, halves, gain, dtab, utab,
               skip_hbm, attn_hbm, q_out, keys, values, low_out, log_out, inv_q, inv_k, summed, act_all, text_kv,
               wq_hbm, wk_hbm, wv_hbm, wo_hbm, wcq, wco, wup,
               skip_out, attn_in, wq, wk, wv, wo, out_sem, shift_row, wskip, wtext, part_x, pgain, sa, tk, tv, qa, qb, kb, vb, oa, mod_in, mod_slice, mod_out, partial_a, left_a, right_a, sr_a, sl_a,
               partial_b, left_b, right_b, sr_b, sl_b, wsend, wrecv, local_sem, msend, mrecv, tsend, trecv,
               xsend, xrecv, *sems):
        me = lax.axis_index("tensor")
        core = lax.axis_index("ctx")
        dp = lax.axis_index("dp")
        always = core >= 0
        peer = {"ctx": 1 - core}
        dp_peers = [{"dp": xor_place(dp, number)} for number in (1, 2, 3)]
        z_peers = [{"tensor": xor_place(me, number)} for number in range(1, count)]
        reduce_line = Line(me, count, *sems[:4])
        scatter_line = Line(me, count, *sems[4:8])
        text_line = Line(me, count, *sems[8:12])
        cross_lines = [Line(me, count, *sems[12:16]), Line(me, count, *sems[16:])]

        def sems_of(number):
            return (wsend, wrecv, number)

        skip = Shared(wskip, rows, sems_of(0))
        shared = {
            name: Shared(target, rows, sems_of(number))
            for name, target, number in (("q", wq, 1), ("k", wk, 2), ("v", wv, 3), ("o", wo, 4))
        }
        words_w = Shared(wtext, text_rows, sems_of(5), split=False, columns=True)
        cross = [Shared(wcq, rows, sems_of(6), stacked=True), Shared(wco, rows, sems_of(7), stacked=True)]
        wide = [Shared(wup, rows, sems_of(8))]
        owns = {"q": q_own, "k": k_own, "v": v_own, "o": o_own}
        half = pl.ds(pl.multiple_of(core * (rows // 2), 16), rows // 2)
        mine = pl.ds(pl.multiple_of(dp * rows, 16), rows)
        my_half = pl.ds(pl.multiple_of(dp * rows + core * (rows // 2), 16), rows // 2)

        for place in range(count):
            @pl.when(me == place)
            def _(place=place):
                side = place * span // width
                start = place * span % width
                pgain[...] = halves[side : side + 1, start : start + span]

        places = [
            pltpu.make_async_copy(source, target.at[mine, :], local_sem.at[number])
            for number, (source, target) in enumerate(
                ((skip_own, wskip), (q_own, wq), (k_own, wk), (v_own, wv), (o_own, wo), (up_own, wup))
            )
        ]
        for place in places:
            place.start()
        crossing = [
            pltpu.make_async_copy(source.at[half, :], target.at[me, my_half, :], local_sem.at[7 + number])
            for number, (source, target) in enumerate(((cq_own, wcq), (co_own, wco)))
        ]
        text_mine = pl.ds(pl.multiple_of(dp * text_rows, 128), text_rows)

        def text_place(source):
            return pltpu.make_async_copy(source, wtext.at[:, text_mine], local_sem.at[9])

        @pl.when(core == 0)
        def _():
            text_place(ck_own).start()

        @pl.when(core == 1)
        def _():
            text_place(cv_own).start()

        for place in crossing:
            place.start()
        value = cond[...].astype(F32)
        act_low = (value / (1.0 + jnp.exp(-value))).astype(BF)
        tag = jnp.full((1, 128), index_ref[0], jnp.int32).astype(F32)
        act_all[dp] = jnp.concatenate([act_low.astype(F32), tag], axis=1)
        greet([(always, device) for device in dp_peers + z_peers + [peer]])
        skip.send_own(skip_own.at[half, :])

        def cross_view(which):
            target = (wcq, wco)[which]
            return lambda block: target.at[block, my_half, :]

        def cross_step(number):
            for which, cross_line in enumerate(cross_lines):
                line_gather_step(cross_line, number, cross_view(which))

        for place in crossing:
            place.wait()
        cross_step(0)
        spread = [
            push(act_all.at[dp], act_all.at[dp], msend.at[0, number], mrecv.at[0, number], device)
            for number, device in enumerate(dp_peers)
        ]
        for copy in spread:
            copy.start()
        take_local(sa, dtab, 0, me, count)
        take_local(tk, utab, OUT_AT[7], me, count)
        take_local(tv, utab, OUT_AT[8], me, count)
        for number, target in enumerate((qb, kb, vb)):
            qa[number * RANK : (number + 1) * RANK, :] = down_of(dtab, 2 + number)
            take_local(target, utab, OUT_AT[2 + number], me, count)
        take_local(oa, dtab, IN_AT[5], me, count)
        skip.wait(0)
        skip.forward()
        for name in ("q", "k", "v", "o"):
            shared[name].send_own(owns[name].at[half, :])

        @pl.when(core == 0)
        def _():
            words_w.send_own(ck_own)

        @pl.when(core == 1)
        def _():
            words_w.send_own(cv_own)

        skip.swap(0)

        skip.wait(1)
        skip.swap(1)
        cross_step(1)

        for number in (1, 2, 3):
            source = act_all.at[xor_place(dp, number)]
            push(source, source, msend.at[0, number - 1], mrecv.at[0, number - 1], dp_peers[number - 1]).wait_recv()
        for owner in range(4):
            @pl.when(dp == owner)
            def _(owner=owner):
                span_of = slice(owner * mod_rows, (owner + 1) * mod_rows)
                for sequence in range(4):
                    mod_slice[sequence : sequence + 1, :] = act_all[sequence, :, span_of]

        skip.wait(2)
        skip.swap(2)
        products = dot_nn(mod_slice[...].astype(BF), wm[...])
        for sequence in range(4):
            mod_out[sequence] = products[sequence : sequence + 1]
        backs = [
            push(mod_out.at[xor_place(dp, number)], mod_in.at[dp], msend.at[1, number - 1], mrecv.at[1, number - 1],
                 dp_peers[number - 1])
            for number in (1, 2, 3)
        ]
        for copy in backs:
            copy.start()
        mod_in[dp] = mod_out[dp]
        places[0].wait()
        skip.wait_swaps()
        cross_step(2)

        def compute(number):
            @pl.when(number % each == 0)
            def _():
                here = rows_of(number // each, block)
                left = hid[here, :].astype(F32)
                right = lsk[here, :].astype(F32)
                mean = (jnp.sum(left, axis=-1, keepdims=True) + jnp.sum(right, axis=-1, keepdims=True)) / (2 * width)
                spread = jnp.sum((left - mean) ** 2, axis=-1, keepdims=True)
                spread += jnp.sum((right - mean) ** 2, axis=-1, keepdims=True)
                inverse = lax.rsqrt(spread / (2 * width) + NORM_EPS)
                for place in range(count):
                    @pl.when(me == place)
                    def _(place=place):
                        source = hid if place * span < width else lsk
                        start = place * span % width
                        part_x[...] = source[here, start : start + span].astype(F32)
                x = ((part_x[...] - mean) * inverse * pgain[...]).astype(BF)
                u = dot_nt(x, sa[...]).astype(BF)
                y = (dot_nt(x, wskip[...]) + dot_nn(u, up_of(utab, 0))).astype(BF)
                for piece in range(each):
                    partial_a[number + piece] = y[piece * chunk : (piece + 1) * chunk]

        def text_product():
            @pl.when(core == 0)
            def _():
                text_place(ck_own).wait()

            @pl.when(core == 1)
            def _():
                text_place(cv_own).wait()

            x = t_ref[...]
            y = dot_nt(x, wtext[...])

            @pl.when(core == 0)
            def _():
                z = y + dot_nn(dot_nt(x, down_of(dtab, 7)).astype(BF), tk[...])
                parts, sides = [], []
                for head in range(heads):
                    normal, inverse = stats(z[:, head * HD : (head + 1) * HD])
                    upper = inverse.astype(BF)
                    parts.append(normal.astype(BF))
                    sides += [upper, (inverse - upper.astype(F32)).astype(BF)]
                text_kv[0, me, :, :local] = jnp.concatenate(parts, axis=1)
                text_kv[0, me, :, local : local + 2 * heads] = jnp.concatenate(sides, axis=1)

            @pl.when(core == 1)
            def _():
                z = y + dot_nn(dot_nt(x, down_of(dtab, 8)).astype(BF), tv[...])
                text_kv[1, me, :, :local] = z.astype(BF)

        text_slots = text_kv.at[core]

        def finish(slot, total):
            here = rows_of(slot, chunk)
            skip_out[here, :] = total
            normal, _ = stats(total)
            attn_in[here, :] = (normal * gain[0:1, :] + shift_row[...]).astype(BF)

        def project(number, carry):
            here = rows_of(number, block)
            x = attn_in[here, :]
            u = dot_nt(x, qa[...]).astype(BF)
            yq = dot_nn(x, wq[...]) + dot_nn(u[:, :RANK], qb[...])
            yk = dot_nn(x, wk[...]) + dot_nn(u[:, RANK : 2 * RANK], kb[...])
            yv = (dot_nn(x, wv[...]) + dot_nn(u[:, 2 * RANK :], vb[...])).astype(BF)
            parts_q, parts_k = [], []
            for head in range(heads):
                span_of = slice(head * HD, (head + 1) * HD)
                normal, inverse = stats(yq[:, span_of])
                q_out[head, here, :] = normal.astype(BF)
                parts_q.append(inverse)
                normal, inverse = stats(yk[:, span_of])
                keys[core, head, here, :] = normal.astype(BF)
                parts_k.append(inverse)
                values[core, head, here, :] = yv[:, span_of]
            inv_q[here, :] = jnp.concatenate(parts_q, axis=1)
            inv_k[here, :] = jnp.concatenate(parts_k, axis=1)
            return carry

        def beside(number):
            @pl.when(number == 1 * pace)
            def _():
                for other in (1, 2, 3):
                    target = mod_in.at[xor_place(dp, other)]
                    push(target, target, msend.at[1, other - 1], mrecv.at[1, other - 1], dp_peers[other - 1]).wait_recv()
                mod_u = dot_nt(act_low, down_of(dtab, 1)).astype(BF)
                shift_row[...] = mod_in[0] + mod_in[1] + mod_in[2] + mod_in[3] + dot_nn(mod_u, up_of(utab, 1))

            @pl.when(number == 3 * pace)
            def _():
                for weight in (*shared.values(), words_w):
                    weight.wait(0)
                    weight.forward()
                for weight in (*shared.values(), words_w):
                    weight.wait(1)
                for weight in shared.values():
                    weight.swap(0)
                    weight.swap(1)

            @pl.when(number == 4 * pace)
            def _():
                cross_step(3)
                for weight in cross:
                    weight.send_own()

            @pl.when(number == 7 * pace)
            def _():
                for weight in (*shared.values(), words_w):
                    weight.wait(2)
                for weight in shared.values():
                    weight.swap(2)

            @pl.when(number == 8 * pace)
            def _():
                for weight in wide:
                    weight.send_own(up_own.at[half, :])
                for place in places[1:5]:
                    place.wait()
                for weight in shared.values():
                    weight.wait_swaps()
                project(0, 0)

            @pl.when(number == steps + count - 3)
            def _():
                text_product()
                line_gather_step(text_line, 0, text_slots)

        line_reduce_all(reduce_line, steps, compute, partial_a, left_a, right_a, sr_a, sl_a, finish, beside)

        lax.fori_loop(1, tokens // block, project, 0)
        stores = [
            pltpu.make_async_copy(source, target, out_sem.at[number])
            for number, (source, target) in enumerate(
                ((skip_out, skip_hbm), (attn_in, attn_hbm), (wq, wq_hbm), (wk, wk_hbm), (wv, wv_hbm), (wo, wo_hbm))
            )
        ]
        for store in stores:
            store.start()

        swaps = [
            push(ref.at[core], ref.at[core], xsend.at[number], xrecv.at[number], peer)
            for number, ref in enumerate((keys, values))
        ]
        for swap in swaps:
            swap.start()
        line_gather_step(text_line, 1, text_slots)
        for weight in cross:
            weight.wait(0)
            weight.forward()
            weight.swap(0)
            weight.swap(3)
        for number, ref in enumerate((keys, values)):
            push(ref.at[1 - core], ref.at[1 - core], xsend.at[number], xrecv.at[number], peer).wait_recv()

        def attend(place, carry):
            dest = scatter_order(me, count, place)
            here = rows_of(dest, share)
            outs, logs = [], []
            for head in range(heads):
                q = q_out[head, here, :]
                s0 = dot_nt(q, keys[0, head]) * scale
                s1 = dot_nt(q, keys[1, head]) * scale
                top = jnp.maximum(jnp.max(s0, axis=-1, keepdims=True), jnp.max(s1, axis=-1, keepdims=True))
                e0 = jnp.exp(s0 - top)
                e1 = jnp.exp(s1 - top)
                total = jnp.sum(e0, axis=-1, keepdims=True) + jnp.sum(e1, axis=-1, keepdims=True)
                share_of = 1.0 / total
                p0 = (e0 * share_of).astype(BF)
                p1 = (e1 * share_of).astype(BF)
                outs.append(dot_nn(p0, values[0, head]) + dot_nn(p1, values[1, head]))
                logs.append(top + jnp.log(total))
            low = jnp.concatenate(outs, axis=1).astype(BF)
            low_out[here, :] = low
            log_out[here, :] = jnp.concatenate(logs, axis=1)
            u = dot_nt(low, oa[...]).astype(BF)
            partial_b[dest] = (dot_nt(low, wo[...]) + dot_nn(u, up_of(utab, 5))).astype(BF)

            @pl.when(place < count - 1)
            def _():
                line_scatter_step(scatter_line, place, partial_b, left_b, right_b, sr_b, sl_b)

            @pl.when(place == 0)
            def _():
                line_gather_step(text_line, 2, text_slots)

            @pl.when(place == 1)
            def _():
                for weight in cross:
                    weight.wait(1)
                    weight.swap(1)
                line_gather_step(text_line, 3, text_slots)
                push(text_slots, text_slots, tsend, trecv, peer).start()

            @pl.when(place == 2)
            def _():
                for weight in cross:
                    weight.wait(2)
                    weight.swap(2)

            return carry

        lax.fori_loop(0, count, attend, 0)
        for weight in wide:
            weight.wait(0)
            weight.forward()
            weight.swap(0)
        for weight in wide:
            weight.wait(1)
            weight.swap(1)
        line_scatter_finish(scatter_line, partial_b, left_b, right_b, sr_b, sl_b, summed)
        for weight in wide:
            weight.wait(2)
            weight.swap(2)
        others = text_kv.at[1 - core]
        push(others, others, tsend, trecv, peer).wait_recv()
        for weight in cross + wide:
            weight.wait_swaps()
        places[5].wait()
        for store in stores:
            store.wait()
        for weight in (skip, *shared.values(), words_w, *cross, *wide):
            weight.drain()
        for which, cross_line in enumerate(cross_lines):
            line_gather_drain(cross_line, cross_view(which))
        for copy in spread + backs:
            copy.wait_send()
        line_gather_drain(text_line, text_slots)
        push(text_slots, text_slots, tsend, trecv, peer).wait_send()
        for swap in swaps:
            swap.wait_send()

    names = ("skip", "q", "k", "v", "o", "ck", "cv", "cq", "co", "up")
    return call(
        kernel,
        [(weights[name], name in ("cq", "co", "up")) for name in names] + [(index, None)]
        + [(array, True) for array in (condition, hidden, long_skip, text, mod_weight, gain_halves, gain_rows, *tables)],
        [
            ((tokens, width), F32, False),
            ((tokens, width), BF, False),
            ((heads, tokens, HD), BF, True),
            ((2, heads, tokens, HD), BF, True),
            ((2, heads, tokens, HD), BF, True),
            ((tokens, local), BF, True),
            ((tokens, heads), F32, True),
            ((tokens, heads), F32, True),
            ((tokens, heads), F32, True),
            ((share, width), F32, True),
            ((4, 1, width + 128), F32, True),
            ((2, count, words, local + 32), BF, True),
        ]
        + [((width, local), BF, False) for _ in range(4)]
        + [((count, width, local), BF, False) for _ in range(2)]
        + [((width, units), BF, False)],
        [vmem(tokens, width, dtype=F32), vmem(tokens, width)] + [vmem(width, local) for _ in range(4)]
        + [dma(6), vmem(1, width, dtype=F32), vmem(width, span), vmem(local, text_width), vmem(block, span, dtype=F32), vmem(1, span, dtype=F32),
         vmem(RANK, span), vmem(RANK, local), vmem(RANK, local), vmem(3 * RANK, width)]
        + [vmem(RANK, local) for _ in range(4)]
        + [vmem(4, 1, width, dtype=F32), vmem(4, mod_rows, dtype=F32),
         vmem(4, 1, width, dtype=F32)]
        + [vmem(steps, chunk, width) for _ in range(5)] + [vmem(count, share, width) for _ in range(5)]
        + [dma(10, 7), dma(10, 7), dma(10), dma(2, 3), dma(2, 3), dma(), dma(),
           dma(2), dma(2)]
        + [dma(steps) for _ in range(4)] + [dma(count) for _ in range(16)],
        collective=1,
        cost=cost_of(8 * tokens * width * local, 60e6),
    )


def attention_backward(count, heads, g_first, query, keys, values, low, logs, inv_q, inv_k, out_weight, tables):
    share, width = g_first.shape
    tokens = query.shape[1]
    local = low.shape[1]
    scale = HD ** (-0.5)

    def kernel(g_ref, q_ref, k_ref, v_ref, low_ref, log_ref, iq_ref, ik_ref, wo, dtab, utab, gq_low, gk_low, gv_low,
               gall, ga_o, gb_o, gk_acc, gv_acc, swap_out, swap_in, ao, xsend, xrecv, *sems):
        me = lax.axis_index("tensor")
        core = lax.axis_index("ctx")
        peer = {"ctx": 1 - core}
        grad_line = Line(me, count, *sems)
        gall[me] = g_ref[...]
        greet(line_partners(me, count) + [(core >= 0, peer)])
        line_gather_step(grad_line, 0, gall)
        for ref in (ga_o, gb_o, gk_acc, gv_acc):
            ref[...] = jnp.zeros_like(ref)
        take_local(ao, dtab, IN_AT[5], me, count)

        def attend(place):
            rows = rows_of(place, share)
            g = gall[place]
            go = dot_nt(g, up_of(utab, 5)).astype(BF)
            g_attn = (dot_nn(g, wo[...]) + dot_nn(go, ao[...])).astype(BF)
            low = low_ref[rows, :]
            uo = dot_nt(low, ao[...]).astype(BF)
            gb_o[...] += dot_tn(uo, g)
            ga_o[...] += dot_tn(go, low)
            parts = []
            for head in range(heads):
                gh = g_attn[:, head * HD : (head + 1) * HD]
                q = q_ref[head, rows, :]
                probs, grads = [], []
                inner = 0.0
                for half in range(2):
                    p = jnp.exp(dot_nt(q, k_ref[half, head]) * scale - log_ref[rows, head : head + 1])
                    dp = dot_nt(gh, v_ref[half, head])
                    inner = inner + jnp.sum(p * dp, axis=-1, keepdims=True)
                    probs.append(p)
                    grads.append(dp)
                dq = 0.0
                for half in range(2):
                    ds = (probs[half] * (grads[half] - inner)).astype(BF)
                    dq = dq + dot_nn(ds, k_ref[half, head])
                    gk_acc[half, head] += dot_tn(ds, q)
                    gv_acc[half, head] += dot_tn(probs[half].astype(BF), gh)
                parts.append(norm_backward(q.astype(F32), iq_ref[rows, head : head + 1], dq * scale))
            gq_low[rows, :] = jnp.concatenate(parts, axis=1).astype(BF)

        def gather(number, carry):
            @pl.when(number > 0)
            def _():
                line_gather_step(grad_line, number, gall)

            def side(which, inner):
                place = me + (2 * which - 1) * number

                @pl.when((place >= 0) & (place < count) & ((number > 0) | (which == 0)))
                def _():
                    attend(lax.clamp(0, place, count - 1))

                return inner

            return lax.fori_loop(0, 2, side, carry)

        lax.fori_loop(0, count, gather, 0)
        swap_out[0] = (gk_acc[1 - core] * scale).astype(BF)
        swap_out[1] = gv_acc[1 - core].astype(BF)
        swap = push(swap_out, swap_in, xsend, xrecv, peer)
        swap.start()
        line_gather_drain(grad_line, gall)
        swap.wait()

        def keys_back(place, carry):
            rows = rows_of(place, share)
            parts_k, parts_v = [], []
            for head in range(heads):
                dk = gk_acc[core, head, rows, :] * scale + swap_in[0, head, rows, :].astype(F32)
                normal = k_ref[core, head, rows, :].astype(F32)
                parts_k.append(norm_backward(normal, ik_ref[rows, head : head + 1], dk))
                parts_v.append(gv_acc[core, head, rows, :] + swap_in[1, head, rows, :].astype(F32))
            gk_low[rows, :] = jnp.concatenate(parts_k, axis=1).astype(BF)
            gv_low[rows, :] = jnp.concatenate(parts_v, axis=1).astype(BF)
            return carry

        lax.fori_loop(0, count, keys_back, 0)

    return call(
        kernel,
        [(array, True) for array in (g_first, query, keys, values, low, logs, inv_q, inv_k, out_weight, *tables)],
        [
            ((tokens, local), BF, True),
            ((tokens, local), BF, True),
            ((tokens, local), BF, True),
            ((count, share, width), BF, True),
            ((RANK, local), F32, True),
            ((RANK, width), F32, True),
        ],
        [vmem(2, heads, tokens, HD, dtype=F32), vmem(2, heads, tokens, HD, dtype=F32), vmem(2, heads, tokens, HD),
         vmem(2, heads, tokens, HD), vmem(RANK, local), dma(), dma()]
        + [dma(count) for _ in range(4)],
        collective=4,
        cost=cost_of(16 * tokens * width * local, 60e6),
    )


EARLY_A, EARLY_B = IN_AT[2], OUT_AT[2]
EARLY = IN_AT[12] - EARLY_A + OUT_AT[12] - EARLY_B
LATE = EARLY_A + EARLY_B


def back_end(count, grads, projections, attn_in, g_first, skip_out, hidden, long_skip, weight, mod_weight, block_sum,
             gain_halves, gain_rows, tables, condition, act_all, wide_grads, local_down, local_up, stacked):
    tokens, width = hidden.shape
    local = grads[0].shape[1]
    span = weight.shape[-1]
    block = tokens // count
    chunk = min(CHUNK, block)
    pace = max(1, 64 // chunk)
    each = block // chunk
    steps = tokens // chunk
    own_rows = RANK // count
    half_e = -(-EARLY // 256) * 128
    half_l = -(-LATE // 256) * 128
    base = IN_AT[12] - EARLY_A
    mod_rows = mod_weight.shape[0]

    def early(column):
        return column - EARLY_A if column < IN_AT[12] else column - EARLY_A - EARLY_B

    wide_at, wide = [early(column) for column in wide_grads], list(wide_grads.values())
    local_at = [early(column) for column in local_down] + [early(IN_AT[12] + column) for column in local_up]
    own_grads = list(local_down.values()) + list(local_up.values())
    stacked_at, stack = [early(column) for column in stacked], list(stacked.values())

    def kernel(gq, gk, gv, wq, wk, wv, x_hbm, gf_hbm, skip_hbm, hid_hbm, lsk_hbm, hbm_w, wm_hbm, b_in, gains, gain, dtab,
               utab, cond, act_ref, *refs):
        wide_refs, refs = refs[: len(wide)], refs[len(wide) :]
        own_refs, refs = refs[: len(own_grads)], refs[len(own_grads) :]
        stack_refs, refs = refs[: len(stack)], refs[len(stack) :]
        (out_h, out_l, out_a, out_b, out_c, ball, w, x_ref, gf_ref, skip_ref, hid, lsk, wm, buf_h, buf_l, low, g_ref, qkv_a, bq, bk, bv, partial_g, left_g, right_g,
         sr_g, sl_g, table, late, swap_out, swap_in, partial_e, left_e, right_e, sr_e, sl_e, summed, late_out, late_in,
         partial_l, slots_l, slots, late_slots, other_out, other_in, later_out, later_in, shifts, shift_in, act_out, act_in, g_act, g_sum,
         wsem, osem, ssem, rsem, dsend, drecv, msend, mrecv, zsend, zrecv, *sems) = refs
        me = lax.axis_index("tensor")
        core = lax.axis_index("ctx")
        dp = lax.axis_index("dp")
        peer = {"ctx": 1 - core}
        grad_line = Line(me, count, *sems[:4])
        early_line = Line(me, count, *sems[4:8])
        block_line = Line(me, count, *sems[8:])
        peers = [{"dp": xor_place(dp, number)} for number in (1, 2, 3)]
        z_peers = [{"tensor": xor_place(me, number)} for number in range(1, count)]
        loads = [
            pltpu.make_async_copy(source, target, wsem.at[number])
            for number, (source, target) in enumerate(
                ((x_hbm, x_ref), (gf_hbm, gf_ref), (skip_hbm, skip_ref), (hid_hbm, hid), (lsk_hbm, lsk), (hbm_w, w),
                 (wm_hbm, wm))
            )
        ]
        for load in loads:
            load.start()
        ball[me] = b_in[...]
        greet([(core >= 0, device) for device in z_peers + peers + [peer]])
        for number, target in enumerate((bq, bk, bv)):
            qkv_a[number * RANK : (number + 1) * RANK, :] = down_of(dtab, 2 + number)
            take_local(target, utab, OUT_AT[2 + number], me, count)
        g_sum[...] = jnp.zeros_like(g_sum)
        act_low = act_ref[dp, :, :width].astype(BF)

        def compute(number):
            @pl.when(number % each == 0)
            def _():
                rows = rows_of(number // each, block)
                gu = jnp.concatenate(
                    [dot_nt(gq[rows, :], bq[...]), dot_nt(gk[rows, :], bk[...]), dot_nt(gv[rows, :], bv[...])], axis=1
                ).astype(BF)
                y = dot_nt(gq[rows, :], wq[...]) + dot_nt(gk[rows, :], wk[...]) + dot_nt(gv[rows, :], wv[...])
                y = (y + dot_nn(gu, qkv_a[...])).astype(BF)
                for piece in range(each):
                    partial_g[number + piece] = y[piece * chunk : (piece + 1) * chunk]

        def finish(slot, total):
            g_ref[rows_of(slot, chunk), :] = total

        def skip_block(number):
            rows = rows_of(number, block)
            ga_in = g_ref[rows, :]
            g_sum[...] += jnp.sum(ga_in, axis=0, keepdims=True)
            normal, inverse = stats(skip_ref[rows, :])
            g_low = (
                gf_ref[number].astype(F32) + norm_backward(normal, inverse, ga_in * gain[0:1, :])
            ).astype(BF)
            left = hid[rows, :].astype(F32)
            right = lsk[rows, :].astype(F32)
            mean = (jnp.sum(left, axis=-1, keepdims=True) + jnp.sum(right, axis=-1, keepdims=True)) / (2 * width)
            left = left - mean
            right = right - mean
            spread = jnp.sum(left * left, axis=-1, keepdims=True) + jnp.sum(right * right, axis=-1, keepdims=True)
            inverse = lax.rsqrt(spread / (2 * width) + NORM_EPS)
            left = left * inverse
            right = right * inverse
            gu = dot_nt(g_low, up_of(utab, 0)).astype(BF)
            a_left, a_right = dtab[:, :width], dtab[:, width : 2 * width]

            @pl.when(number == me)
            def _():
                low_l = (left * gains[0:1, :]).astype(BF)
                low_r = (right * gains[1:2, :]).astype(BF)
                u = (dot_nt(low_l, a_left) + dot_nt(low_r, a_right)).astype(BF)
                late[:, :width] = dot_tn(gu, low_l)
                late[:, width : 2 * width] = dot_tn(gu, low_r)
                late[:, EARLY_A : EARLY_A + width] = dot_tn(u, g_low)

            for place in range(count):
                low[:, place * span : (place + 1) * span] = dot_nn(g_low, w[place])
            gl = (low[:, :width] + dot_nn(gu, a_left)) * gains[0:1, :]
            gr = (low[:, width:] + dot_nn(gu, a_right)) * gains[1:2, :]
            mean = (jnp.sum(gl, axis=-1, keepdims=True) + jnp.sum(gr, axis=-1, keepdims=True)) / (2 * width)
            inner = (
                jnp.sum(gl * left, axis=-1, keepdims=True) + jnp.sum(gr * right, axis=-1, keepdims=True)
            ) / (2 * width)
            buf_h[number] = inverse * (gl - mean - left * inner)
            buf_l[number] = inverse * (gr - mean - right * inner)
            pltpu.make_async_copy(buf_h.at[number], out_h.at[rows, :], osem.at[0, number]).start()
            pltpu.make_async_copy(buf_l.at[number], out_l.at[rows, :], osem.at[1, number]).start()

        swap = push(swap_out, swap_in, ssem.at[0], rsem.at[0], peer)
        sends = [
            push(slots.at[dp], slots.at[dp], dsend.at[0, number], drecv.at[0, number], device)
            for number, device in enumerate(peers)
        ]

        def early_step(number):
            line_scatter_step(early_line, number, partial_e, left_e, right_e, sr_e, sl_e)

        def beside(number):
            @pl.when(number == pace)
            def _():
                for load in loads:
                    load.wait()
                x = x_ref[...]
                u = dot_nt(x, qkv_a[...]).astype(BF)
                table[...] = jnp.zeros_like(table)
                late[...] = jnp.zeros_like(late)
                for start, ref in zip(wide_at, wide_refs):
                    table[:, start : start + ref.shape[1]] = ref[...]
                for start, ref in zip(stacked_at, stack_refs):
                    size = ref.shape[2]
                    for place in range(count):
                        table[:, start + place * size : start + (place + 1) * size] = ref[place]
                qkv_b = []
                for which, (grad, factor) in enumerate(((gq, bq), (gk, bk), (gv, bv))):
                    gu = dot_nt(grad[...], factor[...]).astype(BF)
                    table[:, which * width : (which + 1) * width] = dot_tn(gu, x)
                    qkv_b.append(dot_tn(u[:, which * RANK : (which + 1) * RANK], grad[...]))
                for place in range(count):
                    @pl.when(me == place)
                    def _(place=place):
                        for which, piece in enumerate(qkv_b):
                            start = base + which * width + place * local
                            table[:, start : start + local] = piece
                        for start, ref in zip(local_at, own_refs):
                            size = ref.shape[1]
                            table[:, start + place * size : start + (place + 1) * size] = ref[...]
                for which in range(2):
                    @pl.when(core == which)
                    def _(which=which):
                        swap_out[...] = table[:, (1 - which) * half_e : (2 - which) * half_e].astype(BF)

                swap.start()

            @pl.when(number == 3 * pace)
            def _():
                swap.wait()
                for which in range(2):
                    @pl.when(core == which)
                    def _(which=which):
                        for part in range(count):
                            at = slice(part * own_rows, (part + 1) * own_rows)
                            mine = table[at, which * half_e : (which + 1) * half_e]
                            partial_e[part] = (mine + swap_in[at, :].astype(F32)).astype(BF)

            @pl.when((number >= steps) & (number < steps + count - 1))
            def _():
                early_step(number - steps)

            @pl.when(number == steps - 1)
            def _():
                line_gather_step(block_line, 0, ball)

        def after(slot):
            @pl.when(slot % each == each - 1)
            def _():
                skip_block(slot // each)

        line_reduce_all(
            grad_line, steps, compute, partial_g, left_g, right_g, sr_g, sl_g, finish, beside, after
        )

        g_shift = g_sum[...]
        shift_in[0] = g_shift
        swap_shift = push(shift_in.at[0], shift_in.at[1], ssem.at[2], rsem.at[2], peer)
        swap_shift.start()
        mod_u = dot_nt(act_low, down_of(dtab, 1))
        once = jnp.where(me == 0, 1.0, 0.0)
        shift_u = dot_nt(g_shift.astype(BF), up_of(utab, 1))
        zeros_u, zeros_w = jnp.zeros((7, RANK), F32), jnp.zeros((7, width), F32)
        mod_a = jnp.concatenate([shift_u * once, zeros_u], axis=0).astype(BF)
        mod_b = jnp.concatenate([mod_u * once, zeros_u], axis=0).astype(BF)
        act_pad = jnp.concatenate([act_low.astype(F32), zeros_w], axis=0).astype(BF)
        shift_pad = jnp.concatenate([g_shift, zeros_w], axis=0).astype(BF)
        late[:, IN_AT[1] : IN_AT[2]] = dot_tn(mod_a, act_pad)
        late[:, EARLY_A + OUT_AT[1] : EARLY_A + OUT_AT[2]] = dot_tn(mod_b, shift_pad)
        for which in range(2):
            @pl.when(core == which)
            def _(which=which):
                late_out[...] = late[:, (1 - which) * half_l : (2 - which) * half_l].astype(BF)

        swap_late = push(late_out, late_in, ssem.at[1], rsem.at[1], peer)
        swap_late.start()
        line_gather_step(block_line, 1, ball)
        line_scatter_finish(early_line, partial_e, left_e, right_e, sr_e, sl_e, summed)
        slots[dp] = summed[...].astype(BF)
        for send in sends:
            send.start()
        swap_shift.wait()
        shifts[dp] = shift_in[0] + shift_in[1]
        shift_sends = [
            push(shifts.at[dp], shifts.at[dp], msend.at[0, number], mrecv.at[0, number], device)
            for number, device in enumerate(peers)
        ]
        for send in shift_sends:
            send.start()
        swap_late.wait()
        for which in range(2):
            @pl.when(core == which)
            def _(which=which):
                for part in range(count):
                    at = slice(part * own_rows, (part + 1) * own_rows)
                    mine = late[at, which * half_l : (which + 1) * half_l]
                    partial_l[part] = (mine + late_in[at, :].astype(F32)).astype(BF)

        late_sends = [
            push(partial_l.at[xor_place(me, number + 1)], slots_l.at[me], zsend.at[number], zrecv.at[number], device)
            for number, device in enumerate(z_peers)
        ]
        for send in late_sends:
            send.start()
        slots_l[me] = partial_l[me]
        line_gather_step(block_line, 2, ball)
        for number in (1, 2, 3):
            source = shifts.at[xor_place(dp, number)]
            push(source, source, msend.at[0, number - 1], mrecv.at[0, number - 1], peers[number - 1]).wait_recv()
        every = jnp.concatenate([shifts[sequence] for sequence in range(4)], axis=0).astype(BF)
        products = dot_nt(every, wm[...])
        for sequence in range(4):
            act_out[sequence] = products[sequence : sequence + 1]
        act_sends = [
            push(act_out.at[xor_place(dp, number)], act_in.at[dp], msend.at[1, number - 1], mrecv.at[1, number - 1],
                 peers[number - 1])
            for number in (1, 2, 3)
        ]
        for send in act_sends:
            send.start()
        for number in range(count - 1):
            arrived = slots_l.at[xor_place(me, number + 1)]
            push(arrived, arrived, zsend.at[number], zrecv.at[number], z_peers[number]).wait_recv()
        late_sum = slots_l[0].astype(F32)
        for place in range(1, count):
            late_sum = late_sum + slots_l[place].astype(F32)
        late_slots[dp] = late_sum.astype(BF)
        later_sends = [
            push(late_slots.at[dp], late_slots.at[dp], dsend.at[1, number], drecv.at[1, number], device)
            for number, device in enumerate(peers)
        ]
        for send in later_sends:
            send.start()

        def arrive(ref, which):
            for number in (1, 2, 3):
                source = ref.at[xor_place(dp, number)]
                push(source, source, dsend.at[which, number - 1], drecv.at[which, number - 1], peers[number - 1]).wait_recv()

        def total(ref, which):
            slot = (dp * 2 + which).astype(F32)
            result = jnp.zeros(ref.shape[1:], F32)
            for sequence in range(4):
                chosen = jnp.where(act_ref[sequence, :, width : width + 1] == slot, 1.0, 0.0)
                result = result + ref[sequence].astype(F32) * chosen
            return result

        arrive(slots, 0)
        other_out[...] = total(slots, 1 - core).astype(BF)
        last = push(other_out, other_in, ssem.at[3], rsem.at[3], peer)
        last.start()
        mine_e = total(slots, core)
        line_gather_step(block_line, 3, ball)
        arrive(late_slots, 1)
        later_out[...] = total(late_slots, 1 - core).astype(BF)
        latest = push(later_out, later_in, ssem.at[4], rsem.at[4], peer)
        latest.start()
        mine_l = total(late_slots, core)

        act_in[dp] = act_out[dp]
        for number in (1, 2, 3):
            source = act_in.at[xor_place(dp, number)]
            push(source, source, msend.at[1, number - 1], mrecv.at[1, number - 1], peers[number - 1]).wait_recv()
        for place in range(4):
            g_act[:, place * mod_rows : (place + 1) * mod_rows] = act_in[place]
        full_u = dot_nt(shifts[dp].astype(BF), up_of(utab, 1)).astype(BF)
        grad = g_act[...] + dot_nn(full_u, down_of(dtab, 1))
        value = cond[...].astype(F32)
        gate = 1.0 / (1.0 + jnp.exp(-value))
        out_c[...] = grad * gate * (1.0 + value * (1.0 - gate))

        def lay(mine, arrived, target):
            for which in range(2):
                @pl.when(core == which)
                def _(which=which):
                    target(which, mine)
                    target(1 - which, arrived[...].astype(F32))

        def lay_early(which, values):
            start = which * half_e
            low_a = max(0, min(base - start, half_e))
            if low_a:
                out_a[:, EARLY_A + start : EARLY_A + start + low_a] = values[:, :low_a]
            if low_a < half_e:
                at = EARLY_B + start + low_a - base
                out_b[:, at : at + min(half_e, EARLY - start) - low_a] = values[:, low_a : min(half_e, EARLY - start)]

        def lay_late(which, values):
            start = which * half_l
            low_a = max(0, min(EARLY_A - start, half_l))
            end = min(half_l, LATE - start)
            if low_a:
                out_a[:, start : start + low_a] = values[:, :low_a]
            if low_a < end:
                at = start + low_a - EARLY_A
                out_b[:, at : at + end - low_a] = values[:, low_a:end]

        last.wait_recv()
        lay(mine_e, other_in, lay_early)
        latest.wait_recv()
        lay(mine_l, later_in, lay_late)
        line_gather_drain(block_line, ball)
        last.wait_send()
        latest.wait_send()
        for send in sends + later_sends + shift_sends + act_sends + late_sends:
            send.wait_send()

        def drain(number, carry):
            rows = rows_of(number, block)
            pltpu.make_async_copy(buf_h.at[number], out_h.at[rows, :], osem.at[0, number]).wait()
            pltpu.make_async_copy(buf_l.at[number], out_l.at[rows, :], osem.at[1, number]).wait()
            return carry

        lax.fori_loop(0, count, drain, 0)

    part_e = (own_rows, half_e)
    part_l = (own_rows, half_l)
    return call(
        kernel,
        [(array, True) for array in (*grads, *projections)]
        + [(array, False) for array in (attn_in, g_first, skip_out, hidden, long_skip, weight, mod_weight)]
        + [(array, True) for array in (block_sum, gain_halves, gain_rows, *tables, condition, act_all, *wide, *own_grads,
                                       *stack)],
        [
            ((tokens, width), F32, False),
            ((tokens, width), F32, False),
            ((own_rows, IN_AT[12]), F32, True),
            ((own_rows, OUT_AT[12]), F32, True),
            ((1, width), F32, True),
            ((count, block, width), BF, True),
        ],
        [
            vmem(count, width, span),
            vmem(tokens, width), vmem(count, block, width), vmem(tokens, width, dtype=F32), vmem(tokens, width),
            vmem(tokens, width), vmem(mod_rows, width),
            vmem(count, block, width, dtype=F32),
            vmem(count, block, width, dtype=F32),
            vmem(block, 2 * width, dtype=F32),
            vmem(tokens, width, dtype=F32),
            vmem(3 * RANK, width),
            vmem(RANK, local), vmem(RANK, local), vmem(RANK, local),
        ]
        + [vmem(steps, chunk, width) for _ in range(5)]
        + [vmem(RANK, 2 * half_e, dtype=F32), vmem(RANK, 2 * half_l, dtype=F32), vmem(RANK, half_e), vmem(RANK, half_e)]
        + [vmem(count, *part_e) for _ in range(5)]
        + [vmem(*part_e, dtype=F32), vmem(RANK, half_l), vmem(RANK, half_l), vmem(count, *part_l), vmem(count, *part_l)]
        + [vmem(4, *part_e), vmem(4, *part_l), vmem(*part_e), vmem(*part_e), vmem(*part_l), vmem(*part_l)]
        + [vmem(4, 1, width, dtype=F32), vmem(2, 1, width, dtype=F32), vmem(4, 1, mod_rows, dtype=F32),
           vmem(4, 1, mod_rows, dtype=F32), vmem(1, width, dtype=F32), vmem(1, width, dtype=F32)]
        + [dma(7), dma(2, count), dma(5), dma(5), dma(2, 3), dma(2, 3), dma(2, 3), dma(2, 3), dma(count), dma(count)]
        + [dma(steps) for _ in range(4)] + [dma(count) for _ in range(8)],
        collective=5,
        cost=cost_of(4 * tokens * width * width, 30e6),
    )


def fused_body(
    hidden,
    long_skip_input,
    condition,
    projected_text_tokens,
    sequence_adapter_index,
    skip_projection_weight,
    shift_modulation_weight,
    self_query_weight,
    self_key_weight,
    self_value_weight,
    attention_output_weight,
    cross_query_weight,
    cross_key_weight,
    cross_value_weight,
    cross_output_weight,
    feedforward_up_weight,
    feedforward_down_weight,
    skip_norm_gain,
    norm_gain_rows,
    adapter_down_factor,
    adapter_up_factor,
    cotangent,
):
    rank = lax.axis_index("tensor")
    count = lax.axis_size("tensor")
    core = lax.axis_index("ctx")
    dp = lax.axis_index("dp")
    hidden, long_skip, text, cot = hidden[0], long_skip_input[0], projected_text_tokens[0], cotangent[0]
    local = self_query_weight.shape[1]
    heads = local // HD
    index = sequence_adapter_index[0]
    tables = (
        lax.dynamic_index_in_dim(adapter_down_factor, index, 0, keepdims=False),
        lax.dynamic_index_in_dim(adapter_up_factor, index, 0, keepdims=False),
    )
    gain_halves = skip_norm_gain.reshape(2, MODEL_WIDTH)

    weights = {
        "skip": skip_projection_weight.T,
        "q": self_query_weight,
        "k": self_key_weight,
        "v": self_value_weight,
        "o": attention_output_weight.T,
        "ck": cross_key_weight.T,
        "cv": cross_value_weight.T,
        "cq": cross_query_weight,
        "co": cross_output_weight.T,
        "up": feedforward_up_weight,
        "dn": feedforward_down_weight.T,
    }
    (skip_out, attn_in, query, keys, values, low, logs, inv_q, inv_k, summed, act_all, text_kv, wq, wk, wv, wo, wcq, wco,
     wup) = front(
        count, heads, condition, sequence_adapter_index, hidden, long_skip, text, weights, shift_modulation_weight,
        gain_halves, norm_gain_rows, tables,
    )
    (g_first, block_sum, g_cq_a, g_cq_b, g_ck_a, g_ck_b, g_cv_a, g_cv_b, g_co_a, g_co_b, g_up_a, g_up_b, g_down_a, g_down_b,
     skip_all) = middle(
        count, heads, summed, skip_out, wcq, wco, wup, weights["dn"], weights["skip"], text_kv, text,
        cot.reshape(count, 2, -1, MODEL_WIDTH), norm_gain_rows, tables,
    )
    gq, gk, gv, g_first_all, g_o_a, g_o_b = attention_backward(
        count, heads, g_first, query, keys, values, low, logs, inv_q, inv_k, wo, tables
    )
    base = IN_AT[12]
    hidden_grad, skip_grad, grad_down, grad_up, g_condition, block_all = back_end(
        count, (gq, gk, gv), (wq, wk, wv), attn_in, g_first_all, skip_out, hidden, long_skip, skip_all,
        shift_modulation_weight, block_sum, gain_halves, norm_gain_rows, tables, condition, act_all,
        {
            IN_AT[6]: g_cq_a, IN_AT[7]: g_ck_a, IN_AT[8]: g_cv_a, IN_AT[10]: g_up_a,
            base + OUT_AT[5]: g_o_b, base + OUT_AT[9]: g_co_b, base + OUT_AT[11]: g_down_b,
        },
        {IN_AT[5]: g_o_a, IN_AT[11]: g_down_a},
        {OUT_AT[10]: g_up_b},
        {
            IN_AT[9]: g_co_a, base + OUT_AT[6]: g_cq_b, base + OUT_AT[7]: g_ck_b, base + OUT_AT[8]: g_cv_b,
        },
    )
    block_out = block_all.reshape(hidden.shape)
    size = MODEL_WIDTH // (2 * count)
    condition_gradient = lax.dynamic_slice_in_dim(g_condition[0], (core * count + rank) * size, size, 0)
    return (
        block_out[None],
        hidden_grad[None],
        skip_grad[None],
        condition_gradient,
        grad_down.reshape(-1),
        grad_up.reshape(-1),
    )


def solution(mesh):
    in_specs = (
        P("dp", "ctx", None),
        P("dp", "ctx", None),
        P("dp", None),
        P("dp", None, None),
        P("dp"),
        P("tensor", "dp"),
        P("dp", None),
        P("dp", "tensor"),
        P("dp", "tensor"),
        P("dp", "tensor"),
        P("tensor", "dp"),
        P("dp", "tensor"),
        P("dp", "tensor"),
        P("dp", "tensor"),
        P("tensor", "dp"),
        P("dp", "tensor"),
        P("tensor", "dp"),
        P(),
        P(),
        P(),
        P(),
        P("dp", "ctx", None),
    )
    out_specs = (
        P("dp", "ctx", None),
        P("dp", "ctx", None),
        P("dp", "ctx", None),
        P(("dp", "ctx", "tensor")),
        P(("dp", "ctx", "tensor")),
        P(("dp", "ctx", "tensor")),
    )
    shape = mesh.shape
    fused = shape["dp"] == 4 and shape["ctx"] == 2 and shape["tensor"] == 4
    return jax.shard_map(fused_body if fused else body, mesh=mesh, in_specs=in_specs, out_specs=out_specs, check_vma=False)
```

```python
from functools import partial

import jax
import jax.numpy as jnp
from jax import lax
from jax.experimental import pallas as pl
from jax.experimental.pallas import tpu as pltpu
from jax.sharding import PartitionSpec as P

MODEL_WIDTH = 1408
HD = 88
FF = 6144
TW = 1024


PRECISE = lax.Precision.HIGHEST
NORM_EPS = 1e-06


def row_norm(values):
    centered = values - jnp.mean(values, axis=-1, keepdims=True)
    inverse = lax.rsqrt(jnp.mean(centered * centered, axis=-1, keepdims=True) + NORM_EPS)
    return (centered * inverse, inverse)


def head_norm(values, head_width):
    shaped = values.reshape(values.shape[:-1] + (values.shape[-1] // head_width, head_width))
    centered = shaped - jnp.mean(shaped, axis=-1, keepdims=True)
    inverse = lax.rsqrt(jnp.mean(centered * centered, axis=-1, keepdims=True) + NORM_EPS)
    return (centered * inverse, inverse)


def norm_back(normal, inverse, grad_normal):
    return inverse * (
        grad_normal
        - jnp.mean(grad_normal, axis=-1, keepdims=True)
        - normal * jnp.mean(grad_normal * normal, axis=-1, keepdims=True)
    )


def split_parts(values):
    if values.dtype == jnp.bfloat16:
        return [values]
    upper_half = values.astype(jnp.bfloat16)
    lower_half = (values - upper_half.astype(jnp.float32)).astype(jnp.bfloat16)
    return [upper_half, lower_half]


def paired_product(form, left, right):
    total = None
    for left_number, left_part in enumerate(split_parts(left)):
        for right_number, right_part in enumerate(split_parts(right)):
            if left_number + right_number < 2:
                term = jnp.einsum(form, left_part, right_part, preferred_element_type=jnp.float32)
                total = term if total is None else total + term
    return total


def lowrank_out(input_list, weight_matrix, down_piece, up_factor_piece):
    frozen_term = jnp.einsum(
        "gtb,bx->gtx", input_list, weight_matrix, preferred_element_type=jnp.float32
    )
    rank_activation = jnp.einsum(
        "snd,srd->snr", input_list, down_piece, preferred_element_type=jnp.float32
    )
    adapter_term = paired_product("dti,dip->dtp", rank_activation, up_factor_piece)
    return (frozen_term + adapter_term, rank_activation)


def lowrank_back(
    input_list,
    weight_matrix,
    down_piece,
    up_factor_piece,
    rank_activation,
    output_gradient,
    want_input,
):
    upper_gradient = paired_product("pmf,pmz->pfz", rank_activation, output_gradient)
    rank_gradient = paired_product("hzu,hlu->hzl", output_gradient, up_factor_piece)
    grad_lower = paired_product("snr,snd->srd", rank_gradient, input_list)
    if want_input:
        input_gradients = paired_product("lga,wa->lgw", output_gradient, weight_matrix)
        input_gradients = input_gradients + paired_product(
            "snr,srd->snd", rank_gradient, down_piece
        )
        return (input_gradients, grad_lower, upper_gradient)
    return (None, grad_lower, upper_gradient)


def attend_forward(query, key_rows, values_in, scale_factor):
    scores = (
        jnp.einsum("snhe,smhe->shnm", query, key_rows, preferred_element_type=jnp.float32)
        * scale_factor
    )
    row_top = jnp.max(scores, axis=-1, keepdims=True)
    exp_scores = jnp.exp(scores - row_top)
    row_total = jnp.sum(exp_scores, axis=-1, keepdims=True)
    attn_probs = (exp_scores / row_total).astype(jnp.bfloat16)
    result = jnp.einsum(
        "shnm,smhe->snhe", attn_probs, values_in, preferred_element_type=jnp.float32
    )
    return (result, row_top + jnp.log(row_total))


def attend_back(query, key_rows, values_in, log_total, grad_result, scale_factor):
    scores = (
        jnp.einsum("snhe,smhe->shnm", query, key_rows, preferred_element_type=jnp.float32)
        * scale_factor
    )
    attn_probs = jnp.exp(scores - log_total)
    grad_probs = jnp.einsum(
        "snhe,smhe->shnm", grad_result, values_in, preferred_element_type=jnp.float32
    )
    row_inner = jnp.sum(attn_probs * grad_probs, axis=-1, keepdims=True)
    grad_scores = (attn_probs * (grad_probs - row_inner)).astype(jnp.bfloat16)
    grad_query = (
        jnp.einsum("shnm,smhe->snhe", grad_scores, key_rows, preferred_element_type=jnp.float32)
        * scale_factor
    )
    grad_keys = (
        jnp.einsum("shnm,snhe->smhe", grad_scores, query, preferred_element_type=jnp.float32)
        * scale_factor
    )
    grad_values = jnp.einsum(
        "shnm,snhe->smhe",
        attn_probs.astype(jnp.bfloat16),
        grad_result,
        preferred_element_type=jnp.float32,
    )
    return (grad_query, grad_keys, grad_values)


def body(
    hidden,
    long_skip_input,
    condition,
    projected_text_tokens,
    sequence_adapter_index,
    skip_projection_weight,
    shift_modulation_weight,
    self_query_weight,
    self_key_weight,
    self_value_weight,
    attention_output_weight,
    cross_query_weight,
    cross_key_weight,
    cross_value_weight,
    cross_output_weight,
    feedforward_up_weight,
    feedforward_down_weight,
    skip_norm_gain,
    norm_gain_rows,
    adapter_down_factor,
    adapter_up_factor,
    cotangent,
):
    (
        skip_projection_weight,
        shift_modulation_weight,
        self_query_weight,
        self_key_weight,
        self_value_weight,
        attention_output_weight,
        cross_query_weight,
        cross_key_weight,
        cross_value_weight,
        cross_output_weight,
        feedforward_up_weight,
        feedforward_down_weight,
    ) = (
        lax.all_gather(skip_projection_weight, "dp", axis=1, tiled=True),
        lax.all_gather(shift_modulation_weight, "dp", axis=0, tiled=True),
        lax.all_gather(self_query_weight, "dp", axis=0, tiled=True),
        lax.all_gather(self_key_weight, "dp", axis=0, tiled=True),
        lax.all_gather(self_value_weight, "dp", axis=0, tiled=True),
        lax.all_gather(attention_output_weight, "dp", axis=1, tiled=True),
        lax.all_gather(cross_query_weight, "dp", axis=0, tiled=True),
        lax.all_gather(cross_key_weight, "dp", axis=0, tiled=True),
        lax.all_gather(cross_value_weight, "dp", axis=0, tiled=True),
        lax.all_gather(cross_output_weight, "dp", axis=1, tiled=True),
        lax.all_gather(feedforward_up_weight, "dp", axis=0, tiled=True),
        lax.all_gather(feedforward_down_weight, "dp", axis=1, tiled=True),
    )
    tensor_rank = lax.axis_index("tensor")
    tensor_count = lax.axis_size("tensor")
    seqs_local = hidden.shape[0]
    tokens_local = hidden.shape[1]
    local_width = self_query_weight.shape[1]
    heads_local = local_width // HD
    ff_local = feedforward_up_weight.shape[1]
    skip_width = skip_projection_weight.shape[0]
    scale_factor = HD ** (-0.5)
    in_sizes = [
        2 * MODEL_WIDTH,
        MODEL_WIDTH,
        MODEL_WIDTH,
        MODEL_WIDTH,
        MODEL_WIDTH,
        MODEL_WIDTH,
        MODEL_WIDTH,
        TW,
        TW,
        MODEL_WIDTH,
        MODEL_WIDTH,
        FF,
    ]
    out_sizes = [MODEL_WIDTH] * 10 + [FF, MODEL_WIDTH]
    input_offsets = [sum(in_sizes[:number]) for number in range(12)]
    output_offsets = [sum(out_sizes[:number]) for number in range(12)]
    select_adapter = (
        sequence_adapter_index[:, None]
        == jnp.arange(adapter_down_factor.shape[0], dtype=jnp.int32)[None, :]
    )
    choose_wide = select_adapter.astype(jnp.float32)
    down_seq = jnp.einsum(
        "fn,nge->fge",
        select_adapter.astype(jnp.bfloat16),
        adapter_down_factor,
        preferred_element_type=jnp.float32,
    ).astype(jnp.bfloat16)
    up_seq = jnp.einsum(
        "fn,nge->fge",
        select_adapter.astype(jnp.bfloat16),
        adapter_up_factor,
        preferred_element_type=jnp.float32,
    ).astype(jnp.bfloat16)

    def down_full(number):
        return down_seq[:, :, input_offsets[number] : input_offsets[number] + in_sizes[number]]

    def up_full(number):
        return up_seq[:, :, output_offsets[number] : output_offsets[number] + out_sizes[number]]

    def down_local(number, span_width):
        return lax.dynamic_slice_in_dim(
            down_seq, input_offsets[number] + tensor_rank * span_width, span_width, 2
        )

    def up_local(number, span_width):
        return lax.dynamic_slice_in_dim(
            up_seq, output_offsets[number] + tensor_rank * span_width, span_width, 2
        )

    def to_slots(grad_piece):
        return jnp.einsum("si,srd->ird", choose_wide, grad_piece, precision=PRECISE)

    joined = jnp.concatenate([hidden, long_skip_input], axis=-1).astype(jnp.float32)
    joined_normal, joined_inverse = row_norm(joined)
    joined_low = (joined_normal * skip_norm_gain).astype(jnp.bfloat16)
    joined_part = lax.dynamic_slice_in_dim(joined_low, tensor_rank * skip_width, skip_width, 2)
    skip_partial, skip_rank = lowrank_out(
        joined_part, skip_projection_weight, down_local(0, skip_width), up_full(0)
    )
    skip_out = lax.psum(skip_partial.astype(jnp.bfloat16), "tensor").astype(jnp.float32)
    act_wide, silu_pull = jax.vjp(jax.nn.silu, condition.astype(jnp.float32))
    act_low = act_wide.astype(jnp.bfloat16)[:, None, :]
    shift_row, mod_rank = lowrank_out(act_low, shift_modulation_weight, down_full(1), up_full(1))
    first_normal, first_inverse = row_norm(skip_out)
    attn_in = (first_normal * norm_gain_rows[0] + shift_row).astype(jnp.bfloat16)
    query_proj, query_rank = lowrank_out(
        attn_in, self_query_weight, down_full(2), up_local(2, local_width)
    )
    key_proj, key_rank = lowrank_out(
        attn_in, self_key_weight, down_full(3), up_local(3, local_width)
    )
    value_proj, value_rank = lowrank_out(
        attn_in, self_value_weight, down_full(4), up_local(4, local_width)
    )
    query_normal, query_inverse = head_norm(query_proj, HD)
    key_normal, key_inverse = head_norm(key_proj, HD)
    query_low = query_normal.astype(jnp.bfloat16)
    key_low = key_normal.astype(jnp.bfloat16).reshape(seqs_local, tokens_local, local_width)
    value_low = value_proj.astype(jnp.bfloat16)
    keys_all, values_all = (
        lax.all_gather(key_low, "ctx", axis=1, tiled=True),
        lax.all_gather(value_low, "ctx", axis=1, tiled=True),
    )
    keys_four = keys_all.reshape(seqs_local, -1, heads_local, HD)
    values_four = values_all.reshape(seqs_local, -1, heads_local, HD)
    attn_result, attn_log = attend_forward(query_low, keys_four, values_four, scale_factor)
    attn_low = attn_result.reshape(seqs_local, tokens_local, local_width).astype(jnp.bfloat16)
    attn_partial, out_rank = lowrank_out(
        attn_low, attention_output_weight, down_local(5, local_width), up_full(5)
    )
    first_res = skip_out + lax.psum(attn_partial.astype(jnp.bfloat16), "tensor").astype(jnp.float32)
    second_normal, second_inverse = row_norm(first_res)
    cross_in = (second_normal * norm_gain_rows[1]).astype(jnp.bfloat16)
    cquery_proj, cquery_rank = lowrank_out(
        cross_in, cross_query_weight, down_full(6), up_local(6, local_width)
    )
    ckey_proj, ckey_rank = lowrank_out(
        projected_text_tokens, cross_key_weight, down_full(7), up_local(7, local_width)
    )
    cvalue_proj, cvalue_rank = lowrank_out(
        projected_text_tokens, cross_value_weight, down_full(8), up_local(8, local_width)
    )
    cquery_normal, cquery_inverse = head_norm(cquery_proj, HD)
    ckey_normal, ckey_inverse = head_norm(ckey_proj, HD)
    cquery_low = cquery_normal.astype(jnp.bfloat16)
    ckey_low = ckey_normal.astype(jnp.bfloat16)
    cvalue_low = cvalue_proj.astype(jnp.bfloat16).reshape(seqs_local, -1, heads_local, HD)
    cross_result, cross_log = attend_forward(cquery_low, ckey_low, cvalue_low, scale_factor)
    cross_low = cross_result.reshape(seqs_local, tokens_local, local_width).astype(jnp.bfloat16)
    cross_partial, cout_rank = lowrank_out(
        cross_low, cross_output_weight, down_local(9, local_width), up_full(9)
    )
    second_res = first_res + lax.psum(cross_partial.astype(jnp.bfloat16), "tensor").astype(
        jnp.float32
    )
    third_normal, third_inverse = row_norm(second_res)
    mlp_in = (third_normal * norm_gain_rows[2]).astype(jnp.bfloat16)
    up_proj, up_rank = lowrank_out(
        mlp_in, feedforward_up_weight, down_full(10), up_local(10, ff_local)
    )
    activated, gelu_pull = jax.vjp(partial(jax.nn.gelu, approximate=True), up_proj)
    activated_low = activated.astype(jnp.bfloat16)
    down_partial, down_rank = lowrank_out(
        activated_low, feedforward_down_weight, down_local(11, ff_local), up_full(11)
    )
    block_out = second_res + lax.psum(down_partial.astype(jnp.bfloat16), "tensor").astype(
        jnp.float32
    )
    grad_act, grad_down_lower, grad_down_upper = lowrank_back(
        activated_low,
        feedforward_down_weight,
        down_local(11, ff_local),
        up_full(11),
        down_rank,
        cotangent,
        True,
    )
    grad_pre = gelu_pull(grad_act)[0].astype(jnp.bfloat16)
    grad_mlp_in, grad_up_lower, grad_up_upper = lowrank_back(
        mlp_in,
        feedforward_up_weight,
        down_full(10),
        up_local(10, ff_local),
        up_rank,
        grad_pre,
        True,
    )
    grad_mlp_in = lax.psum(grad_mlp_in.astype(jnp.bfloat16), "tensor").astype(jnp.float32)
    grad_second = cotangent.astype(jnp.float32) + norm_back(
        third_normal, third_inverse, grad_mlp_in * norm_gain_rows[2]
    )
    grad_cross_low, grad_cout_lower, grad_cout_upper = lowrank_back(
        cross_low,
        cross_output_weight,
        down_local(9, local_width),
        up_full(9),
        cout_rank,
        grad_second.astype(jnp.bfloat16),
        True,
    )
    grad_cross_result = grad_cross_low.astype(jnp.bfloat16).reshape(
        seqs_local, tokens_local, heads_local, HD
    )
    grad_cquery, grad_ckey, grad_cvalue = attend_back(
        cquery_low, ckey_low, cvalue_low, cross_log, grad_cross_result, scale_factor
    )
    grad_cquery_proj = (
        norm_back(cquery_normal, cquery_inverse, grad_cquery)
        .reshape(seqs_local, tokens_local, local_width)
        .astype(jnp.bfloat16)
    )
    grad_ckey_proj = norm_back(ckey_normal, ckey_inverse, grad_ckey).reshape(
        seqs_local, -1, local_width
    )
    none_first, grad_ckey_lower, grad_ckey_upper = lowrank_back(
        projected_text_tokens,
        cross_key_weight,
        down_full(7),
        up_local(7, local_width),
        ckey_rank,
        grad_ckey_proj,
        False,
    )
    none_second, grad_cvalue_lower, grad_cvalue_upper = lowrank_back(
        projected_text_tokens,
        cross_value_weight,
        down_full(8),
        up_local(8, local_width),
        cvalue_rank,
        grad_cvalue.reshape(seqs_local, -1, local_width),
        False,
    )
    grad_cross_in, grad_cquery_lower, grad_cquery_upper = lowrank_back(
        cross_in,
        cross_query_weight,
        down_full(6),
        up_local(6, local_width),
        cquery_rank,
        grad_cquery_proj,
        True,
    )
    grad_cross_in = lax.psum(grad_cross_in.astype(jnp.bfloat16), "tensor").astype(jnp.float32)
    grad_first = grad_second + norm_back(
        second_normal, second_inverse, grad_cross_in * norm_gain_rows[1]
    )
    grad_attn_low, grad_aout_lower, grad_aout_upper = lowrank_back(
        attn_low,
        attention_output_weight,
        down_local(5, local_width),
        up_full(5),
        out_rank,
        grad_first.astype(jnp.bfloat16),
        True,
    )
    grad_attn_result = grad_attn_low.astype(jnp.bfloat16).reshape(
        seqs_local, tokens_local, heads_local, HD
    )
    grad_query, grad_keys_all, grad_values_all = attend_back(
        query_low, keys_four, values_four, attn_log, grad_attn_result, scale_factor
    )
    grad_keys, grad_values = (
        lax.psum_scatter(
            grad_keys_all.reshape(seqs_local, -1, local_width).astype(jnp.bfloat16),
            "ctx",
            scatter_dimension=1,
            tiled=True,
        ).astype(jnp.float32),
        lax.psum_scatter(
            grad_values_all.reshape(seqs_local, -1, local_width).astype(jnp.bfloat16),
            "ctx",
            scatter_dimension=1,
            tiled=True,
        ).astype(jnp.float32),
    )
    grad_query_proj = (
        norm_back(query_normal, query_inverse, grad_query)
        .reshape(seqs_local, tokens_local, local_width)
        .astype(jnp.bfloat16)
    )
    grad_key_proj = (
        norm_back(
            key_normal, key_inverse, grad_keys.reshape(seqs_local, tokens_local, heads_local, HD)
        )
        .reshape(seqs_local, tokens_local, local_width)
        .astype(jnp.bfloat16)
    )
    grad_value_proj = grad_values.astype(jnp.bfloat16)
    grad_in_query, grad_query_lower, grad_query_upper = lowrank_back(
        attn_in,
        self_query_weight,
        down_full(2),
        up_local(2, local_width),
        query_rank,
        grad_query_proj,
        True,
    )
    grad_in_key, grad_key_lower, grad_key_upper = lowrank_back(
        attn_in,
        self_key_weight,
        down_full(3),
        up_local(3, local_width),
        key_rank,
        grad_key_proj,
        True,
    )
    grad_in_value, grad_value_lower, grad_value_upper = lowrank_back(
        attn_in,
        self_value_weight,
        down_full(4),
        up_local(4, local_width),
        value_rank,
        grad_value_proj,
        True,
    )
    grad_attn_in = lax.psum(
        (grad_in_query + grad_in_key + grad_in_value).astype(jnp.bfloat16), "tensor"
    ).astype(jnp.float32)
    grad_shift = jnp.sum(grad_attn_in, axis=1, keepdims=True) / tensor_count
    grad_act_low, grad_mod_lower, grad_mod_upper = lowrank_back(
        act_low, shift_modulation_weight, down_full(1), up_full(1), mod_rank, grad_shift, True
    )
    grad_condition = silu_pull(grad_act_low[:, 0, :])[0]
    grad_skip_out = grad_first + norm_back(
        first_normal, first_inverse, grad_attn_in * norm_gain_rows[0]
    )
    grad_joined_part, grad_skip_lower, grad_skip_upper = lowrank_back(
        joined_part,
        skip_projection_weight,
        down_local(0, skip_width),
        up_full(0),
        skip_rank,
        grad_skip_out.astype(jnp.bfloat16),
        True,
    )
    grad_joined = lax.all_gather(
        grad_joined_part.astype(jnp.bfloat16), "tensor", axis=2, tiled=True
    ).astype(grad_joined_part.dtype)
    grad_joined_full = norm_back(joined_normal, joined_inverse, grad_joined * skip_norm_gain)
    hidden_grad = grad_joined_full[:, :, :MODEL_WIDTH]
    skip_grad = grad_joined_full[:, :, MODEL_WIDTH:]
    lower_factor_parts = [
        (0, grad_skip_lower, True),
        (1, grad_mod_lower, False),
        (2, grad_query_lower, False),
        (3, grad_key_lower, False),
        (4, grad_value_lower, False),
        (5, grad_aout_lower, True),
        (6, grad_cquery_lower, False),
        (7, grad_ckey_lower, False),
        (8, grad_cvalue_lower, False),
        (9, grad_cout_lower, True),
        (10, grad_up_lower, False),
        (11, grad_down_lower, True),
    ]
    upper_factor_parts = [
        (0, grad_skip_upper, False),
        (1, grad_mod_upper, False),
        (2, grad_query_upper, True),
        (3, grad_key_upper, True),
        (4, grad_value_upper, True),
        (5, grad_aout_upper, False),
        (6, grad_cquery_upper, True),
        (7, grad_ckey_upper, True),
        (8, grad_cvalue_upper, True),
        (9, grad_cout_upper, False),
        (10, grad_up_upper, True),
        (11, grad_down_upper, False),
    ]
    slot_total = adapter_down_factor.shape[0]
    rank_total = adapter_down_factor.shape[1]
    cond_buffer = jnp.zeros((lax.axis_size("dp") * seqs_local, MODEL_WIDTH), jnp.float32)
    cond_buffer = lax.dynamic_update_slice_in_dim(
        cond_buffer, grad_condition, lax.axis_index("dp") * seqs_local, 0
    )
    cond_flat = cond_buffer.reshape(-1)

    def dense_table(parts_list, starts, total_width, row_count, slot_pieces):
        table = jnp.zeros((row_count, total_width), jnp.float32)
        for position, (number, grad_piece, is_local) in enumerate(parts_list):
            span_width = grad_piece.shape[2]
            column_start = starts[number] + tensor_rank * span_width if is_local else starts[number]
            table = lax.dynamic_update_slice_in_dim(table, slot_pieces[position], column_start, 1)
        return table

    down_factor_slots = [
        to_slots(grad_piece).reshape(slot_total * rank_total, -1)
        for number, grad_piece, is_local in lower_factor_parts
    ]
    up_factor_slots = [
        to_slots(grad_piece).reshape(slot_total * rank_total, -1)
        for number, grad_piece, is_local in upper_factor_parts
    ]
    down_compact = jnp.concatenate(down_factor_slots, axis=1)
    up_compact = jnp.concatenate(up_factor_slots, axis=1)
    cond_rows, down_rows, up_rows = (
        lax.psum_scatter(
            cond_flat.astype(jnp.bfloat16), ("dp", "ctx"), scatter_dimension=0, tiled=True
        ).astype(jnp.float32),
        lax.psum_scatter(
            down_compact.astype(jnp.bfloat16), ("dp", "ctx"), scatter_dimension=0, tiled=True
        ).astype(jnp.float32),
        lax.psum_scatter(
            up_compact.astype(jnp.bfloat16), ("dp", "ctx"), scatter_dimension=0, tiled=True
        ).astype(jnp.float32),
    )
    row_count = down_rows.shape[0]
    down_widths = [grad_piece.shape[2] for number, grad_piece, is_local in lower_factor_parts]
    up_widths = [grad_piece.shape[2] for number, grad_piece, is_local in upper_factor_parts]
    down_pieces = [
        down_rows[:, sum(down_widths[:position]) : sum(down_widths[: position + 1])]
        for position in range(12)
    ]
    up_pieces = [
        up_rows[:, sum(up_widths[:position]) : sum(up_widths[: position + 1])]
        for position in range(12)
    ]
    down_block = dense_table(
        lower_factor_parts, input_offsets, adapter_down_factor.shape[2], row_count, down_pieces
    ).reshape(-1)
    up_block = dense_table(
        upper_factor_parts, output_offsets, adapter_up_factor.shape[2], row_count, up_pieces
    ).reshape(-1)
    condition_gradient, adapter_down_gradient, adapter_up_gradient = (
        lax.psum_scatter(
            cond_rows.astype(jnp.bfloat16), "tensor", scatter_dimension=0, tiled=True
        ).astype(jnp.float32),
        lax.psum_scatter(
            down_block.astype(jnp.bfloat16), "tensor", scatter_dimension=0, tiled=True
        ).astype(jnp.float32),
        lax.psum_scatter(
            up_block.astype(jnp.bfloat16), "tensor", scatter_dimension=0, tiled=True
        ).astype(jnp.float32),
    )
    return (
        block_out.astype(jnp.bfloat16),
        hidden_grad,
        skip_grad,
        condition_gradient,
        adapter_down_gradient,
        adapter_up_gradient,
    )


BF = jnp.bfloat16
F32 = jnp.float32
MESH_ID = pl.DeviceIdType.MESH
RANK = 16
CHUNK = 64
VMEM_BYTES = 60 << 20


def dot_nn(left, right):
    return jnp.dot(left, right, preferred_element_type=F32)


def dot_nt(left, right):
    return lax.dot_general(left, right, (((1,), (1,)), ((), ())), preferred_element_type=F32)


def dot_tn(left, right):
    return lax.dot_general(left, right, (((0,), (0,)), ((), ())), preferred_element_type=F32)


def stats(values):
    centered = values - jnp.mean(values, axis=-1, keepdims=True)
    inverse = lax.rsqrt(jnp.mean(centered * centered, axis=-1, keepdims=True) + NORM_EPS)
    return centered * inverse, inverse


def greet_all(partners):
    barrier = pltpu.get_barrier_semaphore()
    for condition, device in partners:
        @pl.when(condition)
        def _(device=device):
            pl.semaphore_signal(barrier, inc=1, device_id=device, device_id_type=MESH_ID)


def await_all(partners):
    expected = sum(jnp.where(condition, 1, 0) for condition, _ in partners)
    pl.semaphore_wait(pltpu.get_barrier_semaphore(), expected)


def greet(partners):
    greet_all(partners)
    await_all(partners)


def line_partners(me, count):
    return [(me > 0, {"tensor": lax.max(me - 1, 0)}), (me < count - 1, {"tensor": lax.min(me + 1, count - 1)})]


def push(source, target, send_sem, recv_sem, device):
    return pltpu.make_async_remote_copy(
        src_ref=source,
        dst_ref=target,
        send_sem=send_sem,
        recv_sem=recv_sem,
        device_id=device,
        device_id_type=MESH_ID,
    )


class Line:
    def __init__(self, me, count, send_right, recv_left, send_left, recv_right):
        self.me, self.count = me, count
        self.sems = (send_right, recv_left, send_left, recv_right)
        self.left = {"tensor": lax.max(me - 1, 0)}
        self.right = {"tensor": lax.min(me + 1, count - 1)}
        self.has_left, self.has_right = me > 0, me < count - 1

    def to_right(self, source, target, slot):
        return push(source, target, self.sems[0].at[slot], self.sems[1].at[slot], self.right)

    def to_left(self, source, target, slot):
        return push(source, target, self.sems[2].at[slot], self.sems[3].at[slot], self.left)


def line_reduce_all(line, steps, compute, partial_ref, from_left, from_right, stage_right, stage_left, finish,
                    beside=None, after=None):
    me, count = line.me, line.count
    far = count - 1 - me

    def step(number, carry):
        @pl.when(number < steps)
        def _():
            compute(number)

        slot_r = number - me

        @pl.when((slot_r >= 0) & (slot_r < steps))
        def _():
            slot = lax.clamp(0, slot_r, steps - 1)

            @pl.when(line.has_left)
            def _():
                line.to_right(stage_right.at[slot], from_left.at[slot], slot).wait_recv()

            @pl.when(line.has_right)
            def _():
                @pl.when(line.has_left)
                def _():
                    total = partial_ref[slot].astype(F32) + from_left[slot].astype(F32)
                    stage_right[slot] = total.astype(BF)

                @pl.when(jnp.logical_not(line.has_left))
                def _():
                    stage_right[slot] = partial_ref[slot]

                line.to_right(stage_right.at[slot], from_left.at[slot], slot).start()

        slot_l = number - far

        @pl.when((slot_l >= 0) & (slot_l < steps))
        def _():
            slot = lax.clamp(0, slot_l, steps - 1)

            @pl.when(line.has_right)
            def _():
                line.to_left(stage_left.at[slot], from_right.at[slot], slot).wait_recv()

            @pl.when(line.has_left)
            def _():
                @pl.when(line.has_right)
                def _():
                    total = partial_ref[slot].astype(F32) + from_right[slot].astype(F32)
                    stage_left[slot] = total.astype(BF)

                @pl.when(jnp.logical_not(line.has_right))
                def _():
                    stage_left[slot] = partial_ref[slot]

                line.to_left(stage_left.at[slot], from_right.at[slot], slot).start()

        if beside is not None:
            beside(number)
        slot_f = number - lax.max(me, far)

        @pl.when((slot_f >= 0) & (slot_f < steps))
        def _():
            slot = lax.clamp(0, slot_f, steps - 1)

            @pl.when(jnp.logical_not(line.has_left))
            def _():
                finish(slot, partial_ref[slot].astype(F32) + from_right[slot].astype(F32))

            @pl.when(line.has_left)
            def _():
                @pl.when(line.has_right)
                def _():
                    finish(
                        slot,
                        partial_ref[slot].astype(F32)
                        + from_left[slot].astype(F32)
                        + from_right[slot].astype(F32),
                    )

                @pl.when(jnp.logical_not(line.has_right))
                def _():
                    finish(slot, partial_ref[slot].astype(F32) + from_left[slot].astype(F32))

            if after is not None:
                after(slot)

        return carry

    lax.fori_loop(0, steps + count - 1, step, 0)

    def drain(slot, carry):
        @pl.when(line.has_right)
        def _():
            line.to_right(stage_right.at[slot], from_left.at[slot], slot).wait_send()

        @pl.when(line.has_left)
        def _():
            line.to_left(stage_left.at[slot], from_right.at[slot], slot).wait_send()

        return carry

    lax.fori_loop(0, steps, drain, 0)


def scatter_order(me, count, place):
    near = lax.min(me, count - 1 - me)
    base = count - 1 - 2 * near
    index = place - base
    block = jnp.where(
        place < base,
        count - 1 - place,
        jnp.where(index % 2 == 0, 2 * near - index // 2, index // 2),
    )
    return jnp.where(2 * me > count - 1, count - 1 - block, block)


def line_scatter_step(line, number, partial_ref, from_left, from_right, stage_right, stage_left):
    me, count = line.me, line.count
    block_r = count - 1 - number + me

    @pl.when((number >= me) & line.has_right & (block_r > me))
    def _():
        block = lax.clamp(0, block_r, count - 1)

        @pl.when(line.has_left)
        def _():
            line.to_right(stage_right.at[block], from_left.at[block], block).wait_recv()
            total = partial_ref[block].astype(F32) + from_left[block].astype(F32)
            stage_right[block] = total.astype(BF)

        @pl.when(jnp.logical_not(line.has_left))
        def _():
            stage_right[block] = partial_ref[block]

        line.to_right(stage_right.at[block], from_left.at[block], block).start()

    block_l = number - (count - 1 - me)

    @pl.when((block_l >= 0) & line.has_left & (block_l < me))
    def _():
        block = lax.clamp(0, block_l, count - 1)

        @pl.when(line.has_right)
        def _():
            line.to_left(stage_left.at[block], from_right.at[block], block).wait_recv()
            total = partial_ref[block].astype(F32) + from_right[block].astype(F32)
            stage_left[block] = total.astype(BF)

        @pl.when(jnp.logical_not(line.has_right))
        def _():
            stage_left[block] = partial_ref[block]

        line.to_left(stage_left.at[block], from_right.at[block], block).start()


def line_scatter_finish(line, partial_ref, from_left, from_right, stage_right, stage_left, total_ref):
    me, count = line.me, line.count
    total_ref[...] = partial_ref[me].astype(F32)

    @pl.when(line.has_left)
    def _():
        line.to_right(stage_right.at[me], from_left.at[me], me).wait_recv()
        total_ref[...] += from_left[me].astype(F32)

    @pl.when(line.has_right)
    def _():
        line.to_left(stage_left.at[me], from_right.at[me], me).wait_recv()
        total_ref[...] += from_right[me].astype(F32)

    def drain(block, carry):
        @pl.when(block > me)
        def _():
            line.to_right(stage_right.at[block], from_left.at[block], block).wait_send()

        @pl.when(block < me)
        def _():
            line.to_left(stage_left.at[block], from_right.at[block], block).wait_send()

        return carry

    lax.fori_loop(0, count, drain, 0)


def line_gather_step(line, number, slots):
    me, count = line.me, line.count
    block_l = lax.clamp(0, me - number, count - 1)
    block_r = lax.clamp(0, me + number, count - 1)
    view = slots if callable(slots) else lambda block: slots.at[block]

    @pl.when(number <= me)
    def _():
        @pl.when(number > 0)
        def _():
            line.to_right(view(block_l), view(block_l), block_l).wait_recv()

        @pl.when(line.has_right)
        def _():
            line.to_right(view(block_l), view(block_l), block_l).start()

    @pl.when(me + number <= count - 1)
    def _():
        @pl.when(number > 0)
        def _():
            line.to_left(view(block_r), view(block_r), block_r).wait_recv()

        @pl.when(line.has_left)
        def _():
            line.to_left(view(block_r), view(block_r), block_r).start()


def line_gather_drain(line, slots):
    me, count = line.me, line.count
    view = slots if callable(slots) else lambda block: slots.at[block]

    def drain(block, carry):
        @pl.when((block <= me) & line.has_right)
        def _():
            line.to_right(view(block), view(block), block).wait_send()

        @pl.when((block >= me) & line.has_left)
        def _():
            line.to_left(view(block), view(block), block).wait_send()

        return carry

    lax.fori_loop(0, count, drain, 0)


def xor_place(place, number):
    if number == 0:
        return place
    if number == 1:
        return place + 1 - 2 * (place % 2)
    if number == 2:
        return place + 2 - 4 * (place // 2)
    return 3 - place


def call(kernel, inputs, outs, scratch, collective=None, cost=None):
    space = {True: pltpu.VMEM, False: pl.ANY, None: pltpu.SMEM}
    return pl.pallas_call(
        kernel,
        out_shape=[jax.ShapeDtypeStruct(shape, dtype) for shape, dtype, _ in outs],
        in_specs=[pl.BlockSpec(memory_space=space[where]) for _, where in inputs],
        out_specs=[pl.BlockSpec(memory_space=space[where]) for _, _, where in outs],
        scratch_shapes=scratch,
        cost_estimate=cost,
        compiler_params=pltpu.CompilerParams(
            collective_id=collective,
            has_side_effects=collective is not None,
            vmem_limit_bytes=VMEM_BYTES,
        ),
    )(*[array for array, _ in inputs])


def cost_of(flops, moved):
    return pl.CostEstimate(flops=int(flops), bytes_accessed=int(moved), transcendentals=0)


def vmem(*shape, dtype=BF):
    return pltpu.VMEM(shape, dtype)


def dma(*shape):
    return pltpu.SemaphoreType.DMA(shape)


def whole_wait(target, sem):
    pltpu.make_async_copy(target, target, sem).wait()


def rows_of(index, size):
    return pl.ds(pl.multiple_of(index * size, size), size)


IN_SIZES = [2 * MODEL_WIDTH] + [MODEL_WIDTH] * 6 + [TW, TW, MODEL_WIDTH, MODEL_WIDTH, FF]
OUT_SIZES = [MODEL_WIDTH] * 10 + [FF, MODEL_WIDTH]
IN_AT = [sum(IN_SIZES[:number]) for number in range(13)]
OUT_AT = [sum(OUT_SIZES[:number]) for number in range(13)]


def down_of(table, number):
    return table[:, IN_AT[number] : IN_AT[number + 1]]


def up_of(table, number):
    return table[:, OUT_AT[number] : OUT_AT[number + 1]]


def take_local(target, table, start, me, count):
    size = target.shape[-1]
    for place in range(count):
        @pl.when(me == place)
        def _(place=place):
            target[...] = table[:, start + place * size : start + (place + 1) * size]


def take_stack(target, table, start, count):
    size = target.shape[-1]
    for place in range(count):
        target[place] = table[:, start + place * size : start + (place + 1) * size]


def norm_backward(normal, inverse, grad):
    return inverse * (
        grad
        - jnp.mean(grad, axis=-1, keepdims=True)
        - normal * jnp.mean(grad * normal, axis=-1, keepdims=True)
    )


def middle(count, heads, summed, skip_out, query_weight, out_weight, up_weight, down_piece, skip_piece, text_kv, text,
           cotangent, gains, tables):
    share, width = summed.shape
    tokens = skip_out.shape[0]
    local = query_weight.shape[-1]
    units = up_weight.shape[1]
    words, text_width = text.shape
    rows, span = skip_piece.shape
    scale = HD ** (-0.5)
    part_rows = share // 2
    wide = count * part_rows

    def kernel(sum_ref, skip_hbm, q_hbm, o_hbm, u_hbm, d_own, piece, kv, text_hbm, cot_hbm, gain, dtab, utab,
               g_first, block_sum, ga_q, gb_q, ga_k, gb_k, ga_v, gb_v, ga_o, gb_o, g_ua, g_ub, g_da, g_db, skip_all,
               wq, wo, wu, wd, cot, t_ref, first_ref, second_ref, x_ref, x_low, q_ref, inv_ref, log_ref, low_ref, acc, b_ref, ao,
               bk, bv, ub, da, slots, skip_half, active, grads, u_all, ud_all, gu_all, gd_all, partial_g, left_g, right_g,
               sr_g, sl_g, partial_b, left_b, right_b, sr_b, sl_b, lsem, wsend, wrecv, zsend, zrecv, *sems):
        me = lax.axis_index("tensor")
        core = lax.axis_index("ctx")
        dp = lax.axis_index("dp")
        always = core >= 0
        half = pl.ds(pl.multiple_of(core * (rows // 2), 16), rows // 2)
        down_rows = d_own.shape[0]
        down_half = pl.ds(pl.multiple_of(core * (down_rows // 2), 16), down_rows // 2)
        mine = pl.ds(pl.multiple_of(dp * down_rows, 16), down_rows)
        loads = [
            pltpu.make_async_copy(source, target, lsem.at[number])
            for number, (source, target) in enumerate(
                ((skip_hbm.at[rows_of(me, share), :], first_ref), (piece.at[half, :], skip_half.at[me]), (q_hbm, wq),
                 (o_hbm, wo), (d_own, wd.at[mine, :]), (cot_hbm.at[:, 0], cot.at[0]), (u_hbm.at[mine, :], wu.at[mine, :]), (text_hbm, t_ref),
                 (cot_hbm.at[:, 1], cot.at[1]))
            )
        ]
        for load in loads:
            load.start()
        gather_lines = [Line(me, count, *sems[:4]), Line(me, count, *sems[4:8])]
        grad_lines = [Line(me, count, *sems[8:12]), Line(me, count, *sems[12:16])]
        block_line = Line(me, count, *sems[16:])

        def gather(which, number):
            line_gather_step(gather_lines[which], number, slots.at[which])

        def scatter(which, number):
            line_scatter_step(
                grad_lines[which], number, partial_g.at[which], left_g.at[which], right_g.at[which], sr_g.at[which],
                sl_g.at[which],
            )

        down = Shared(wd, down_rows, (wsend, wrecv, 0))
        up_w = Shared(wu, down_rows, (wsend, wrecv, 2))
        arrived_up = [
            pltpu.make_async_copy(Shared(u_hbm, down_rows, (wsend, wrecv, 2)).view(block, core), up_w.view(block, core),
                                  lsem.at[10 + number])
            for number, block in enumerate((up_w.first, up_w.second))
        ]
        for load in arrived_up:
            load.start()
        skip = Shared(skip_all, rows, (wsend, wrecv, 1), stacked=True)
        z_peers = [{"tensor": xor_place(me, number)} for number in range(1, count)]
        others = [{"dp": xor_place(dp, 1)}, {"dp": xor_place(dp, 2)}, {"ctx": 1 - core}]
        greet([(always, device) for device in z_peers + others])
        down.send_own(d_own.at[down_half, :])
        z_sends = [
            push(piece.at[half, :], skip_half.at[me], zsend.at[number], zrecv.at[number], device)
            for number, device in enumerate(z_peers)
        ]
        for send in z_sends:
            send.start()
        take_stack(b_ref, utab, OUT_AT[6], count)
        take_stack(ao, dtab, IN_AT[9], count)
        take_stack(bk, utab, OUT_AT[7], count)
        take_stack(bv, utab, OUT_AT[8], count)
        take_local(ub, utab, OUT_AT[10], me, count)
        take_local(da, dtab, IN_AT[11], me, count)

        for load in arrived_up:
            load.wait()
        up_w.forward()
        up_w.swap(0)
        up_w.swap(1)

        loads[0].wait()
        first = first_ref[...] + sum_ref[...]
        first_ref[...] = first
        second_ref[...] = first
        normal, _ = stats(first)
        x = (normal * gain[1:2, :]).astype(BF)
        x_ref[...] = x
        u = dot_nt(x, down_of(dtab, 6)).astype(BF)
        loads[2].wait()
        loads[3].wait()

        def cross(place, u_low):
            y = dot_nn(x_ref[...], wq[place]) + dot_nn(u, b_ref[place])
            outs, inverses, logs = [], [], []
            for head in range(heads):
                at = slice(head * HD, (head + 1) * HD)
                normal, inverse = stats(y[:, at])
                q = normal.astype(BF)
                q_ref[place, head] = q
                inverses.append(inverse)
                s = dot_nt(q, kv[0, place, :, at]) * scale
                top = jnp.max(s, axis=-1, keepdims=True)
                e = jnp.exp(s - top)
                total = jnp.sum(e, axis=-1, keepdims=True)
                p = (e * (1.0 / total)).astype(BF)
                outs.append(dot_nn(p, kv[1, place, :, at]))
                logs.append(top + jnp.log(total))
            inv_ref[place] = jnp.concatenate(inverses, axis=1)
            log_ref[place] = jnp.concatenate(logs, axis=1)
            low = jnp.concatenate(outs, axis=1).astype(BF)
            low_ref[place] = low
            second_ref[...] += dot_nt(low, wo[place])
            return u_low + dot_nt(low, ao[place])

        u_low = lax.fori_loop(0, count, cross, jnp.zeros((share, RANK), F32)).astype(BF)
        second = second_ref[...] + dot_nn(u_low, up_of(utab, 9))
        second_ref[...] = second
        normal, _ = stats(second)
        x_mlp = (normal * gain[2:3, :]).astype(BF)
        slots[0, me] = x_mlp[:part_rows]
        slots[1, me] = x_mlp[part_rows:]

        gather(0, 0)
        up_w.wait(2)
        up_w.swap(2)
        down.wait(0)
        down.forward()
        down.swap(0)
        down.wait(1)
        down.swap(1)
        gather(0, 1)
        gather(1, 0)
        loads[1].wait()
        for number in range(count - 1):
            arrived = skip_half.at[xor_place(me, number + 1)]
            push(arrived, arrived, zsend.at[number], zrecv.at[number], z_peers[number]).wait_recv()
        skip_place = pltpu.make_async_copy(skip_half, skip.view(dp, core), lsem.at[9])
        skip_place.start()
        skip.send_own(skip_half)
        down.wait(2)
        down.swap(2)
        for number in (4, 5, 6, 8):
            loads[number].wait()
        ua, db = down_of(dtab, 10), up_of(utab, 11)
        gather(0, 2)
        gather(1, 1)
        down.wait_swaps()
        up_w.wait_swaps()

        def part(number):
            return pl.ds(pl.multiple_of(number * wide, wide), wide)

        def first_grads(number, carry):
            ct = cot[number].reshape(wide, width)
            gd = dot_nt(ct, db).astype(BF)
            gd_all[part(number), :] = gd
            grads[part(number), :] = (dot_nn(ct, wd[...]) + dot_nn(gd, da[...])).astype(BF)
            return carry

        lax.fori_loop(0, 1, first_grads, 0)
        gather(0, 3)

        def forward_part(number, carry):
            here = part(number)

            @pl.when(number == 1)
            def _():
                first_grads(1, 0)
                gather(1, 3)
                scatter(0, 1)

            x = slots[number].reshape(wide, width)
            u = dot_nt(x, ua).astype(BF)
            u_all[here, :] = u
            up = dot_nn(x, wu[...]) + dot_nn(u, ub[...])
            square = up * up
            curve = jnp.tanh(0.7978845608028654 * (up + 0.044715 * square * up))
            flat = 0.5 * (1.0 + curve)
            active[here, :] = (up * flat).astype(BF)
            slope = flat + 0.5 * up * (1.0 - curve * curve) * (0.7978845608028654 * (1.0 + 0.134145 * square))
            g_up = (grads[here, :].astype(F32) * slope).astype(BF)
            grads[here, :] = g_up
            gu = dot_nt(g_up, ub[...]).astype(BF)
            gu_all[here, :] = gu
            g_x = (dot_nt(g_up, wu[...]) + dot_nn(gu, ua)).astype(BF)
            partial_g[number] = g_x.reshape(count, part_rows, width)

            @pl.when(number == 0)
            def _():
                scatter(0, 0)
                gather(1, 2)

            return carry

        lax.fori_loop(0, 2, forward_part, 0)
        scatter(0, 2)
        scatter(1, 0)
        skip.wait(0)
        skip.forward()
        skip.wait(1)

        def down_product(number, carry):
            here = part(number)
            act = active[here, :]
            ud = dot_nt(act, da[...]).astype(BF)
            ud_all[here, :] = ud
            y = dot_nt(act, wd[...]) + dot_nn(ud, db)
            piece_rows = rows_of(number, part_rows)
            for block in range(count):
                own = jnp.where(block == me, 1.0, 0.0)
                one = y[block * part_rows : (block + 1) * part_rows] + second_ref[piece_rows, :] * own
                partial_b[block, piece_rows, :] = one.astype(BF)

            @pl.when(number == 0)
            def _():
                scatter(1, 1)

            return carry

        lax.fori_loop(0, 2, down_product, 0)
        scatter(1, 2)
        skip_place.wait()
        skip.swap(0)
        skip.swap(1)
        skip.swap(3)
        line_scatter_step(block_line, 0, partial_b, left_b, right_b, sr_b, sl_b)
        g_ub[...] = dot_tn(u_all[...], grads[...])
        g_ua[...] = dot_tn(gu_all[...], slots[...].reshape(tokens, width))
        g_db[...] = dot_tn(ud_all[...], cot[...].reshape(tokens, width))
        g_da[...] = dot_tn(gd_all[...], active[...])
        loads[7].wait()
        uq = dot_nt(x_ref[...], down_of(dtab, 6)).astype(BF)
        words_in = t_ref[...]
        uk = dot_nt(words_in, down_of(dtab, 7)).astype(BF)
        uv = dot_nt(words_in, down_of(dtab, 8)).astype(BF)
        for which in range(2):
            line_gather_drain(gather_lines[which], slots.at[which])
            line_scatter_finish(
                grad_lines[which], partial_g.at[which], left_g.at[which], right_g.at[which], sr_g.at[which],
                sl_g.at[which], acc.at[which * part_rows : (which + 1) * part_rows, :],
            )
        skip.wait(2)
        skip.swap(2)

        normal, inverse = stats(second_ref[...])
        own_cot = jnp.concatenate([cot[0, me], cot[1, me]], axis=0).astype(F32)
        g_second = own_cot + norm_backward(normal, inverse, acc[...] * gain[2:3, :])
        second_ref[...] = g_second
        g_low = g_second.astype(BF)
        x_low[...] = g_low
        go = dot_nt(g_low, up_of(utab, 9)).astype(BF)
        gb_o[...] = dot_tn(u_low, g_low)
        acc[...] = jnp.zeros_like(acc)

        def cross_grads(place, carry):
            gq_sum, gk_sum, gv_sum = carry

            @pl.when((place > 0) & (place < count - 1))
            def _():
                line_scatter_step(block_line, place, partial_b, left_b, right_b, sr_b, sl_b)

            g_attn = (dot_nn(x_low[...], wo[place]) + dot_nn(go, ao[place])).astype(BF)
            ga_o[place] = dot_tn(go, low_ref[place])
            gq_parts, gk_parts, gv_parts = [], [], []
            for head in range(heads):
                at = slice(head * HD, (head + 1) * HD)
                gh = g_attn[:, at]
                q = q_ref[place, head]
                k = kv[0, place, :, at]
                v = kv[1, place, :, at]
                p = jnp.exp(dot_nt(q, k) * scale - log_ref[place, :, head : head + 1])
                dp_ = dot_nt(gh, v)
                inner = jnp.sum(p * dp_, axis=-1, keepdims=True)
                ds = (p * (dp_ - inner)).astype(BF)
                dq = dot_nn(ds, k) * scale
                dk = dot_tn(ds, q) * scale
                gq_parts.append(norm_backward(q.astype(F32), inv_ref[place, :, head : head + 1], dq))
                side = kv[0, place, :, local + 2 * head : local + 2 * head + 2].astype(F32)
                gk_parts.append(norm_backward(k.astype(F32), side[:, 0:1] + side[:, 1:2], dk))
                gv_parts.append(dot_tn(p.astype(BF), gh))
            gq = jnp.concatenate(gq_parts, axis=1).astype(BF)
            gk = jnp.concatenate(gk_parts, axis=1).astype(BF)
            gv = jnp.concatenate(gv_parts, axis=1).astype(BF)
            acc[...] += dot_nt(gq, wq[place])
            gb_q[place] = dot_tn(uq, gq)
            gb_k[place] = dot_tn(uk, gk)
            gb_v[place] = dot_tn(uv, gv)
            return (
                gq_sum + dot_nt(gq, b_ref[place]),
                gk_sum + dot_nt(gk, bk[place]),
                gv_sum + dot_nt(gv, bv[place]),
            )

        start = (jnp.zeros((share, RANK), F32), jnp.zeros((words, RANK), F32), jnp.zeros((words, RANK), F32))
        gq_sum, gk_sum, gv_sum = lax.fori_loop(0, count, cross_grads, start)
        gq_sum = gq_sum.astype(BF)
        ga_q[...] = dot_tn(gq_sum, x_ref[...])
        ga_k[...] = dot_tn(gk_sum.astype(BF), words_in)
        ga_v[...] = dot_tn(gv_sum.astype(BF), words_in)
        g_x = acc[...] + dot_nn(gq_sum, down_of(dtab, 6))
        normal, inverse = stats(first_ref[...])
        g_first[...] = (second_ref[...] + norm_backward(normal, inverse, g_x * gain[1:2, :])).astype(BF)
        line_scatter_finish(block_line, partial_b, left_b, right_b, sr_b, sl_b, acc)
        block_sum[...] = acc[...].astype(BF)
        skip.wait_swaps()
        skip.drain()
        down.drain()
        up_w.drain_rest()
        for send in z_sends:
            send.wait_send()

    buffers = [vmem(count, share, width) for _ in range(5)]
    return call(
        kernel,
        [(summed, True)]
        + [(array, False) for array in (skip_out, query_weight, out_weight, up_weight, down_piece, skip_piece)]
        + [(text_kv, True), (text, False), (cotangent, False)]
        + [(array, True) for array in (gains, *tables)],
        [
            ((share, width), BF, True),
            ((share, width), BF, True),
            ((RANK, width), F32, True),
            ((count, RANK, local), F32, True),
            ((RANK, text_width), F32, True),
            ((count, RANK, local), F32, True),
            ((RANK, text_width), F32, True),
            ((count, RANK, local), F32, True),
            ((count, RANK, local), F32, True),
            ((RANK, width), F32, True),
            ((RANK, width), F32, True),
            ((RANK, units), F32, True),
            ((RANK, units), F32, True),
            ((RANK, width), F32, True),
            ((count, 4 * rows, span), BF, False),
        ],
        [vmem(count, width, local), vmem(count, width, local), vmem(width, units), vmem(width, units),
         vmem(2, count, part_rows, width), vmem(words, text_width), vmem(share, width, dtype=F32),
         vmem(share, width, dtype=F32), vmem(share, width), vmem(share, width), vmem(count, heads, share, HD), vmem(count, share, heads, dtype=F32),
         vmem(count, share, heads, dtype=F32), vmem(count, share, local), vmem(share, width, dtype=F32)]
        + [vmem(count, RANK, local) for _ in range(4)] + [vmem(RANK, units) for _ in range(2)]
        + [vmem(2, count, part_rows, width), vmem(count, rows // 2, span), vmem(tokens, units), vmem(tokens, units)]
        + [vmem(tokens, RANK) for _ in range(4)] + [vmem(2, count, part_rows, width) for _ in range(5)] + buffers
        + [dma(12), dma(3, 7), dma(3, 7), dma(count), dma(count)] + [dma(count) for _ in range(20)],
        collective=3,
        cost=cost_of(12 * tokens * width * units, 60e6),
    )


class Shared:
    def __init__(self, target, rows, sems, stacked=False, split=True, columns=False):
        self.target, self.rows, self.stacked, self.split, self.columns = target, rows, stacked, split, columns
        self.send_sem, self.recv_sem, self.index = sems
        dp, core = lax.axis_index("dp"), lax.axis_index("ctx")
        self.dp, self.core = dp, core
        self.first = jnp.where(core == 0, xor_place(dp, 1), xor_place(dp, 2))
        self.second = jnp.where(core == 0, xor_place(dp, 2), xor_place(dp, 1))
        self.third = xor_place(dp, 3)

    def view(self, block, which):
        if self.columns:
            return self.target.at[:, pl.ds(pl.multiple_of(block * self.rows, 128), self.rows)]
        size = self.rows // 2 if self.split else self.rows
        start = block * self.rows + (which * size if self.split else 0)
        rows = pl.ds(pl.multiple_of(start, 16), size)
        return self.target.at[:, rows, :] if self.stacked else self.target.at[rows, :]

    def copy(self, number, source, block, which, device):
        target = self.view(block, which)
        source = target if source is None else source
        return push(source, target, self.send_sem.at[self.index, number], self.recv_sem.at[self.index, number], device)

    def send_own(self, source=None):
        self.copy(0, source, self.dp, self.core, {"dp": self.first}).start()
        self.copy(1, source, self.dp, self.core, {"dp": self.second}).start()

    def blocks(self):
        return [self.first, self.second, self.third] + ([self.dp] if self.stacked else [])

    def wait(self, number):
        self.copy(number, None, self.blocks()[number], self.core, {"dp": self.first}).wait_recv()

    def forward(self):
        self.copy(2, None, self.first, self.core, {"dp": self.second}).start()

    def swap(self, number):
        self.copy(3 + number, None, self.blocks()[number], self.core, {"ctx": 1 - self.core}).start()

    def wait_swaps(self):
        other = [self.second, self.first, self.third, self.dp]
        for number in range(len(self.blocks())):
            self.copy(3 + number, None, other[number], 1 - self.core, {"ctx": 1 - self.core}).wait_recv()

    def drain_own(self):
        for number in range(2):
            self.copy(number, None, self.dp, self.core, {"dp": self.first}).wait_send()

    def drain_rest(self):
        for number in range(2, 6):
            self.copy(number, None, self.dp, self.core, {"dp": self.first}).wait_send()

    def drain(self):
        for number in range(3 + (len(self.blocks()) if self.split else 0)):
            self.copy(number, None, self.dp, self.core, {"dp": self.first}).wait_send()


def front(count, heads, condition, index, hidden, long_skip, text, weights, mod_weight, gain_halves, gain_rows, tables):
    tokens, width = hidden.shape
    span = weights["skip"].shape[1]
    words, text_width = text.shape
    local = weights["q"].shape[1]
    units = weights["up"].shape[1]
    share = tokens // count
    block = min(128, tokens)
    chunk = min(CHUNK, tokens)
    pace = max(1, 64 // chunk)
    steps = tokens // chunk
    each = block // chunk
    scale = HD ** (-0.5)
    rows = weights["q"].shape[0]
    text_rows = weights["ck"].shape[1]
    mod_rows = mod_weight.shape[0]

    def kernel(skip_own, q_own, k_own, v_own, o_own, ck_own, cv_own, cq_own, co_own, up_own,
               index_ref, cond, hid, lsk, t_ref, wm, halves, gain, dtab, utab,
               skip_hbm, attn_hbm, q_out, keys, values, low_out, log_out, inv_q, inv_k, summed, act_all, text_kv,
               wq_hbm, wk_hbm, wv_hbm, wo_hbm, wcq, wco, wup,
               skip_out, attn_in, wq, wk, wv, wo, out_sem, shift_row, wskip, wtext, part_x, pgain, sa, tk, tv, qa, qb, kb, vb, oa, mod_in, mod_slice, mod_out, partial_a, left_a, right_a, sr_a, sl_a,
               partial_b, left_b, right_b, sr_b, sl_b, wsend, wrecv, local_sem, msend, mrecv, tsend, trecv,
               xsend, xrecv, *sems):
        me = lax.axis_index("tensor")
        core = lax.axis_index("ctx")
        dp = lax.axis_index("dp")
        always = core >= 0
        peer = {"ctx": 1 - core}
        dp_peers = [{"dp": xor_place(dp, number)} for number in (1, 2, 3)]
        z_peers = [{"tensor": xor_place(me, number)} for number in range(1, count)]
        reduce_line = Line(me, count, *sems[:4])
        scatter_line = Line(me, count, *sems[4:8])
        text_line = Line(me, count, *sems[8:12])
        cross_lines = [Line(me, count, *sems[12:16]), Line(me, count, *sems[16:])]

        def sems_of(number):
            return (wsend, wrecv, number)

        skip = Shared(wskip, rows, sems_of(0))
        shared = {
            name: Shared(target, rows, sems_of(number))
            for name, target, number in (("q", wq, 1), ("k", wk, 2), ("v", wv, 3), ("o", wo, 4))
        }
        words_w = Shared(wtext, text_rows, sems_of(5), split=False, columns=True)
        cross = [Shared(wcq, rows, sems_of(6), stacked=True), Shared(wco, rows, sems_of(7), stacked=True)]
        wide = [Shared(wup, rows, sems_of(8))]
        owns = {"q": q_own, "k": k_own, "v": v_own, "o": o_own}
        half = pl.ds(pl.multiple_of(core * (rows // 2), 16), rows // 2)
        mine = pl.ds(pl.multiple_of(dp * rows, 16), rows)
        my_half = pl.ds(pl.multiple_of(dp * rows + core * (rows // 2), 16), rows // 2)

        for place in range(count):
            @pl.when(me == place)
            def _(place=place):
                side = place * span // width
                start = place * span % width
                pgain[...] = halves[side : side + 1, start : start + span]

        places = [
            pltpu.make_async_copy(source, target.at[mine, :], local_sem.at[number])
            for number, (source, target) in enumerate(
                ((skip_own, wskip), (q_own, wq), (k_own, wk), (v_own, wv), (o_own, wo), (up_own, wup))
            )
        ]
        for place in places:
            place.start()
        crossing = [
            pltpu.make_async_copy(source.at[half, :], target.at[me, my_half, :], local_sem.at[7 + number])
            for number, (source, target) in enumerate(((cq_own, wcq), (co_own, wco)))
        ]
        text_mine = pl.ds(pl.multiple_of(dp * text_rows, 128), text_rows)

        def text_place(source):
            return pltpu.make_async_copy(source, wtext.at[:, text_mine], local_sem.at[9])

        @pl.when(core == 0)
        def _():
            text_place(ck_own).start()

        @pl.when(core == 1)
        def _():
            text_place(cv_own).start()

        for place in crossing:
            place.start()
        value = cond[...].astype(F32)
        act_low = (value / (1.0 + jnp.exp(-value))).astype(BF)
        tag = jnp.full((1, 128), index_ref[0], jnp.int32).astype(F32)
        act_all[dp] = jnp.concatenate([act_low.astype(F32), tag], axis=1)
        greet([(always, device) for device in dp_peers + z_peers + [peer]])
        skip.send_own(skip_own.at[half, :])

        def cross_view(which):
            target = (wcq, wco)[which]
            return lambda block: target.at[block, my_half, :]

        def cross_step(number):
            for which, cross_line in enumerate(cross_lines):
                line_gather_step(cross_line, number, cross_view(which))

        for place in crossing:
            place.wait()
        cross_step(0)
        spread = [
            push(act_all.at[dp], act_all.at[dp], msend.at[0, number], mrecv.at[0, number], device)
            for number, device in enumerate(dp_peers)
        ]
        for copy in spread:
            copy.start()
        take_local(sa, dtab, 0, me, count)
        take_local(tk, utab, OUT_AT[7], me, count)
        take_local(tv, utab, OUT_AT[8], me, count)
        for number, target in enumerate((qb, kb, vb)):
            qa[number * RANK : (number + 1) * RANK, :] = down_of(dtab, 2 + number)
            take_local(target, utab, OUT_AT[2 + number], me, count)
        take_local(oa, dtab, IN_AT[5], me, count)
        skip.wait(0)
        skip.forward()
        for name in ("q", "k", "v", "o"):
            shared[name].send_own(owns[name].at[half, :])

        @pl.when(core == 0)
        def _():
            words_w.send_own(ck_own)

        @pl.when(core == 1)
        def _():
            words_w.send_own(cv_own)

        skip.swap(0)

        skip.wait(1)
        skip.swap(1)
        cross_step(1)

        for number in (1, 2, 3):
            source = act_all.at[xor_place(dp, number)]
            push(source, source, msend.at[0, number - 1], mrecv.at[0, number - 1], dp_peers[number - 1]).wait_recv()
        for owner in range(4):
            @pl.when(dp == owner)
            def _(owner=owner):
                span_of = slice(owner * mod_rows, (owner + 1) * mod_rows)
                for sequence in range(4):
                    mod_slice[sequence : sequence + 1, :] = act_all[sequence, :, span_of]

        skip.wait(2)
        skip.swap(2)
        products = dot_nn(mod_slice[...].astype(BF), wm[...])
        for sequence in range(4):
            mod_out[sequence] = products[sequence : sequence + 1]
        backs = [
            push(mod_out.at[xor_place(dp, number)], mod_in.at[dp], msend.at[1, number - 1], mrecv.at[1, number - 1],
                 dp_peers[number - 1])
            for number in (1, 2, 3)
        ]
        for copy in backs:
            copy.start()
        mod_in[dp] = mod_out[dp]
        places[0].wait()
        skip.wait_swaps()
        cross_step(2)

        def compute(number):
            @pl.when(number % each == 0)
            def _():
                here = rows_of(number // each, block)
                left = hid[here, :].astype(F32)
                right = lsk[here, :].astype(F32)
                mean = (jnp.sum(left, axis=-1, keepdims=True) + jnp.sum(right, axis=-1, keepdims=True)) / (2 * width)
                spread = jnp.sum((left - mean) ** 2, axis=-1, keepdims=True)
                spread += jnp.sum((right - mean) ** 2, axis=-1, keepdims=True)
                inverse = lax.rsqrt(spread / (2 * width) + NORM_EPS)
                for place in range(count):
                    @pl.when(me == place)
                    def _(place=place):
                        source = hid if place * span < width else lsk
                        start = place * span % width
                        part_x[...] = source[here, start : start + span].astype(F32)
                x = ((part_x[...] - mean) * inverse * pgain[...]).astype(BF)
                u = dot_nt(x, sa[...]).astype(BF)
                y = (dot_nt(x, wskip[...]) + dot_nn(u, up_of(utab, 0))).astype(BF)
                for piece in range(each):
                    partial_a[number + piece] = y[piece * chunk : (piece + 1) * chunk]

        def text_product():
            @pl.when(core == 0)
            def _():
                text_place(ck_own).wait()

            @pl.when(core == 1)
            def _():
                text_place(cv_own).wait()

            x = t_ref[...]
            y = dot_nt(x, wtext[...])

            @pl.when(core == 0)
            def _():
                z = y + dot_nn(dot_nt(x, down_of(dtab, 7)).astype(BF), tk[...])
                parts, sides = [], []
                for head in range(heads):
                    normal, inverse = stats(z[:, head * HD : (head + 1) * HD])
                    upper = inverse.astype(BF)
                    parts.append(normal.astype(BF))
                    sides += [upper, (inverse - upper.astype(F32)).astype(BF)]
                text_kv[0, me, :, :local] = jnp.concatenate(parts, axis=1)
                text_kv[0, me, :, local : local + 2 * heads] = jnp.concatenate(sides, axis=1)

            @pl.when(core == 1)
            def _():
                z = y + dot_nn(dot_nt(x, down_of(dtab, 8)).astype(BF), tv[...])
                text_kv[1, me, :, :local] = z.astype(BF)

        text_slots = text_kv.at[core]

        def finish(slot, total):
            here = rows_of(slot, chunk)
            skip_out[here, :] = total
            normal, _ = stats(total)
            attn_in[here, :] = (normal * gain[0:1, :] + shift_row[...]).astype(BF)

        def project(number, carry):
            here = rows_of(number, block)
            x = attn_in[here, :]
            u = dot_nt(x, qa[...]).astype(BF)
            yq = dot_nn(x, wq[...]) + dot_nn(u[:, :RANK], qb[...])
            yk = dot_nn(x, wk[...]) + dot_nn(u[:, RANK : 2 * RANK], kb[...])
            yv = (dot_nn(x, wv[...]) + dot_nn(u[:, 2 * RANK :], vb[...])).astype(BF)
            parts_q, parts_k = [], []
            for head in range(heads):
                span_of = slice(head * HD, (head + 1) * HD)
                normal, inverse = stats(yq[:, span_of])
                q_out[head, here, :] = normal.astype(BF)
                parts_q.append(inverse)
                normal, inverse = stats(yk[:, span_of])
                keys[core, head, here, :] = normal.astype(BF)
                parts_k.append(inverse)
                values[core, head, here, :] = yv[:, span_of]
            inv_q[here, :] = jnp.concatenate(parts_q, axis=1)
            inv_k[here, :] = jnp.concatenate(parts_k, axis=1)
            return carry

        def beside(number):
            @pl.when(number == 1 * pace)
            def _():
                for other in (1, 2, 3):
                    target = mod_in.at[xor_place(dp, other)]
                    push(target, target, msend.at[1, other - 1], mrecv.at[1, other - 1], dp_peers[other - 1]).wait_recv()
                mod_u = dot_nt(act_low, down_of(dtab, 1)).astype(BF)
                shift_row[...] = mod_in[0] + mod_in[1] + mod_in[2] + mod_in[3] + dot_nn(mod_u, up_of(utab, 1))

            @pl.when(number == 3 * pace)
            def _():
                for weight in (*shared.values(), words_w):
                    weight.wait(0)
                    weight.forward()
                for weight in (*shared.values(), words_w):
                    weight.wait(1)
                for weight in shared.values():
                    weight.swap(0)
                    weight.swap(1)

            @pl.when(number == 4 * pace)
            def _():
                cross_step(3)
                for weight in cross:
                    weight.send_own()

            @pl.when(number == 7 * pace)
            def _():
                for weight in (*shared.values(), words_w):
                    weight.wait(2)
                for weight in shared.values():
                    weight.swap(2)

            @pl.when(number == 8 * pace)
            def _():
                for weight in wide:
                    weight.send_own(up_own.at[half, :])
                for place in places[1:5]:
                    place.wait()
                for weight in shared.values():
                    weight.wait_swaps()
                project(0, 0)

            @pl.when(number == steps + count - 3)
            def _():
                text_product()
                line_gather_step(text_line, 0, text_slots)

        line_reduce_all(reduce_line, steps, compute, partial_a, left_a, right_a, sr_a, sl_a, finish, beside)

        lax.fori_loop(1, tokens // block, project, 0)
        stores = [
            pltpu.make_async_copy(source, target, out_sem.at[number])
            for number, (source, target) in enumerate(
                ((skip_out, skip_hbm), (attn_in, attn_hbm), (wq, wq_hbm), (wk, wk_hbm), (wv, wv_hbm), (wo, wo_hbm))
            )
        ]
        for store in stores:
            store.start()

        swaps = [
            push(ref.at[core], ref.at[core], xsend.at[number], xrecv.at[number], peer)
            for number, ref in enumerate((keys, values))
        ]
        for swap in swaps:
            swap.start()
        line_gather_step(text_line, 1, text_slots)
        for weight in cross:
            weight.wait(0)
            weight.forward()
            weight.swap(0)
            weight.swap(3)
        for number, ref in enumerate((keys, values)):
            push(ref.at[1 - core], ref.at[1 - core], xsend.at[number], xrecv.at[number], peer).wait_recv()

        def attend(place, carry):
            dest = scatter_order(me, count, place)
            here = rows_of(dest, share)
            outs, logs = [], []
            for head in range(heads):
                q = q_out[head, here, :]
                s0 = dot_nt(q, keys[0, head]) * scale
                s1 = dot_nt(q, keys[1, head]) * scale
                top = jnp.maximum(jnp.max(s0, axis=-1, keepdims=True), jnp.max(s1, axis=-1, keepdims=True))
                e0 = jnp.exp(s0 - top)
                e1 = jnp.exp(s1 - top)
                total = jnp.sum(e0, axis=-1, keepdims=True) + jnp.sum(e1, axis=-1, keepdims=True)
                share_of = 1.0 / total
                p0 = (e0 * share_of).astype(BF)
                p1 = (e1 * share_of).astype(BF)
                outs.append(dot_nn(p0, values[0, head]) + dot_nn(p1, values[1, head]))
                logs.append(top + jnp.log(total))
            low = jnp.concatenate(outs, axis=1).astype(BF)
            low_out[here, :] = low
            log_out[here, :] = jnp.concatenate(logs, axis=1)
            u = dot_nt(low, oa[...]).astype(BF)
            partial_b[dest] = (dot_nt(low, wo[...]) + dot_nn(u, up_of(utab, 5))).astype(BF)

            @pl.when(place < count - 1)
            def _():
                line_scatter_step(scatter_line, place, partial_b, left_b, right_b, sr_b, sl_b)

            @pl.when(place == 0)
            def _():
                line_gather_step(text_line, 2, text_slots)

            @pl.when(place == 1)
            def _():
                for weight in cross:
                    weight.wait(1)
                    weight.swap(1)
                line_gather_step(text_line, 3, text_slots)
                push(text_slots, text_slots, tsend, trecv, peer).start()

            @pl.when(place == 2)
            def _():
                for weight in cross:
                    weight.wait(2)
                    weight.swap(2)

            return carry

        lax.fori_loop(0, count, attend, 0)
        line_scatter_finish(scatter_line, partial_b, left_b, right_b, sr_b, sl_b, summed)
        for weight in wide:
            weight.wait(0)
            weight.wait(1)
        others = text_kv.at[1 - core]
        push(others, others, tsend, trecv, peer).wait_recv()
        for weight in cross:
            weight.wait_swaps()
        places[5].wait()
        for store in stores:
            store.wait()
        for weight in (skip, *shared.values(), words_w, *cross):
            weight.drain()
        for weight in wide:
            weight.drain_own()
        for which, cross_line in enumerate(cross_lines):
            line_gather_drain(cross_line, cross_view(which))
        for copy in spread + backs:
            copy.wait_send()
        line_gather_drain(text_line, text_slots)
        push(text_slots, text_slots, tsend, trecv, peer).wait_send()
        for swap in swaps:
            swap.wait_send()

    names = ("skip", "q", "k", "v", "o", "ck", "cv", "cq", "co", "up")
    return call(
        kernel,
        [(weights[name], name in ("cq", "co", "up")) for name in names] + [(index, None)]
        + [(array, True) for array in (condition, hidden, long_skip, text, mod_weight, gain_halves, gain_rows, *tables)],
        [
            ((tokens, width), F32, False),
            ((tokens, width), BF, False),
            ((heads, tokens, HD), BF, True),
            ((2, heads, tokens, HD), BF, True),
            ((2, heads, tokens, HD), BF, True),
            ((tokens, local), BF, True),
            ((tokens, heads), F32, True),
            ((tokens, heads), F32, True),
            ((tokens, heads), F32, True),
            ((share, width), F32, True),
            ((4, 1, width + 128), F32, True),
            ((2, count, words, local + 32), BF, True),
        ]
        + [((width, local), BF, False) for _ in range(4)]
        + [((count, width, local), BF, False) for _ in range(2)]
        + [((width, units), BF, False)],
        [vmem(tokens, width, dtype=F32), vmem(tokens, width)] + [vmem(width, local) for _ in range(4)]
        + [dma(6), vmem(1, width, dtype=F32), vmem(width, span), vmem(local, text_width), vmem(block, span, dtype=F32), vmem(1, span, dtype=F32),
         vmem(RANK, span), vmem(RANK, local), vmem(RANK, local), vmem(3 * RANK, width)]
        + [vmem(RANK, local) for _ in range(4)]
        + [vmem(4, 1, width, dtype=F32), vmem(4, mod_rows, dtype=F32),
         vmem(4, 1, width, dtype=F32)]
        + [vmem(steps, chunk, width) for _ in range(5)] + [vmem(count, share, width) for _ in range(5)]
        + [dma(10, 7), dma(10, 7), dma(10), dma(2, 3), dma(2, 3), dma(), dma(),
           dma(2), dma(2)]
        + [dma(steps) for _ in range(4)] + [dma(count) for _ in range(16)],
        collective=1,
        cost=cost_of(8 * tokens * width * local, 60e6),
    )


def attention_backward(count, heads, g_first, query, keys, values, low, logs, inv_q, inv_k, out_weight, tables):
    share, width = g_first.shape
    tokens = query.shape[1]
    local = low.shape[1]
    scale = HD ** (-0.5)

    def kernel(g_ref, *refs):
        sources, refs = refs[:10], refs[10:]
        (gq_low, gk_low, gv_low, gall, ga_o, gb_o, q_ref, k_ref, v_ref, low_ref, log_ref, iq_ref, ik_ref, wo, dtab, utab,
         gk_acc, gv_acc, swap_out, swap_in, ao, lsem, xsend, xrecv, *sems) = refs
        loads = [
            pltpu.make_async_copy(source, target, lsem.at[number])
            for number, (source, target) in enumerate(
                zip(sources, (q_ref, k_ref, v_ref, low_ref, log_ref, iq_ref, ik_ref, wo, dtab, utab))
            )
        ]
        for load in loads:
            load.start()
        me = lax.axis_index("tensor")
        core = lax.axis_index("ctx")
        peer = {"ctx": 1 - core}
        grad_line = Line(me, count, *sems)
        gall[me] = g_ref[...]
        greet(line_partners(me, count) + [(core >= 0, peer)])
        line_gather_step(grad_line, 0, gall)
        for ref in (ga_o, gb_o, gk_acc, gv_acc):
            ref[...] = jnp.zeros_like(ref)
        for load in loads:
            load.wait()
        take_local(ao, dtab, IN_AT[5], me, count)

        def attend(place):
            rows = rows_of(place, share)
            g = gall[place]
            go = dot_nt(g, up_of(utab, 5)).astype(BF)
            g_attn = (dot_nn(g, wo[...]) + dot_nn(go, ao[...])).astype(BF)
            low = low_ref[rows, :]
            uo = dot_nt(low, ao[...]).astype(BF)
            gb_o[...] += dot_tn(uo, g)
            ga_o[...] += dot_tn(go, low)
            parts = []
            for head in range(heads):
                gh = g_attn[:, head * HD : (head + 1) * HD]
                q = q_ref[head, rows, :]
                probs, grads = [], []
                inner = 0.0
                for half in range(2):
                    p = jnp.exp(dot_nt(q, k_ref[half, head]) * scale - log_ref[rows, head : head + 1])
                    dp = dot_nt(gh, v_ref[half, head])
                    inner = inner + jnp.sum(p * dp, axis=-1, keepdims=True)
                    probs.append(p)
                    grads.append(dp)
                dq = 0.0
                for half in range(2):
                    ds = (probs[half] * (grads[half] - inner)).astype(BF)
                    dq = dq + dot_nn(ds, k_ref[half, head])
                    gk_acc[half, head] += dot_tn(ds, q)
                    gv_acc[half, head] += dot_tn(probs[half].astype(BF), gh)
                parts.append(norm_backward(q.astype(F32), iq_ref[rows, head : head + 1], dq * scale))
            gq_low[rows, :] = jnp.concatenate(parts, axis=1).astype(BF)

        def gather(number, carry):
            @pl.when(number > 0)
            def _():
                line_gather_step(grad_line, number, gall)

            def side(which, inner):
                place = me + (2 * which - 1) * number

                @pl.when((place >= 0) & (place < count) & ((number > 0) | (which == 0)))
                def _():
                    attend(lax.clamp(0, place, count - 1))

                return inner

            return lax.fori_loop(0, 2, side, carry)

        lax.fori_loop(0, count, gather, 0)
        swaps = []
        for head in range(heads):
            swap_out[head, 0] = (gk_acc[1 - core, head] * scale).astype(BF)
            swap_out[head, 1] = gv_acc[1 - core, head].astype(BF)
            swaps.append(push(swap_out.at[head], swap_in.at[head], xsend.at[head], xrecv.at[head], peer))
            swaps[-1].start()
        line_gather_drain(grad_line, gall)
        for head in range(heads):
            at = slice(head * HD, (head + 1) * HD)
            swaps[head].wait_recv()
            dk = gk_acc[core, head] * scale + swap_in[head, 0].astype(F32)
            normal = k_ref[core, head].astype(F32)
            gk_low[:, at] = norm_backward(normal, ik_ref[:, head : head + 1], dk).astype(BF)
            gv_low[:, at] = (gv_acc[core, head] + swap_in[head, 1].astype(F32)).astype(BF)
        for swap in swaps:
            swap.wait_send()

    return call(
        kernel,
        [(g_first, True)]
        + [(array, False) for array in (query, keys, values, low, logs, inv_q, inv_k, out_weight, *tables)],
        [
            ((tokens, local), BF, True),
            ((tokens, local), BF, True),
            ((tokens, local), BF, True),
            ((count, share, width), BF, True),
            ((RANK, local), F32, True),
            ((RANK, width), F32, True),
        ],
        [pltpu.VMEM(array.shape, array.dtype)
         for array in (query, keys, values, low, logs, inv_q, inv_k, out_weight, *tables)]
        + [vmem(2, heads, tokens, HD, dtype=F32), vmem(2, heads, tokens, HD, dtype=F32), vmem(heads, 2, tokens, HD),
           vmem(heads, 2, tokens, HD), vmem(RANK, local), dma(10), dma(heads), dma(heads)]
        + [dma(count) for _ in range(4)],
        collective=4,
        cost=cost_of(16 * tokens * width * local, 60e6),
    )


EARLY_A, EARLY_B = IN_AT[2], OUT_AT[2]
EARLY = IN_AT[12] - EARLY_A + OUT_AT[12] - EARLY_B
LATE = EARLY_A + EARLY_B


def back_end(count, grads, projections, attn_in, g_first, skip_out, hidden, long_skip, weight, mod_weight, block_sum,
             gain_halves, gain_rows, tables, condition, act_all, wide_grads, local_down, local_up, stacked):
    tokens, width = hidden.shape
    local = grads[0].shape[1]
    span = weight.shape[-1]
    block = tokens // count
    chunk = min(CHUNK, block)
    pace = max(1, 64 // chunk)
    each = block // chunk
    steps = tokens // chunk
    own_rows = RANK // count
    half_e = -(-EARLY // 256) * 128
    half_l = -(-LATE // 256) * 128
    base = IN_AT[12] - EARLY_A
    mod_rows = mod_weight.shape[0]

    def early(column):
        return column - EARLY_A if column < IN_AT[12] else column - EARLY_A - EARLY_B

    wide_at, wide = [early(column) for column in wide_grads], list(wide_grads.values())
    local_at = [early(column) for column in local_down] + [early(IN_AT[12] + column) for column in local_up]
    own_grads = list(local_down.values()) + list(local_up.values())
    stacked_at, stack = [early(column) for column in stacked], list(stacked.values())

    def kernel(gq, gk, gv, wq, wk, wv, x_hbm, gf_hbm, skip_hbm, hid_hbm, lsk_hbm, hbm_w, wm_hbm, b_in, gains, gain, dtab,
               utab, cond, act_ref, *refs):
        wide_refs, refs = refs[: len(wide)], refs[len(wide) :]
        own_refs, refs = refs[: len(own_grads)], refs[len(own_grads) :]
        stack_refs, refs = refs[: len(stack)], refs[len(stack) :]
        (out_h, out_l, out_a, out_b, out_c, ball, w, x_ref, gf_ref, skip_ref, hid, lsk, wm, buf_h, buf_l, low, g_ref, qkv_a, bq, bk, bv, partial_g, left_g, right_g,
         sr_g, sl_g, table, late, swap_out, swap_in, partial_e, left_e, right_e, sr_e, sl_e, summed, late_out, late_in,
         partial_l, slots_l, slots, late_slots, other_out, other_in, later_out, later_in, shifts, shift_in, act_out, act_in, g_act, g_sum,
         wsem, osem, ssem, rsem, dsend, drecv, msend, mrecv, zsend, zrecv, *sems) = refs
        me = lax.axis_index("tensor")
        core = lax.axis_index("ctx")
        dp = lax.axis_index("dp")
        peer = {"ctx": 1 - core}
        grad_line = Line(me, count, *sems[:4])
        early_line = Line(me, count, *sems[4:8])
        block_line = Line(me, count, *sems[8:])
        peers = [{"dp": xor_place(dp, number)} for number in (1, 2, 3)]
        z_peers = [{"tensor": xor_place(me, number)} for number in range(1, count)]
        loads = [
            pltpu.make_async_copy(source, target, wsem.at[number])
            for number, (source, target) in enumerate(
                ((x_hbm, x_ref), (gf_hbm, gf_ref), (skip_hbm, skip_ref), (hid_hbm, hid), (lsk_hbm, lsk), (hbm_w, w),
                 (wm_hbm, wm))
            )
        ]
        for load in loads:
            load.start()
        ball[me] = b_in[...]
        everyone = [(core >= 0, device) for device in z_peers + peers + [peer]]
        greet_all(everyone)
        for number, target in enumerate((bq, bk, bv)):
            qkv_a[number * RANK : (number + 1) * RANK, :] = down_of(dtab, 2 + number)
            take_local(target, utab, OUT_AT[2 + number], me, count)
        g_sum[...] = jnp.zeros_like(g_sum)
        act_low = act_ref[dp, :, :width].astype(BF)

        def compute(number):
            @pl.when((number % each == 0) & (number > 0))
            def _():
                product(number)

        def product(number):
            rows = rows_of(number // each, block)
            gu = jnp.concatenate(
                [dot_nt(gq[rows, :], bq[...]), dot_nt(gk[rows, :], bk[...]), dot_nt(gv[rows, :], bv[...])], axis=1
            ).astype(BF)
            y = dot_nt(gq[rows, :], wq[...]) + dot_nt(gk[rows, :], wk[...]) + dot_nt(gv[rows, :], wv[...])
            y = (y + dot_nn(gu, qkv_a[...])).astype(BF)
            for piece in range(each):
                partial_g[number + piece] = y[piece * chunk : (piece + 1) * chunk]

        def finish(slot, total):
            g_ref[rows_of(slot, chunk), :] = total

        def skip_block(number):
            rows = rows_of(number, block)
            ga_in = g_ref[rows, :]
            g_sum[...] += jnp.sum(ga_in, axis=0, keepdims=True)
            normal, inverse = stats(skip_ref[rows, :])
            g_low = (
                gf_ref[number].astype(F32) + norm_backward(normal, inverse, ga_in * gain[0:1, :])
            ).astype(BF)
            left = hid[rows, :].astype(F32)
            right = lsk[rows, :].astype(F32)
            mean = (jnp.sum(left, axis=-1, keepdims=True) + jnp.sum(right, axis=-1, keepdims=True)) / (2 * width)
            left = left - mean
            right = right - mean
            spread = jnp.sum(left * left, axis=-1, keepdims=True) + jnp.sum(right * right, axis=-1, keepdims=True)
            inverse = lax.rsqrt(spread / (2 * width) + NORM_EPS)
            left = left * inverse
            right = right * inverse
            gu = dot_nt(g_low, up_of(utab, 0)).astype(BF)
            a_left, a_right = dtab[:, :width], dtab[:, width : 2 * width]

            @pl.when(number == me)
            def _():
                low_l = (left * gains[0:1, :]).astype(BF)
                low_r = (right * gains[1:2, :]).astype(BF)
                u = (dot_nt(low_l, a_left) + dot_nt(low_r, a_right)).astype(BF)
                late[:, :width] = dot_tn(gu, low_l)
                late[:, width : 2 * width] = dot_tn(gu, low_r)
                late[:, EARLY_A : EARLY_A + width] = dot_tn(u, g_low)

            for place in range(count):
                low[:, place * span : (place + 1) * span] = dot_nn(g_low, w[place])
            gl = (low[:, :width] + dot_nn(gu, a_left)) * gains[0:1, :]
            gr = (low[:, width:] + dot_nn(gu, a_right)) * gains[1:2, :]
            mean = (jnp.sum(gl, axis=-1, keepdims=True) + jnp.sum(gr, axis=-1, keepdims=True)) / (2 * width)
            inner = (
                jnp.sum(gl * left, axis=-1, keepdims=True) + jnp.sum(gr * right, axis=-1, keepdims=True)
            ) / (2 * width)
            buf_h[number] = inverse * (gl - mean - left * inner)
            buf_l[number] = inverse * (gr - mean - right * inner)
            pltpu.make_async_copy(buf_h.at[number], out_h.at[rows, :], osem.at[0, number]).start()
            pltpu.make_async_copy(buf_l.at[number], out_l.at[rows, :], osem.at[1, number]).start()

        swap = push(swap_out, swap_in, ssem.at[0], rsem.at[0], peer)
        sends = [
            push(slots.at[dp], slots.at[dp], dsend.at[0, number], drecv.at[0, number], device)
            for number, device in enumerate(peers)
        ]

        def early_step(number):
            line_scatter_step(early_line, number, partial_e, left_e, right_e, sr_e, sl_e)

        def beside(number):
            @pl.when(number == pace)
            def _():
                for load in loads:
                    load.wait()
                x = x_ref[...]
                u = dot_nt(x, qkv_a[...]).astype(BF)
                table[...] = jnp.zeros_like(table)
                late[...] = jnp.zeros_like(late)
                for start, ref in zip(wide_at, wide_refs):
                    table[:, start : start + ref.shape[1]] = ref[...]
                for start, ref in zip(stacked_at, stack_refs):
                    size = ref.shape[2]
                    for place in range(count):
                        table[:, start + place * size : start + (place + 1) * size] = ref[place]
                qkv_b = []
                for which, (grad, factor) in enumerate(((gq, bq), (gk, bk), (gv, bv))):
                    gu = dot_nt(grad[...], factor[...]).astype(BF)
                    table[:, which * width : (which + 1) * width] = dot_tn(gu, x)
                    qkv_b.append(dot_tn(u[:, which * RANK : (which + 1) * RANK], grad[...]))
                for place in range(count):
                    @pl.when(me == place)
                    def _(place=place):
                        for which, piece in enumerate(qkv_b):
                            start = base + which * width + place * local
                            table[:, start : start + local] = piece
                        for start, ref in zip(local_at, own_refs):
                            size = ref.shape[1]
                            table[:, start + place * size : start + (place + 1) * size] = ref[...]
                for which in range(2):
                    @pl.when(core == which)
                    def _(which=which):
                        swap_out[...] = table[:, (1 - which) * half_e : (2 - which) * half_e].astype(BF)

                swap.start()

            @pl.when(number == 3 * pace)
            def _():
                swap.wait()
                for which in range(2):
                    @pl.when(core == which)
                    def _(which=which):
                        for part in range(count):
                            at = slice(part * own_rows, (part + 1) * own_rows)
                            mine = table[at, which * half_e : (which + 1) * half_e]
                            partial_e[part] = (mine + swap_in[at, :].astype(F32)).astype(BF)

            @pl.when((number >= steps) & (number < steps + count - 1))
            def _():
                early_step(number - steps)

            @pl.when(number == steps - 1)
            def _():
                line_gather_step(block_line, 0, ball)

        def after(slot):
            @pl.when(slot % each == each - 1)
            def _():
                skip_block(slot // each)

        product(0)
        await_all(everyone)
        line_reduce_all(
            grad_line, steps, compute, partial_g, left_g, right_g, sr_g, sl_g, finish, beside, after
        )

        g_shift = g_sum[...]
        shift_in[0] = g_shift
        swap_shift = push(shift_in.at[0], shift_in.at[1], ssem.at[2], rsem.at[2], peer)
        swap_shift.start()
        mod_u = dot_nt(act_low, down_of(dtab, 1))
        once = jnp.where(me == 0, 1.0, 0.0)
        shift_u = dot_nt(g_shift.astype(BF), up_of(utab, 1))
        zeros_u, zeros_w = jnp.zeros((7, RANK), F32), jnp.zeros((7, width), F32)
        mod_a = jnp.concatenate([shift_u * once, zeros_u], axis=0).astype(BF)
        mod_b = jnp.concatenate([mod_u * once, zeros_u], axis=0).astype(BF)
        act_pad = jnp.concatenate([act_low.astype(F32), zeros_w], axis=0).astype(BF)
        shift_pad = jnp.concatenate([g_shift, zeros_w], axis=0).astype(BF)
        late[:, IN_AT[1] : IN_AT[2]] = dot_tn(mod_a, act_pad)
        late[:, EARLY_A + OUT_AT[1] : EARLY_A + OUT_AT[2]] = dot_tn(mod_b, shift_pad)
        for which in range(2):
            @pl.when(core == which)
            def _(which=which):
                late_out[...] = late[:, (1 - which) * half_l : (2 - which) * half_l].astype(BF)

        swap_late = push(late_out, late_in, ssem.at[1], rsem.at[1], peer)
        swap_late.start()
        line_gather_step(block_line, 1, ball)
        line_scatter_finish(early_line, partial_e, left_e, right_e, sr_e, sl_e, summed)
        slots[dp] = summed[...].astype(BF)
        for send in sends:
            send.start()
        swap_shift.wait()
        shifts[dp] = shift_in[0] + shift_in[1]
        shift_sends = [
            push(shifts.at[dp], shifts.at[dp], msend.at[0, number], mrecv.at[0, number], device)
            for number, device in enumerate(peers)
        ]
        for send in shift_sends:
            send.start()
        swap_late.wait()
        for which in range(2):
            @pl.when(core == which)
            def _(which=which):
                for part in range(count):
                    at = slice(part * own_rows, (part + 1) * own_rows)
                    mine = late[at, which * half_l : (which + 1) * half_l]
                    partial_l[part] = (mine + late_in[at, :].astype(F32)).astype(BF)

        late_sends = [
            push(partial_l.at[xor_place(me, number + 1)], slots_l.at[me], zsend.at[number], zrecv.at[number], device)
            for number, device in enumerate(z_peers)
        ]
        for send in late_sends:
            send.start()
        slots_l[me] = partial_l[me]
        line_gather_step(block_line, 2, ball)
        for number in (1, 2, 3):
            source = shifts.at[xor_place(dp, number)]
            push(source, source, msend.at[0, number - 1], mrecv.at[0, number - 1], peers[number - 1]).wait_recv()
        every = jnp.concatenate([shifts[sequence] for sequence in range(4)], axis=0).astype(BF)
        products = dot_nt(every, wm[...])
        for sequence in range(4):
            act_out[sequence] = products[sequence : sequence + 1]
        act_sends = [
            push(act_out.at[xor_place(dp, number)], act_in.at[dp], msend.at[1, number - 1], mrecv.at[1, number - 1],
                 peers[number - 1])
            for number in (1, 2, 3)
        ]
        for send in act_sends:
            send.start()
        for number in range(count - 1):
            arrived = slots_l.at[xor_place(me, number + 1)]
            push(arrived, arrived, zsend.at[number], zrecv.at[number], z_peers[number]).wait_recv()
        late_sum = slots_l[0].astype(F32)
        for place in range(1, count):
            late_sum = late_sum + slots_l[place].astype(F32)
        late_slots[dp] = late_sum.astype(BF)
        later_sends = [
            push(late_slots.at[dp], late_slots.at[dp], dsend.at[1, number], drecv.at[1, number], device)
            for number, device in enumerate(peers)
        ]
        for send in later_sends:
            send.start()

        def arrive(ref, which):
            for number in (1, 2, 3):
                source = ref.at[xor_place(dp, number)]
                push(source, source, dsend.at[which, number - 1], drecv.at[which, number - 1], peers[number - 1]).wait_recv()

        def total(ref, which):
            slot = (dp * 2 + which).astype(F32)
            result = jnp.zeros(ref.shape[1:], F32)
            for sequence in range(4):
                chosen = jnp.where(act_ref[sequence, :, width : width + 1] == slot, 1.0, 0.0)
                result = result + ref[sequence].astype(F32) * chosen
            return result

        arrive(slots, 0)
        other_out[...] = total(slots, 1 - core).astype(BF)
        last = push(other_out, other_in, ssem.at[3], rsem.at[3], peer)
        last.start()
        mine_e = total(slots, core)
        line_gather_step(block_line, 3, ball)
        arrive(late_slots, 1)
        later_out[...] = total(late_slots, 1 - core).astype(BF)
        latest = push(later_out, later_in, ssem.at[4], rsem.at[4], peer)
        latest.start()
        mine_l = total(late_slots, core)

        act_in[dp] = act_out[dp]
        for number in (1, 2, 3):
            source = act_in.at[xor_place(dp, number)]
            push(source, source, msend.at[1, number - 1], mrecv.at[1, number - 1], peers[number - 1]).wait_recv()
        for place in range(4):
            g_act[:, place * mod_rows : (place + 1) * mod_rows] = act_in[place]
        full_u = dot_nt(shifts[dp].astype(BF), up_of(utab, 1)).astype(BF)
        grad = g_act[...] + dot_nn(full_u, down_of(dtab, 1))
        value = cond[...].astype(F32)
        gate = 1.0 / (1.0 + jnp.exp(-value))
        out_c[...] = grad * gate * (1.0 + value * (1.0 - gate))

        def lay(mine, arrived, target):
            for which in range(2):
                @pl.when(core == which)
                def _(which=which):
                    target(which, mine)
                    target(1 - which, arrived[...].astype(F32))

        def lay_early(which, values):
            start = which * half_e
            low_a = max(0, min(base - start, half_e))
            if low_a:
                out_a[:, EARLY_A + start : EARLY_A + start + low_a] = values[:, :low_a]
            if low_a < half_e:
                at = EARLY_B + start + low_a - base
                out_b[:, at : at + min(half_e, EARLY - start) - low_a] = values[:, low_a : min(half_e, EARLY - start)]

        def lay_late(which, values):
            start = which * half_l
            low_a = max(0, min(EARLY_A - start, half_l))
            end = min(half_l, LATE - start)
            if low_a:
                out_a[:, start : start + low_a] = values[:, :low_a]
            if low_a < end:
                at = start + low_a - EARLY_A
                out_b[:, at : at + end - low_a] = values[:, low_a:end]

        last.wait_recv()
        lay(mine_e, other_in, lay_early)
        latest.wait_recv()
        lay(mine_l, later_in, lay_late)
        line_gather_drain(block_line, ball)
        last.wait_send()
        latest.wait_send()
        for send in sends + later_sends + shift_sends + act_sends + late_sends:
            send.wait_send()

        def drain(number, carry):
            rows = rows_of(number, block)
            pltpu.make_async_copy(buf_h.at[number], out_h.at[rows, :], osem.at[0, number]).wait()
            pltpu.make_async_copy(buf_l.at[number], out_l.at[rows, :], osem.at[1, number]).wait()
            return carry

        lax.fori_loop(0, count, drain, 0)

    part_e = (own_rows, half_e)
    part_l = (own_rows, half_l)
    return call(
        kernel,
        [(array, True) for array in (*grads, *projections)]
        + [(array, False) for array in (attn_in, g_first, skip_out, hidden, long_skip, weight, mod_weight)]
        + [(array, True) for array in (block_sum, gain_halves, gain_rows, *tables, condition, act_all, *wide, *own_grads,
                                       *stack)],
        [
            ((tokens, width), F32, False),
            ((tokens, width), F32, False),
            ((own_rows, IN_AT[12]), F32, True),
            ((own_rows, OUT_AT[12]), F32, True),
            ((1, width), F32, True),
            ((count, block, width), BF, True),
        ],
        [
            vmem(count, width, span),
            vmem(tokens, width), vmem(count, block, width), vmem(tokens, width, dtype=F32), vmem(tokens, width),
            vmem(tokens, width), vmem(mod_rows, width),
            vmem(count, block, width, dtype=F32),
            vmem(count, block, width, dtype=F32),
            vmem(block, 2 * width, dtype=F32),
            vmem(tokens, width, dtype=F32),
            vmem(3 * RANK, width),
            vmem(RANK, local), vmem(RANK, local), vmem(RANK, local),
        ]
        + [vmem(steps, chunk, width) for _ in range(5)]
        + [vmem(RANK, 2 * half_e, dtype=F32), vmem(RANK, 2 * half_l, dtype=F32), vmem(RANK, half_e), vmem(RANK, half_e)]
        + [vmem(count, *part_e) for _ in range(5)]
        + [vmem(*part_e, dtype=F32), vmem(RANK, half_l), vmem(RANK, half_l), vmem(count, *part_l), vmem(count, *part_l)]
        + [vmem(4, *part_e), vmem(4, *part_l), vmem(*part_e), vmem(*part_e), vmem(*part_l), vmem(*part_l)]
        + [vmem(4, 1, width, dtype=F32), vmem(2, 1, width, dtype=F32), vmem(4, 1, mod_rows, dtype=F32),
           vmem(4, 1, mod_rows, dtype=F32), vmem(1, width, dtype=F32), vmem(1, width, dtype=F32)]
        + [dma(7), dma(2, count), dma(5), dma(5), dma(2, 3), dma(2, 3), dma(2, 3), dma(2, 3), dma(count), dma(count)]
        + [dma(steps) for _ in range(4)] + [dma(count) for _ in range(8)],
        collective=5,
        cost=cost_of(4 * tokens * width * width, 30e6),
    )


def prepare(index, down_factor, up_factor, gain, transposed):
    def kernel(index_ref, down_ref, up_ref, gain_ref, *refs):
        count = len(transposed)
        weight_refs, (down_out, up_out, gain_out), outs = refs[:count], refs[count : count + 3], refs[count + 3 :]
        down_out[...] = down_ref[0]
        up_out[...] = up_ref[0]
        gain_out[0, :] = gain_ref[:MODEL_WIDTH]
        gain_out[1, :] = gain_ref[MODEL_WIDTH:]
        for source, target in zip(weight_refs, outs):
            target[...] = source[...].T

    def whole(shape):
        return pl.BlockSpec(shape, lambda step, index_ref: (0,) * len(shape))

    shapes = [down_factor.shape[1:], up_factor.shape[1:]]
    out_shapes = [(shape, BF) for shape in shapes] + [((2, MODEL_WIDTH), F32)]
    out_shapes += [(weight.shape[::-1], BF) for weight in transposed]
    return pl.pallas_call(
        kernel,
        grid_spec=pltpu.PrefetchScalarGridSpec(
            num_scalar_prefetch=1,
            grid=(1,),
            in_specs=[pl.BlockSpec((1, *shape), lambda step, index_ref: (index_ref[0], 0, 0)) for shape in shapes]
            + [whole((2 * MODEL_WIDTH,))] + [whole(weight.shape) for weight in transposed],
            out_specs=[whole(shape) for shape, _ in out_shapes],
        ),
        out_shape=[jax.ShapeDtypeStruct(shape, dtype) for shape, dtype in out_shapes],
        compiler_params=pltpu.CompilerParams(vmem_limit_bytes=VMEM_BYTES),
    )(index, down_factor, up_factor, gain, *transposed)


def fused_body(
    hidden,
    long_skip_input,
    condition,
    projected_text_tokens,
    sequence_adapter_index,
    skip_projection_weight,
    shift_modulation_weight,
    self_query_weight,
    self_key_weight,
    self_value_weight,
    attention_output_weight,
    cross_query_weight,
    cross_key_weight,
    cross_value_weight,
    cross_output_weight,
    feedforward_up_weight,
    feedforward_down_weight,
    skip_norm_gain,
    norm_gain_rows,
    adapter_down_factor,
    adapter_up_factor,
    cotangent,
):
    rank = lax.axis_index("tensor")
    count = lax.axis_size("tensor")
    core = lax.axis_index("ctx")
    dp = lax.axis_index("dp")
    hidden, long_skip, text, cot = hidden[0], long_skip_input[0], projected_text_tokens[0], cotangent[0]
    local = self_query_weight.shape[1]
    heads = local // HD
    down_table, up_table, gain_halves, skip_t, attn_out_t, cross_out_t = prepare(
        sequence_adapter_index, adapter_down_factor, adapter_up_factor, skip_norm_gain,
        (skip_projection_weight, attention_output_weight, cross_output_weight),
    )
    tables = (down_table, up_table)

    weights = {
        "skip": skip_t,
        "q": self_query_weight,
        "k": self_key_weight,
        "v": self_value_weight,
        "o": attn_out_t,
        "ck": cross_key_weight.T,
        "cv": cross_value_weight.T,
        "cq": cross_query_weight,
        "co": cross_out_t,
        "up": feedforward_up_weight,
        "dn": feedforward_down_weight.T,
    }
    (skip_out, attn_in, query, keys, values, low, logs, inv_q, inv_k, summed, act_all, text_kv, wq, wk, wv, wo, wcq, wco,
     wup) = front(
        count, heads, condition, sequence_adapter_index, hidden, long_skip, text, weights, shift_modulation_weight,
        gain_halves, norm_gain_rows, tables,
    )
    (g_first, block_sum, g_cq_a, g_cq_b, g_ck_a, g_ck_b, g_cv_a, g_cv_b, g_co_a, g_co_b, g_up_a, g_up_b, g_down_a, g_down_b,
     skip_all) = middle(
        count, heads, summed, skip_out, wcq, wco, wup, weights["dn"], weights["skip"], text_kv, text,
        cot.reshape(count, 2, -1, MODEL_WIDTH), norm_gain_rows, tables,
    )
    gq, gk, gv, g_first_all, g_o_a, g_o_b = attention_backward(
        count, heads, g_first, query, keys, values, low, logs, inv_q, inv_k, wo, tables
    )
    base = IN_AT[12]
    hidden_grad, skip_grad, grad_down, grad_up, g_condition, block_all = back_end(
        count, (gq, gk, gv), (wq, wk, wv), attn_in, g_first_all, skip_out, hidden, long_skip, skip_all,
        shift_modulation_weight, block_sum, gain_halves, norm_gain_rows, tables, condition, act_all,
        {
            IN_AT[6]: g_cq_a, IN_AT[7]: g_ck_a, IN_AT[8]: g_cv_a, IN_AT[10]: g_up_a,
            base + OUT_AT[5]: g_o_b, base + OUT_AT[9]: g_co_b, base + OUT_AT[11]: g_down_b,
        },
        {IN_AT[5]: g_o_a, IN_AT[11]: g_down_a},
        {OUT_AT[10]: g_up_b},
        {
            IN_AT[9]: g_co_a, base + OUT_AT[6]: g_cq_b, base + OUT_AT[7]: g_ck_b, base + OUT_AT[8]: g_cv_b,
        },
    )
    block_out = block_all.reshape(hidden.shape)
    size = MODEL_WIDTH // (2 * count)
    condition_gradient = lax.dynamic_slice_in_dim(g_condition[0], (core * count + rank) * size, size, 0)
    return (
        block_out[None],
        hidden_grad[None],
        skip_grad[None],
        condition_gradient,
        grad_down.reshape(-1),
        grad_up.reshape(-1),
    )


def solution(mesh):
    in_specs = (
        P("dp", "ctx", None),
        P("dp", "ctx", None),
        P("dp", None),
        P("dp", None, None),
        P("dp"),
        P("tensor", "dp"),
        P("dp", None),
        P("dp", "tensor"),
        P("dp", "tensor"),
        P("dp", "tensor"),
        P("tensor", "dp"),
        P("dp", "tensor"),
        P("dp", "tensor"),
        P("dp", "tensor"),
        P("tensor", "dp"),
        P("dp", "tensor"),
        P("tensor", "dp"),
        P(),
        P(),
        P(),
        P(),
        P("dp", "ctx", None),
    )
    out_specs = (
        P("dp", "ctx", None),
        P("dp", "ctx", None),
        P("dp", "ctx", None),
        P(("dp", "ctx", "tensor")),
        P(("dp", "ctx", "tensor")),
        P(("dp", "ctx", "tensor")),
    )
    shape = mesh.shape
    fused = shape["dp"] == 4 and shape["ctx"] == 2 and shape["tensor"] == 4
    return jax.shard_map(fused_body if fused else body, mesh=mesh, in_specs=in_specs, out_specs=out_specs, check_vma=False)
```

```python
from functools import partial

import jax
import jax.numpy as jnp
from jax import lax
from jax.experimental import pallas as pl
from jax.experimental.pallas import tpu as pltpu
from jax.sharding import PartitionSpec as P

MODEL_WIDTH = 1408
HD = 88
FF = 6144
TW = 1024


PRECISE = lax.Precision.HIGHEST
NORM_EPS = 1e-06


def row_norm(values):
    centered = values - jnp.mean(values, axis=-1, keepdims=True)
    inverse = lax.rsqrt(jnp.mean(centered * centered, axis=-1, keepdims=True) + NORM_EPS)
    return (centered * inverse, inverse)


def head_norm(values, head_width):
    shaped = values.reshape(values.shape[:-1] + (values.shape[-1] // head_width, head_width))
    centered = shaped - jnp.mean(shaped, axis=-1, keepdims=True)
    inverse = lax.rsqrt(jnp.mean(centered * centered, axis=-1, keepdims=True) + NORM_EPS)
    return (centered * inverse, inverse)


def norm_back(normal, inverse, grad_normal):
    return inverse * (
        grad_normal
        - jnp.mean(grad_normal, axis=-1, keepdims=True)
        - normal * jnp.mean(grad_normal * normal, axis=-1, keepdims=True)
    )


def split_parts(values):
    if values.dtype == jnp.bfloat16:
        return [values]
    upper_half = values.astype(jnp.bfloat16)
    lower_half = (values - upper_half.astype(jnp.float32)).astype(jnp.bfloat16)
    return [upper_half, lower_half]


def paired_product(form, left, right):
    total = None
    for left_number, left_part in enumerate(split_parts(left)):
        for right_number, right_part in enumerate(split_parts(right)):
            if left_number + right_number < 2:
                term = jnp.einsum(form, left_part, right_part, preferred_element_type=jnp.float32)
                total = term if total is None else total + term
    return total


def lowrank_out(input_list, weight_matrix, down_piece, up_factor_piece):
    frozen_term = jnp.einsum(
        "gtb,bx->gtx", input_list, weight_matrix, preferred_element_type=jnp.float32
    )
    rank_activation = jnp.einsum(
        "snd,srd->snr", input_list, down_piece, preferred_element_type=jnp.float32
    )
    adapter_term = paired_product("dti,dip->dtp", rank_activation, up_factor_piece)
    return (frozen_term + adapter_term, rank_activation)


def lowrank_back(
    input_list,
    weight_matrix,
    down_piece,
    up_factor_piece,
    rank_activation,
    output_gradient,
    want_input,
):
    upper_gradient = paired_product("pmf,pmz->pfz", rank_activation, output_gradient)
    rank_gradient = paired_product("hzu,hlu->hzl", output_gradient, up_factor_piece)
    grad_lower = paired_product("snr,snd->srd", rank_gradient, input_list)
    if want_input:
        input_gradients = paired_product("lga,wa->lgw", output_gradient, weight_matrix)
        input_gradients = input_gradients + paired_product(
            "snr,srd->snd", rank_gradient, down_piece
        )
        return (input_gradients, grad_lower, upper_gradient)
    return (None, grad_lower, upper_gradient)


def attend_forward(query, key_rows, values_in, scale_factor):
    scores = (
        jnp.einsum("snhe,smhe->shnm", query, key_rows, preferred_element_type=jnp.float32)
        * scale_factor
    )
    row_top = jnp.max(scores, axis=-1, keepdims=True)
    exp_scores = jnp.exp(scores - row_top)
    row_total = jnp.sum(exp_scores, axis=-1, keepdims=True)
    attn_probs = (exp_scores / row_total).astype(jnp.bfloat16)
    result = jnp.einsum(
        "shnm,smhe->snhe", attn_probs, values_in, preferred_element_type=jnp.float32
    )
    return (result, row_top + jnp.log(row_total))


def attend_back(query, key_rows, values_in, log_total, grad_result, scale_factor):
    scores = (
        jnp.einsum("snhe,smhe->shnm", query, key_rows, preferred_element_type=jnp.float32)
        * scale_factor
    )
    attn_probs = jnp.exp(scores - log_total)
    grad_probs = jnp.einsum(
        "snhe,smhe->shnm", grad_result, values_in, preferred_element_type=jnp.float32
    )
    row_inner = jnp.sum(attn_probs * grad_probs, axis=-1, keepdims=True)
    grad_scores = (attn_probs * (grad_probs - row_inner)).astype(jnp.bfloat16)
    grad_query = (
        jnp.einsum("shnm,smhe->snhe", grad_scores, key_rows, preferred_element_type=jnp.float32)
        * scale_factor
    )
    grad_keys = (
        jnp.einsum("shnm,snhe->smhe", grad_scores, query, preferred_element_type=jnp.float32)
        * scale_factor
    )
    grad_values = jnp.einsum(
        "shnm,snhe->smhe",
        attn_probs.astype(jnp.bfloat16),
        grad_result,
        preferred_element_type=jnp.float32,
    )
    return (grad_query, grad_keys, grad_values)


def body(
    hidden,
    long_skip_input,
    condition,
    projected_text_tokens,
    sequence_adapter_index,
    skip_projection_weight,
    shift_modulation_weight,
    self_query_weight,
    self_key_weight,
    self_value_weight,
    attention_output_weight,
    cross_query_weight,
    cross_key_weight,
    cross_value_weight,
    cross_output_weight,
    feedforward_up_weight,
    feedforward_down_weight,
    skip_norm_gain,
    norm_gain_rows,
    adapter_down_factor,
    adapter_up_factor,
    cotangent,
):
    (
        skip_projection_weight,
        shift_modulation_weight,
        self_query_weight,
        self_key_weight,
        self_value_weight,
        attention_output_weight,
        cross_query_weight,
        cross_key_weight,
        cross_value_weight,
        cross_output_weight,
        feedforward_up_weight,
        feedforward_down_weight,
    ) = (
        lax.all_gather(skip_projection_weight, "dp", axis=1, tiled=True),
        lax.all_gather(shift_modulation_weight, "dp", axis=0, tiled=True),
        lax.all_gather(self_query_weight, "dp", axis=0, tiled=True),
        lax.all_gather(self_key_weight, "dp", axis=0, tiled=True),
        lax.all_gather(self_value_weight, "dp", axis=0, tiled=True),
        lax.all_gather(attention_output_weight, "dp", axis=1, tiled=True),
        lax.all_gather(cross_query_weight, "dp", axis=0, tiled=True),
        lax.all_gather(cross_key_weight, "dp", axis=0, tiled=True),
        lax.all_gather(cross_value_weight, "dp", axis=0, tiled=True),
        lax.all_gather(cross_output_weight, "dp", axis=1, tiled=True),
        lax.all_gather(feedforward_up_weight, "dp", axis=0, tiled=True),
        lax.all_gather(feedforward_down_weight, "dp", axis=1, tiled=True),
    )
    tensor_rank = lax.axis_index("tensor")
    tensor_count = lax.axis_size("tensor")
    seqs_local = hidden.shape[0]
    tokens_local = hidden.shape[1]
    local_width = self_query_weight.shape[1]
    heads_local = local_width // HD
    ff_local = feedforward_up_weight.shape[1]
    skip_width = skip_projection_weight.shape[0]
    scale_factor = HD ** (-0.5)
    in_sizes = [
        2 * MODEL_WIDTH,
        MODEL_WIDTH,
        MODEL_WIDTH,
        MODEL_WIDTH,
        MODEL_WIDTH,
        MODEL_WIDTH,
        MODEL_WIDTH,
        TW,
        TW,
        MODEL_WIDTH,
        MODEL_WIDTH,
        FF,
    ]
    out_sizes = [MODEL_WIDTH] * 10 + [FF, MODEL_WIDTH]
    input_offsets = [sum(in_sizes[:number]) for number in range(12)]
    output_offsets = [sum(out_sizes[:number]) for number in range(12)]
    select_adapter = (
        sequence_adapter_index[:, None]
        == jnp.arange(adapter_down_factor.shape[0], dtype=jnp.int32)[None, :]
    )
    choose_wide = select_adapter.astype(jnp.float32)
    down_seq = jnp.einsum(
        "fn,nge->fge",
        select_adapter.astype(jnp.bfloat16),
        adapter_down_factor,
        preferred_element_type=jnp.float32,
    ).astype(jnp.bfloat16)
    up_seq = jnp.einsum(
        "fn,nge->fge",
        select_adapter.astype(jnp.bfloat16),
        adapter_up_factor,
        preferred_element_type=jnp.float32,
    ).astype(jnp.bfloat16)

    def down_full(number):
        return down_seq[:, :, input_offsets[number] : input_offsets[number] + in_sizes[number]]

    def up_full(number):
        return up_seq[:, :, output_offsets[number] : output_offsets[number] + out_sizes[number]]

    def down_local(number, span_width):
        return lax.dynamic_slice_in_dim(
            down_seq, input_offsets[number] + tensor_rank * span_width, span_width, 2
        )

    def up_local(number, span_width):
        return lax.dynamic_slice_in_dim(
            up_seq, output_offsets[number] + tensor_rank * span_width, span_width, 2
        )

    def to_slots(grad_piece):
        return jnp.einsum("si,srd->ird", choose_wide, grad_piece, precision=PRECISE)

    joined = jnp.concatenate([hidden, long_skip_input], axis=-1).astype(jnp.float32)
    joined_normal, joined_inverse = row_norm(joined)
    joined_low = (joined_normal * skip_norm_gain).astype(jnp.bfloat16)
    joined_part = lax.dynamic_slice_in_dim(joined_low, tensor_rank * skip_width, skip_width, 2)
    skip_partial, skip_rank = lowrank_out(
        joined_part, skip_projection_weight, down_local(0, skip_width), up_full(0)
    )
    skip_out = lax.psum(skip_partial.astype(jnp.bfloat16), "tensor").astype(jnp.float32)
    act_wide, silu_pull = jax.vjp(jax.nn.silu, condition.astype(jnp.float32))
    act_low = act_wide.astype(jnp.bfloat16)[:, None, :]
    shift_row, mod_rank = lowrank_out(act_low, shift_modulation_weight, down_full(1), up_full(1))
    first_normal, first_inverse = row_norm(skip_out)
    attn_in = (first_normal * norm_gain_rows[0] + shift_row).astype(jnp.bfloat16)
    query_proj, query_rank = lowrank_out(
        attn_in, self_query_weight, down_full(2), up_local(2, local_width)
    )
    key_proj, key_rank = lowrank_out(
        attn_in, self_key_weight, down_full(3), up_local(3, local_width)
    )
    value_proj, value_rank = lowrank_out(
        attn_in, self_value_weight, down_full(4), up_local(4, local_width)
    )
    query_normal, query_inverse = head_norm(query_proj, HD)
    key_normal, key_inverse = head_norm(key_proj, HD)
    query_low = query_normal.astype(jnp.bfloat16)
    key_low = key_normal.astype(jnp.bfloat16).reshape(seqs_local, tokens_local, local_width)
    value_low = value_proj.astype(jnp.bfloat16)
    keys_all, values_all = (
        lax.all_gather(key_low, "ctx", axis=1, tiled=True),
        lax.all_gather(value_low, "ctx", axis=1, tiled=True),
    )
    keys_four = keys_all.reshape(seqs_local, -1, heads_local, HD)
    values_four = values_all.reshape(seqs_local, -1, heads_local, HD)
    attn_result, attn_log = attend_forward(query_low, keys_four, values_four, scale_factor)
    attn_low = attn_result.reshape(seqs_local, tokens_local, local_width).astype(jnp.bfloat16)
    attn_partial, out_rank = lowrank_out(
        attn_low, attention_output_weight, down_local(5, local_width), up_full(5)
    )
    first_res = skip_out + lax.psum(attn_partial.astype(jnp.bfloat16), "tensor").astype(jnp.float32)
    second_normal, second_inverse = row_norm(first_res)
    cross_in = (second_normal * norm_gain_rows[1]).astype(jnp.bfloat16)
    cquery_proj, cquery_rank = lowrank_out(
        cross_in, cross_query_weight, down_full(6), up_local(6, local_width)
    )
    ckey_proj, ckey_rank = lowrank_out(
        projected_text_tokens, cross_key_weight, down_full(7), up_local(7, local_width)
    )
    cvalue_proj, cvalue_rank = lowrank_out(
        projected_text_tokens, cross_value_weight, down_full(8), up_local(8, local_width)
    )
    cquery_normal, cquery_inverse = head_norm(cquery_proj, HD)
    ckey_normal, ckey_inverse = head_norm(ckey_proj, HD)
    cquery_low = cquery_normal.astype(jnp.bfloat16)
    ckey_low = ckey_normal.astype(jnp.bfloat16)
    cvalue_low = cvalue_proj.astype(jnp.bfloat16).reshape(seqs_local, -1, heads_local, HD)
    cross_result, cross_log = attend_forward(cquery_low, ckey_low, cvalue_low, scale_factor)
    cross_low = cross_result.reshape(seqs_local, tokens_local, local_width).astype(jnp.bfloat16)
    cross_partial, cout_rank = lowrank_out(
        cross_low, cross_output_weight, down_local(9, local_width), up_full(9)
    )
    second_res = first_res + lax.psum(cross_partial.astype(jnp.bfloat16), "tensor").astype(
        jnp.float32
    )
    third_normal, third_inverse = row_norm(second_res)
    mlp_in = (third_normal * norm_gain_rows[2]).astype(jnp.bfloat16)
    up_proj, up_rank = lowrank_out(
        mlp_in, feedforward_up_weight, down_full(10), up_local(10, ff_local)
    )
    activated, gelu_pull = jax.vjp(partial(jax.nn.gelu, approximate=True), up_proj)
    activated_low = activated.astype(jnp.bfloat16)
    down_partial, down_rank = lowrank_out(
        activated_low, feedforward_down_weight, down_local(11, ff_local), up_full(11)
    )
    block_out = second_res + lax.psum(down_partial.astype(jnp.bfloat16), "tensor").astype(
        jnp.float32
    )
    grad_act, grad_down_lower, grad_down_upper = lowrank_back(
        activated_low,
        feedforward_down_weight,
        down_local(11, ff_local),
        up_full(11),
        down_rank,
        cotangent,
        True,
    )
    grad_pre = gelu_pull(grad_act)[0].astype(jnp.bfloat16)
    grad_mlp_in, grad_up_lower, grad_up_upper = lowrank_back(
        mlp_in,
        feedforward_up_weight,
        down_full(10),
        up_local(10, ff_local),
        up_rank,
        grad_pre,
        True,
    )
    grad_mlp_in = lax.psum(grad_mlp_in.astype(jnp.bfloat16), "tensor").astype(jnp.float32)
    grad_second = cotangent.astype(jnp.float32) + norm_back(
        third_normal, third_inverse, grad_mlp_in * norm_gain_rows[2]
    )
    grad_cross_low, grad_cout_lower, grad_cout_upper = lowrank_back(
        cross_low,
        cross_output_weight,
        down_local(9, local_width),
        up_full(9),
        cout_rank,
        grad_second.astype(jnp.bfloat16),
        True,
    )
    grad_cross_result = grad_cross_low.astype(jnp.bfloat16).reshape(
        seqs_local, tokens_local, heads_local, HD
    )
    grad_cquery, grad_ckey, grad_cvalue = attend_back(
        cquery_low, ckey_low, cvalue_low, cross_log, grad_cross_result, scale_factor
    )
    grad_cquery_proj = (
        norm_back(cquery_normal, cquery_inverse, grad_cquery)
        .reshape(seqs_local, tokens_local, local_width)
        .astype(jnp.bfloat16)
    )
    grad_ckey_proj = norm_back(ckey_normal, ckey_inverse, grad_ckey).reshape(
        seqs_local, -1, local_width
    )
    none_first, grad_ckey_lower, grad_ckey_upper = lowrank_back(
        projected_text_tokens,
        cross_key_weight,
        down_full(7),
        up_local(7, local_width),
        ckey_rank,
        grad_ckey_proj,
        False,
    )
    none_second, grad_cvalue_lower, grad_cvalue_upper = lowrank_back(
        projected_text_tokens,
        cross_value_weight,
        down_full(8),
        up_local(8, local_width),
        cvalue_rank,
        grad_cvalue.reshape(seqs_local, -1, local_width),
        False,
    )
    grad_cross_in, grad_cquery_lower, grad_cquery_upper = lowrank_back(
        cross_in,
        cross_query_weight,
        down_full(6),
        up_local(6, local_width),
        cquery_rank,
        grad_cquery_proj,
        True,
    )
    grad_cross_in = lax.psum(grad_cross_in.astype(jnp.bfloat16), "tensor").astype(jnp.float32)
    grad_first = grad_second + norm_back(
        second_normal, second_inverse, grad_cross_in * norm_gain_rows[1]
    )
    grad_attn_low, grad_aout_lower, grad_aout_upper = lowrank_back(
        attn_low,
        attention_output_weight,
        down_local(5, local_width),
        up_full(5),
        out_rank,
        grad_first.astype(jnp.bfloat16),
        True,
    )
    grad_attn_result = grad_attn_low.astype(jnp.bfloat16).reshape(
        seqs_local, tokens_local, heads_local, HD
    )
    grad_query, grad_keys_all, grad_values_all = attend_back(
        query_low, keys_four, values_four, attn_log, grad_attn_result, scale_factor
    )
    grad_keys, grad_values = (
        lax.psum_scatter(
            grad_keys_all.reshape(seqs_local, -1, local_width).astype(jnp.bfloat16),
            "ctx",
            scatter_dimension=1,
            tiled=True,
        ).astype(jnp.float32),
        lax.psum_scatter(
            grad_values_all.reshape(seqs_local, -1, local_width).astype(jnp.bfloat16),
            "ctx",
            scatter_dimension=1,
            tiled=True,
        ).astype(jnp.float32),
    )
    grad_query_proj = (
        norm_back(query_normal, query_inverse, grad_query)
        .reshape(seqs_local, tokens_local, local_width)
        .astype(jnp.bfloat16)
    )
    grad_key_proj = (
        norm_back(
            key_normal, key_inverse, grad_keys.reshape(seqs_local, tokens_local, heads_local, HD)
        )
        .reshape(seqs_local, tokens_local, local_width)
        .astype(jnp.bfloat16)
    )
    grad_value_proj = grad_values.astype(jnp.bfloat16)
    grad_in_query, grad_query_lower, grad_query_upper = lowrank_back(
        attn_in,
        self_query_weight,
        down_full(2),
        up_local(2, local_width),
        query_rank,
        grad_query_proj,
        True,
    )
    grad_in_key, grad_key_lower, grad_key_upper = lowrank_back(
        attn_in,
        self_key_weight,
        down_full(3),
        up_local(3, local_width),
        key_rank,
        grad_key_proj,
        True,
    )
    grad_in_value, grad_value_lower, grad_value_upper = lowrank_back(
        attn_in,
        self_value_weight,
        down_full(4),
        up_local(4, local_width),
        value_rank,
        grad_value_proj,
        True,
    )
    grad_attn_in = lax.psum(
        (grad_in_query + grad_in_key + grad_in_value).astype(jnp.bfloat16), "tensor"
    ).astype(jnp.float32)
    grad_shift = jnp.sum(grad_attn_in, axis=1, keepdims=True) / tensor_count
    grad_act_low, grad_mod_lower, grad_mod_upper = lowrank_back(
        act_low, shift_modulation_weight, down_full(1), up_full(1), mod_rank, grad_shift, True
    )
    grad_condition = silu_pull(grad_act_low[:, 0, :])[0]
    grad_skip_out = grad_first + norm_back(
        first_normal, first_inverse, grad_attn_in * norm_gain_rows[0]
    )
    grad_joined_part, grad_skip_lower, grad_skip_upper = lowrank_back(
        joined_part,
        skip_projection_weight,
        down_local(0, skip_width),
        up_full(0),
        skip_rank,
        grad_skip_out.astype(jnp.bfloat16),
        True,
    )
    grad_joined = lax.all_gather(
        grad_joined_part.astype(jnp.bfloat16), "tensor", axis=2, tiled=True
    ).astype(grad_joined_part.dtype)
    grad_joined_full = norm_back(joined_normal, joined_inverse, grad_joined * skip_norm_gain)
    hidden_grad = grad_joined_full[:, :, :MODEL_WIDTH]
    skip_grad = grad_joined_full[:, :, MODEL_WIDTH:]
    lower_factor_parts = [
        (0, grad_skip_lower, True),
        (1, grad_mod_lower, False),
        (2, grad_query_lower, False),
        (3, grad_key_lower, False),
        (4, grad_value_lower, False),
        (5, grad_aout_lower, True),
        (6, grad_cquery_lower, False),
        (7, grad_ckey_lower, False),
        (8, grad_cvalue_lower, False),
        (9, grad_cout_lower, True),
        (10, grad_up_lower, False),
        (11, grad_down_lower, True),
    ]
    upper_factor_parts = [
        (0, grad_skip_upper, False),
        (1, grad_mod_upper, False),
        (2, grad_query_upper, True),
        (3, grad_key_upper, True),
        (4, grad_value_upper, True),
        (5, grad_aout_upper, False),
        (6, grad_cquery_upper, True),
        (7, grad_ckey_upper, True),
        (8, grad_cvalue_upper, True),
        (9, grad_cout_upper, False),
        (10, grad_up_upper, True),
        (11, grad_down_upper, False),
    ]
    slot_total = adapter_down_factor.shape[0]
    rank_total = adapter_down_factor.shape[1]
    cond_buffer = jnp.zeros((lax.axis_size("dp") * seqs_local, MODEL_WIDTH), jnp.float32)
    cond_buffer = lax.dynamic_update_slice_in_dim(
        cond_buffer, grad_condition, lax.axis_index("dp") * seqs_local, 0
    )
    cond_flat = cond_buffer.reshape(-1)

    def dense_table(parts_list, starts, total_width, row_count, slot_pieces):
        table = jnp.zeros((row_count, total_width), jnp.float32)
        for position, (number, grad_piece, is_local) in enumerate(parts_list):
            span_width = grad_piece.shape[2]
            column_start = starts[number] + tensor_rank * span_width if is_local else starts[number]
            table = lax.dynamic_update_slice_in_dim(table, slot_pieces[position], column_start, 1)
        return table

    down_factor_slots = [
        to_slots(grad_piece).reshape(slot_total * rank_total, -1)
        for number, grad_piece, is_local in lower_factor_parts
    ]
    up_factor_slots = [
        to_slots(grad_piece).reshape(slot_total * rank_total, -1)
        for number, grad_piece, is_local in upper_factor_parts
    ]
    down_compact = jnp.concatenate(down_factor_slots, axis=1)
    up_compact = jnp.concatenate(up_factor_slots, axis=1)
    cond_rows, down_rows, up_rows = (
        lax.psum_scatter(
            cond_flat.astype(jnp.bfloat16), ("dp", "ctx"), scatter_dimension=0, tiled=True
        ).astype(jnp.float32),
        lax.psum_scatter(
            down_compact.astype(jnp.bfloat16), ("dp", "ctx"), scatter_dimension=0, tiled=True
        ).astype(jnp.float32),
        lax.psum_scatter(
            up_compact.astype(jnp.bfloat16), ("dp", "ctx"), scatter_dimension=0, tiled=True
        ).astype(jnp.float32),
    )
    row_count = down_rows.shape[0]
    down_widths = [grad_piece.shape[2] for number, grad_piece, is_local in lower_factor_parts]
    up_widths = [grad_piece.shape[2] for number, grad_piece, is_local in upper_factor_parts]
    down_pieces = [
        down_rows[:, sum(down_widths[:position]) : sum(down_widths[: position + 1])]
        for position in range(12)
    ]
    up_pieces = [
        up_rows[:, sum(up_widths[:position]) : sum(up_widths[: position + 1])]
        for position in range(12)
    ]
    down_block = dense_table(
        lower_factor_parts, input_offsets, adapter_down_factor.shape[2], row_count, down_pieces
    ).reshape(-1)
    up_block = dense_table(
        upper_factor_parts, output_offsets, adapter_up_factor.shape[2], row_count, up_pieces
    ).reshape(-1)
    condition_gradient, adapter_down_gradient, adapter_up_gradient = (
        lax.psum_scatter(
            cond_rows.astype(jnp.bfloat16), "tensor", scatter_dimension=0, tiled=True
        ).astype(jnp.float32),
        lax.psum_scatter(
            down_block.astype(jnp.bfloat16), "tensor", scatter_dimension=0, tiled=True
        ).astype(jnp.float32),
        lax.psum_scatter(
            up_block.astype(jnp.bfloat16), "tensor", scatter_dimension=0, tiled=True
        ).astype(jnp.float32),
    )
    return (
        block_out.astype(jnp.bfloat16),
        hidden_grad,
        skip_grad,
        condition_gradient,
        adapter_down_gradient,
        adapter_up_gradient,
    )


BF = jnp.bfloat16
F32 = jnp.float32
MESH_ID = pl.DeviceIdType.MESH
RANK = 16
CHUNK = 64
VMEM_BYTES = 60 << 20


def dot_nn(left, right):
    return jnp.dot(left, right, preferred_element_type=F32)


def dot_nt(left, right):
    return lax.dot_general(left, right, (((1,), (1,)), ((), ())), preferred_element_type=F32)


def dot_tn(left, right):
    return lax.dot_general(left, right, (((0,), (0,)), ((), ())), preferred_element_type=F32)


def stats(values):
    centered = values - jnp.mean(values, axis=-1, keepdims=True)
    inverse = lax.rsqrt(jnp.mean(centered * centered, axis=-1, keepdims=True) + NORM_EPS)
    return centered * inverse, inverse


def greet_all(partners):
    barrier = pltpu.get_barrier_semaphore()
    for condition, device in partners:
        @pl.when(condition)
        def _(device=device):
            pl.semaphore_signal(barrier, inc=1, device_id=device, device_id_type=MESH_ID)


def await_all(partners):
    expected = sum(jnp.where(condition, 1, 0) for condition, _ in partners)
    pl.semaphore_wait(pltpu.get_barrier_semaphore(), expected)


def greet(partners):
    greet_all(partners)
    await_all(partners)


def line_partners(me, count):
    return [(me > 0, {"tensor": lax.max(me - 1, 0)}), (me < count - 1, {"tensor": lax.min(me + 1, count - 1)})]


def push(source, target, send_sem, recv_sem, device):
    return pltpu.make_async_remote_copy(
        src_ref=source,
        dst_ref=target,
        send_sem=send_sem,
        recv_sem=recv_sem,
        device_id=device,
        device_id_type=MESH_ID,
    )


class Line:
    def __init__(self, me, count, send_right, recv_left, send_left, recv_right):
        self.me, self.count = me, count
        self.sems = (send_right, recv_left, send_left, recv_right)
        self.left = {"tensor": lax.max(me - 1, 0)}
        self.right = {"tensor": lax.min(me + 1, count - 1)}
        self.has_left, self.has_right = me > 0, me < count - 1

    def to_right(self, source, target, slot):
        return push(source, target, self.sems[0].at[slot], self.sems[1].at[slot], self.right)

    def to_left(self, source, target, slot):
        return push(source, target, self.sems[2].at[slot], self.sems[3].at[slot], self.left)


def line_reduce_all(line, steps, compute, partial_ref, from_left, from_right, stage_right, stage_left, finish,
                    beside=None, after=None):
    me, count = line.me, line.count
    far = count - 1 - me

    def step(number, carry):
        @pl.when(number < steps)
        def _():
            compute(number)

        slot_r = number - me

        @pl.when((slot_r >= 0) & (slot_r < steps))
        def _():
            slot = lax.clamp(0, slot_r, steps - 1)

            @pl.when(line.has_left)
            def _():
                line.to_right(stage_right.at[slot], from_left.at[slot], slot).wait_recv()

            @pl.when(line.has_right)
            def _():
                @pl.when(line.has_left)
                def _():
                    total = partial_ref[slot].astype(F32) + from_left[slot].astype(F32)
                    stage_right[slot] = total.astype(BF)

                @pl.when(jnp.logical_not(line.has_left))
                def _():
                    stage_right[slot] = partial_ref[slot]

                line.to_right(stage_right.at[slot], from_left.at[slot], slot).start()

        slot_l = number - far

        @pl.when((slot_l >= 0) & (slot_l < steps))
        def _():
            slot = lax.clamp(0, slot_l, steps - 1)

            @pl.when(line.has_right)
            def _():
                line.to_left(stage_left.at[slot], from_right.at[slot], slot).wait_recv()

            @pl.when(line.has_left)
            def _():
                @pl.when(line.has_right)
                def _():
                    total = partial_ref[slot].astype(F32) + from_right[slot].astype(F32)
                    stage_left[slot] = total.astype(BF)

                @pl.when(jnp.logical_not(line.has_right))
                def _():
                    stage_left[slot] = partial_ref[slot]

                line.to_left(stage_left.at[slot], from_right.at[slot], slot).start()

        if beside is not None:
            beside(number)
        slot_f = number - lax.max(me, far)

        @pl.when((slot_f >= 0) & (slot_f < steps))
        def _():
            slot = lax.clamp(0, slot_f, steps - 1)

            @pl.when(jnp.logical_not(line.has_left))
            def _():
                finish(slot, partial_ref[slot].astype(F32) + from_right[slot].astype(F32))

            @pl.when(line.has_left)
            def _():
                @pl.when(line.has_right)
                def _():
                    finish(
                        slot,
                        partial_ref[slot].astype(F32)
                        + from_left[slot].astype(F32)
                        + from_right[slot].astype(F32),
                    )

                @pl.when(jnp.logical_not(line.has_right))
                def _():
                    finish(slot, partial_ref[slot].astype(F32) + from_left[slot].astype(F32))

            if after is not None:
                after(slot)

        return carry

    lax.fori_loop(0, steps + count - 1, step, 0)

    def drain(slot, carry):
        @pl.when(line.has_right)
        def _():
            line.to_right(stage_right.at[slot], from_left.at[slot], slot).wait_send()

        @pl.when(line.has_left)
        def _():
            line.to_left(stage_left.at[slot], from_right.at[slot], slot).wait_send()

        return carry

    lax.fori_loop(0, steps, drain, 0)


def scatter_order(me, count, place):
    near = lax.min(me, count - 1 - me)
    base = count - 1 - 2 * near
    index = place - base
    block = jnp.where(
        place < base,
        count - 1 - place,
        jnp.where(index % 2 == 0, 2 * near - index // 2, index // 2),
    )
    return jnp.where(2 * me > count - 1, count - 1 - block, block)


def line_scatter_step(line, number, partial_ref, from_left, from_right, stage_right, stage_left):
    me, count = line.me, line.count
    block_r = count - 1 - number + me

    @pl.when((number >= me) & line.has_right & (block_r > me))
    def _():
        block = lax.clamp(0, block_r, count - 1)

        @pl.when(line.has_left)
        def _():
            line.to_right(stage_right.at[block], from_left.at[block], block).wait_recv()
            total = partial_ref[block].astype(F32) + from_left[block].astype(F32)
            stage_right[block] = total.astype(BF)

        @pl.when(jnp.logical_not(line.has_left))
        def _():
            stage_right[block] = partial_ref[block]

        line.to_right(stage_right.at[block], from_left.at[block], block).start()

    block_l = number - (count - 1 - me)

    @pl.when((block_l >= 0) & line.has_left & (block_l < me))
    def _():
        block = lax.clamp(0, block_l, count - 1)

        @pl.when(line.has_right)
        def _():
            line.to_left(stage_left.at[block], from_right.at[block], block).wait_recv()
            total = partial_ref[block].astype(F32) + from_right[block].astype(F32)
            stage_left[block] = total.astype(BF)

        @pl.when(jnp.logical_not(line.has_right))
        def _():
            stage_left[block] = partial_ref[block]

        line.to_left(stage_left.at[block], from_right.at[block], block).start()


def line_scatter_finish(line, partial_ref, from_left, from_right, stage_right, stage_left, total_ref):
    me, count = line.me, line.count
    total_ref[...] = partial_ref[me].astype(F32)

    @pl.when(line.has_left)
    def _():
        line.to_right(stage_right.at[me], from_left.at[me], me).wait_recv()
        total_ref[...] += from_left[me].astype(F32)

    @pl.when(line.has_right)
    def _():
        line.to_left(stage_left.at[me], from_right.at[me], me).wait_recv()
        total_ref[...] += from_right[me].astype(F32)

    def drain(block, carry):
        @pl.when(block > me)
        def _():
            line.to_right(stage_right.at[block], from_left.at[block], block).wait_send()

        @pl.when(block < me)
        def _():
            line.to_left(stage_left.at[block], from_right.at[block], block).wait_send()

        return carry

    lax.fori_loop(0, count, drain, 0)


def line_gather_step(line, number, slots):
    me, count = line.me, line.count
    block_l = lax.clamp(0, me - number, count - 1)
    block_r = lax.clamp(0, me + number, count - 1)
    view = slots if callable(slots) else lambda block: slots.at[block]

    @pl.when(number <= me)
    def _():
        @pl.when(number > 0)
        def _():
            line.to_right(view(block_l), view(block_l), block_l).wait_recv()

        @pl.when(line.has_right)
        def _():
            line.to_right(view(block_l), view(block_l), block_l).start()

    @pl.when(me + number <= count - 1)
    def _():
        @pl.when(number > 0)
        def _():
            line.to_left(view(block_r), view(block_r), block_r).wait_recv()

        @pl.when(line.has_left)
        def _():
            line.to_left(view(block_r), view(block_r), block_r).start()


def line_gather_drain(line, slots):
    me, count = line.me, line.count
    view = slots if callable(slots) else lambda block: slots.at[block]

    def drain(block, carry):
        @pl.when((block <= me) & line.has_right)
        def _():
            line.to_right(view(block), view(block), block).wait_send()

        @pl.when((block >= me) & line.has_left)
        def _():
            line.to_left(view(block), view(block), block).wait_send()

        return carry

    lax.fori_loop(0, count, drain, 0)


def xor_place(place, number):
    if number == 0:
        return place
    if number == 1:
        return place + 1 - 2 * (place % 2)
    if number == 2:
        return place + 2 - 4 * (place // 2)
    return 3 - place


def call(kernel, inputs, outs, scratch, collective=None, cost=None):
    space = {True: pltpu.VMEM, False: pl.ANY, None: pltpu.SMEM}
    return pl.pallas_call(
        kernel,
        out_shape=[jax.ShapeDtypeStruct(shape, dtype) for shape, dtype, _ in outs],
        in_specs=[pl.BlockSpec(memory_space=space[where]) for _, where in inputs],
        out_specs=[pl.BlockSpec(memory_space=space[where]) for _, _, where in outs],
        scratch_shapes=scratch,
        cost_estimate=cost,
        compiler_params=pltpu.CompilerParams(
            collective_id=collective,
            has_side_effects=collective is not None,
            vmem_limit_bytes=VMEM_BYTES,
        ),
    )(*[array for array, _ in inputs])


def cost_of(flops, moved):
    return pl.CostEstimate(flops=int(flops), bytes_accessed=int(moved), transcendentals=0)


def vmem(*shape, dtype=BF):
    return pltpu.VMEM(shape, dtype)


def dma(*shape):
    return pltpu.SemaphoreType.DMA(shape)


def whole_wait(target, sem):
    pltpu.make_async_copy(target, target, sem).wait()


def rows_of(index, size):
    return pl.ds(pl.multiple_of(index * size, size), size)


IN_SIZES = [2 * MODEL_WIDTH] + [MODEL_WIDTH] * 6 + [TW, TW, MODEL_WIDTH, MODEL_WIDTH, FF]
OUT_SIZES = [MODEL_WIDTH] * 10 + [FF, MODEL_WIDTH]
IN_AT = [sum(IN_SIZES[:number]) for number in range(13)]
OUT_AT = [sum(OUT_SIZES[:number]) for number in range(13)]


def down_of(table, number):
    return table[:, IN_AT[number] : IN_AT[number + 1]]


def up_of(table, number):
    return table[:, OUT_AT[number] : OUT_AT[number + 1]]


def take_local(target, table, start, me, count):
    size = target.shape[-1]
    for place in range(count):
        @pl.when(me == place)
        def _(place=place):
            target[...] = table[:, start + place * size : start + (place + 1) * size]


def take_stack(target, table, start, count):
    size = target.shape[-1]
    for place in range(count):
        target[place] = table[:, start + place * size : start + (place + 1) * size]


def norm_backward(normal, inverse, grad):
    return inverse * (
        grad
        - jnp.mean(grad, axis=-1, keepdims=True)
        - normal * jnp.mean(grad * normal, axis=-1, keepdims=True)
    )


def middle(count, heads, summed, skip_out, query_weight, out_weight, up_weight, down_piece, skip_piece, text_kv, text,
           cotangent, gains, tables):
    share, width = summed.shape
    tokens = skip_out.shape[0]
    local = query_weight.shape[-1]
    units = up_weight.shape[1]
    words, text_width = text.shape
    rows, span = skip_piece.shape
    scale = HD ** (-0.5)
    part_rows = share // 2
    wide = count * part_rows

    def kernel(sum_ref, skip_hbm, q_hbm, o_hbm, u_hbm, d_own, piece, kv_hbm, text_hbm, cot_hbm, gain, dtab, utab,
               g_first, block_sum, ga_q, gb_q, ga_k, gb_k, ga_v, gb_v, ga_o, gb_o, g_ua, g_ub, g_da, g_db, skip_all,
               kv, wq, wo, wu, wd, cot, t_ref, first_ref, second_ref, x_ref, x_low, q_ref, inv_ref, log_ref, low_ref, acc, b_ref, ao,
               bk, bv, ub, da, slots, skip_half, active, grads, u_all, ud_all, gu_all, gd_all, partial_g, left_g, right_g,
               sr_g, sl_g, partial_b, left_b, right_b, sr_b, sl_b, lsem, wsend, wrecv, zsend, zrecv, *sems):
        me = lax.axis_index("tensor")
        core = lax.axis_index("ctx")
        dp = lax.axis_index("dp")
        always = core >= 0
        half = pl.ds(pl.multiple_of(core * (rows // 2), 16), rows // 2)
        down_rows = d_own.shape[0]
        down_half = pl.ds(pl.multiple_of(core * (down_rows // 2), 16), down_rows // 2)
        mine = pl.ds(pl.multiple_of(dp * down_rows, 16), down_rows)
        loads = [
            pltpu.make_async_copy(source, target, lsem.at[number])
            for number, (source, target) in enumerate(
                ((skip_hbm.at[rows_of(me, share), :], first_ref), (piece.at[half, :], skip_half.at[me]), (q_hbm, wq),
                 (o_hbm, wo), (d_own, wd.at[mine, :]), (cot_hbm.at[:, 0], cot.at[0]), (u_hbm.at[mine, :], wu.at[mine, :]), (text_hbm, t_ref),
                 (cot_hbm.at[:, 1], cot.at[1]))
            )
        ]
        z_peers = [{"tensor": xor_place(me, number)} for number in range(1, count)]
        others = [{"dp": xor_place(dp, 1)}, {"dp": xor_place(dp, 2)}, {"ctx": 1 - core}]
        everyone = [(always, device) for device in z_peers + others]
        greet_all(everyone)
        load_kv = pltpu.make_async_copy(kv_hbm, kv, lsem.at[12])
        for load in loads[:4]:
            load.start()
        load_kv.start()
        for load in loads[4:]:
            load.start()
        gather_lines = [Line(me, count, *sems[:4]), Line(me, count, *sems[4:8])]
        grad_lines = [Line(me, count, *sems[8:12]), Line(me, count, *sems[12:16])]
        block_line = Line(me, count, *sems[16:])

        def gather(which, number):
            line_gather_step(gather_lines[which], number, slots.at[which])

        def scatter(which, number):
            line_scatter_step(
                grad_lines[which], number, partial_g.at[which], left_g.at[which], right_g.at[which], sr_g.at[which],
                sl_g.at[which],
            )

        down = Shared(wd, down_rows, (wsend, wrecv, 0))
        up_w = Shared(wu, down_rows, (wsend, wrecv, 2))
        arrived_up = [
            pltpu.make_async_copy(Shared(u_hbm, down_rows, (wsend, wrecv, 2)).view(block, core), up_w.view(block, core),
                                  lsem.at[10 + number])
            for number, block in enumerate((up_w.first, up_w.second))
        ]
        for load in arrived_up:
            load.start()
        skip = Shared(skip_all, rows, (wsend, wrecv, 1), stacked=True)
        await_all(everyone)
        down.send_own(d_own.at[down_half, :])
        z_sends = [
            push(piece.at[half, :], skip_half.at[me], zsend.at[number], zrecv.at[number], device)
            for number, device in enumerate(z_peers)
        ]
        for send in z_sends:
            send.start()
        take_stack(b_ref, utab, OUT_AT[6], count)
        take_stack(ao, dtab, IN_AT[9], count)
        take_stack(bk, utab, OUT_AT[7], count)
        take_stack(bv, utab, OUT_AT[8], count)
        take_local(ub, utab, OUT_AT[10], me, count)
        take_local(da, dtab, IN_AT[11], me, count)

        for load in arrived_up:
            load.wait()
        up_w.forward()
        up_w.swap(0)
        up_w.swap(1)

        loads[0].wait()
        first = first_ref[...] + sum_ref[...]
        first_ref[...] = first
        second_ref[...] = first
        normal, _ = stats(first)
        x = (normal * gain[1:2, :]).astype(BF)
        x_ref[...] = x
        u = dot_nt(x, down_of(dtab, 6)).astype(BF)
        loads[2].wait()
        loads[3].wait()
        load_kv.wait()

        def cross(place, u_low):
            y = dot_nn(x_ref[...], wq[place]) + dot_nn(u, b_ref[place])
            outs, inverses, logs = [], [], []
            for head in range(heads):
                at = slice(head * HD, (head + 1) * HD)
                normal, inverse = stats(y[:, at])
                q = normal.astype(BF)
                q_ref[place, head] = q
                inverses.append(inverse)
                s = dot_nt(q, kv[0, place, :, at]) * scale
                top = jnp.max(s, axis=-1, keepdims=True)
                e = jnp.exp(s - top)
                total = jnp.sum(e, axis=-1, keepdims=True)
                p = (e * (1.0 / total)).astype(BF)
                outs.append(dot_nn(p, kv[1, place, :, at]))
                logs.append(top + jnp.log(total))
            inv_ref[place] = jnp.concatenate(inverses, axis=1)
            log_ref[place] = jnp.concatenate(logs, axis=1)
            low = jnp.concatenate(outs, axis=1).astype(BF)
            low_ref[place] = low
            second_ref[...] += dot_nt(low, wo[place])
            return u_low + dot_nt(low, ao[place])

        u_low = lax.fori_loop(0, count, cross, jnp.zeros((share, RANK), F32)).astype(BF)
        second = second_ref[...] + dot_nn(u_low, up_of(utab, 9))
        second_ref[...] = second
        normal, _ = stats(second)
        x_mlp = (normal * gain[2:3, :]).astype(BF)
        slots[0, me] = x_mlp[:part_rows]
        slots[1, me] = x_mlp[part_rows:]

        gather(0, 0)
        up_w.wait(2)
        up_w.swap(2)
        down.wait(0)
        down.forward()
        down.swap(0)
        down.wait(1)
        down.swap(1)
        gather(0, 1)
        gather(1, 0)
        loads[1].wait()
        for number in range(count - 1):
            arrived = skip_half.at[xor_place(me, number + 1)]
            push(arrived, arrived, zsend.at[number], zrecv.at[number], z_peers[number]).wait_recv()
        skip_place = pltpu.make_async_copy(skip_half, skip.view(dp, core), lsem.at[9])
        skip_place.start()
        skip.send_own(skip_half)
        down.wait(2)
        down.swap(2)
        for number in (4, 5, 6, 8):
            loads[number].wait()
        ua, db = down_of(dtab, 10), up_of(utab, 11)
        gather(0, 2)
        gather(1, 1)
        down.wait_swaps()
        up_w.wait_swaps()

        def part(number):
            return pl.ds(pl.multiple_of(number * wide, wide), wide)

        def first_grads(number, carry):
            ct = cot[number].reshape(wide, width)
            gd = dot_nt(ct, db).astype(BF)
            gd_all[part(number), :] = gd
            grads[part(number), :] = (dot_nn(ct, wd[...]) + dot_nn(gd, da[...])).astype(BF)
            return carry

        lax.fori_loop(0, 1, first_grads, 0)
        gather(0, 3)

        def forward_part(number, carry):
            here = part(number)

            @pl.when(number == 1)
            def _():
                first_grads(1, 0)
                gather(1, 3)
                scatter(0, 1)

            x = slots[number].reshape(wide, width)
            u = dot_nt(x, ua).astype(BF)
            u_all[here, :] = u
            up = dot_nn(x, wu[...]) + dot_nn(u, ub[...])
            square = up * up
            curve = jnp.tanh(0.7978845608028654 * (up + 0.044715 * square * up))
            flat = 0.5 * (1.0 + curve)
            active[here, :] = (up * flat).astype(BF)
            slope = flat + 0.5 * up * (1.0 - curve * curve) * (0.7978845608028654 * (1.0 + 0.134145 * square))
            g_up = (grads[here, :].astype(F32) * slope).astype(BF)
            grads[here, :] = g_up
            gu = dot_nt(g_up, ub[...]).astype(BF)
            gu_all[here, :] = gu
            g_x = (dot_nt(g_up, wu[...]) + dot_nn(gu, ua)).astype(BF)
            partial_g[number] = g_x.reshape(count, part_rows, width)

            @pl.when(number == 0)
            def _():
                scatter(0, 0)
                gather(1, 2)

            return carry

        lax.fori_loop(0, 2, forward_part, 0)
        scatter(0, 2)
        scatter(1, 0)
        skip.wait(0)
        skip.forward()
        skip.wait(1)

        def down_product(number, carry):
            here = part(number)
            act = active[here, :]
            ud = dot_nt(act, da[...]).astype(BF)
            ud_all[here, :] = ud
            y = dot_nt(act, wd[...]) + dot_nn(ud, db)
            piece_rows = rows_of(number, part_rows)
            for block in range(count):
                own = jnp.where(block == me, 1.0, 0.0)
                one = y[block * part_rows : (block + 1) * part_rows] + second_ref[piece_rows, :] * own
                partial_b[block, piece_rows, :] = one.astype(BF)

            @pl.when(number == 0)
            def _():
                scatter(1, 1)

            return carry

        lax.fori_loop(0, 2, down_product, 0)
        scatter(1, 2)
        skip_place.wait()
        skip.swap(0)
        skip.swap(1)
        skip.swap(3)
        line_scatter_step(block_line, 0, partial_b, left_b, right_b, sr_b, sl_b)
        g_ub[...] = dot_tn(u_all[...], grads[...])
        g_ua[...] = dot_tn(gu_all[...], slots[...].reshape(tokens, width))
        g_db[...] = dot_tn(ud_all[...], cot[...].reshape(tokens, width))
        g_da[...] = dot_tn(gd_all[...], active[...])
        loads[7].wait()
        uq = dot_nt(x_ref[...], down_of(dtab, 6)).astype(BF)
        words_in = t_ref[...]
        uk = dot_nt(words_in, down_of(dtab, 7)).astype(BF)
        uv = dot_nt(words_in, down_of(dtab, 8)).astype(BF)
        for which in range(2):
            line_gather_drain(gather_lines[which], slots.at[which])
            line_scatter_finish(
                grad_lines[which], partial_g.at[which], left_g.at[which], right_g.at[which], sr_g.at[which],
                sl_g.at[which], acc.at[which * part_rows : (which + 1) * part_rows, :],
            )
        skip.wait(2)
        skip.swap(2)

        normal, inverse = stats(second_ref[...])
        own_cot = jnp.concatenate([cot[0, me], cot[1, me]], axis=0).astype(F32)
        g_second = own_cot + norm_backward(normal, inverse, acc[...] * gain[2:3, :])
        second_ref[...] = g_second
        g_low = g_second.astype(BF)
        x_low[...] = g_low
        go = dot_nt(g_low, up_of(utab, 9)).astype(BF)
        gb_o[...] = dot_tn(u_low, g_low)
        acc[...] = jnp.zeros_like(acc)

        def cross_grads(place, carry):
            gq_sum, gk_sum, gv_sum = carry

            @pl.when((place > 0) & (place < count - 1))
            def _():
                line_scatter_step(block_line, place, partial_b, left_b, right_b, sr_b, sl_b)

            g_attn = (dot_nn(x_low[...], wo[place]) + dot_nn(go, ao[place])).astype(BF)
            ga_o[place] = dot_tn(go, low_ref[place])
            gq_parts, gk_parts, gv_parts = [], [], []
            for head in range(heads):
                at = slice(head * HD, (head + 1) * HD)
                gh = g_attn[:, at]
                q = q_ref[place, head]
                k = kv[0, place, :, at]
                v = kv[1, place, :, at]
                p = jnp.exp(dot_nt(q, k) * scale - log_ref[place, :, head : head + 1])
                dp_ = dot_nt(gh, v)
                inner = jnp.sum(p * dp_, axis=-1, keepdims=True)
                ds = (p * (dp_ - inner)).astype(BF)
                dq = dot_nn(ds, k) * scale
                dk = dot_tn(ds, q) * scale
                gq_parts.append(norm_backward(q.astype(F32), inv_ref[place, :, head : head + 1], dq))
                side = kv[0, place, :, local + 2 * head : local + 2 * head + 2].astype(F32)
                gk_parts.append(norm_backward(k.astype(F32), side[:, 0:1] + side[:, 1:2], dk))
                gv_parts.append(dot_tn(p.astype(BF), gh))
            gq = jnp.concatenate(gq_parts, axis=1).astype(BF)
            gk = jnp.concatenate(gk_parts, axis=1).astype(BF)
            gv = jnp.concatenate(gv_parts, axis=1).astype(BF)
            acc[...] += dot_nt(gq, wq[place])
            gb_q[place] = dot_tn(uq, gq)
            gb_k[place] = dot_tn(uk, gk)
            gb_v[place] = dot_tn(uv, gv)
            return (
                gq_sum + dot_nt(gq, b_ref[place]),
                gk_sum + dot_nt(gk, bk[place]),
                gv_sum + dot_nt(gv, bv[place]),
            )

        start = (jnp.zeros((share, RANK), F32), jnp.zeros((words, RANK), F32), jnp.zeros((words, RANK), F32))
        gq_sum, gk_sum, gv_sum = lax.fori_loop(0, count, cross_grads, start)
        gq_sum = gq_sum.astype(BF)
        ga_q[...] = dot_tn(gq_sum, x_ref[...])
        ga_k[...] = dot_tn(gk_sum.astype(BF), words_in)
        ga_v[...] = dot_tn(gv_sum.astype(BF), words_in)
        g_x = acc[...] + dot_nn(gq_sum, down_of(dtab, 6))
        normal, inverse = stats(first_ref[...])
        g_first[...] = (second_ref[...] + norm_backward(normal, inverse, g_x * gain[1:2, :])).astype(BF)
        line_scatter_finish(block_line, partial_b, left_b, right_b, sr_b, sl_b, acc)
        block_sum[...] = acc[...].astype(BF)
        skip.wait_swaps()
        skip.drain()
        down.drain()
        up_w.drain_rest()
        for send in z_sends:
            send.wait_send()

    buffers = [vmem(count, share, width) for _ in range(5)]
    return call(
        kernel,
        [(summed, True)]
        + [(array, False) for array in (skip_out, query_weight, out_weight, up_weight, down_piece, skip_piece)]
        + [(text_kv, False), (text, False), (cotangent, False)]
        + [(array, True) for array in (gains, *tables)],
        [
            ((share, width), BF, True),
            ((share, width), BF, True),
            ((RANK, width), F32, True),
            ((count, RANK, local), F32, True),
            ((RANK, text_width), F32, True),
            ((count, RANK, local), F32, True),
            ((RANK, text_width), F32, True),
            ((count, RANK, local), F32, True),
            ((count, RANK, local), F32, True),
            ((RANK, width), F32, True),
            ((RANK, width), F32, True),
            ((RANK, units), F32, True),
            ((RANK, units), F32, True),
            ((RANK, width), F32, True),
            ((count, 4 * rows, span), BF, False),
        ],
        [pltpu.VMEM(text_kv.shape, BF), vmem(count, width, local), vmem(count, width, local), vmem(width, units),
         vmem(width, units), vmem(2, count, part_rows, width), vmem(words, text_width), vmem(share, width, dtype=F32),
         vmem(share, width, dtype=F32), vmem(share, width), vmem(share, width), vmem(count, heads, share, HD), vmem(count, share, heads, dtype=F32),
         vmem(count, share, heads, dtype=F32), vmem(count, share, local), vmem(share, width, dtype=F32)]
        + [vmem(count, RANK, local) for _ in range(4)] + [vmem(RANK, units) for _ in range(2)]
        + [vmem(2, count, part_rows, width), vmem(count, rows // 2, span), vmem(tokens, units), vmem(tokens, units)]
        + [vmem(tokens, RANK) for _ in range(4)] + [vmem(2, count, part_rows, width) for _ in range(5)] + buffers
        + [dma(13), dma(3, 7), dma(3, 7), dma(count), dma(count)] + [dma(count) for _ in range(20)],
        collective=3,
        cost=cost_of(12 * tokens * width * units, 60e6),
    )


class Shared:
    def __init__(self, target, rows, sems, stacked=False, split=True, columns=False):
        self.target, self.rows, self.stacked, self.split, self.columns = target, rows, stacked, split, columns
        self.send_sem, self.recv_sem, self.index = sems
        dp, core = lax.axis_index("dp"), lax.axis_index("ctx")
        self.dp, self.core = dp, core
        self.first = jnp.where(core == 0, xor_place(dp, 1), xor_place(dp, 2))
        self.second = jnp.where(core == 0, xor_place(dp, 2), xor_place(dp, 1))
        self.third = xor_place(dp, 3)

    def view(self, block, which):
        if self.columns:
            return self.target.at[:, pl.ds(pl.multiple_of(block * self.rows, 128), self.rows)]
        size = self.rows // 2 if self.split else self.rows
        start = block * self.rows + (which * size if self.split else 0)
        rows = pl.ds(pl.multiple_of(start, 16), size)
        return self.target.at[:, rows, :] if self.stacked else self.target.at[rows, :]

    def copy(self, number, source, block, which, device):
        target = self.view(block, which)
        source = target if source is None else source
        return push(source, target, self.send_sem.at[self.index, number], self.recv_sem.at[self.index, number], device)

    def send_own(self, source=None):
        self.copy(0, source, self.dp, self.core, {"dp": self.first}).start()
        self.copy(1, source, self.dp, self.core, {"dp": self.second}).start()

    def blocks(self):
        return [self.first, self.second, self.third] + ([self.dp] if self.stacked else [])

    def wait(self, number):
        self.copy(number, None, self.blocks()[number], self.core, {"dp": self.first}).wait_recv()

    def forward(self):
        self.copy(2, None, self.first, self.core, {"dp": self.second}).start()

    def swap(self, number):
        self.copy(3 + number, None, self.blocks()[number], self.core, {"ctx": 1 - self.core}).start()

    def wait_swaps(self):
        other = [self.second, self.first, self.third, self.dp]
        for number in range(len(self.blocks())):
            self.copy(3 + number, None, other[number], 1 - self.core, {"ctx": 1 - self.core}).wait_recv()

    def drain_own(self):
        for number in range(2):
            self.copy(number, None, self.dp, self.core, {"dp": self.first}).wait_send()

    def drain_rest(self):
        for number in range(2, 6):
            self.copy(number, None, self.dp, self.core, {"dp": self.first}).wait_send()

    def drain(self):
        for number in range(3 + (len(self.blocks()) if self.split else 0)):
            self.copy(number, None, self.dp, self.core, {"dp": self.first}).wait_send()


def front(count, heads, condition, index, hidden, long_skip, text, weights, mod_weight, gain_halves, gain_rows, tables):
    tokens, width = hidden.shape
    span = weights["skip"].shape[1]
    words, text_width = text.shape
    local = weights["q"].shape[1]
    units = weights["up"].shape[1]
    share = tokens // count
    block = min(128, tokens)
    chunk = min(CHUNK, tokens)
    pace = max(1, 64 // chunk)
    steps = tokens // chunk
    each = block // chunk
    scale = HD ** (-0.5)
    rows = weights["q"].shape[0]
    text_rows = weights["ck"].shape[1]
    mod_rows = mod_weight.shape[0]

    def kernel(skip_own, q_own, k_own, v_own, o_own, ck_own, cv_own, cq_own, co_own, up_own,
               index_ref, cond, hid_hbm, lsk_hbm, t_hbm, wm_hbm, halves, gain, dtab, utab,
               skip_hbm, attn_hbm, q_out, keys, values, low_out, log_out, inv_q, inv_k, summed, act_all, text_kv,
               wq_hbm, wk_hbm, wv_hbm, wo_hbm, wcq, wco, wup,
               hid, lsk, t_ref, wm, load_sem, skip_out, attn_in, wq, wk, wv, wo, out_sem, shift_row, wskip, wtext, part_x, pgain, sa, tk, tv, qa, qb, kb, vb, oa, mod_in, mod_slice, mod_out, partial_a, left_a, right_a, sr_a, sl_a,
               partial_b, left_b, right_b, sr_b, sl_b, wsend, wrecv, local_sem, msend, mrecv, tsend, trecv,
               xsend, xrecv, *sems):
        me = lax.axis_index("tensor")
        core = lax.axis_index("ctx")
        dp = lax.axis_index("dp")
        always = core >= 0
        peer = {"ctx": 1 - core}
        dp_peers = [{"dp": xor_place(dp, number)} for number in (1, 2, 3)]
        z_peers = [{"tensor": xor_place(me, number)} for number in range(1, count)]
        reduce_line = Line(me, count, *sems[:4])
        scatter_line = Line(me, count, *sems[4:8])
        text_line = Line(me, count, *sems[8:12])
        cross_lines = [Line(me, count, *sems[12:16]), Line(me, count, *sems[16:])]

        def sems_of(number):
            return (wsend, wrecv, number)

        skip = Shared(wskip, rows, sems_of(0))
        shared = {
            name: Shared(target, rows, sems_of(number))
            for name, target, number in (("q", wq, 1), ("k", wk, 2), ("v", wv, 3), ("o", wo, 4))
        }
        words_w = Shared(wtext, text_rows, sems_of(5), split=False, columns=True)
        cross = [Shared(wcq, rows, sems_of(6), stacked=True), Shared(wco, rows, sems_of(7), stacked=True)]
        wide = [Shared(wup, rows, sems_of(8))]
        owns = {"q": q_own, "k": k_own, "v": v_own, "o": o_own}
        half = pl.ds(pl.multiple_of(core * (rows // 2), 16), rows // 2)
        mine = pl.ds(pl.multiple_of(dp * rows, 16), rows)
        my_half = pl.ds(pl.multiple_of(dp * rows + core * (rows // 2), 16), rows // 2)

        everyone = [(always, device) for device in dp_peers + z_peers + [peer]]
        greet_all(everyone)
        loads = [
            pltpu.make_async_copy(source, target, load_sem.at[number])
            for number, (source, target) in enumerate(((hid_hbm, hid), (lsk_hbm, lsk), (t_hbm, t_ref), (wm_hbm, wm)))
        ]

        for place in range(count):
            @pl.when(me == place)
            def _(place=place):
                side = place * span // width
                start = place * span % width
                pgain[...] = halves[side : side + 1, start : start + span]

        places = [
            pltpu.make_async_copy(source, target.at[mine, :], local_sem.at[number])
            for number, (source, target) in enumerate(
                ((skip_own, wskip), (q_own, wq), (k_own, wk), (v_own, wv), (o_own, wo), (up_own, wup))
            )
        ]
        for place in places:
            place.start()
        crossing = [
            pltpu.make_async_copy(source.at[half, :], target.at[me, my_half, :], local_sem.at[7 + number])
            for number, (source, target) in enumerate(((cq_own, wcq), (co_own, wco)))
        ]
        text_mine = pl.ds(pl.multiple_of(dp * text_rows, 128), text_rows)

        def text_place(source):
            return pltpu.make_async_copy(source, wtext.at[:, text_mine], local_sem.at[9])

        @pl.when(core == 0)
        def _():
            text_place(ck_own).start()

        @pl.when(core == 1)
        def _():
            text_place(cv_own).start()

        for place in crossing:
            place.start()
        value = cond[...].astype(F32)
        act_low = (value / (1.0 + jnp.exp(-value))).astype(BF)
        tag = jnp.full((1, 128), index_ref[0], jnp.int32).astype(F32)
        act_all[dp] = jnp.concatenate([act_low.astype(F32), tag], axis=1)
        for load in loads:
            load.start()
        await_all(everyone)
        skip.send_own(skip_own.at[half, :])

        def cross_view(which):
            target = (wcq, wco)[which]
            return lambda block: target.at[block, my_half, :]

        def cross_step(number):
            for which, cross_line in enumerate(cross_lines):
                line_gather_step(cross_line, number, cross_view(which))

        for place in crossing:
            place.wait()
        cross_step(0)
        spread = [
            push(act_all.at[dp], act_all.at[dp], msend.at[0, number], mrecv.at[0, number], device)
            for number, device in enumerate(dp_peers)
        ]
        for copy in spread:
            copy.start()
        take_local(sa, dtab, 0, me, count)
        take_local(tk, utab, OUT_AT[7], me, count)
        take_local(tv, utab, OUT_AT[8], me, count)
        for number, target in enumerate((qb, kb, vb)):
            qa[number * RANK : (number + 1) * RANK, :] = down_of(dtab, 2 + number)
            take_local(target, utab, OUT_AT[2 + number], me, count)
        take_local(oa, dtab, IN_AT[5], me, count)
        skip.wait(0)
        skip.forward()
        for name in ("q", "k", "v", "o"):
            shared[name].send_own(owns[name].at[half, :])

        @pl.when(core == 0)
        def _():
            words_w.send_own(ck_own)

        @pl.when(core == 1)
        def _():
            words_w.send_own(cv_own)

        skip.swap(0)

        skip.wait(1)
        skip.swap(1)
        cross_step(1)

        for number in (1, 2, 3):
            source = act_all.at[xor_place(dp, number)]
            push(source, source, msend.at[0, number - 1], mrecv.at[0, number - 1], dp_peers[number - 1]).wait_recv()
        for owner in range(4):
            @pl.when(dp == owner)
            def _(owner=owner):
                span_of = slice(owner * mod_rows, (owner + 1) * mod_rows)
                for sequence in range(4):
                    mod_slice[sequence : sequence + 1, :] = act_all[sequence, :, span_of]

        skip.wait(2)
        skip.swap(2)
        loads[3].wait()
        products = dot_nn(mod_slice[...].astype(BF), wm[...])
        for sequence in range(4):
            mod_out[sequence] = products[sequence : sequence + 1]
        backs = [
            push(mod_out.at[xor_place(dp, number)], mod_in.at[dp], msend.at[1, number - 1], mrecv.at[1, number - 1],
                 dp_peers[number - 1])
            for number in (1, 2, 3)
        ]
        for copy in backs:
            copy.start()
        mod_in[dp] = mod_out[dp]
        places[0].wait()
        skip.wait_swaps()
        cross_step(2)
        for load in loads[:3]:
            load.wait()

        def compute(number):
            @pl.when(number % each == 0)
            def _():
                here = rows_of(number // each, block)
                left = hid[here, :].astype(F32)
                right = lsk[here, :].astype(F32)
                mean = (jnp.sum(left, axis=-1, keepdims=True) + jnp.sum(right, axis=-1, keepdims=True)) / (2 * width)
                spread = jnp.sum((left - mean) ** 2, axis=-1, keepdims=True)
                spread += jnp.sum((right - mean) ** 2, axis=-1, keepdims=True)
                inverse = lax.rsqrt(spread / (2 * width) + NORM_EPS)
                for place in range(count):
                    @pl.when(me == place)
                    def _(place=place):
                        source = hid if place * span < width else lsk
                        start = place * span % width
                        part_x[...] = source[here, start : start + span].astype(F32)
                x = ((part_x[...] - mean) * inverse * pgain[...]).astype(BF)
                u = dot_nt(x, sa[...]).astype(BF)
                y = (dot_nt(x, wskip[...]) + dot_nn(u, up_of(utab, 0))).astype(BF)
                for piece in range(each):
                    partial_a[number + piece] = y[piece * chunk : (piece + 1) * chunk]

        def text_product():
            @pl.when(core == 0)
            def _():
                text_place(ck_own).wait()

            @pl.when(core == 1)
            def _():
                text_place(cv_own).wait()

            x = t_ref[...]
            y = dot_nt(x, wtext[...])

            @pl.when(core == 0)
            def _():
                z = y + dot_nn(dot_nt(x, down_of(dtab, 7)).astype(BF), tk[...])
                parts, sides = [], []
                for head in range(heads):
                    normal, inverse = stats(z[:, head * HD : (head + 1) * HD])
                    upper = inverse.astype(BF)
                    parts.append(normal.astype(BF))
                    sides += [upper, (inverse - upper.astype(F32)).astype(BF)]
                text_kv[0, me, :, :local] = jnp.concatenate(parts, axis=1)
                text_kv[0, me, :, local : local + 2 * heads] = jnp.concatenate(sides, axis=1)

            @pl.when(core == 1)
            def _():
                z = y + dot_nn(dot_nt(x, down_of(dtab, 8)).astype(BF), tv[...])
                text_kv[1, me, :, :local] = z.astype(BF)

        text_slots = text_kv.at[core]

        def finish(slot, total):
            here = rows_of(slot, chunk)
            skip_out[here, :] = total
            normal, _ = stats(total)
            attn_in[here, :] = (normal * gain[0:1, :] + shift_row[...]).astype(BF)

        def project(number, carry):
            here = rows_of(number, block)
            x = attn_in[here, :]
            u = dot_nt(x, qa[...]).astype(BF)
            yq = dot_nn(x, wq[...]) + dot_nn(u[:, :RANK], qb[...])
            yk = dot_nn(x, wk[...]) + dot_nn(u[:, RANK : 2 * RANK], kb[...])
            yv = (dot_nn(x, wv[...]) + dot_nn(u[:, 2 * RANK :], vb[...])).astype(BF)
            parts_q, parts_k = [], []
            for head in range(heads):
                span_of = slice(head * HD, (head + 1) * HD)
                normal, inverse = stats(yq[:, span_of])
                q_out[head, here, :] = normal.astype(BF)
                parts_q.append(inverse)
                normal, inverse = stats(yk[:, span_of])
                keys[core, head, here, :] = normal.astype(BF)
                parts_k.append(inverse)
                values[core, head, here, :] = yv[:, span_of]
            inv_q[here, :] = jnp.concatenate(parts_q, axis=1)
            inv_k[here, :] = jnp.concatenate(parts_k, axis=1)
            return carry

        def beside(number):
            @pl.when(number == 1 * pace)
            def _():
                for other in (1, 2, 3):
                    target = mod_in.at[xor_place(dp, other)]
                    push(target, target, msend.at[1, other - 1], mrecv.at[1, other - 1], dp_peers[other - 1]).wait_recv()
                mod_u = dot_nt(act_low, down_of(dtab, 1)).astype(BF)
                shift_row[...] = mod_in[0] + mod_in[1] + mod_in[2] + mod_in[3] + dot_nn(mod_u, up_of(utab, 1))

            @pl.when(number == 2 * pace)
            def _():
                for weight in (*shared.values(), words_w):
                    weight.wait(0)
                    weight.forward()
                for weight in (*shared.values(), words_w):
                    weight.wait(1)
                for weight in shared.values():
                    weight.swap(0)
                    weight.swap(1)

            @pl.when(number == 4 * pace)
            def _():
                cross_step(3)
                for weight in cross:
                    weight.send_own()

            @pl.when(number == 5 * pace)
            def _():
                for weight in (*shared.values(), words_w):
                    weight.wait(2)
                for weight in shared.values():
                    weight.swap(2)

            @pl.when(number == 7 * pace)
            def _():
                for weight in wide:
                    weight.send_own(up_own.at[half, :])
                for place in places[1:5]:
                    place.wait()
                for weight in shared.values():
                    weight.wait_swaps()
                project(0, 0)

            @pl.when(number == 8 * pace)
            def _():
                project(1, 0)

            @pl.when(number == steps + count - 3)
            def _():
                text_product()
                line_gather_step(text_line, 0, text_slots)

        line_reduce_all(reduce_line, steps, compute, partial_a, left_a, right_a, sr_a, sl_a, finish, beside)

        lax.fori_loop(2, tokens // block, project, 0)
        stores = [
            pltpu.make_async_copy(source, target, out_sem.at[number])
            for number, (source, target) in enumerate(
                ((skip_out, skip_hbm), (attn_in, attn_hbm), (wq, wq_hbm), (wk, wk_hbm), (wv, wv_hbm), (wo, wo_hbm))
            )
        ]
        for store in stores:
            store.start()

        swaps = [
            push(ref.at[core], ref.at[core], xsend.at[number], xrecv.at[number], peer)
            for number, ref in enumerate((keys, values))
        ]
        for swap in swaps:
            swap.start()
        line_gather_step(text_line, 1, text_slots)
        for weight in cross:
            weight.wait(0)
            weight.forward()
            weight.swap(0)
            weight.swap(3)
        for number, ref in enumerate((keys, values)):
            push(ref.at[1 - core], ref.at[1 - core], xsend.at[number], xrecv.at[number], peer).wait_recv()

        def attend(place, carry):
            dest = scatter_order(me, count, place)
            here = rows_of(dest, share)
            outs, logs = [], []
            for head in range(heads):
                q = q_out[head, here, :]
                s0 = dot_nt(q, keys[0, head]) * scale
                s1 = dot_nt(q, keys[1, head]) * scale
                top = jnp.maximum(jnp.max(s0, axis=-1, keepdims=True), jnp.max(s1, axis=-1, keepdims=True))
                e0 = jnp.exp(s0 - top)
                e1 = jnp.exp(s1 - top)
                total = jnp.sum(e0, axis=-1, keepdims=True) + jnp.sum(e1, axis=-1, keepdims=True)
                share_of = 1.0 / total
                p0 = (e0 * share_of).astype(BF)
                p1 = (e1 * share_of).astype(BF)
                outs.append(dot_nn(p0, values[0, head]) + dot_nn(p1, values[1, head]))
                logs.append(top + jnp.log(total))
            low = jnp.concatenate(outs, axis=1).astype(BF)
            low_out[here, :] = low
            log_out[here, :] = jnp.concatenate(logs, axis=1)
            u = dot_nt(low, oa[...]).astype(BF)
            partial_b[dest] = (dot_nt(low, wo[...]) + dot_nn(u, up_of(utab, 5))).astype(BF)

            @pl.when(place < count - 1)
            def _():
                line_scatter_step(scatter_line, place, partial_b, left_b, right_b, sr_b, sl_b)

            @pl.when(place == 0)
            def _():
                line_gather_step(text_line, 2, text_slots)

            @pl.when(place == 1)
            def _():
                for weight in cross:
                    weight.wait(1)
                    weight.swap(1)
                line_gather_step(text_line, 3, text_slots)
                push(text_slots, text_slots, tsend, trecv, peer).start()

            @pl.when(place == 2)
            def _():
                for weight in cross:
                    weight.wait(2)
                    weight.swap(2)

            return carry

        lax.fori_loop(0, count, attend, 0)
        line_scatter_finish(scatter_line, partial_b, left_b, right_b, sr_b, sl_b, summed)
        for weight in wide:
            weight.wait(0)
            weight.wait(1)
        others = text_kv.at[1 - core]
        push(others, others, tsend, trecv, peer).wait_recv()
        for weight in cross:
            weight.wait_swaps()
        places[5].wait()
        for store in stores:
            store.wait()
        for weight in (skip, *shared.values(), words_w, *cross):
            weight.drain()
        for weight in wide:
            weight.drain_own()
        for which, cross_line in enumerate(cross_lines):
            line_gather_drain(cross_line, cross_view(which))
        for copy in spread + backs:
            copy.wait_send()
        line_gather_drain(text_line, text_slots)
        push(text_slots, text_slots, tsend, trecv, peer).wait_send()
        for swap in swaps:
            swap.wait_send()

    names = ("skip", "q", "k", "v", "o", "ck", "cv", "cq", "co", "up")
    return call(
        kernel,
        [(weights[name], name in ("cq", "co", "up")) for name in names] + [(index, None)]
        + [(condition, True)] + [(array, False) for array in (hidden, long_skip, text, mod_weight)]
        + [(array, True) for array in (gain_halves, gain_rows, *tables)],
        [
            ((tokens, width), F32, False),
            ((tokens, width), BF, False),
            ((heads, tokens, HD), BF, True),
            ((2, heads, tokens, HD), BF, True),
            ((2, heads, tokens, HD), BF, True),
            ((tokens, local), BF, True),
            ((tokens, heads), F32, True),
            ((tokens, heads), F32, True),
            ((tokens, heads), F32, True),
            ((share, width), F32, True),
            ((4, 1, width + 128), F32, True),
            ((2, count, words, local + 32), BF, True),
        ]
        + [((width, local), BF, False) for _ in range(4)]
        + [((count, width, local), BF, False) for _ in range(2)]
        + [((width, units), BF, False)],
        [vmem(tokens, width), vmem(tokens, width), vmem(words, text_width), vmem(mod_rows, width), dma(4),
         vmem(tokens, width, dtype=F32), vmem(tokens, width)] + [vmem(width, local) for _ in range(4)]
        + [dma(6), vmem(1, width, dtype=F32), vmem(width, span), vmem(local, text_width), vmem(block, span, dtype=F32), vmem(1, span, dtype=F32),
         vmem(RANK, span), vmem(RANK, local), vmem(RANK, local), vmem(3 * RANK, width)]
        + [vmem(RANK, local) for _ in range(4)]
        + [vmem(4, 1, width, dtype=F32), vmem(4, mod_rows, dtype=F32),
         vmem(4, 1, width, dtype=F32)]
        + [vmem(steps, chunk, width) for _ in range(5)] + [vmem(count, share, width) for _ in range(5)]
        + [dma(10, 7), dma(10, 7), dma(10), dma(2, 3), dma(2, 3), dma(), dma(),
           dma(2), dma(2)]
        + [dma(steps) for _ in range(4)] + [dma(count) for _ in range(16)],
        collective=1,
        cost=cost_of(8 * tokens * width * local, 60e6),
    )


def attention_backward(count, heads, g_first, query, keys, values, low, logs, inv_q, inv_k, out_weight, tables):
    share, width = g_first.shape
    tokens = query.shape[1]
    local = low.shape[1]
    scale = HD ** (-0.5)

    def kernel(g_ref, *refs):
        sources, refs = refs[:10], refs[10:]
        (gq_low, gk_low, gv_low, gall, ga_o, gb_o, q_ref, k_ref, v_ref, low_ref, log_ref, iq_ref, ik_ref, wo, dtab, utab,
         gk_acc, gv_acc, swap_out, swap_in, ao, lsem, xsend, xrecv, *sems) = refs
        loads = [
            pltpu.make_async_copy(source, target, lsem.at[number])
            for number, (source, target) in enumerate(
                zip(sources, (q_ref, k_ref, v_ref, low_ref, log_ref, iq_ref, ik_ref, wo, dtab, utab))
            )
        ]
        for load in loads:
            load.start()
        me = lax.axis_index("tensor")
        core = lax.axis_index("ctx")
        peer = {"ctx": 1 - core}
        grad_line = Line(me, count, *sems)
        gall[me] = g_ref[...]
        greet(line_partners(me, count) + [(core >= 0, peer)])
        line_gather_step(grad_line, 0, gall)
        for ref in (ga_o, gb_o, gk_acc, gv_acc):
            ref[...] = jnp.zeros_like(ref)
        for load in loads:
            load.wait()
        take_local(ao, dtab, IN_AT[5], me, count)

        def attend(place):
            rows = rows_of(place, share)
            g = gall[place]
            go = dot_nt(g, up_of(utab, 5)).astype(BF)
            g_attn = (dot_nn(g, wo[...]) + dot_nn(go, ao[...])).astype(BF)
            low = low_ref[rows, :]
            uo = dot_nt(low, ao[...]).astype(BF)
            gb_o[...] += dot_tn(uo, g)
            ga_o[...] += dot_tn(go, low)
            parts = []
            for head in range(heads):
                gh = g_attn[:, head * HD : (head + 1) * HD]
                q = q_ref[head, rows, :]
                probs, grads = [], []
                inner = 0.0
                for half in range(2):
                    p = jnp.exp(dot_nt(q, k_ref[half, head]) * scale - log_ref[rows, head : head + 1])
                    dp = dot_nt(gh, v_ref[half, head])
                    inner = inner + jnp.sum(p * dp, axis=-1, keepdims=True)
                    probs.append(p)
                    grads.append(dp)
                dq = 0.0
                for half in range(2):
                    ds = (probs[half] * (grads[half] - inner)).astype(BF)
                    dq = dq + dot_nn(ds, k_ref[half, head])
                    gk_acc[half, head] += dot_tn(ds, q)
                    gv_acc[half, head] += dot_tn(probs[half].astype(BF), gh)
                parts.append(norm_backward(q.astype(F32), iq_ref[rows, head : head + 1], dq * scale))
            gq_low[rows, :] = jnp.concatenate(parts, axis=1).astype(BF)

        def gather(number, carry):
            @pl.when(number > 0)
            def _():
                line_gather_step(grad_line, number, gall)

            def side(which, inner):
                place = me + (2 * which - 1) * number

                @pl.when((place >= 0) & (place < count) & ((number > 0) | (which == 0)))
                def _():
                    attend(lax.clamp(0, place, count - 1))

                return inner

            return lax.fori_loop(0, 2, side, carry)

        lax.fori_loop(0, count, gather, 0)
        swaps = []
        for head in range(heads):
            swap_out[head, 0] = (gk_acc[1 - core, head] * scale).astype(BF)
            swap_out[head, 1] = gv_acc[1 - core, head].astype(BF)
            swaps.append(push(swap_out.at[head], swap_in.at[head], xsend.at[head], xrecv.at[head], peer))
            swaps[-1].start()
        line_gather_drain(grad_line, gall)
        for head in range(heads):
            at = slice(head * HD, (head + 1) * HD)
            swaps[head].wait_recv()
            dk = gk_acc[core, head] * scale + swap_in[head, 0].astype(F32)
            normal = k_ref[core, head].astype(F32)
            gk_low[:, at] = norm_backward(normal, ik_ref[:, head : head + 1], dk).astype(BF)
            gv_low[:, at] = (gv_acc[core, head] + swap_in[head, 1].astype(F32)).astype(BF)
        for swap in swaps:
            swap.wait_send()

    return call(
        kernel,
        [(g_first, True)]
        + [(array, False) for array in (query, keys, values, low, logs, inv_q, inv_k, out_weight, *tables)],
        [
            ((tokens, local), BF, True),
            ((tokens, local), BF, True),
            ((tokens, local), BF, True),
            ((count, share, width), BF, True),
            ((RANK, local), F32, True),
            ((RANK, width), F32, True),
        ],
        [pltpu.VMEM(array.shape, array.dtype)
         for array in (query, keys, values, low, logs, inv_q, inv_k, out_weight, *tables)]
        + [vmem(2, heads, tokens, HD, dtype=F32), vmem(2, heads, tokens, HD, dtype=F32), vmem(heads, 2, tokens, HD),
           vmem(heads, 2, tokens, HD), vmem(RANK, local), dma(10), dma(heads), dma(heads)]
        + [dma(count) for _ in range(4)],
        collective=4,
        cost=cost_of(16 * tokens * width * local, 60e6),
    )


EARLY_A, EARLY_B = IN_AT[2], OUT_AT[2]
EARLY = IN_AT[12] - EARLY_A + OUT_AT[12] - EARLY_B
LATE = EARLY_A + EARLY_B


def back_end(count, grads, projections, attn_in, g_first, skip_out, hidden, long_skip, weight, mod_weight, block_sum,
             gain_halves, gain_rows, tables, condition, act_all, wide_grads, local_down, local_up, stacked):
    tokens, width = hidden.shape
    local = grads[0].shape[1]
    span = weight.shape[-1]
    block = tokens // count
    chunk = min(CHUNK, block)
    pace = max(1, 64 // chunk)
    each = block // chunk
    steps = tokens // chunk
    own_rows = RANK // count
    half_e = -(-EARLY // 256) * 128
    half_l = -(-LATE // 256) * 128
    base = IN_AT[12] - EARLY_A
    mod_rows = mod_weight.shape[0]

    def early(column):
        return column - EARLY_A if column < IN_AT[12] else column - EARLY_A - EARLY_B

    wide_at, wide = [early(column) for column in wide_grads], list(wide_grads.values())
    local_at = [early(column) for column in local_down] + [early(IN_AT[12] + column) for column in local_up]
    own_grads = list(local_down.values()) + list(local_up.values())
    stacked_at, stack = [early(column) for column in stacked], list(stacked.values())

    def kernel(gq, gk, gv, wq, wk, wv, x_hbm, gf_hbm, skip_hbm, hid_hbm, lsk_hbm, hbm_w, wm_hbm, b_in, gains, gain, dtab,
               utab, cond, act_ref, *refs):
        wide_refs, refs = refs[: len(wide)], refs[len(wide) :]
        own_refs, refs = refs[: len(own_grads)], refs[len(own_grads) :]
        stack_refs, refs = refs[: len(stack)], refs[len(stack) :]
        (out_h, out_l, out_a, out_b, out_c, ball, w, x_ref, gf_ref, skip_ref, hid, lsk, wm, buf_h, buf_l, low, g_ref, qkv_a, bq, bk, bv, partial_g, left_g, right_g,
         sr_g, sl_g, table, late, swap_out, swap_in, partial_e, left_e, right_e, sr_e, sl_e, summed, late_out, late_in,
         partial_l, slots_l, slots, late_slots, other_out, other_in, later_out, later_in, shifts, shift_in, act_out, act_in, g_act, g_sum,
         wsem, osem, ssem, rsem, dsend, drecv, msend, mrecv, zsend, zrecv, *sems) = refs
        me = lax.axis_index("tensor")
        core = lax.axis_index("ctx")
        dp = lax.axis_index("dp")
        peer = {"ctx": 1 - core}
        grad_line = Line(me, count, *sems[:4])
        early_line = Line(me, count, *sems[4:8])
        block_line = Line(me, count, *sems[8:])
        peers = [{"dp": xor_place(dp, number)} for number in (1, 2, 3)]
        z_peers = [{"tensor": xor_place(me, number)} for number in range(1, count)]
        loads = [
            pltpu.make_async_copy(source, target, wsem.at[number])
            for number, (source, target) in enumerate(
                ((x_hbm, x_ref), (gf_hbm, gf_ref), (skip_hbm, skip_ref), (hid_hbm, hid), (lsk_hbm, lsk), (hbm_w, w),
                 (wm_hbm, wm))
            )
        ]
        for load in loads:
            load.start()
        ball[me] = b_in[...]
        everyone = [(core >= 0, device) for device in z_peers + peers + [peer]]
        greet_all(everyone)
        for number, target in enumerate((bq, bk, bv)):
            qkv_a[number * RANK : (number + 1) * RANK, :] = down_of(dtab, 2 + number)
            take_local(target, utab, OUT_AT[2 + number], me, count)
        g_sum[...] = jnp.zeros_like(g_sum)
        act_low = act_ref[dp, :, :width].astype(BF)

        def compute(number):
            @pl.when((number % each == 0) & (number > 0))
            def _():
                product(number)

        def product(number):
            rows = rows_of(number // each, block)
            gu = jnp.concatenate(
                [dot_nt(gq[rows, :], bq[...]), dot_nt(gk[rows, :], bk[...]), dot_nt(gv[rows, :], bv[...])], axis=1
            ).astype(BF)
            y = dot_nt(gq[rows, :], wq[...]) + dot_nt(gk[rows, :], wk[...]) + dot_nt(gv[rows, :], wv[...])
            y = (y + dot_nn(gu, qkv_a[...])).astype(BF)
            for piece in range(each):
                partial_g[number + piece] = y[piece * chunk : (piece + 1) * chunk]

        def finish(slot, total):
            g_ref[rows_of(slot, chunk), :] = total

        def skip_block(number):
            rows = rows_of(number, block)
            ga_in = g_ref[rows, :]
            g_sum[...] += jnp.sum(ga_in, axis=0, keepdims=True)
            normal, inverse = stats(skip_ref[rows, :])
            g_low = (
                gf_ref[number].astype(F32) + norm_backward(normal, inverse, ga_in * gain[0:1, :])
            ).astype(BF)
            left = hid[rows, :].astype(F32)
            right = lsk[rows, :].astype(F32)
            mean = (jnp.sum(left, axis=-1, keepdims=True) + jnp.sum(right, axis=-1, keepdims=True)) / (2 * width)
            left = left - mean
            right = right - mean
            spread = jnp.sum(left * left, axis=-1, keepdims=True) + jnp.sum(right * right, axis=-1, keepdims=True)
            inverse = lax.rsqrt(spread / (2 * width) + NORM_EPS)
            left = left * inverse
            right = right * inverse
            gu = dot_nt(g_low, up_of(utab, 0)).astype(BF)
            a_left, a_right = dtab[:, :width], dtab[:, width : 2 * width]

            @pl.when(number == me)
            def _():
                low_l = (left * gains[0:1, :]).astype(BF)
                low_r = (right * gains[1:2, :]).astype(BF)
                u = (dot_nt(low_l, a_left) + dot_nt(low_r, a_right)).astype(BF)
                late[:, :width] = dot_tn(gu, low_l)
                late[:, width : 2 * width] = dot_tn(gu, low_r)
                late[:, EARLY_A : EARLY_A + width] = dot_tn(u, g_low)

            for place in range(count):
                low[:, place * span : (place + 1) * span] = dot_nn(g_low, w[place])
            gl = (low[:, :width] + dot_nn(gu, a_left)) * gains[0:1, :]
            gr = (low[:, width:] + dot_nn(gu, a_right)) * gains[1:2, :]
            mean = (jnp.sum(gl, axis=-1, keepdims=True) + jnp.sum(gr, axis=-1, keepdims=True)) / (2 * width)
            inner = (
                jnp.sum(gl * left, axis=-1, keepdims=True) + jnp.sum(gr * right, axis=-1, keepdims=True)
            ) / (2 * width)
            buf_h[number] = inverse * (gl - mean - left * inner)
            buf_l[number] = inverse * (gr - mean - right * inner)
            pltpu.make_async_copy(buf_h.at[number], out_h.at[rows, :], osem.at[0, number]).start()
            pltpu.make_async_copy(buf_l.at[number], out_l.at[rows, :], osem.at[1, number]).start()

        swap = push(swap_out, swap_in, ssem.at[0], rsem.at[0], peer)
        sends = [
            push(slots.at[dp], slots.at[dp], dsend.at[0, number], drecv.at[0, number], device)
            for number, device in enumerate(peers)
        ]

        def early_step(number):
            line_scatter_step(early_line, number, partial_e, left_e, right_e, sr_e, sl_e)

        def beside(number):
            @pl.when(number == pace)
            def _():
                for load in loads:
                    load.wait()
                x = x_ref[...]
                u = dot_nt(x, qkv_a[...]).astype(BF)
                table[...] = jnp.zeros_like(table)
                late[...] = jnp.zeros_like(late)
                for start, ref in zip(wide_at, wide_refs):
                    table[:, start : start + ref.shape[1]] = ref[...]
                for start, ref in zip(stacked_at, stack_refs):
                    size = ref.shape[2]
                    for place in range(count):
                        table[:, start + place * size : start + (place + 1) * size] = ref[place]
                qkv_b = []
                for which, (grad, factor) in enumerate(((gq, bq), (gk, bk), (gv, bv))):
                    gu = dot_nt(grad[...], factor[...]).astype(BF)
                    table[:, which * width : (which + 1) * width] = dot_tn(gu, x)
                    qkv_b.append(dot_tn(u[:, which * RANK : (which + 1) * RANK], grad[...]))
                for place in range(count):
                    @pl.when(me == place)
                    def _(place=place):
                        for which, piece in enumerate(qkv_b):
                            start = base + which * width + place * local
                            table[:, start : start + local] = piece
                        for start, ref in zip(local_at, own_refs):
                            size = ref.shape[1]
                            table[:, start + place * size : start + (place + 1) * size] = ref[...]
                for which in range(2):
                    @pl.when(core == which)
                    def _(which=which):
                        swap_out[...] = table[:, (1 - which) * half_e : (2 - which) * half_e].astype(BF)

                swap.start()

            @pl.when(number == 3 * pace)
            def _():
                swap.wait()
                for which in range(2):
                    @pl.when(core == which)
                    def _(which=which):
                        for part in range(count):
                            at = slice(part * own_rows, (part + 1) * own_rows)
                            mine = table[at, which * half_e : (which + 1) * half_e]
                            partial_e[part] = (mine + swap_in[at, :].astype(F32)).astype(BF)

            @pl.when((number >= steps) & (number < steps + count - 1))
            def _():
                early_step(number - steps)

            @pl.when(number == steps - 1)
            def _():
                line_gather_step(block_line, 0, ball)

        def after(slot):
            @pl.when(slot % each == each - 1)
            def _():
                skip_block(slot // each)

        product(0)
        await_all(everyone)
        line_reduce_all(
            grad_line, steps, compute, partial_g, left_g, right_g, sr_g, sl_g, finish, beside, after
        )

        g_shift = g_sum[...]
        shift_in[0] = g_shift
        swap_shift = push(shift_in.at[0], shift_in.at[1], ssem.at[2], rsem.at[2], peer)
        swap_shift.start()
        mod_u = dot_nt(act_low, down_of(dtab, 1))
        once = jnp.where(me == 0, 1.0, 0.0)
        shift_u = dot_nt(g_shift.astype(BF), up_of(utab, 1))
        zeros_u, zeros_w = jnp.zeros((7, RANK), F32), jnp.zeros((7, width), F32)
        mod_a = jnp.concatenate([shift_u * once, zeros_u], axis=0).astype(BF)
        mod_b = jnp.concatenate([mod_u * once, zeros_u], axis=0).astype(BF)
        act_pad = jnp.concatenate([act_low.astype(F32), zeros_w], axis=0).astype(BF)
        shift_pad = jnp.concatenate([g_shift, zeros_w], axis=0).astype(BF)
        late[:, IN_AT[1] : IN_AT[2]] = dot_tn(mod_a, act_pad)
        late[:, EARLY_A + OUT_AT[1] : EARLY_A + OUT_AT[2]] = dot_tn(mod_b, shift_pad)
        for which in range(2):
            @pl.when(core == which)
            def _(which=which):
                late_out[...] = late[:, (1 - which) * half_l : (2 - which) * half_l].astype(BF)

        swap_late = push(late_out, late_in, ssem.at[1], rsem.at[1], peer)
        swap_late.start()
        line_gather_step(block_line, 1, ball)
        line_scatter_finish(early_line, partial_e, left_e, right_e, sr_e, sl_e, summed)
        slots[dp] = summed[...].astype(BF)
        for send in sends:
            send.start()
        swap_shift.wait()
        shifts[dp] = shift_in[0] + shift_in[1]
        shift_sends = [
            push(shifts.at[dp], shifts.at[dp], msend.at[0, number], mrecv.at[0, number], device)
            for number, device in enumerate(peers)
        ]
        for send in shift_sends:
            send.start()
        swap_late.wait()
        for which in range(2):
            @pl.when(core == which)
            def _(which=which):
                for part in range(count):
                    at = slice(part * own_rows, (part + 1) * own_rows)
                    mine = late[at, which * half_l : (which + 1) * half_l]
                    partial_l[part] = (mine + late_in[at, :].astype(F32)).astype(BF)

        late_sends = [
            push(partial_l.at[xor_place(me, number + 1)], slots_l.at[me], zsend.at[number], zrecv.at[number], device)
            for number, device in enumerate(z_peers)
        ]
        for send in late_sends:
            send.start()
        slots_l[me] = partial_l[me]
        line_gather_step(block_line, 2, ball)
        for number in (1, 2, 3):
            source = shifts.at[xor_place(dp, number)]
            push(source, source, msend.at[0, number - 1], mrecv.at[0, number - 1], peers[number - 1]).wait_recv()
        every = jnp.concatenate([shifts[sequence] for sequence in range(4)], axis=0).astype(BF)
        products = dot_nt(every, wm[...])
        for sequence in range(4):
            act_out[sequence] = products[sequence : sequence + 1]
        act_sends = [
            push(act_out.at[xor_place(dp, number)], act_in.at[dp], msend.at[1, number - 1], mrecv.at[1, number - 1],
                 peers[number - 1])
            for number in (1, 2, 3)
        ]
        for send in act_sends:
            send.start()
        for number in range(count - 1):
            arrived = slots_l.at[xor_place(me, number + 1)]
            push(arrived, arrived, zsend.at[number], zrecv.at[number], z_peers[number]).wait_recv()
        late_sum = slots_l[0].astype(F32)
        for place in range(1, count):
            late_sum = late_sum + slots_l[place].astype(F32)
        late_slots[dp] = late_sum.astype(BF)
        later_sends = [
            push(late_slots.at[dp], late_slots.at[dp], dsend.at[1, number], drecv.at[1, number], device)
            for number, device in enumerate(peers)
        ]
        for send in later_sends:
            send.start()

        def arrive(ref, which):
            for number in (1, 2, 3):
                source = ref.at[xor_place(dp, number)]
                push(source, source, dsend.at[which, number - 1], drecv.at[which, number - 1], peers[number - 1]).wait_recv()

        def total(ref, which):
            slot = (dp * 2 + which).astype(F32)
            result = jnp.zeros(ref.shape[1:], F32)
            for sequence in range(4):
                chosen = jnp.where(act_ref[sequence, :, width : width + 1] == slot, 1.0, 0.0)
                result = result + ref[sequence].astype(F32) * chosen
            return result

        arrive(slots, 0)
        other_out[...] = total(slots, 1 - core).astype(BF)
        last = push(other_out, other_in, ssem.at[3], rsem.at[3], peer)
        last.start()
        mine_e = total(slots, core)
        line_gather_step(block_line, 3, ball)
        arrive(late_slots, 1)
        later_out[...] = total(late_slots, 1 - core).astype(BF)
        latest = push(later_out, later_in, ssem.at[4], rsem.at[4], peer)
        latest.start()
        mine_l = total(late_slots, core)

        act_in[dp] = act_out[dp]
        for number in (1, 2, 3):
            source = act_in.at[xor_place(dp, number)]
            push(source, source, msend.at[1, number - 1], mrecv.at[1, number - 1], peers[number - 1]).wait_recv()
        for place in range(4):
            g_act[:, place * mod_rows : (place + 1) * mod_rows] = act_in[place]
        full_u = dot_nt(shifts[dp].astype(BF), up_of(utab, 1)).astype(BF)
        grad = g_act[...] + dot_nn(full_u, down_of(dtab, 1))
        value = cond[...].astype(F32)
        gate = 1.0 / (1.0 + jnp.exp(-value))
        out_c[...] = grad * gate * (1.0 + value * (1.0 - gate))

        def lay(mine, arrived, target):
            for which in range(2):
                @pl.when(core == which)
                def _(which=which):
                    target(which, mine)
                    target(1 - which, arrived[...].astype(F32))

        def lay_early(which, values):
            start = which * half_e
            low_a = max(0, min(base - start, half_e))
            if low_a:
                out_a[:, EARLY_A + start : EARLY_A + start + low_a] = values[:, :low_a]
            if low_a < half_e:
                at = EARLY_B + start + low_a - base
                out_b[:, at : at + min(half_e, EARLY - start) - low_a] = values[:, low_a : min(half_e, EARLY - start)]

        def lay_late(which, values):
            start = which * half_l
            low_a = max(0, min(EARLY_A - start, half_l))
            end = min(half_l, LATE - start)
            if low_a:
                out_a[:, start : start + low_a] = values[:, :low_a]
            if low_a < end:
                at = start + low_a - EARLY_A
                out_b[:, at : at + end - low_a] = values[:, low_a:end]

        last.wait_recv()
        lay(mine_e, other_in, lay_early)
        latest.wait_recv()
        lay(mine_l, later_in, lay_late)
        line_gather_drain(block_line, ball)
        last.wait_send()
        latest.wait_send()
        for send in sends + later_sends + shift_sends + act_sends + late_sends:
            send.wait_send()

        def drain(number, carry):
            rows = rows_of(number, block)
            pltpu.make_async_copy(buf_h.at[number], out_h.at[rows, :], osem.at[0, number]).wait()
            pltpu.make_async_copy(buf_l.at[number], out_l.at[rows, :], osem.at[1, number]).wait()
            return carry

        lax.fori_loop(0, count, drain, 0)

    part_e = (own_rows, half_e)
    part_l = (own_rows, half_l)
    return call(
        kernel,
        [(array, True) for array in (*grads, *projections)]
        + [(array, False) for array in (attn_in, g_first, skip_out, hidden, long_skip, weight, mod_weight)]
        + [(array, True) for array in (block_sum, gain_halves, gain_rows, *tables, condition, act_all, *wide, *own_grads,
                                       *stack)],
        [
            ((tokens, width), F32, False),
            ((tokens, width), F32, False),
            ((own_rows, IN_AT[12]), F32, True),
            ((own_rows, OUT_AT[12]), F32, True),
            ((1, width), F32, True),
            ((count, block, width), BF, True),
        ],
        [
            vmem(count, width, span),
            vmem(tokens, width), vmem(count, block, width), vmem(tokens, width, dtype=F32), vmem(tokens, width),
            vmem(tokens, width), vmem(mod_rows, width),
            vmem(count, block, width, dtype=F32),
            vmem(count, block, width, dtype=F32),
            vmem(block, 2 * width, dtype=F32),
            vmem(tokens, width, dtype=F32),
            vmem(3 * RANK, width),
            vmem(RANK, local), vmem(RANK, local), vmem(RANK, local),
        ]
        + [vmem(steps, chunk, width) for _ in range(5)]
        + [vmem(RANK, 2 * half_e, dtype=F32), vmem(RANK, 2 * half_l, dtype=F32), vmem(RANK, half_e), vmem(RANK, half_e)]
        + [vmem(count, *part_e) for _ in range(5)]
        + [vmem(*part_e, dtype=F32), vmem(RANK, half_l), vmem(RANK, half_l), vmem(count, *part_l), vmem(count, *part_l)]
        + [vmem(4, *part_e), vmem(4, *part_l), vmem(*part_e), vmem(*part_e), vmem(*part_l), vmem(*part_l)]
        + [vmem(4, 1, width, dtype=F32), vmem(2, 1, width, dtype=F32), vmem(4, 1, mod_rows, dtype=F32),
           vmem(4, 1, mod_rows, dtype=F32), vmem(1, width, dtype=F32), vmem(1, width, dtype=F32)]
        + [dma(7), dma(2, count), dma(5), dma(5), dma(2, 3), dma(2, 3), dma(2, 3), dma(2, 3), dma(count), dma(count)]
        + [dma(steps) for _ in range(4)] + [dma(count) for _ in range(8)],
        collective=5,
        cost=cost_of(4 * tokens * width * width, 30e6),
    )


def prepare(index, down_factor, up_factor, gain, transposed):
    def kernel(index_ref, down_ref, up_ref, gain_ref, *refs):
        count = len(transposed)
        weight_refs, (down_out, up_out, gain_out), outs = refs[:count], refs[count : count + 3], refs[count + 3 :]
        down_out[...] = down_ref[0]
        up_out[...] = up_ref[0]
        gain_out[0, :] = gain_ref[:MODEL_WIDTH]
        gain_out[1, :] = gain_ref[MODEL_WIDTH:]
        for source, target in zip(weight_refs, outs):
            target[...] = source[...].T

    def whole(shape):
        return pl.BlockSpec(shape, lambda step, index_ref: (0,) * len(shape))

    shapes = [down_factor.shape[1:], up_factor.shape[1:]]
    out_shapes = [(shape, BF) for shape in shapes] + [((2, MODEL_WIDTH), F32)]
    out_shapes += [(weight.shape[::-1], BF) for weight in transposed]
    return pl.pallas_call(
        kernel,
        grid_spec=pltpu.PrefetchScalarGridSpec(
            num_scalar_prefetch=1,
            grid=(1,),
            in_specs=[pl.BlockSpec((1, *shape), lambda step, index_ref: (index_ref[0], 0, 0)) for shape in shapes]
            + [whole((2 * MODEL_WIDTH,))] + [whole(weight.shape) for weight in transposed],
            out_specs=[whole(shape) for shape, _ in out_shapes],
        ),
        out_shape=[jax.ShapeDtypeStruct(shape, dtype) for shape, dtype in out_shapes],
        compiler_params=pltpu.CompilerParams(vmem_limit_bytes=VMEM_BYTES),
    )(index, down_factor, up_factor, gain, *transposed)


def fused_body(
    hidden,
    long_skip_input,
    condition,
    projected_text_tokens,
    sequence_adapter_index,
    skip_projection_weight,
    shift_modulation_weight,
    self_query_weight,
    self_key_weight,
    self_value_weight,
    attention_output_weight,
    cross_query_weight,
    cross_key_weight,
    cross_value_weight,
    cross_output_weight,
    feedforward_up_weight,
    feedforward_down_weight,
    skip_norm_gain,
    norm_gain_rows,
    adapter_down_factor,
    adapter_up_factor,
    cotangent,
):
    rank = lax.axis_index("tensor")
    count = lax.axis_size("tensor")
    core = lax.axis_index("ctx")
    dp = lax.axis_index("dp")
    hidden, long_skip, text, cot = hidden[0], long_skip_input[0], projected_text_tokens[0], cotangent[0]
    local = self_query_weight.shape[1]
    heads = local // HD
    down_table, up_table, gain_halves, skip_t, attn_out_t, cross_out_t = prepare(
        sequence_adapter_index, adapter_down_factor, adapter_up_factor, skip_norm_gain,
        (skip_projection_weight, attention_output_weight, cross_output_weight),
    )
    tables = (down_table, up_table)

    weights = {
        "skip": skip_t,
        "q": self_query_weight,
        "k": self_key_weight,
        "v": self_value_weight,
        "o": attn_out_t,
        "ck": cross_key_weight.T,
        "cv": cross_value_weight.T,
        "cq": cross_query_weight,
        "co": cross_out_t,
        "up": feedforward_up_weight,
        "dn": feedforward_down_weight.T,
    }
    (skip_out, attn_in, query, keys, values, low, logs, inv_q, inv_k, summed, act_all, text_kv, wq, wk, wv, wo, wcq, wco,
     wup) = front(
        count, heads, condition, sequence_adapter_index, hidden, long_skip, text, weights, shift_modulation_weight,
        gain_halves, norm_gain_rows, tables,
    )
    (g_first, block_sum, g_cq_a, g_cq_b, g_ck_a, g_ck_b, g_cv_a, g_cv_b, g_co_a, g_co_b, g_up_a, g_up_b, g_down_a, g_down_b,
     skip_all) = middle(
        count, heads, summed, skip_out, wcq, wco, wup, weights["dn"], weights["skip"], text_kv, text,
        cot.reshape(count, 2, -1, MODEL_WIDTH), norm_gain_rows, tables,
    )
    gq, gk, gv, g_first_all, g_o_a, g_o_b = attention_backward(
        count, heads, g_first, query, keys, values, low, logs, inv_q, inv_k, wo, tables
    )
    base = IN_AT[12]
    hidden_grad, skip_grad, grad_down, grad_up, g_condition, block_all = back_end(
        count, (gq, gk, gv), (wq, wk, wv), attn_in, g_first_all, skip_out, hidden, long_skip, skip_all,
        shift_modulation_weight, block_sum, gain_halves, norm_gain_rows, tables, condition, act_all,
        {
            IN_AT[6]: g_cq_a, IN_AT[7]: g_ck_a, IN_AT[8]: g_cv_a, IN_AT[10]: g_up_a,
            base + OUT_AT[5]: g_o_b, base + OUT_AT[9]: g_co_b, base + OUT_AT[11]: g_down_b,
        },
        {IN_AT[5]: g_o_a, IN_AT[11]: g_down_a},
        {OUT_AT[10]: g_up_b},
        {
            IN_AT[9]: g_co_a, base + OUT_AT[6]: g_cq_b, base + OUT_AT[7]: g_ck_b, base + OUT_AT[8]: g_cv_b,
        },
    )
    block_out = block_all.reshape(hidden.shape)
    size = MODEL_WIDTH // (2 * count)
    condition_gradient = lax.dynamic_slice_in_dim(g_condition[0], (core * count + rank) * size, size, 0)
    return (
        block_out[None],
        hidden_grad[None],
        skip_grad[None],
        condition_gradient,
        grad_down.reshape(-1),
        grad_up.reshape(-1),
    )


def solution(mesh):
    in_specs = (
        P("dp", "ctx", None),
        P("dp", "ctx", None),
        P("dp", None),
        P("dp", None, None),
        P("dp"),
        P("tensor", "dp"),
        P("dp", None),
        P("dp", "tensor"),
        P("dp", "tensor"),
        P("dp", "tensor"),
        P("tensor", "dp"),
        P("dp", "tensor"),
        P("dp", "tensor"),
        P("dp", "tensor"),
        P("tensor", "dp"),
        P("dp", "tensor"),
        P("tensor", "dp"),
        P(),
        P(),
        P(),
        P(),
        P("dp", "ctx", None),
    )
    out_specs = (
        P("dp", "ctx", None),
        P("dp", "ctx", None),
        P("dp", "ctx", None),
        P(("dp", "ctx", "tensor")),
        P(("dp", "ctx", "tensor")),
        P(("dp", "ctx", "tensor")),
    )
    shape = mesh.shape
    fused = shape["dp"] == 4 and shape["ctx"] == 2 and shape["tensor"] == 4
    return jax.shard_map(fused_body if fused else body, mesh=mesh, in_specs=in_specs, out_specs=out_specs, check_vma=False)
```

```python
from functools import partial

import jax
import jax.numpy as jnp
from jax import lax
from jax.experimental import pallas as pl
from jax.experimental.pallas import tpu as pltpu
from jax.sharding import PartitionSpec as P

MODEL_WIDTH = 1408
HD = 88
FF = 6144
TW = 1024


PRECISE = lax.Precision.HIGHEST
NORM_EPS = 1e-06


def row_norm(values):
    centered = values - jnp.mean(values, axis=-1, keepdims=True)
    inverse = lax.rsqrt(jnp.mean(centered * centered, axis=-1, keepdims=True) + NORM_EPS)
    return (centered * inverse, inverse)


def head_norm(values, head_width):
    shaped = values.reshape(values.shape[:-1] + (values.shape[-1] // head_width, head_width))
    centered = shaped - jnp.mean(shaped, axis=-1, keepdims=True)
    inverse = lax.rsqrt(jnp.mean(centered * centered, axis=-1, keepdims=True) + NORM_EPS)
    return (centered * inverse, inverse)


def norm_back(normal, inverse, grad_normal):
    return inverse * (
        grad_normal
        - jnp.mean(grad_normal, axis=-1, keepdims=True)
        - normal * jnp.mean(grad_normal * normal, axis=-1, keepdims=True)
    )


def split_parts(values):
    if values.dtype == jnp.bfloat16:
        return [values]
    upper_half = values.astype(jnp.bfloat16)
    lower_half = (values - upper_half.astype(jnp.float32)).astype(jnp.bfloat16)
    return [upper_half, lower_half]


def paired_product(form, left, right):
    total = None
    for left_number, left_part in enumerate(split_parts(left)):
        for right_number, right_part in enumerate(split_parts(right)):
            if left_number + right_number < 2:
                term = jnp.einsum(form, left_part, right_part, preferred_element_type=jnp.float32)
                total = term if total is None else total + term
    return total


def lowrank_out(input_list, weight_matrix, down_piece, up_factor_piece):
    frozen_term = jnp.einsum(
        "gtb,bx->gtx", input_list, weight_matrix, preferred_element_type=jnp.float32
    )
    rank_activation = jnp.einsum(
        "snd,srd->snr", input_list, down_piece, preferred_element_type=jnp.float32
    )
    adapter_term = paired_product("dti,dip->dtp", rank_activation, up_factor_piece)
    return (frozen_term + adapter_term, rank_activation)


def lowrank_back(
    input_list,
    weight_matrix,
    down_piece,
    up_factor_piece,
    rank_activation,
    output_gradient,
    want_input,
):
    upper_gradient = paired_product("pmf,pmz->pfz", rank_activation, output_gradient)
    rank_gradient = paired_product("hzu,hlu->hzl", output_gradient, up_factor_piece)
    grad_lower = paired_product("snr,snd->srd", rank_gradient, input_list)
    if want_input:
        input_gradients = paired_product("lga,wa->lgw", output_gradient, weight_matrix)
        input_gradients = input_gradients + paired_product(
            "snr,srd->snd", rank_gradient, down_piece
        )
        return (input_gradients, grad_lower, upper_gradient)
    return (None, grad_lower, upper_gradient)


def attend_forward(query, key_rows, values_in, scale_factor):
    scores = (
        jnp.einsum("snhe,smhe->shnm", query, key_rows, preferred_element_type=jnp.float32)
        * scale_factor
    )
    row_top = jnp.max(scores, axis=-1, keepdims=True)
    exp_scores = jnp.exp(scores - row_top)
    row_total = jnp.sum(exp_scores, axis=-1, keepdims=True)
    attn_probs = (exp_scores / row_total).astype(jnp.bfloat16)
    result = jnp.einsum(
        "shnm,smhe->snhe", attn_probs, values_in, preferred_element_type=jnp.float32
    )
    return (result, row_top + jnp.log(row_total))


def attend_back(query, key_rows, values_in, log_total, grad_result, scale_factor):
    scores = (
        jnp.einsum("snhe,smhe->shnm", query, key_rows, preferred_element_type=jnp.float32)
        * scale_factor
    )
    attn_probs = jnp.exp(scores - log_total)
    grad_probs = jnp.einsum(
        "snhe,smhe->shnm", grad_result, values_in, preferred_element_type=jnp.float32
    )
    row_inner = jnp.sum(attn_probs * grad_probs, axis=-1, keepdims=True)
    grad_scores = (attn_probs * (grad_probs - row_inner)).astype(jnp.bfloat16)
    grad_query = (
        jnp.einsum("shnm,smhe->snhe", grad_scores, key_rows, preferred_element_type=jnp.float32)
        * scale_factor
    )
    grad_keys = (
        jnp.einsum("shnm,snhe->smhe", grad_scores, query, preferred_element_type=jnp.float32)
        * scale_factor
    )
    grad_values = jnp.einsum(
        "shnm,snhe->smhe",
        attn_probs.astype(jnp.bfloat16),
        grad_result,
        preferred_element_type=jnp.float32,
    )
    return (grad_query, grad_keys, grad_values)


def body(
    hidden,
    long_skip_input,
    condition,
    projected_text_tokens,
    sequence_adapter_index,
    skip_projection_weight,
    shift_modulation_weight,
    self_query_weight,
    self_key_weight,
    self_value_weight,
    attention_output_weight,
    cross_query_weight,
    cross_key_weight,
    cross_value_weight,
    cross_output_weight,
    feedforward_up_weight,
    feedforward_down_weight,
    skip_norm_gain,
    norm_gain_rows,
    adapter_down_factor,
    adapter_up_factor,
    cotangent,
):
    (
        skip_projection_weight,
        shift_modulation_weight,
        self_query_weight,
        self_key_weight,
        self_value_weight,
        attention_output_weight,
        cross_query_weight,
        cross_key_weight,
        cross_value_weight,
        cross_output_weight,
        feedforward_up_weight,
        feedforward_down_weight,
    ) = (
        lax.all_gather(skip_projection_weight, "dp", axis=1, tiled=True),
        lax.all_gather(shift_modulation_weight, "dp", axis=0, tiled=True),
        lax.all_gather(self_query_weight, "dp", axis=0, tiled=True),
        lax.all_gather(self_key_weight, "dp", axis=0, tiled=True),
        lax.all_gather(self_value_weight, "dp", axis=0, tiled=True),
        lax.all_gather(attention_output_weight, "dp", axis=1, tiled=True),
        lax.all_gather(cross_query_weight, "dp", axis=0, tiled=True),
        lax.all_gather(cross_key_weight, "dp", axis=0, tiled=True),
        lax.all_gather(cross_value_weight, "dp", axis=0, tiled=True),
        lax.all_gather(cross_output_weight, "dp", axis=1, tiled=True),
        lax.all_gather(feedforward_up_weight, "dp", axis=0, tiled=True),
        lax.all_gather(feedforward_down_weight, "dp", axis=1, tiled=True),
    )
    tensor_rank = lax.axis_index("tensor")
    tensor_count = lax.axis_size("tensor")
    seqs_local = hidden.shape[0]
    tokens_local = hidden.shape[1]
    local_width = self_query_weight.shape[1]
    heads_local = local_width // HD
    ff_local = feedforward_up_weight.shape[1]
    skip_width = skip_projection_weight.shape[0]
    scale_factor = HD ** (-0.5)
    in_sizes = [
        2 * MODEL_WIDTH,
        MODEL_WIDTH,
        MODEL_WIDTH,
        MODEL_WIDTH,
        MODEL_WIDTH,
        MODEL_WIDTH,
        MODEL_WIDTH,
        TW,
        TW,
        MODEL_WIDTH,
        MODEL_WIDTH,
        FF,
    ]
    out_sizes = [MODEL_WIDTH] * 10 + [FF, MODEL_WIDTH]
    input_offsets = [sum(in_sizes[:number]) for number in range(12)]
    output_offsets = [sum(out_sizes[:number]) for number in range(12)]
    select_adapter = (
        sequence_adapter_index[:, None]
        == jnp.arange(adapter_down_factor.shape[0], dtype=jnp.int32)[None, :]
    )
    choose_wide = select_adapter.astype(jnp.float32)
    down_seq = jnp.einsum(
        "fn,nge->fge",
        select_adapter.astype(jnp.bfloat16),
        adapter_down_factor,
        preferred_element_type=jnp.float32,
    ).astype(jnp.bfloat16)
    up_seq = jnp.einsum(
        "fn,nge->fge",
        select_adapter.astype(jnp.bfloat16),
        adapter_up_factor,
        preferred_element_type=jnp.float32,
    ).astype(jnp.bfloat16)

    def down_full(number):
        return down_seq[:, :, input_offsets[number] : input_offsets[number] + in_sizes[number]]

    def up_full(number):
        return up_seq[:, :, output_offsets[number] : output_offsets[number] + out_sizes[number]]

    def down_local(number, span_width):
        return lax.dynamic_slice_in_dim(
            down_seq, input_offsets[number] + tensor_rank * span_width, span_width, 2
        )

    def up_local(number, span_width):
        return lax.dynamic_slice_in_dim(
            up_seq, output_offsets[number] + tensor_rank * span_width, span_width, 2
        )

    def to_slots(grad_piece):
        return jnp.einsum("si,srd->ird", choose_wide, grad_piece, precision=PRECISE)

    joined = jnp.concatenate([hidden, long_skip_input], axis=-1).astype(jnp.float32)
    joined_normal, joined_inverse = row_norm(joined)
    joined_low = (joined_normal * skip_norm_gain).astype(jnp.bfloat16)
    joined_part = lax.dynamic_slice_in_dim(joined_low, tensor_rank * skip_width, skip_width, 2)
    skip_partial, skip_rank = lowrank_out(
        joined_part, skip_projection_weight, down_local(0, skip_width), up_full(0)
    )
    skip_out = lax.psum(skip_partial.astype(jnp.bfloat16), "tensor").astype(jnp.float32)
    act_wide, silu_pull = jax.vjp(jax.nn.silu, condition.astype(jnp.float32))
    act_low = act_wide.astype(jnp.bfloat16)[:, None, :]
    shift_row, mod_rank = lowrank_out(act_low, shift_modulation_weight, down_full(1), up_full(1))
    first_normal, first_inverse = row_norm(skip_out)
    attn_in = (first_normal * norm_gain_rows[0] + shift_row).astype(jnp.bfloat16)
    query_proj, query_rank = lowrank_out(
        attn_in, self_query_weight, down_full(2), up_local(2, local_width)
    )
    key_proj, key_rank = lowrank_out(
        attn_in, self_key_weight, down_full(3), up_local(3, local_width)
    )
    value_proj, value_rank = lowrank_out(
        attn_in, self_value_weight, down_full(4), up_local(4, local_width)
    )
    query_normal, query_inverse = head_norm(query_proj, HD)
    key_normal, key_inverse = head_norm(key_proj, HD)
    query_low = query_normal.astype(jnp.bfloat16)
    key_low = key_normal.astype(jnp.bfloat16).reshape(seqs_local, tokens_local, local_width)
    value_low = value_proj.astype(jnp.bfloat16)
    keys_all, values_all = (
        lax.all_gather(key_low, "ctx", axis=1, tiled=True),
        lax.all_gather(value_low, "ctx", axis=1, tiled=True),
    )
    keys_four = keys_all.reshape(seqs_local, -1, heads_local, HD)
    values_four = values_all.reshape(seqs_local, -1, heads_local, HD)
    attn_result, attn_log = attend_forward(query_low, keys_four, values_four, scale_factor)
    attn_low = attn_result.reshape(seqs_local, tokens_local, local_width).astype(jnp.bfloat16)
    attn_partial, out_rank = lowrank_out(
        attn_low, attention_output_weight, down_local(5, local_width), up_full(5)
    )
    first_res = skip_out + lax.psum(attn_partial.astype(jnp.bfloat16), "tensor").astype(jnp.float32)
    second_normal, second_inverse = row_norm(first_res)
    cross_in = (second_normal * norm_gain_rows[1]).astype(jnp.bfloat16)
    cquery_proj, cquery_rank = lowrank_out(
        cross_in, cross_query_weight, down_full(6), up_local(6, local_width)
    )
    ckey_proj, ckey_rank = lowrank_out(
        projected_text_tokens, cross_key_weight, down_full(7), up_local(7, local_width)
    )
    cvalue_proj, cvalue_rank = lowrank_out(
        projected_text_tokens, cross_value_weight, down_full(8), up_local(8, local_width)
    )
    cquery_normal, cquery_inverse = head_norm(cquery_proj, HD)
    ckey_normal, ckey_inverse = head_norm(ckey_proj, HD)
    cquery_low = cquery_normal.astype(jnp.bfloat16)
    ckey_low = ckey_normal.astype(jnp.bfloat16)
    cvalue_low = cvalue_proj.astype(jnp.bfloat16).reshape(seqs_local, -1, heads_local, HD)
    cross_result, cross_log = attend_forward(cquery_low, ckey_low, cvalue_low, scale_factor)
    cross_low = cross_result.reshape(seqs_local, tokens_local, local_width).astype(jnp.bfloat16)
    cross_partial, cout_rank = lowrank_out(
        cross_low, cross_output_weight, down_local(9, local_width), up_full(9)
    )
    second_res = first_res + lax.psum(cross_partial.astype(jnp.bfloat16), "tensor").astype(
        jnp.float32
    )
    third_normal, third_inverse = row_norm(second_res)
    mlp_in = (third_normal * norm_gain_rows[2]).astype(jnp.bfloat16)
    up_proj, up_rank = lowrank_out(
        mlp_in, feedforward_up_weight, down_full(10), up_local(10, ff_local)
    )
    activated, gelu_pull = jax.vjp(partial(jax.nn.gelu, approximate=True), up_proj)
    activated_low = activated.astype(jnp.bfloat16)
    down_partial, down_rank = lowrank_out(
        activated_low, feedforward_down_weight, down_local(11, ff_local), up_full(11)
    )
    block_out = second_res + lax.psum(down_partial.astype(jnp.bfloat16), "tensor").astype(
        jnp.float32
    )
    grad_act, grad_down_lower, grad_down_upper = lowrank_back(
        activated_low,
        feedforward_down_weight,
        down_local(11, ff_local),
        up_full(11),
        down_rank,
        cotangent,
        True,
    )
    grad_pre = gelu_pull(grad_act)[0].astype(jnp.bfloat16)
    grad_mlp_in, grad_up_lower, grad_up_upper = lowrank_back(
        mlp_in,
        feedforward_up_weight,
        down_full(10),
        up_local(10, ff_local),
        up_rank,
        grad_pre,
        True,
    )
    grad_mlp_in = lax.psum(grad_mlp_in.astype(jnp.bfloat16), "tensor").astype(jnp.float32)
    grad_second = cotangent.astype(jnp.float32) + norm_back(
        third_normal, third_inverse, grad_mlp_in * norm_gain_rows[2]
    )
    grad_cross_low, grad_cout_lower, grad_cout_upper = lowrank_back(
        cross_low,
        cross_output_weight,
        down_local(9, local_width),
        up_full(9),
        cout_rank,
        grad_second.astype(jnp.bfloat16),
        True,
    )
    grad_cross_result = grad_cross_low.astype(jnp.bfloat16).reshape(
        seqs_local, tokens_local, heads_local, HD
    )
    grad_cquery, grad_ckey, grad_cvalue = attend_back(
        cquery_low, ckey_low, cvalue_low, cross_log, grad_cross_result, scale_factor
    )
    grad_cquery_proj = (
        norm_back(cquery_normal, cquery_inverse, grad_cquery)
        .reshape(seqs_local, tokens_local, local_width)
        .astype(jnp.bfloat16)
    )
    grad_ckey_proj = norm_back(ckey_normal, ckey_inverse, grad_ckey).reshape(
        seqs_local, -1, local_width
    )
    none_first, grad_ckey_lower, grad_ckey_upper = lowrank_back(
        projected_text_tokens,
        cross_key_weight,
        down_full(7),
        up_local(7, local_width),
        ckey_rank,
        grad_ckey_proj,
        False,
    )
    none_second, grad_cvalue_lower, grad_cvalue_upper = lowrank_back(
        projected_text_tokens,
        cross_value_weight,
        down_full(8),
        up_local(8, local_width),
        cvalue_rank,
        grad_cvalue.reshape(seqs_local, -1, local_width),
        False,
    )
    grad_cross_in, grad_cquery_lower, grad_cquery_upper = lowrank_back(
        cross_in,
        cross_query_weight,
        down_full(6),
        up_local(6, local_width),
        cquery_rank,
        grad_cquery_proj,
        True,
    )
    grad_cross_in = lax.psum(grad_cross_in.astype(jnp.bfloat16), "tensor").astype(jnp.float32)
    grad_first = grad_second + norm_back(
        second_normal, second_inverse, grad_cross_in * norm_gain_rows[1]
    )
    grad_attn_low, grad_aout_lower, grad_aout_upper = lowrank_back(
        attn_low,
        attention_output_weight,
        down_local(5, local_width),
        up_full(5),
        out_rank,
        grad_first.astype(jnp.bfloat16),
        True,
    )
    grad_attn_result = grad_attn_low.astype(jnp.bfloat16).reshape(
        seqs_local, tokens_local, heads_local, HD
    )
    grad_query, grad_keys_all, grad_values_all = attend_back(
        query_low, keys_four, values_four, attn_log, grad_attn_result, scale_factor
    )
    grad_keys, grad_values = (
        lax.psum_scatter(
            grad_keys_all.reshape(seqs_local, -1, local_width).astype(jnp.bfloat16),
            "ctx",
            scatter_dimension=1,
            tiled=True,
        ).astype(jnp.float32),
        lax.psum_scatter(
            grad_values_all.reshape(seqs_local, -1, local_width).astype(jnp.bfloat16),
            "ctx",
            scatter_dimension=1,
            tiled=True,
        ).astype(jnp.float32),
    )
    grad_query_proj = (
        norm_back(query_normal, query_inverse, grad_query)
        .reshape(seqs_local, tokens_local, local_width)
        .astype(jnp.bfloat16)
    )
    grad_key_proj = (
        norm_back(
            key_normal, key_inverse, grad_keys.reshape(seqs_local, tokens_local, heads_local, HD)
        )
        .reshape(seqs_local, tokens_local, local_width)
        .astype(jnp.bfloat16)
    )
    grad_value_proj = grad_values.astype(jnp.bfloat16)
    grad_in_query, grad_query_lower, grad_query_upper = lowrank_back(
        attn_in,
        self_query_weight,
        down_full(2),
        up_local(2, local_width),
        query_rank,
        grad_query_proj,
        True,
    )
    grad_in_key, grad_key_lower, grad_key_upper = lowrank_back(
        attn_in,
        self_key_weight,
        down_full(3),
        up_local(3, local_width),
        key_rank,
        grad_key_proj,
        True,
    )
    grad_in_value, grad_value_lower, grad_value_upper = lowrank_back(
        attn_in,
        self_value_weight,
        down_full(4),
        up_local(4, local_width),
        value_rank,
        grad_value_proj,
        True,
    )
    grad_attn_in = lax.psum(
        (grad_in_query + grad_in_key + grad_in_value).astype(jnp.bfloat16), "tensor"
    ).astype(jnp.float32)
    grad_shift = jnp.sum(grad_attn_in, axis=1, keepdims=True) / tensor_count
    grad_act_low, grad_mod_lower, grad_mod_upper = lowrank_back(
        act_low, shift_modulation_weight, down_full(1), up_full(1), mod_rank, grad_shift, True
    )
    grad_condition = silu_pull(grad_act_low[:, 0, :])[0]
    grad_skip_out = grad_first + norm_back(
        first_normal, first_inverse, grad_attn_in * norm_gain_rows[0]
    )
    grad_joined_part, grad_skip_lower, grad_skip_upper = lowrank_back(
        joined_part,
        skip_projection_weight,
        down_local(0, skip_width),
        up_full(0),
        skip_rank,
        grad_skip_out.astype(jnp.bfloat16),
        True,
    )
    grad_joined = lax.all_gather(
        grad_joined_part.astype(jnp.bfloat16), "tensor", axis=2, tiled=True
    ).astype(grad_joined_part.dtype)
    grad_joined_full = norm_back(joined_normal, joined_inverse, grad_joined * skip_norm_gain)
    hidden_grad = grad_joined_full[:, :, :MODEL_WIDTH]
    skip_grad = grad_joined_full[:, :, MODEL_WIDTH:]
    lower_factor_parts = [
        (0, grad_skip_lower, True),
        (1, grad_mod_lower, False),
        (2, grad_query_lower, False),
        (3, grad_key_lower, False),
        (4, grad_value_lower, False),
        (5, grad_aout_lower, True),
        (6, grad_cquery_lower, False),
        (7, grad_ckey_lower, False),
        (8, grad_cvalue_lower, False),
        (9, grad_cout_lower, True),
        (10, grad_up_lower, False),
        (11, grad_down_lower, True),
    ]
    upper_factor_parts = [
        (0, grad_skip_upper, False),
        (1, grad_mod_upper, False),
        (2, grad_query_upper, True),
        (3, grad_key_upper, True),
        (4, grad_value_upper, True),
        (5, grad_aout_upper, False),
        (6, grad_cquery_upper, True),
        (7, grad_ckey_upper, True),
        (8, grad_cvalue_upper, True),
        (9, grad_cout_upper, False),
        (10, grad_up_upper, True),
        (11, grad_down_upper, False),
    ]
    slot_total = adapter_down_factor.shape[0]
    rank_total = adapter_down_factor.shape[1]
    cond_buffer = jnp.zeros((lax.axis_size("dp") * seqs_local, MODEL_WIDTH), jnp.float32)
    cond_buffer = lax.dynamic_update_slice_in_dim(
        cond_buffer, grad_condition, lax.axis_index("dp") * seqs_local, 0
    )
    cond_flat = cond_buffer.reshape(-1)

    def dense_table(parts_list, starts, total_width, row_count, slot_pieces):
        table = jnp.zeros((row_count, total_width), jnp.float32)
        for position, (number, grad_piece, is_local) in enumerate(parts_list):
            span_width = grad_piece.shape[2]
            column_start = starts[number] + tensor_rank * span_width if is_local else starts[number]
            table = lax.dynamic_update_slice_in_dim(table, slot_pieces[position], column_start, 1)
        return table

    down_factor_slots = [
        to_slots(grad_piece).reshape(slot_total * rank_total, -1)
        for number, grad_piece, is_local in lower_factor_parts
    ]
    up_factor_slots = [
        to_slots(grad_piece).reshape(slot_total * rank_total, -1)
        for number, grad_piece, is_local in upper_factor_parts
    ]
    down_compact = jnp.concatenate(down_factor_slots, axis=1)
    up_compact = jnp.concatenate(up_factor_slots, axis=1)
    cond_rows, down_rows, up_rows = (
        lax.psum_scatter(
            cond_flat.astype(jnp.bfloat16), ("dp", "ctx"), scatter_dimension=0, tiled=True
        ).astype(jnp.float32),
        lax.psum_scatter(
            down_compact.astype(jnp.bfloat16), ("dp", "ctx"), scatter_dimension=0, tiled=True
        ).astype(jnp.float32),
        lax.psum_scatter(
            up_compact.astype(jnp.bfloat16), ("dp", "ctx"), scatter_dimension=0, tiled=True
        ).astype(jnp.float32),
    )
    row_count = down_rows.shape[0]
    down_widths = [grad_piece.shape[2] for number, grad_piece, is_local in lower_factor_parts]
    up_widths = [grad_piece.shape[2] for number, grad_piece, is_local in upper_factor_parts]
    down_pieces = [
        down_rows[:, sum(down_widths[:position]) : sum(down_widths[: position + 1])]
        for position in range(12)
    ]
    up_pieces = [
        up_rows[:, sum(up_widths[:position]) : sum(up_widths[: position + 1])]
        for position in range(12)
    ]
    down_block = dense_table(
        lower_factor_parts, input_offsets, adapter_down_factor.shape[2], row_count, down_pieces
    ).reshape(-1)
    up_block = dense_table(
        upper_factor_parts, output_offsets, adapter_up_factor.shape[2], row_count, up_pieces
    ).reshape(-1)
    condition_gradient, adapter_down_gradient, adapter_up_gradient = (
        lax.psum_scatter(
            cond_rows.astype(jnp.bfloat16), "tensor", scatter_dimension=0, tiled=True
        ).astype(jnp.float32),
        lax.psum_scatter(
            down_block.astype(jnp.bfloat16), "tensor", scatter_dimension=0, tiled=True
        ).astype(jnp.float32),
        lax.psum_scatter(
            up_block.astype(jnp.bfloat16), "tensor", scatter_dimension=0, tiled=True
        ).astype(jnp.float32),
    )
    return (
        block_out.astype(jnp.bfloat16),
        hidden_grad,
        skip_grad,
        condition_gradient,
        adapter_down_gradient,
        adapter_up_gradient,
    )


BF = jnp.bfloat16
F32 = jnp.float32
MESH_ID = pl.DeviceIdType.MESH
RANK = 16
CHUNK = 64
VMEM_BYTES = 60 << 20


def dot_nn(left, right):
    return jnp.dot(left, right, preferred_element_type=F32)


def dot_nt(left, right):
    return lax.dot_general(left, right, (((1,), (1,)), ((), ())), preferred_element_type=F32)


def dot_tn(left, right):
    return lax.dot_general(left, right, (((0,), (0,)), ((), ())), preferred_element_type=F32)


def stats(values):
    centered = values - jnp.mean(values, axis=-1, keepdims=True)
    inverse = lax.rsqrt(jnp.mean(centered * centered, axis=-1, keepdims=True) + NORM_EPS)
    return centered * inverse, inverse


def greet_all(partners):
    barrier = pltpu.get_barrier_semaphore()
    for condition, device in partners:
        @pl.when(condition)
        def _(device=device):
            pl.semaphore_signal(barrier, inc=1, device_id=device, device_id_type=MESH_ID)


def await_all(partners):
    expected = sum(jnp.where(condition, 1, 0) for condition, _ in partners)
    pl.semaphore_wait(pltpu.get_barrier_semaphore(), expected)


def greet(partners):
    greet_all(partners)
    await_all(partners)


def line_partners(me, count):
    return [(me > 0, {"tensor": lax.max(me - 1, 0)}), (me < count - 1, {"tensor": lax.min(me + 1, count - 1)})]


def push(source, target, send_sem, recv_sem, device):
    return pltpu.make_async_remote_copy(
        src_ref=source,
        dst_ref=target,
        send_sem=send_sem,
        recv_sem=recv_sem,
        device_id=device,
        device_id_type=MESH_ID,
    )


class Line:
    def __init__(self, me, count, send_right, recv_left, send_left, recv_right):
        self.me, self.count = me, count
        self.sems = (send_right, recv_left, send_left, recv_right)
        self.left = {"tensor": lax.max(me - 1, 0)}
        self.right = {"tensor": lax.min(me + 1, count - 1)}
        self.has_left, self.has_right = me > 0, me < count - 1

    def to_right(self, source, target, slot):
        return push(source, target, self.sems[0].at[slot], self.sems[1].at[slot], self.right)

    def to_left(self, source, target, slot):
        return push(source, target, self.sems[2].at[slot], self.sems[3].at[slot], self.left)


def line_reduce_all(line, steps, compute, partial_ref, from_left, from_right, stage_right, stage_left, finish,
                    beside=None, after=None):
    me, count = line.me, line.count
    far = count - 1 - me

    def step(number, carry):
        @pl.when(number < steps)
        def _():
            compute(number)

        slot_r = number - me

        @pl.when((slot_r >= 0) & (slot_r < steps))
        def _():
            slot = lax.clamp(0, slot_r, steps - 1)

            @pl.when(line.has_left)
            def _():
                line.to_right(stage_right.at[slot], from_left.at[slot], slot).wait_recv()

            @pl.when(line.has_right)
            def _():
                @pl.when(line.has_left)
                def _():
                    total = partial_ref[slot].astype(F32) + from_left[slot].astype(F32)
                    stage_right[slot] = total.astype(BF)

                @pl.when(jnp.logical_not(line.has_left))
                def _():
                    stage_right[slot] = partial_ref[slot]

                line.to_right(stage_right.at[slot], from_left.at[slot], slot).start()

        slot_l = number - far

        @pl.when((slot_l >= 0) & (slot_l < steps))
        def _():
            slot = lax.clamp(0, slot_l, steps - 1)

            @pl.when(line.has_right)
            def _():
                line.to_left(stage_left.at[slot], from_right.at[slot], slot).wait_recv()

            @pl.when(line.has_left)
            def _():
                @pl.when(line.has_right)
                def _():
                    total = partial_ref[slot].astype(F32) + from_right[slot].astype(F32)
                    stage_left[slot] = total.astype(BF)

                @pl.when(jnp.logical_not(line.has_right))
                def _():
                    stage_left[slot] = partial_ref[slot]

                line.to_left(stage_left.at[slot], from_right.at[slot], slot).start()

        if beside is not None:
            beside(number)
        slot_f = number - lax.max(me, far)

        @pl.when((slot_f >= 0) & (slot_f < steps))
        def _():
            slot = lax.clamp(0, slot_f, steps - 1)

            @pl.when(jnp.logical_not(line.has_left))
            def _():
                finish(slot, partial_ref[slot].astype(F32) + from_right[slot].astype(F32))

            @pl.when(line.has_left)
            def _():
                @pl.when(line.has_right)
                def _():
                    finish(
                        slot,
                        partial_ref[slot].astype(F32)
                        + from_left[slot].astype(F32)
                        + from_right[slot].astype(F32),
                    )

                @pl.when(jnp.logical_not(line.has_right))
                def _():
                    finish(slot, partial_ref[slot].astype(F32) + from_left[slot].astype(F32))

            if after is not None:
                after(slot)

        return carry

    lax.fori_loop(0, steps + count - 1, step, 0)

    def drain(slot, carry):
        @pl.when(line.has_right)
        def _():
            line.to_right(stage_right.at[slot], from_left.at[slot], slot).wait_send()

        @pl.when(line.has_left)
        def _():
            line.to_left(stage_left.at[slot], from_right.at[slot], slot).wait_send()

        return carry

    lax.fori_loop(0, steps, drain, 0)


def scatter_order(me, count, place):
    near = lax.min(me, count - 1 - me)
    base = count - 1 - 2 * near
    index = place - base
    block = jnp.where(
        place < base,
        count - 1 - place,
        jnp.where(index % 2 == 0, 2 * near - index // 2, index // 2),
    )
    return jnp.where(2 * me > count - 1, count - 1 - block, block)


def line_scatter_step(line, number, partial_ref, from_left, from_right, stage_right, stage_left):
    me, count = line.me, line.count
    block_r = count - 1 - number + me

    @pl.when((number >= me) & line.has_right & (block_r > me))
    def _():
        block = lax.clamp(0, block_r, count - 1)

        @pl.when(line.has_left)
        def _():
            line.to_right(stage_right.at[block], from_left.at[block], block).wait_recv()
            total = partial_ref[block].astype(F32) + from_left[block].astype(F32)
            stage_right[block] = total.astype(BF)

        @pl.when(jnp.logical_not(line.has_left))
        def _():
            stage_right[block] = partial_ref[block]

        line.to_right(stage_right.at[block], from_left.at[block], block).start()

    block_l = number - (count - 1 - me)

    @pl.when((block_l >= 0) & line.has_left & (block_l < me))
    def _():
        block = lax.clamp(0, block_l, count - 1)

        @pl.when(line.has_right)
        def _():
            line.to_left(stage_left.at[block], from_right.at[block], block).wait_recv()
            total = partial_ref[block].astype(F32) + from_right[block].astype(F32)
            stage_left[block] = total.astype(BF)

        @pl.when(jnp.logical_not(line.has_right))
        def _():
            stage_left[block] = partial_ref[block]

        line.to_left(stage_left.at[block], from_right.at[block], block).start()


def line_scatter_finish(line, partial_ref, from_left, from_right, stage_right, stage_left, total_ref):
    me, count = line.me, line.count
    total_ref[...] = partial_ref[me].astype(F32)

    @pl.when(line.has_left)
    def _():
        line.to_right(stage_right.at[me], from_left.at[me], me).wait_recv()
        total_ref[...] += from_left[me].astype(F32)

    @pl.when(line.has_right)
    def _():
        line.to_left(stage_left.at[me], from_right.at[me], me).wait_recv()
        total_ref[...] += from_right[me].astype(F32)

    def drain(block, carry):
        @pl.when(block > me)
        def _():
            line.to_right(stage_right.at[block], from_left.at[block], block).wait_send()

        @pl.when(block < me)
        def _():
            line.to_left(stage_left.at[block], from_right.at[block], block).wait_send()

        return carry

    lax.fori_loop(0, count, drain, 0)


def line_gather_step(line, number, slots):
    me, count = line.me, line.count
    block_l = lax.clamp(0, me - number, count - 1)
    block_r = lax.clamp(0, me + number, count - 1)
    view = slots if callable(slots) else lambda block: slots.at[block]

    @pl.when(number <= me)
    def _():
        @pl.when(number > 0)
        def _():
            line.to_right(view(block_l), view(block_l), block_l).wait_recv()

        @pl.when(line.has_right)
        def _():
            line.to_right(view(block_l), view(block_l), block_l).start()

    @pl.when(me + number <= count - 1)
    def _():
        @pl.when(number > 0)
        def _():
            line.to_left(view(block_r), view(block_r), block_r).wait_recv()

        @pl.when(line.has_left)
        def _():
            line.to_left(view(block_r), view(block_r), block_r).start()


def line_gather_drain(line, slots):
    me, count = line.me, line.count
    view = slots if callable(slots) else lambda block: slots.at[block]

    def drain(block, carry):
        @pl.when((block <= me) & line.has_right)
        def _():
            line.to_right(view(block), view(block), block).wait_send()

        @pl.when((block >= me) & line.has_left)
        def _():
            line.to_left(view(block), view(block), block).wait_send()

        return carry

    lax.fori_loop(0, count, drain, 0)


def xor_place(place, number):
    if number == 0:
        return place
    if number == 1:
        return place + 1 - 2 * (place % 2)
    if number == 2:
        return place + 2 - 4 * (place // 2)
    return 3 - place


def call(kernel, inputs, outs, scratch, collective=None, cost=None):
    space = {True: pltpu.VMEM, False: pl.ANY, None: pltpu.SMEM}
    return pl.pallas_call(
        kernel,
        out_shape=[jax.ShapeDtypeStruct(shape, dtype) for shape, dtype, _ in outs],
        in_specs=[pl.BlockSpec(memory_space=space[where]) for _, where in inputs],
        out_specs=[pl.BlockSpec(memory_space=space[where]) for _, _, where in outs],
        scratch_shapes=scratch,
        cost_estimate=cost,
        compiler_params=pltpu.CompilerParams(
            collective_id=collective,
            has_side_effects=collective is not None,
            vmem_limit_bytes=VMEM_BYTES,
        ),
    )(*[array for array, _ in inputs])


def cost_of(flops, moved):
    return pl.CostEstimate(flops=int(flops), bytes_accessed=int(moved), transcendentals=0)


def vmem(*shape, dtype=BF):
    return pltpu.VMEM(shape, dtype)


def dma(*shape):
    return pltpu.SemaphoreType.DMA(shape)


def whole_wait(target, sem):
    pltpu.make_async_copy(target, target, sem).wait()


def rows_of(index, size):
    return pl.ds(pl.multiple_of(index * size, size), size)


IN_SIZES = [2 * MODEL_WIDTH] + [MODEL_WIDTH] * 6 + [TW, TW, MODEL_WIDTH, MODEL_WIDTH, FF]
OUT_SIZES = [MODEL_WIDTH] * 10 + [FF, MODEL_WIDTH]
IN_AT = [sum(IN_SIZES[:number]) for number in range(13)]
OUT_AT = [sum(OUT_SIZES[:number]) for number in range(13)]


def down_of(table, number):
    return table[:, IN_AT[number] : IN_AT[number + 1]]


def up_of(table, number):
    return table[:, OUT_AT[number] : OUT_AT[number + 1]]


def take_local(target, table, start, me, count):
    size = target.shape[-1]
    for place in range(count):
        @pl.when(me == place)
        def _(place=place):
            target[...] = table[:, start + place * size : start + (place + 1) * size]


def take_stack(target, table, start, count):
    size = target.shape[-1]
    for place in range(count):
        target[place] = table[:, start + place * size : start + (place + 1) * size]


def norm_backward(normal, inverse, grad):
    return inverse * (
        grad
        - jnp.mean(grad, axis=-1, keepdims=True)
        - normal * jnp.mean(grad * normal, axis=-1, keepdims=True)
    )


def middle(count, heads, summed, skip_out, query_weight, out_weight, up_weight, down_piece, skip_piece, text_kv, text,
           cotangent, gains, tables):
    share, width = summed.shape
    tokens = skip_out.shape[0]
    local = query_weight.shape[-1]
    units = up_weight.shape[1]
    words, text_width = text.shape
    rows, span = skip_piece.shape
    scale = HD ** (-0.5)
    part_rows = share // 2
    wide = count * part_rows

    def kernel(sum_ref, skip_hbm, q_hbm, o_hbm, u_hbm, d_own, piece, kv_hbm, text_hbm, cot_hbm, gain, dtab, utab,
               g_first, block_sum, ga_q, gb_q, ga_k, gb_k, ga_v, gb_v, ga_o, gb_o, g_ua, g_ub, g_da, g_db, skip_all,
               kv, wq, wo, wu, wd, cot, t_ref, first_ref, second_ref, x_ref, x_low, q_ref, inv_ref, log_ref, low_ref, acc, b_ref, ao,
               bk, bv, ub, da, slots, skip_half, active, grads, u_all, ud_all, gu_all, gd_all, partial_g, left_g, right_g,
               sr_g, sl_g, partial_b, left_b, right_b, sr_b, sl_b, lsem, wsend, wrecv, zsend, zrecv, *sems):
        me = lax.axis_index("tensor")
        core = lax.axis_index("ctx")
        dp = lax.axis_index("dp")
        always = core >= 0
        half = pl.ds(pl.multiple_of(core * (rows // 2), 16), rows // 2)
        down_rows = d_own.shape[0]
        down_half = pl.ds(pl.multiple_of(core * (down_rows // 2), 16), down_rows // 2)
        mine = pl.ds(pl.multiple_of(dp * down_rows, 16), down_rows)
        loads = [
            pltpu.make_async_copy(source, target, lsem.at[number])
            for number, (source, target) in enumerate(
                ((skip_hbm.at[rows_of(me, share), :], first_ref), (piece.at[half, :], skip_half.at[me]), (q_hbm, wq),
                 (o_hbm, wo), (d_own, wd.at[mine, :]), (cot_hbm.at[:, 0], cot.at[0]), (u_hbm.at[mine, :], wu.at[mine, :]), (text_hbm, t_ref),
                 (cot_hbm.at[:, 1], cot.at[1]))
            )
        ]
        z_peers = [{"tensor": xor_place(me, number)} for number in range(1, count)]
        others = [{"dp": xor_place(dp, 1)}, {"dp": xor_place(dp, 2)}, {"ctx": 1 - core}]
        everyone = [(always, device) for device in z_peers + others]
        greet_all(everyone)
        load_kv = pltpu.make_async_copy(kv_hbm, kv, lsem.at[12])
        for load in loads[:4]:
            load.start()
        load_kv.start()
        for load in loads[4:]:
            load.start()
        gather_lines = [Line(me, count, *sems[:4]), Line(me, count, *sems[4:8])]
        grad_lines = [Line(me, count, *sems[8:12]), Line(me, count, *sems[12:16])]
        block_line = Line(me, count, *sems[16:])

        def gather(which, number):
            line_gather_step(gather_lines[which], number, slots.at[which])

        def scatter(which, number):
            line_scatter_step(
                grad_lines[which], number, partial_g.at[which], left_g.at[which], right_g.at[which], sr_g.at[which],
                sl_g.at[which],
            )

        down = Shared(wd, down_rows, (wsend, wrecv, 0))
        up_w = Shared(wu, down_rows, (wsend, wrecv, 2))
        arrived_up = [
            pltpu.make_async_copy(Shared(u_hbm, down_rows, (wsend, wrecv, 2)).view(block, core), up_w.view(block, core),
                                  lsem.at[10 + number])
            for number, block in enumerate((up_w.first, up_w.second))
        ]
        for load in arrived_up:
            load.start()
        skip = Shared(skip_all, rows, (wsend, wrecv, 1), stacked=True)
        await_all(everyone)
        down.send_own(d_own.at[down_half, :])
        z_sends = [
            push(piece.at[half, :], skip_half.at[me], zsend.at[number], zrecv.at[number], device)
            for number, device in enumerate(z_peers)
        ]
        for send in z_sends:
            send.start()
        take_stack(b_ref, utab, OUT_AT[6], count)
        take_stack(ao, dtab, IN_AT[9], count)
        take_stack(bk, utab, OUT_AT[7], count)
        take_stack(bv, utab, OUT_AT[8], count)
        take_local(ub, utab, OUT_AT[10], me, count)
        take_local(da, dtab, IN_AT[11], me, count)

        for load in arrived_up:
            load.wait()
        up_w.forward()
        up_w.swap(0)
        up_w.swap(1)

        loads[0].wait()
        first = first_ref[...] + sum_ref[...]
        first_ref[...] = first
        second_ref[...] = first
        normal, _ = stats(first)
        x = (normal * gain[1:2, :]).astype(BF)
        x_ref[...] = x
        u = dot_nt(x, down_of(dtab, 6)).astype(BF)
        loads[2].wait()
        loads[3].wait()
        load_kv.wait()

        def cross(place, u_low):
            y = dot_nn(x_ref[...], wq[place]) + dot_nn(u, b_ref[place])
            outs, inverses, logs = [], [], []
            for head in range(heads):
                at = slice(head * HD, (head + 1) * HD)
                normal, inverse = stats(y[:, at])
                q = normal.astype(BF)
                q_ref[place, head] = q
                inverses.append(inverse)
                s = dot_nt(q, kv[0, place, :, at]) * scale
                top = jnp.max(s, axis=-1, keepdims=True)
                e = jnp.exp(s - top)
                total = jnp.sum(e, axis=-1, keepdims=True)
                p = (e * (1.0 / total)).astype(BF)
                outs.append(dot_nn(p, kv[1, place, :, at]))
                logs.append(top + jnp.log(total))
            inv_ref[place] = jnp.concatenate(inverses, axis=1)
            log_ref[place] = jnp.concatenate(logs, axis=1)
            low = jnp.concatenate(outs, axis=1).astype(BF)
            low_ref[place] = low
            second_ref[...] += dot_nt(low, wo[place])
            return u_low + dot_nt(low, ao[place])

        u_low = lax.fori_loop(0, count, cross, jnp.zeros((share, RANK), F32)).astype(BF)
        second = second_ref[...] + dot_nn(u_low, up_of(utab, 9))
        second_ref[...] = second
        normal, _ = stats(second)
        x_mlp = (normal * gain[2:3, :]).astype(BF)
        slots[0, me] = x_mlp[:part_rows]
        slots[1, me] = x_mlp[part_rows:]

        gather(0, 0)
        up_w.wait(2)
        up_w.swap(2)
        down.wait(0)
        down.forward()
        down.swap(0)
        down.wait(1)
        down.swap(1)
        gather(0, 1)
        gather(1, 0)
        loads[1].wait()
        for number in range(count - 1):
            arrived = skip_half.at[xor_place(me, number + 1)]
            push(arrived, arrived, zsend.at[number], zrecv.at[number], z_peers[number]).wait_recv()
        skip_place = pltpu.make_async_copy(skip_half, skip.view(dp, core), lsem.at[9])
        skip_place.start()
        skip.send_own(skip_half)
        down.wait(2)
        down.swap(2)
        for number in (4, 5, 6, 8):
            loads[number].wait()
        ua, db = down_of(dtab, 10), up_of(utab, 11)
        gather(0, 2)
        gather(1, 1)
        down.wait_swaps()
        up_w.wait_swaps()

        def part(number):
            return pl.ds(pl.multiple_of(number * wide, wide), wide)

        def first_grads(number, carry):
            ct = cot[number].reshape(wide, width)
            gd = dot_nt(ct, db).astype(BF)
            gd_all[part(number), :] = gd
            grads[part(number), :] = (dot_nn(ct, wd[...]) + dot_nn(gd, da[...])).astype(BF)
            return carry

        lax.fori_loop(0, 1, first_grads, 0)
        gather(0, 3)

        def forward_part(number, carry):
            here = part(number)

            @pl.when(number == 1)
            def _():
                first_grads(1, 0)
                gather(1, 3)
                scatter(0, 1)

            x = slots[number].reshape(wide, width)
            u = dot_nt(x, ua).astype(BF)
            u_all[here, :] = u
            up = dot_nn(x, wu[...]) + dot_nn(u, ub[...])
            square = up * up
            curve = jnp.tanh(0.7978845608028654 * (up + 0.044715 * square * up))
            flat = 0.5 * (1.0 + curve)
            active[here, :] = (up * flat).astype(BF)
            slope = flat + 0.5 * up * (1.0 - curve * curve) * (0.7978845608028654 * (1.0 + 0.134145 * square))
            g_up = (grads[here, :].astype(F32) * slope).astype(BF)
            grads[here, :] = g_up
            gu = dot_nt(g_up, ub[...]).astype(BF)
            gu_all[here, :] = gu
            g_x = (dot_nt(g_up, wu[...]) + dot_nn(gu, ua)).astype(BF)
            partial_g[number] = g_x.reshape(count, part_rows, width)

            @pl.when(number == 0)
            def _():
                scatter(0, 0)
                gather(1, 2)

            return carry

        lax.fori_loop(0, 2, forward_part, 0)
        scatter(0, 2)
        scatter(1, 0)
        skip.wait(0)
        skip.forward()
        skip.wait(1)

        def down_product(number, carry):
            here = part(number)
            act = active[here, :]
            ud = dot_nt(act, da[...]).astype(BF)
            ud_all[here, :] = ud
            y = dot_nt(act, wd[...]) + dot_nn(ud, db)
            piece_rows = rows_of(number, part_rows)
            for block in range(count):
                own = jnp.where(block == me, 1.0, 0.0)
                one = y[block * part_rows : (block + 1) * part_rows] + second_ref[piece_rows, :] * own
                partial_b[block, piece_rows, :] = one.astype(BF)

            @pl.when(number == 0)
            def _():
                scatter(1, 1)

            return carry

        lax.fori_loop(0, 2, down_product, 0)
        scatter(1, 2)
        skip_place.wait()
        skip.swap(0)
        skip.swap(1)
        skip.swap(3)
        line_scatter_step(block_line, 0, partial_b, left_b, right_b, sr_b, sl_b)
        g_ub[...] = dot_tn(u_all[...], grads[...])
        g_ua[...] = dot_tn(gu_all[...], slots[...].reshape(tokens, width))
        g_db[...] = dot_tn(ud_all[...], cot[...].reshape(tokens, width))
        g_da[...] = dot_tn(gd_all[...], active[...])
        loads[7].wait()
        uq = dot_nt(x_ref[...], down_of(dtab, 6)).astype(BF)
        words_in = t_ref[...]
        uk = dot_nt(words_in, down_of(dtab, 7)).astype(BF)
        uv = dot_nt(words_in, down_of(dtab, 8)).astype(BF)
        for which in range(2):
            line_gather_drain(gather_lines[which], slots.at[which])
            line_scatter_finish(
                grad_lines[which], partial_g.at[which], left_g.at[which], right_g.at[which], sr_g.at[which],
                sl_g.at[which], acc.at[which * part_rows : (which + 1) * part_rows, :],
            )
        skip.wait(2)
        skip.swap(2)

        normal, inverse = stats(second_ref[...])
        own_cot = jnp.concatenate([cot[0, me], cot[1, me]], axis=0).astype(F32)
        g_second = own_cot + norm_backward(normal, inverse, acc[...] * gain[2:3, :])
        second_ref[...] = g_second
        g_low = g_second.astype(BF)
        x_low[...] = g_low
        go = dot_nt(g_low, up_of(utab, 9)).astype(BF)
        gb_o[...] = dot_tn(u_low, g_low)
        acc[...] = jnp.zeros_like(acc)

        def cross_grads(place, carry):
            gq_sum, gk_sum, gv_sum = carry

            @pl.when((place > 0) & (place < count - 1))
            def _():
                line_scatter_step(block_line, place, partial_b, left_b, right_b, sr_b, sl_b)

            g_attn = (dot_nn(x_low[...], wo[place]) + dot_nn(go, ao[place])).astype(BF)
            ga_o[place] = dot_tn(go, low_ref[place])
            gq_parts, gk_parts, gv_parts = [], [], []
            for head in range(heads):
                at = slice(head * HD, (head + 1) * HD)
                gh = g_attn[:, at]
                q = q_ref[place, head]
                k = kv[0, place, :, at]
                v = kv[1, place, :, at]
                p = jnp.exp(dot_nt(q, k) * scale - log_ref[place, :, head : head + 1])
                dp_ = dot_nt(gh, v)
                inner = jnp.sum(p * dp_, axis=-1, keepdims=True)
                ds = (p * (dp_ - inner)).astype(BF)
                dq = dot_nn(ds, k) * scale
                dk = dot_tn(ds, q) * scale
                gq_parts.append(norm_backward(q.astype(F32), inv_ref[place, :, head : head + 1], dq))
                side = kv[0, place, :, local + 2 * head : local + 2 * head + 2].astype(F32)
                gk_parts.append(norm_backward(k.astype(F32), side[:, 0:1] + side[:, 1:2], dk))
                gv_parts.append(dot_tn(p.astype(BF), gh))
            gq = jnp.concatenate(gq_parts, axis=1).astype(BF)
            gk = jnp.concatenate(gk_parts, axis=1).astype(BF)
            gv = jnp.concatenate(gv_parts, axis=1).astype(BF)
            acc[...] += dot_nt(gq, wq[place])
            gb_q[place] = dot_tn(uq, gq)
            gb_k[place] = dot_tn(uk, gk)
            gb_v[place] = dot_tn(uv, gv)
            return (
                gq_sum + dot_nt(gq, b_ref[place]),
                gk_sum + dot_nt(gk, bk[place]),
                gv_sum + dot_nt(gv, bv[place]),
            )

        start = (jnp.zeros((share, RANK), F32), jnp.zeros((words, RANK), F32), jnp.zeros((words, RANK), F32))
        gq_sum, gk_sum, gv_sum = lax.fori_loop(0, count, cross_grads, start)
        gq_sum = gq_sum.astype(BF)
        ga_q[...] = dot_tn(gq_sum, x_ref[...])
        ga_k[...] = dot_tn(gk_sum.astype(BF), words_in)
        ga_v[...] = dot_tn(gv_sum.astype(BF), words_in)
        g_x = acc[...] + dot_nn(gq_sum, down_of(dtab, 6))
        normal, inverse = stats(first_ref[...])
        g_first[...] = (second_ref[...] + norm_backward(normal, inverse, g_x * gain[1:2, :])).astype(BF)
        line_scatter_finish(block_line, partial_b, left_b, right_b, sr_b, sl_b, acc)
        block_sum[...] = acc[...].astype(BF)
        skip.wait_swaps()
        skip.drain()
        down.drain()
        up_w.drain_rest()
        for send in z_sends:
            send.wait_send()

    buffers = [vmem(count, share, width) for _ in range(5)]
    return call(
        kernel,
        [(summed, True)]
        + [(array, False) for array in (skip_out, query_weight, out_weight, up_weight, down_piece, skip_piece)]
        + [(text_kv, False), (text, False), (cotangent, False)]
        + [(array, True) for array in (gains, *tables)],
        [
            ((share, width), BF, True),
            ((share, width), BF, True),
            ((RANK, width), F32, True),
            ((count, RANK, local), F32, True),
            ((RANK, text_width), F32, True),
            ((count, RANK, local), F32, True),
            ((RANK, text_width), F32, True),
            ((count, RANK, local), F32, True),
            ((count, RANK, local), F32, True),
            ((RANK, width), F32, True),
            ((RANK, width), F32, True),
            ((RANK, units), F32, True),
            ((RANK, units), F32, True),
            ((RANK, width), F32, True),
            ((count, 4 * rows, span), BF, False),
        ],
        [pltpu.VMEM(text_kv.shape, BF), vmem(count, width, local), vmem(count, width, local), vmem(width, units),
         vmem(width, units), vmem(2, count, part_rows, width), vmem(words, text_width), vmem(share, width, dtype=F32),
         vmem(share, width, dtype=F32), vmem(share, width), vmem(share, width), vmem(count, heads, share, HD), vmem(count, share, heads, dtype=F32),
         vmem(count, share, heads, dtype=F32), vmem(count, share, local), vmem(share, width, dtype=F32)]
        + [vmem(count, RANK, local) for _ in range(4)] + [vmem(RANK, units) for _ in range(2)]
        + [vmem(2, count, part_rows, width), vmem(count, rows // 2, span), vmem(tokens, units), vmem(tokens, units)]
        + [vmem(tokens, RANK) for _ in range(4)] + [vmem(2, count, part_rows, width) for _ in range(5)] + buffers
        + [dma(13), dma(3, 7), dma(3, 7), dma(count), dma(count)] + [dma(count) for _ in range(20)],
        collective=3,
        cost=cost_of(12 * tokens * width * units, 60e6),
    )


class Shared:
    def __init__(self, target, rows, sems, stacked=False, split=True, columns=False):
        self.target, self.rows, self.stacked, self.split, self.columns = target, rows, stacked, split, columns
        self.send_sem, self.recv_sem, self.index = sems
        dp, core = lax.axis_index("dp"), lax.axis_index("ctx")
        self.dp, self.core = dp, core
        self.first = jnp.where(core == 0, xor_place(dp, 1), xor_place(dp, 2))
        self.second = jnp.where(core == 0, xor_place(dp, 2), xor_place(dp, 1))
        self.third = xor_place(dp, 3)

    def view(self, block, which):
        if self.columns:
            return self.target.at[:, pl.ds(pl.multiple_of(block * self.rows, 128), self.rows)]
        size = self.rows // 2 if self.split else self.rows
        start = block * self.rows + (which * size if self.split else 0)
        rows = pl.ds(pl.multiple_of(start, 16), size)
        return self.target.at[:, rows, :] if self.stacked else self.target.at[rows, :]

    def copy(self, number, source, block, which, device):
        target = self.view(block, which)
        source = target if source is None else source
        return push(source, target, self.send_sem.at[self.index, number], self.recv_sem.at[self.index, number], device)

    def send_own(self, source=None):
        self.copy(0, source, self.dp, self.core, {"dp": self.first}).start()
        self.copy(1, source, self.dp, self.core, {"dp": self.second}).start()

    def blocks(self):
        return [self.first, self.second, self.third] + ([self.dp] if self.stacked else [])

    def wait(self, number):
        self.copy(number, None, self.blocks()[number], self.core, {"dp": self.first}).wait_recv()

    def forward(self):
        self.copy(2, None, self.first, self.core, {"dp": self.second}).start()

    def swap(self, number):
        self.copy(3 + number, None, self.blocks()[number], self.core, {"ctx": 1 - self.core}).start()

    def wait_swaps(self):
        other = [self.second, self.first, self.third, self.dp]
        for number in range(len(self.blocks())):
            self.copy(3 + number, None, other[number], 1 - self.core, {"ctx": 1 - self.core}).wait_recv()

    def drain_own(self):
        for number in range(2):
            self.copy(number, None, self.dp, self.core, {"dp": self.first}).wait_send()

    def drain_rest(self):
        for number in range(2, 6):
            self.copy(number, None, self.dp, self.core, {"dp": self.first}).wait_send()

    def drain(self):
        for number in range(3 + (len(self.blocks()) if self.split else 0)):
            self.copy(number, None, self.dp, self.core, {"dp": self.first}).wait_send()


def front(count, heads, condition, index, hidden, long_skip, text, weights, mod_weight, gain_halves, gain_rows, tables):
    tokens, width = hidden.shape
    span = weights["skip"].shape[1]
    words, text_width = text.shape
    local = weights["q"].shape[1]
    units = weights["up"].shape[1]
    share = tokens // count
    block = min(128, tokens)
    chunk = min(CHUNK, tokens)
    pace = max(1, 64 // chunk)
    steps = tokens // chunk
    each = block // chunk
    scale = HD ** (-0.5)
    rows = weights["q"].shape[0]
    text_rows = weights["ck"].shape[1]
    mod_rows = mod_weight.shape[0]

    def kernel(skip_own, q_own, k_own, v_own, o_own, ck_own, cv_own, cq_own, co_own, up_own,
               index_ref, cond, hid_hbm, lsk_hbm, t_hbm, wm_hbm, halves, gain, dtab, utab,
               skip_hbm, attn_hbm, q_out, keys, values, low_out, log_out, inv_q, inv_k, summed, act_all, text_kv,
               wq_hbm, wk_hbm, wv_hbm, wo_hbm, wcq, wco, wup,
               hid, lsk, t_ref, wm, load_sem, skip_out, attn_in, wq, wk, wv, wo, out_sem, shift_row, wskip, wtext, part_x, pgain, sa, tk, tv, qa, qb, kb, vb, oa, mod_in, mod_slice, mod_out, partial_a, left_a, right_a, sr_a, sl_a,
               partial_b, left_b, right_b, sr_b, sl_b, wsend, wrecv, local_sem, msend, mrecv, tsend, trecv,
               xsend, xrecv, *sems):
        me = lax.axis_index("tensor")
        core = lax.axis_index("ctx")
        dp = lax.axis_index("dp")
        always = core >= 0
        peer = {"ctx": 1 - core}
        dp_peers = [{"dp": xor_place(dp, number)} for number in (1, 2, 3)]
        z_peers = [{"tensor": xor_place(me, number)} for number in range(1, count)]
        reduce_line = Line(me, count, *sems[:4])
        scatter_line = Line(me, count, *sems[4:8])
        text_line = Line(me, count, *sems[8:12])
        cross_lines = [Line(me, count, *sems[12:16]), Line(me, count, *sems[16:])]

        def sems_of(number):
            return (wsend, wrecv, number)

        skip = Shared(wskip, rows, sems_of(0))
        shared = {
            name: Shared(target, rows, sems_of(number))
            for name, target, number in (("q", wq, 1), ("k", wk, 2), ("v", wv, 3), ("o", wo, 4))
        }
        words_w = Shared(wtext, text_rows, sems_of(5), split=False, columns=True)
        cross = [Shared(wcq, rows, sems_of(6), stacked=True), Shared(wco, rows, sems_of(7), stacked=True)]
        wide = [Shared(wup, rows, sems_of(8))]
        owns = {"q": q_own, "k": k_own, "v": v_own, "o": o_own}
        half = pl.ds(pl.multiple_of(core * (rows // 2), 16), rows // 2)
        mine = pl.ds(pl.multiple_of(dp * rows, 16), rows)
        my_half = pl.ds(pl.multiple_of(dp * rows + core * (rows // 2), 16), rows // 2)

        everyone = [(always, device) for device in dp_peers + z_peers + [peer]]
        greet_all(everyone)
        loads = [
            pltpu.make_async_copy(source, target, load_sem.at[number])
            for number, (source, target) in enumerate(((hid_hbm, hid), (lsk_hbm, lsk), (t_hbm, t_ref), (wm_hbm, wm)))
        ]

        for place in range(count):
            @pl.when(me == place)
            def _(place=place):
                side = place * span // width
                start = place * span % width
                pgain[...] = halves[side : side + 1, start : start + span]

        places = [
            pltpu.make_async_copy(source, target.at[mine, :], local_sem.at[number])
            for number, (source, target) in enumerate(
                ((skip_own, wskip), (q_own, wq), (k_own, wk), (v_own, wv), (o_own, wo), (up_own, wup))
            )
        ]
        for place in places:
            place.start()
        crossing = [
            pltpu.make_async_copy(source.at[half, :], target.at[me, my_half, :], local_sem.at[7 + number])
            for number, (source, target) in enumerate(((cq_own, wcq), (co_own, wco)))
        ]
        text_mine = pl.ds(pl.multiple_of(dp * text_rows, 128), text_rows)

        def text_place(source):
            return pltpu.make_async_copy(source, wtext.at[:, text_mine], local_sem.at[9])

        @pl.when(core == 0)
        def _():
            text_place(ck_own).start()

        @pl.when(core == 1)
        def _():
            text_place(cv_own).start()

        for place in crossing:
            place.start()
        value = cond[...].astype(F32)
        act_low = (value / (1.0 + jnp.exp(-value))).astype(BF)
        tag = jnp.full((1, 128), index_ref[0], jnp.int32).astype(F32)
        act_all[dp] = jnp.concatenate([act_low.astype(F32), tag], axis=1)
        for load in loads:
            load.start()
        await_all(everyone)
        skip.send_own(skip_own.at[half, :])

        def cross_view(which):
            target = (wcq, wco)[which]
            return lambda block: target.at[block, my_half, :]

        def cross_step(number):
            for which, cross_line in enumerate(cross_lines):
                line_gather_step(cross_line, number, cross_view(which))

        for place in crossing:
            place.wait()
        cross_step(0)
        spread = [
            push(act_all.at[dp], act_all.at[dp], msend.at[0, number], mrecv.at[0, number], device)
            for number, device in enumerate(dp_peers)
        ]
        for copy in spread:
            copy.start()
        take_local(sa, dtab, 0, me, count)
        take_local(tk, utab, OUT_AT[7], me, count)
        take_local(tv, utab, OUT_AT[8], me, count)
        for number, target in enumerate((qb, kb, vb)):
            qa[number * RANK : (number + 1) * RANK, :] = down_of(dtab, 2 + number)
            take_local(target, utab, OUT_AT[2 + number], me, count)
        take_local(oa, dtab, IN_AT[5], me, count)
        skip.wait(0)
        skip.forward()
        for name in ("q", "k", "v", "o"):
            shared[name].send_own(owns[name].at[half, :])

        @pl.when(core == 0)
        def _():
            words_w.send_own(ck_own)

        @pl.when(core == 1)
        def _():
            words_w.send_own(cv_own)

        skip.swap(0)

        skip.wait(1)
        skip.swap(1)
        cross_step(1)

        for number in (1, 2, 3):
            source = act_all.at[xor_place(dp, number)]
            push(source, source, msend.at[0, number - 1], mrecv.at[0, number - 1], dp_peers[number - 1]).wait_recv()
        for owner in range(4):
            @pl.when(dp == owner)
            def _(owner=owner):
                span_of = slice(owner * mod_rows, (owner + 1) * mod_rows)
                for sequence in range(4):
                    mod_slice[sequence : sequence + 1, :] = act_all[sequence, :, span_of]

        skip.wait(2)
        skip.swap(2)
        loads[3].wait()
        products = dot_nn(mod_slice[...].astype(BF), wm[...])
        for sequence in range(4):
            mod_out[sequence] = products[sequence : sequence + 1]
        backs = [
            push(mod_out.at[xor_place(dp, number)], mod_in.at[dp], msend.at[1, number - 1], mrecv.at[1, number - 1],
                 dp_peers[number - 1])
            for number in (1, 2, 3)
        ]
        for copy in backs:
            copy.start()
        mod_in[dp] = mod_out[dp]
        places[0].wait()
        skip.wait_swaps()
        cross_step(2)
        for load in loads[:3]:
            load.wait()

        def compute(number):
            @pl.when(number % each == 0)
            def _():
                here = rows_of(number // each, block)
                left = hid[here, :].astype(F32)
                right = lsk[here, :].astype(F32)
                mean = (jnp.sum(left, axis=-1, keepdims=True) + jnp.sum(right, axis=-1, keepdims=True)) / (2 * width)
                spread = jnp.sum((left - mean) ** 2, axis=-1, keepdims=True)
                spread += jnp.sum((right - mean) ** 2, axis=-1, keepdims=True)
                inverse = lax.rsqrt(spread / (2 * width) + NORM_EPS)
                for place in range(count):
                    @pl.when(me == place)
                    def _(place=place):
                        source = hid if place * span < width else lsk
                        start = place * span % width
                        part_x[...] = source[here, start : start + span].astype(F32)
                x = ((part_x[...] - mean) * inverse * pgain[...]).astype(BF)
                u = dot_nt(x, sa[...]).astype(BF)
                y = (dot_nt(x, wskip[...]) + dot_nn(u, up_of(utab, 0))).astype(BF)
                for piece in range(each):
                    partial_a[number + piece] = y[piece * chunk : (piece + 1) * chunk]

        def text_product():
            @pl.when(core == 0)
            def _():
                text_place(ck_own).wait()

            @pl.when(core == 1)
            def _():
                text_place(cv_own).wait()

            x = t_ref[...]
            y = dot_nt(x, wtext[...])

            @pl.when(core == 0)
            def _():
                z = y + dot_nn(dot_nt(x, down_of(dtab, 7)).astype(BF), tk[...])
                parts, sides = [], []
                for head in range(heads):
                    normal, inverse = stats(z[:, head * HD : (head + 1) * HD])
                    upper = inverse.astype(BF)
                    parts.append(normal.astype(BF))
                    sides += [upper, (inverse - upper.astype(F32)).astype(BF)]
                text_kv[0, me, :, :local] = jnp.concatenate(parts, axis=1)
                text_kv[0, me, :, local : local + 2 * heads] = jnp.concatenate(sides, axis=1)

            @pl.when(core == 1)
            def _():
                z = y + dot_nn(dot_nt(x, down_of(dtab, 8)).astype(BF), tv[...])
                text_kv[1, me, :, :local] = z.astype(BF)

        text_slots = text_kv.at[core]

        def finish(slot, total):
            here = rows_of(slot, chunk)
            skip_out[here, :] = total
            normal, _ = stats(total)
            attn_in[here, :] = (normal * gain[0:1, :] + shift_row[...]).astype(BF)

        def project(number, carry):
            here = rows_of(number, block)
            x = attn_in[here, :]
            u = dot_nt(x, qa[...]).astype(BF)
            yq = dot_nn(x, wq[...]) + dot_nn(u[:, :RANK], qb[...])
            yk = dot_nn(x, wk[...]) + dot_nn(u[:, RANK : 2 * RANK], kb[...])
            yv = (dot_nn(x, wv[...]) + dot_nn(u[:, 2 * RANK :], vb[...])).astype(BF)
            parts_q, parts_k = [], []
            for head in range(heads):
                span_of = slice(head * HD, (head + 1) * HD)
                normal, inverse = stats(yq[:, span_of])
                q_out[head, here, :] = normal.astype(BF)
                parts_q.append(inverse)
                normal, inverse = stats(yk[:, span_of])
                keys[core, head, here, :] = normal.astype(BF)
                parts_k.append(inverse)
                values[core, head, here, :] = yv[:, span_of]
            inv_q[here, :] = jnp.concatenate(parts_q, axis=1)
            inv_k[here, :] = jnp.concatenate(parts_k, axis=1)
            return carry

        def beside(number):
            @pl.when(number == 1 * pace)
            def _():
                for other in (1, 2, 3):
                    target = mod_in.at[xor_place(dp, other)]
                    push(target, target, msend.at[1, other - 1], mrecv.at[1, other - 1], dp_peers[other - 1]).wait_recv()
                mod_u = dot_nt(act_low, down_of(dtab, 1)).astype(BF)
                shift_row[...] = mod_in[0] + mod_in[1] + mod_in[2] + mod_in[3] + dot_nn(mod_u, up_of(utab, 1))

            @pl.when(number == 2 * pace)
            def _():
                for weight in (*shared.values(), words_w):
                    weight.wait(0)
                    weight.forward()
                for weight in (*shared.values(), words_w):
                    weight.wait(1)
                for weight in shared.values():
                    weight.swap(0)
                    weight.swap(1)

            @pl.when(number == 4 * pace)
            def _():
                cross_step(3)
                for weight in cross:
                    weight.send_own()

            @pl.when(number == 5 * pace)
            def _():
                for weight in (*shared.values(), words_w):
                    weight.wait(2)
                for weight in shared.values():
                    weight.swap(2)

            @pl.when(number == 7 * pace)
            def _():
                for weight in wide:
                    weight.send_own(up_own.at[half, :])
                for place in places[1:5]:
                    place.wait()
                for weight in shared.values():
                    weight.wait_swaps()
                project(0, 0)

            @pl.when(number == 8 * pace)
            def _():
                project(1, 0)

            @pl.when(number == steps + count - 3)
            def _():
                text_product()
                line_gather_step(text_line, 0, text_slots)

        line_reduce_all(reduce_line, steps, compute, partial_a, left_a, right_a, sr_a, sl_a, finish, beside)

        lax.fori_loop(2, tokens // block, project, 0)
        stores = [
            pltpu.make_async_copy(source, target, out_sem.at[number])
            for number, (source, target) in enumerate(
                ((skip_out, skip_hbm), (attn_in, attn_hbm), (wq, wq_hbm), (wk, wk_hbm), (wv, wv_hbm), (wo, wo_hbm))
            )
        ]
        for store in stores:
            store.start()

        swaps = [
            push(ref.at[core], ref.at[core], xsend.at[number], xrecv.at[number], peer)
            for number, ref in enumerate((keys, values))
        ]
        for swap in swaps:
            swap.start()
        line_gather_step(text_line, 1, text_slots)
        for weight in cross:
            weight.wait(0)
            weight.forward()
            weight.swap(0)
            weight.swap(3)
        for number, ref in enumerate((keys, values)):
            push(ref.at[1 - core], ref.at[1 - core], xsend.at[number], xrecv.at[number], peer).wait_recv()

        def attend(place, carry):
            dest = scatter_order(me, count, place)
            here = rows_of(dest, share)
            outs, logs = [], []
            for head in range(heads):
                q = q_out[head, here, :]
                s0 = dot_nt(q, keys[0, head]) * scale
                s1 = dot_nt(q, keys[1, head]) * scale
                top = jnp.maximum(jnp.max(s0, axis=-1, keepdims=True), jnp.max(s1, axis=-1, keepdims=True))
                e0 = jnp.exp(s0 - top)
                e1 = jnp.exp(s1 - top)
                total = jnp.sum(e0, axis=-1, keepdims=True) + jnp.sum(e1, axis=-1, keepdims=True)
                share_of = 1.0 / total
                p0 = (e0 * share_of).astype(BF)
                p1 = (e1 * share_of).astype(BF)
                outs.append(dot_nn(p0, values[0, head]) + dot_nn(p1, values[1, head]))
                logs.append(top + jnp.log(total))
            low = jnp.concatenate(outs, axis=1).astype(BF)
            low_out[here, :] = low
            log_out[here, :] = jnp.concatenate(logs, axis=1)
            u = dot_nt(low, oa[...]).astype(BF)
            partial_b[dest] = (dot_nt(low, wo[...]) + dot_nn(u, up_of(utab, 5))).astype(BF)

            @pl.when(place < count - 1)
            def _():
                line_scatter_step(scatter_line, place, partial_b, left_b, right_b, sr_b, sl_b)

            @pl.when(place == 0)
            def _():
                line_gather_step(text_line, 2, text_slots)

            @pl.when(place == 1)
            def _():
                for weight in cross:
                    weight.wait(1)
                    weight.swap(1)
                line_gather_step(text_line, 3, text_slots)
                push(text_slots, text_slots, tsend, trecv, peer).start()

            @pl.when(place == 2)
            def _():
                for weight in cross:
                    weight.wait(2)
                    weight.swap(2)

            return carry

        lax.fori_loop(0, count, attend, 0)
        line_scatter_finish(scatter_line, partial_b, left_b, right_b, sr_b, sl_b, summed)
        for weight in wide:
            weight.wait(0)
            weight.wait(1)
        others = text_kv.at[1 - core]
        push(others, others, tsend, trecv, peer).wait_recv()
        for weight in cross:
            weight.wait_swaps()
        places[5].wait()
        for store in stores:
            store.wait()
        for weight in (skip, *shared.values(), words_w, *cross):
            weight.drain()
        for weight in wide:
            weight.drain_own()
        for which, cross_line in enumerate(cross_lines):
            line_gather_drain(cross_line, cross_view(which))
        for copy in spread + backs:
            copy.wait_send()
        line_gather_drain(text_line, text_slots)
        push(text_slots, text_slots, tsend, trecv, peer).wait_send()
        for swap in swaps:
            swap.wait_send()

    names = ("skip", "q", "k", "v", "o", "ck", "cv", "cq", "co", "up")
    return call(
        kernel,
        [(weights[name], name in ("cq", "co", "up")) for name in names] + [(index, None)]
        + [(condition, True)] + [(array, False) for array in (hidden, long_skip, text, mod_weight)]
        + [(array, True) for array in (gain_halves, gain_rows, *tables)],
        [
            ((tokens, width), F32, False),
            ((tokens, width), BF, False),
            ((heads, tokens, HD), BF, True),
            ((2, heads, tokens, HD), BF, True),
            ((2, heads, tokens, HD), BF, True),
            ((tokens, local), BF, True),
            ((tokens, heads), F32, True),
            ((tokens, heads), F32, True),
            ((tokens, heads), F32, True),
            ((share, width), F32, True),
            ((4, 1, width + 128), F32, True),
            ((2, count, words, local + 32), BF, True),
        ]
        + [((width, local), BF, False) for _ in range(4)]
        + [((count, width, local), BF, False) for _ in range(2)]
        + [((width, units), BF, False)],
        [vmem(tokens, width), vmem(tokens, width), vmem(words, text_width), vmem(mod_rows, width), dma(4),
         vmem(tokens, width, dtype=F32), vmem(tokens, width)] + [vmem(width, local) for _ in range(4)]
        + [dma(6), vmem(1, width, dtype=F32), vmem(width, span), vmem(local, text_width), vmem(block, span, dtype=F32), vmem(1, span, dtype=F32),
         vmem(RANK, span), vmem(RANK, local), vmem(RANK, local), vmem(3 * RANK, width)]
        + [vmem(RANK, local) for _ in range(4)]
        + [vmem(4, 1, width, dtype=F32), vmem(4, mod_rows, dtype=F32),
         vmem(4, 1, width, dtype=F32)]
        + [vmem(steps, chunk, width) for _ in range(5)] + [vmem(count, share, width) for _ in range(5)]
        + [dma(10, 7), dma(10, 7), dma(10), dma(2, 3), dma(2, 3), dma(), dma(),
           dma(2), dma(2)]
        + [dma(steps) for _ in range(4)] + [dma(count) for _ in range(16)],
        collective=1,
        cost=cost_of(8 * tokens * width * local, 60e6),
    )


def attention_backward(count, heads, g_first, query, keys, values, low, logs, inv_q, inv_k, out_weight, tables):
    share, width = g_first.shape
    tokens = query.shape[1]
    local = low.shape[1]
    scale = HD ** (-0.5)

    def kernel(g_ref, *refs):
        sources, refs = refs[:10], refs[10:]
        (gq_low, gk_low, gv_low, gall, ga_o, gb_o, q_ref, k_ref, v_ref, low_ref, log_ref, iq_ref, ik_ref, wo, dtab, utab,
         gk_acc, gv_acc, swap_out, swap_in, ao, lsem, xsend, xrecv, *sems) = refs
        loads = [
            pltpu.make_async_copy(source, target, lsem.at[number])
            for number, (source, target) in enumerate(
                zip(sources, (q_ref, k_ref, v_ref, low_ref, log_ref, iq_ref, ik_ref, wo, dtab, utab))
            )
        ]
        for load in loads:
            load.start()
        me = lax.axis_index("tensor")
        core = lax.axis_index("ctx")
        peer = {"ctx": 1 - core}
        grad_line = Line(me, count, *sems)
        gall[me] = g_ref[...]
        greet(line_partners(me, count) + [(core >= 0, peer)])
        line_gather_step(grad_line, 0, gall)
        for ref in (ga_o, gb_o, gk_acc, gv_acc):
            ref[...] = jnp.zeros_like(ref)
        for load in loads:
            load.wait()
        take_local(ao, dtab, IN_AT[5], me, count)

        def attend(place):
            rows = rows_of(place, share)
            g = gall[place]
            go = dot_nt(g, up_of(utab, 5)).astype(BF)
            g_attn = (dot_nn(g, wo[...]) + dot_nn(go, ao[...])).astype(BF)
            low = low_ref[rows, :]
            uo = dot_nt(low, ao[...]).astype(BF)
            gb_o[...] += dot_tn(uo, g)
            ga_o[...] += dot_tn(go, low)
            parts = []
            for head in range(heads):
                gh = g_attn[:, head * HD : (head + 1) * HD]
                q = q_ref[head, rows, :]
                probs, grads = [], []
                inner = 0.0
                for half in range(2):
                    p = jnp.exp(dot_nt(q, k_ref[half, head]) * scale - log_ref[rows, head : head + 1])
                    dp = dot_nt(gh, v_ref[half, head])
                    inner = inner + jnp.sum(p * dp, axis=-1, keepdims=True)
                    probs.append(p)
                    grads.append(dp)
                dq = 0.0
                for half in range(2):
                    ds = (probs[half] * (grads[half] - inner)).astype(BF)
                    dq = dq + dot_nn(ds, k_ref[half, head])
                    gk_acc[half, head] += dot_tn(ds, q)
                    gv_acc[half, head] += dot_tn(probs[half].astype(BF), gh)
                parts.append(norm_backward(q.astype(F32), iq_ref[rows, head : head + 1], dq * scale))
            gq_low[rows, :] = jnp.concatenate(parts, axis=1).astype(BF)

        def gather(number, carry):
            @pl.when(number > 0)
            def _():
                line_gather_step(grad_line, number, gall)

            def side(which, inner):
                place = me + (2 * which - 1) * number

                @pl.when((place >= 0) & (place < count) & ((number > 0) | (which == 0)))
                def _():
                    attend(lax.clamp(0, place, count - 1))

                return inner

            return lax.fori_loop(0, 2, side, carry)

        lax.fori_loop(0, count, gather, 0)
        swaps = []
        for head in range(heads):
            swap_out[head, 0] = (gk_acc[1 - core, head] * scale).astype(BF)
            swap_out[head, 1] = gv_acc[1 - core, head].astype(BF)
            swaps.append(push(swap_out.at[head], swap_in.at[head], xsend.at[head], xrecv.at[head], peer))
            swaps[-1].start()
        line_gather_drain(grad_line, gall)
        for head in range(heads):
            at = slice(head * HD, (head + 1) * HD)
            swaps[head].wait_recv()
            dk = gk_acc[core, head] * scale + swap_in[head, 0].astype(F32)
            normal = k_ref[core, head].astype(F32)
            gk_low[:, at] = norm_backward(normal, ik_ref[:, head : head + 1], dk).astype(BF)
            gv_low[:, at] = (gv_acc[core, head] + swap_in[head, 1].astype(F32)).astype(BF)
        for swap in swaps:
            swap.wait_send()

    return call(
        kernel,
        [(g_first, True)]
        + [(array, False) for array in (query, keys, values, low, logs, inv_q, inv_k, out_weight, *tables)],
        [
            ((tokens, local), BF, True),
            ((tokens, local), BF, True),
            ((tokens, local), BF, True),
            ((count, share, width), BF, True),
            ((RANK, local), F32, True),
            ((RANK, width), F32, True),
        ],
        [pltpu.VMEM(array.shape, array.dtype)
         for array in (query, keys, values, low, logs, inv_q, inv_k, out_weight, *tables)]
        + [vmem(2, heads, tokens, HD, dtype=F32), vmem(2, heads, tokens, HD, dtype=F32), vmem(heads, 2, tokens, HD),
           vmem(heads, 2, tokens, HD), vmem(RANK, local), dma(10), dma(heads), dma(heads)]
        + [dma(count) for _ in range(4)],
        collective=4,
        cost=cost_of(16 * tokens * width * local, 60e6),
    )


EARLY_A, EARLY_B = IN_AT[2], OUT_AT[2]
EARLY = IN_AT[12] - EARLY_A + OUT_AT[12] - EARLY_B
LATE = EARLY_A + EARLY_B


def back_end(count, grads, projections, attn_in, g_first, skip_out, hidden, long_skip, weight, mod_weight, block_sum,
             gain_halves, gain_rows, tables, condition, act_all, wide_grads, local_down, local_up, stacked):
    tokens, width = hidden.shape
    local = grads[0].shape[1]
    span = weight.shape[-1]
    block = tokens // count
    chunk = min(CHUNK, block)
    pace = max(1, 64 // chunk)
    each = block // chunk
    steps = tokens // chunk
    own_rows = RANK // count
    half_e = -(-EARLY // 256) * 128
    half_l = -(-LATE // 256) * 128
    base = IN_AT[12] - EARLY_A
    mod_rows = mod_weight.shape[0]

    def early(column):
        return column - EARLY_A if column < IN_AT[12] else column - EARLY_A - EARLY_B

    wide_at, wide = [early(column) for column in wide_grads], list(wide_grads.values())
    local_at = [early(column) for column in local_down] + [early(IN_AT[12] + column) for column in local_up]
    own_grads = list(local_down.values()) + list(local_up.values())
    stacked_at, stack = [early(column) for column in stacked], list(stacked.values())

    def kernel(gq, gk, gv, wq, wk, wv, x_hbm, gf_hbm, skip_hbm, hid_hbm, lsk_hbm, hbm_w, wm_hbm, b_in, gains, gain, dtab,
               utab, cond, act_ref, *refs):
        wide_refs, refs = refs[: len(wide)], refs[len(wide) :]
        own_refs, refs = refs[: len(own_grads)], refs[len(own_grads) :]
        stack_refs, refs = refs[: len(stack)], refs[len(stack) :]
        (out_h, out_l, out_a, out_b, out_c, ball, w, x_ref, gf_ref, skip_ref, hid, lsk, wm, buf_h, buf_l, low, g_ref, qkv_a, bq, bk, bv, partial_g, left_g, right_g,
         sr_g, sl_g, table, late, swap_out, swap_in, partial_e, left_e, right_e, sr_e, sl_e, summed, late_out, late_in,
         partial_l, slots_l, slots, late_slots, other_out, other_in, later_out, later_in, shifts, shift_in, act_out, act_in, g_act, g_sum,
         wsem, osem, ssem, rsem, dsend, drecv, msend, mrecv, zsend, zrecv, *sems) = refs
        me = lax.axis_index("tensor")
        core = lax.axis_index("ctx")
        dp = lax.axis_index("dp")
        peer = {"ctx": 1 - core}
        grad_line = Line(me, count, *sems[:4])
        early_line = Line(me, count, *sems[4:8])
        block_line = Line(me, count, *sems[8:])
        peers = [{"dp": xor_place(dp, number)} for number in (1, 2, 3)]
        z_peers = [{"tensor": xor_place(me, number)} for number in range(1, count)]
        loads = [
            pltpu.make_async_copy(source, target, wsem.at[number])
            for number, (source, target) in enumerate(
                ((x_hbm, x_ref), (gf_hbm, gf_ref), (skip_hbm, skip_ref), (hid_hbm, hid), (lsk_hbm, lsk), (hbm_w, w),
                 (wm_hbm, wm))
            )
        ]
        for load in loads:
            load.start()
        ball[me] = b_in[...]
        everyone = [(core >= 0, device) for device in z_peers + peers + [peer]]
        greet_all(everyone)
        for number, target in enumerate((bq, bk, bv)):
            qkv_a[number * RANK : (number + 1) * RANK, :] = down_of(dtab, 2 + number)
            take_local(target, utab, OUT_AT[2 + number], me, count)
        g_sum[...] = jnp.zeros_like(g_sum)
        act_low = act_ref[dp, :, :width].astype(BF)

        def compute(number):
            @pl.when((number % each == 0) & (number > 0))
            def _():
                product(number)

        def product(number):
            rows = rows_of(number // each, block)
            gu = jnp.concatenate(
                [dot_nt(gq[rows, :], bq[...]), dot_nt(gk[rows, :], bk[...]), dot_nt(gv[rows, :], bv[...])], axis=1
            ).astype(BF)
            y = dot_nt(gq[rows, :], wq[...]) + dot_nt(gk[rows, :], wk[...]) + dot_nt(gv[rows, :], wv[...])
            y = (y + dot_nn(gu, qkv_a[...])).astype(BF)
            for piece in range(each):
                partial_g[number + piece] = y[piece * chunk : (piece + 1) * chunk]

        def finish(slot, total):
            g_ref[rows_of(slot, chunk), :] = total

        def skip_block(number):
            rows = rows_of(number, block)
            ga_in = g_ref[rows, :]
            g_sum[...] += jnp.sum(ga_in, axis=0, keepdims=True)
            normal, inverse = stats(skip_ref[rows, :])
            g_low = (
                gf_ref[number].astype(F32) + norm_backward(normal, inverse, ga_in * gain[0:1, :])
            ).astype(BF)
            left = hid[rows, :].astype(F32)
            right = lsk[rows, :].astype(F32)
            mean = (jnp.sum(left, axis=-1, keepdims=True) + jnp.sum(right, axis=-1, keepdims=True)) / (2 * width)
            left = left - mean
            right = right - mean
            spread = jnp.sum(left * left, axis=-1, keepdims=True) + jnp.sum(right * right, axis=-1, keepdims=True)
            inverse = lax.rsqrt(spread / (2 * width) + NORM_EPS)
            left = left * inverse
            right = right * inverse
            gu = dot_nt(g_low, up_of(utab, 0)).astype(BF)
            a_left, a_right = dtab[:, :width], dtab[:, width : 2 * width]

            @pl.when(number == me)
            def _():
                low_l = (left * gains[0:1, :]).astype(BF)
                low_r = (right * gains[1:2, :]).astype(BF)
                u = (dot_nt(low_l, a_left) + dot_nt(low_r, a_right)).astype(BF)
                late[:, :width] = dot_tn(gu, low_l)
                late[:, width : 2 * width] = dot_tn(gu, low_r)
                late[:, EARLY_A : EARLY_A + width] = dot_tn(u, g_low)

            for place in range(count):
                low[:, place * span : (place + 1) * span] = dot_nn(g_low, w[place])
            gl = (low[:, :width] + dot_nn(gu, a_left)) * gains[0:1, :]
            gr = (low[:, width:] + dot_nn(gu, a_right)) * gains[1:2, :]
            mean = (jnp.sum(gl, axis=-1, keepdims=True) + jnp.sum(gr, axis=-1, keepdims=True)) / (2 * width)
            inner = (
                jnp.sum(gl * left, axis=-1, keepdims=True) + jnp.sum(gr * right, axis=-1, keepdims=True)
            ) / (2 * width)
            buf_h[number] = inverse * (gl - mean - left * inner)
            buf_l[number] = inverse * (gr - mean - right * inner)
            pltpu.make_async_copy(buf_h.at[number], out_h.at[rows, :], osem.at[0, number]).start()
            pltpu.make_async_copy(buf_l.at[number], out_l.at[rows, :], osem.at[1, number]).start()

        swap = push(swap_out, swap_in, ssem.at[0], rsem.at[0], peer)
        sends = [
            push(slots.at[dp], slots.at[dp], dsend.at[0, number], drecv.at[0, number], device)
            for number, device in enumerate(peers)
        ]

        def early_step(number):
            line_scatter_step(early_line, number, partial_e, left_e, right_e, sr_e, sl_e)

        def beside(number):
            @pl.when(number == pace)
            def _():
                for load in loads:
                    load.wait()
                x = x_ref[...]
                u = dot_nt(x, qkv_a[...]).astype(BF)
                table[...] = jnp.zeros_like(table)
                late[...] = jnp.zeros_like(late)
                for start, ref in zip(wide_at, wide_refs):
                    table[:, start : start + ref.shape[1]] = ref[...]
                for start, ref in zip(stacked_at, stack_refs):
                    size = ref.shape[2]
                    for place in range(count):
                        table[:, start + place * size : start + (place + 1) * size] = ref[place]
                qkv_b = []
                for which, (grad, factor) in enumerate(((gq, bq), (gk, bk), (gv, bv))):
                    gu = dot_nt(grad[...], factor[...]).astype(BF)
                    table[:, which * width : (which + 1) * width] = dot_tn(gu, x)
                    qkv_b.append(dot_tn(u[:, which * RANK : (which + 1) * RANK], grad[...]))
                for place in range(count):
                    @pl.when(me == place)
                    def _(place=place):
                        for which, piece in enumerate(qkv_b):
                            start = base + which * width + place * local
                            table[:, start : start + local] = piece
                        for start, ref in zip(local_at, own_refs):
                            size = ref.shape[1]
                            table[:, start + place * size : start + (place + 1) * size] = ref[...]
                for which in range(2):
                    @pl.when(core == which)
                    def _(which=which):
                        swap_out[...] = table[:, (1 - which) * half_e : (2 - which) * half_e].astype(BF)

                swap.start()

            @pl.when(number == 3 * pace)
            def _():
                swap.wait()
                for which in range(2):
                    @pl.when(core == which)
                    def _(which=which):
                        for part in range(count):
                            at = slice(part * own_rows, (part + 1) * own_rows)
                            mine = table[at, which * half_e : (which + 1) * half_e]
                            partial_e[part] = (mine + swap_in[at, :].astype(F32)).astype(BF)

            @pl.when((number >= steps) & (number < steps + count - 1))
            def _():
                early_step(number - steps)

            @pl.when(number == steps - 1)
            def _():
                line_gather_step(block_line, 0, ball)

        def after(slot):
            @pl.when(slot % each == each - 1)
            def _():
                skip_block(slot // each)

        product(0)
        await_all(everyone)
        line_reduce_all(
            grad_line, steps, compute, partial_g, left_g, right_g, sr_g, sl_g, finish, beside, after
        )

        g_shift = g_sum[...]
        shift_in[0] = g_shift
        swap_shift = push(shift_in.at[0], shift_in.at[1], ssem.at[2], rsem.at[2], peer)
        swap_shift.start()
        mod_u = dot_nt(act_low, down_of(dtab, 1))
        once = jnp.where(me == 0, 1.0, 0.0)
        shift_u = dot_nt(g_shift.astype(BF), up_of(utab, 1))
        zeros_u, zeros_w = jnp.zeros((7, RANK), F32), jnp.zeros((7, width), F32)
        mod_a = jnp.concatenate([shift_u * once, zeros_u], axis=0).astype(BF)
        mod_b = jnp.concatenate([mod_u * once, zeros_u], axis=0).astype(BF)
        act_pad = jnp.concatenate([act_low.astype(F32), zeros_w], axis=0).astype(BF)
        shift_pad = jnp.concatenate([g_shift, zeros_w], axis=0).astype(BF)
        late[:, IN_AT[1] : IN_AT[2]] = dot_tn(mod_a, act_pad)
        late[:, EARLY_A + OUT_AT[1] : EARLY_A + OUT_AT[2]] = dot_tn(mod_b, shift_pad)
        for which in range(2):
            @pl.when(core == which)
            def _(which=which):
                late_out[...] = late[:, (1 - which) * half_l : (2 - which) * half_l].astype(BF)

        swap_late = push(late_out, late_in, ssem.at[1], rsem.at[1], peer)
        swap_late.start()
        line_gather_step(block_line, 1, ball)
        line_scatter_finish(early_line, partial_e, left_e, right_e, sr_e, sl_e, summed)
        slots[dp] = summed[...].astype(BF)
        for send in sends:
            send.start()
        swap_shift.wait()
        shifts[dp] = shift_in[0] + shift_in[1]
        shift_sends = [
            push(shifts.at[dp], shifts.at[dp], msend.at[0, number], mrecv.at[0, number], device)
            for number, device in enumerate(peers)
        ]
        for send in shift_sends:
            send.start()
        swap_late.wait()
        for which in range(2):
            @pl.when(core == which)
            def _(which=which):
                for part in range(count):
                    at = slice(part * own_rows, (part + 1) * own_rows)
                    mine = late[at, which * half_l : (which + 1) * half_l]
                    partial_l[part] = (mine + late_in[at, :].astype(F32)).astype(BF)

        late_sends = [
            push(partial_l.at[xor_place(me, number + 1)], slots_l.at[me], zsend.at[number], zrecv.at[number], device)
            for number, device in enumerate(z_peers)
        ]
        for send in late_sends:
            send.start()
        slots_l[me] = partial_l[me]
        line_gather_step(block_line, 2, ball)
        for number in (1, 2, 3):
            source = shifts.at[xor_place(dp, number)]
            push(source, source, msend.at[0, number - 1], mrecv.at[0, number - 1], peers[number - 1]).wait_recv()
        every = jnp.concatenate([shifts[sequence] for sequence in range(4)], axis=0).astype(BF)
        products = dot_nt(every, wm[...])
        for sequence in range(4):
            act_out[sequence] = products[sequence : sequence + 1]
        act_sends = [
            push(act_out.at[xor_place(dp, number)], act_in.at[dp], msend.at[1, number - 1], mrecv.at[1, number - 1],
                 peers[number - 1])
            for number in (1, 2, 3)
        ]
        for send in act_sends:
            send.start()
        for number in range(count - 1):
            arrived = slots_l.at[xor_place(me, number + 1)]
            push(arrived, arrived, zsend.at[number], zrecv.at[number], z_peers[number]).wait_recv()
        late_sum = slots_l[0].astype(F32)
        for place in range(1, count):
            late_sum = late_sum + slots_l[place].astype(F32)
        late_slots[dp] = late_sum.astype(BF)
        later_sends = [
            push(late_slots.at[dp], late_slots.at[dp], dsend.at[1, number], drecv.at[1, number], device)
            for number, device in enumerate(peers)
        ]
        for send in later_sends:
            send.start()

        def arrive(ref, which):
            for number in (1, 2, 3):
                source = ref.at[xor_place(dp, number)]
                push(source, source, dsend.at[which, number - 1], drecv.at[which, number - 1], peers[number - 1]).wait_recv()

        def total(ref, which):
            slot = (dp * 2 + which).astype(F32)
            result = jnp.zeros(ref.shape[1:], F32)
            for sequence in range(4):
                chosen = jnp.where(act_ref[sequence, :, width : width + 1] == slot, 1.0, 0.0)
                result = result + ref[sequence].astype(F32) * chosen
            return result

        arrive(slots, 0)
        other_out[...] = total(slots, 1 - core).astype(BF)
        last = push(other_out, other_in, ssem.at[3], rsem.at[3], peer)
        last.start()
        mine_e = total(slots, core)
        line_gather_step(block_line, 3, ball)
        arrive(late_slots, 1)
        later_out[...] = total(late_slots, 1 - core).astype(BF)
        latest = push(later_out, later_in, ssem.at[4], rsem.at[4], peer)
        latest.start()
        mine_l = total(late_slots, core)

        act_in[dp] = act_out[dp]
        for number in (1, 2, 3):
            source = act_in.at[xor_place(dp, number)]
            push(source, source, msend.at[1, number - 1], mrecv.at[1, number - 1], peers[number - 1]).wait_recv()
        for place in range(4):
            g_act[:, place * mod_rows : (place + 1) * mod_rows] = act_in[place]
        full_u = dot_nt(shifts[dp].astype(BF), up_of(utab, 1)).astype(BF)
        grad = g_act[...] + dot_nn(full_u, down_of(dtab, 1))
        value = cond[...].astype(F32)
        gate = 1.0 / (1.0 + jnp.exp(-value))
        whole_c = grad * gate * (1.0 + value * (1.0 - gate))
        size_c = width // (2 * count)
        for place in range(2 * count):
            @pl.when(core * count + me == place)
            def _(place=place):
                out_c[...] = whole_c[:, place * size_c : (place + 1) * size_c]


        def lay(mine, arrived, target):
            for which in range(2):
                @pl.when(core == which)
                def _(which=which):
                    target(which, mine)
                    target(1 - which, arrived[...].astype(F32))

        def lay_early(which, values):
            start = which * half_e
            low_a = max(0, min(base - start, half_e))
            if low_a:
                out_a[:, EARLY_A + start : EARLY_A + start + low_a] = values[:, :low_a]
            if low_a < half_e:
                at = EARLY_B + start + low_a - base
                out_b[:, at : at + min(half_e, EARLY - start) - low_a] = values[:, low_a : min(half_e, EARLY - start)]

        def lay_late(which, values):
            start = which * half_l
            low_a = max(0, min(EARLY_A - start, half_l))
            end = min(half_l, LATE - start)
            if low_a:
                out_a[:, start : start + low_a] = values[:, :low_a]
            if low_a < end:
                at = start + low_a - EARLY_A
                out_b[:, at : at + end - low_a] = values[:, low_a:end]

        last.wait_recv()
        lay(mine_e, other_in, lay_early)
        latest.wait_recv()
        lay(mine_l, later_in, lay_late)
        line_gather_drain(block_line, ball)
        last.wait_send()
        latest.wait_send()
        for send in sends + later_sends + shift_sends + act_sends + late_sends:
            send.wait_send()

        def drain(number, carry):
            rows = rows_of(number, block)
            pltpu.make_async_copy(buf_h.at[number], out_h.at[rows, :], osem.at[0, number]).wait()
            pltpu.make_async_copy(buf_l.at[number], out_l.at[rows, :], osem.at[1, number]).wait()
            return carry

        lax.fori_loop(0, count, drain, 0)

    part_e = (own_rows, half_e)
    part_l = (own_rows, half_l)
    return call(
        kernel,
        [(array, True) for array in (*grads, *projections)]
        + [(array, False) for array in (attn_in, g_first, skip_out, hidden, long_skip, weight, mod_weight)]
        + [(array, True) for array in (block_sum, gain_halves, gain_rows, *tables, condition, act_all, *wide, *own_grads,
                                       *stack)],
        [
            ((tokens, width), F32, False),
            ((tokens, width), F32, False),
            ((own_rows, IN_AT[12]), F32, True),
            ((own_rows, OUT_AT[12]), F32, True),
            ((1, width // (2 * count)), F32, True),
            ((count, block, width), BF, True),
        ],
        [
            vmem(count, width, span),
            vmem(tokens, width), vmem(count, block, width), vmem(tokens, width, dtype=F32), vmem(tokens, width),
            vmem(tokens, width), vmem(mod_rows, width),
            vmem(count, block, width, dtype=F32),
            vmem(count, block, width, dtype=F32),
            vmem(block, 2 * width, dtype=F32),
            vmem(tokens, width, dtype=F32),
            vmem(3 * RANK, width),
            vmem(RANK, local), vmem(RANK, local), vmem(RANK, local),
        ]
        + [vmem(steps, chunk, width) for _ in range(5)]
        + [vmem(RANK, 2 * half_e, dtype=F32), vmem(RANK, 2 * half_l, dtype=F32), vmem(RANK, half_e), vmem(RANK, half_e)]
        + [vmem(count, *part_e) for _ in range(5)]
        + [vmem(*part_e, dtype=F32), vmem(RANK, half_l), vmem(RANK, half_l), vmem(count, *part_l), vmem(count, *part_l)]
        + [vmem(4, *part_e), vmem(4, *part_l), vmem(*part_e), vmem(*part_e), vmem(*part_l), vmem(*part_l)]
        + [vmem(4, 1, width, dtype=F32), vmem(2, 1, width, dtype=F32), vmem(4, 1, mod_rows, dtype=F32),
           vmem(4, 1, mod_rows, dtype=F32), vmem(1, width, dtype=F32), vmem(1, width, dtype=F32)]
        + [dma(7), dma(2, count), dma(5), dma(5), dma(2, 3), dma(2, 3), dma(2, 3), dma(2, 3), dma(count), dma(count)]
        + [dma(steps) for _ in range(4)] + [dma(count) for _ in range(8)],
        collective=5,
        cost=cost_of(4 * tokens * width * width, 30e6),
    )


def prepare(index, down_factor, up_factor, gain, transposed):
    def kernel(index_ref, down_ref, up_ref, gain_ref, *refs):
        count = len(transposed)
        weight_refs, (down_out, up_out, gain_out), outs = refs[:count], refs[count : count + 3], refs[count + 3 :]
        down_out[...] = down_ref[0]
        up_out[...] = up_ref[0]
        gain_out[0, :] = gain_ref[:MODEL_WIDTH]
        gain_out[1, :] = gain_ref[MODEL_WIDTH:]
        for source, target in zip(weight_refs, outs):
            target[...] = source[...].T

    def whole(shape):
        return pl.BlockSpec(shape, lambda step, index_ref: (0,) * len(shape))

    shapes = [down_factor.shape[1:], up_factor.shape[1:]]
    out_shapes = [(shape, BF) for shape in shapes] + [((2, MODEL_WIDTH), F32)]
    out_shapes += [(weight.shape[::-1], BF) for weight in transposed]
    return pl.pallas_call(
        kernel,
        grid_spec=pltpu.PrefetchScalarGridSpec(
            num_scalar_prefetch=1,
            grid=(1,),
            in_specs=[pl.BlockSpec((1, *shape), lambda step, index_ref: (index_ref[0], 0, 0)) for shape in shapes]
            + [whole((2 * MODEL_WIDTH,))] + [whole(weight.shape) for weight in transposed],
            out_specs=[whole(shape) for shape, _ in out_shapes],
        ),
        out_shape=[jax.ShapeDtypeStruct(shape, dtype) for shape, dtype in out_shapes],
        compiler_params=pltpu.CompilerParams(vmem_limit_bytes=VMEM_BYTES),
    )(index, down_factor, up_factor, gain, *transposed)


def fused_body(
    hidden,
    long_skip_input,
    condition,
    projected_text_tokens,
    sequence_adapter_index,
    skip_projection_weight,
    shift_modulation_weight,
    self_query_weight,
    self_key_weight,
    self_value_weight,
    attention_output_weight,
    cross_query_weight,
    cross_key_weight,
    cross_value_weight,
    cross_output_weight,
    feedforward_up_weight,
    feedforward_down_weight,
    skip_norm_gain,
    norm_gain_rows,
    adapter_down_factor,
    adapter_up_factor,
    cotangent,
):
    rank = lax.axis_index("tensor")
    count = lax.axis_size("tensor")
    core = lax.axis_index("ctx")
    dp = lax.axis_index("dp")
    hidden, long_skip, text, cot = hidden[0], long_skip_input[0], projected_text_tokens[0], cotangent[0]
    local = self_query_weight.shape[1]
    heads = local // HD
    down_table, up_table, gain_halves, skip_t, attn_out_t, cross_out_t = prepare(
        sequence_adapter_index, adapter_down_factor, adapter_up_factor, skip_norm_gain,
        (skip_projection_weight, attention_output_weight, cross_output_weight),
    )
    tables = (down_table, up_table)

    weights = {
        "skip": skip_t,
        "q": self_query_weight,
        "k": self_key_weight,
        "v": self_value_weight,
        "o": attn_out_t,
        "ck": cross_key_weight.T,
        "cv": cross_value_weight.T,
        "cq": cross_query_weight,
        "co": cross_out_t,
        "up": feedforward_up_weight,
        "dn": feedforward_down_weight.T,
    }
    (skip_out, attn_in, query, keys, values, low, logs, inv_q, inv_k, summed, act_all, text_kv, wq, wk, wv, wo, wcq, wco,
     wup) = front(
        count, heads, condition, sequence_adapter_index, hidden, long_skip, text, weights, shift_modulation_weight,
        gain_halves, norm_gain_rows, tables,
    )
    (g_first, block_sum, g_cq_a, g_cq_b, g_ck_a, g_ck_b, g_cv_a, g_cv_b, g_co_a, g_co_b, g_up_a, g_up_b, g_down_a, g_down_b,
     skip_all) = middle(
        count, heads, summed, skip_out, wcq, wco, wup, weights["dn"], weights["skip"], text_kv, text,
        cot.reshape(count, 2, -1, MODEL_WIDTH), norm_gain_rows, tables,
    )
    gq, gk, gv, g_first_all, g_o_a, g_o_b = attention_backward(
        count, heads, g_first, query, keys, values, low, logs, inv_q, inv_k, wo, tables
    )
    base = IN_AT[12]
    hidden_grad, skip_grad, grad_down, grad_up, g_condition, block_all = back_end(
        count, (gq, gk, gv), (wq, wk, wv), attn_in, g_first_all, skip_out, hidden, long_skip, skip_all,
        shift_modulation_weight, block_sum, gain_halves, norm_gain_rows, tables, condition, act_all,
        {
            IN_AT[6]: g_cq_a, IN_AT[7]: g_ck_a, IN_AT[8]: g_cv_a, IN_AT[10]: g_up_a,
            base + OUT_AT[5]: g_o_b, base + OUT_AT[9]: g_co_b, base + OUT_AT[11]: g_down_b,
        },
        {IN_AT[5]: g_o_a, IN_AT[11]: g_down_a},
        {OUT_AT[10]: g_up_b},
        {
            IN_AT[9]: g_co_a, base + OUT_AT[6]: g_cq_b, base + OUT_AT[7]: g_ck_b, base + OUT_AT[8]: g_cv_b,
        },
    )
    block_out = block_all.reshape(hidden.shape)
    condition_gradient = g_condition[0]
    return (
        block_out[None],
        hidden_grad[None],
        skip_grad[None],
        condition_gradient,
        grad_down.reshape(-1),
        grad_up.reshape(-1),
    )


def solution(mesh):
    in_specs = (
        P("dp", "ctx", None),
        P("dp", "ctx", None),
        P("dp", None),
        P("dp", None, None),
        P("dp"),
        P("tensor", "dp"),
        P("dp", None),
        P("dp", "tensor"),
        P("dp", "tensor"),
        P("dp", "tensor"),
        P("tensor", "dp"),
        P("dp", "tensor"),
        P("dp", "tensor"),
        P("dp", "tensor"),
        P("tensor", "dp"),
        P("dp", "tensor"),
        P("tensor", "dp"),
        P(),
        P(),
        P(),
        P(),
        P("dp", "ctx", None),
    )
    out_specs = (
        P("dp", "ctx", None),
        P("dp", "ctx", None),
        P("dp", "ctx", None),
        P(("dp", "ctx", "tensor")),
        P(("dp", "ctx", "tensor")),
        P(("dp", "ctx", "tensor")),
    )
    shape = mesh.shape
    fused = shape["dp"] == 4 and shape["ctx"] == 2 and shape["tensor"] == 4
    return jax.shard_map(fused_body if fused else body, mesh=mesh, in_specs=in_specs, out_specs=out_specs, check_vma=False)
```
